32 devices in a mesh: dp: 8 (over z, x), mp: 4 (over y, core).
Axes of the slice: x: 2, y: 2, z: 4, core: 2. Of those that a mesh axis runs over, the one named last changes fastest.
Arguments:
- noisy_rows: bfloat16 [16384, 768], P('dp'), may hold values from -6 to 6
- clean_rows: bfloat16 [16384, 768], P('dp'), may hold values from -6 to 6
- block_size: int32 [16], P('dp'), may hold values from 4 to 16, as said below
- cotangent: bfloat16 [16384, 768], P('dp'), may hold values from -6 to 6
- norm_gains: float32 [2, 768], replicated, may hold values from 0.5 to 1.5
- weight_qkv: bfloat16 [768, 2304], P(None, 'mp'), may hold values from -0.21875 to 0.21875
- weight_out: bfloat16 [768, 768], P('mp'), may hold values from -1.75 to 1.75
- weight_up: bfloat16 [768, 3072], P(None, 'mp'), may hold values from -0.21875 to 0.21875
- weight_down: bfloat16 [3072, 768], P('mp'), may hold values from -0.109375 to 0.109375
- master_qkv: float32 [768, 2304], P('dp', 'mp'), may hold values from -0.21875 to 0.21875
- master_out: float32 [768, 768], P('mp', 'dp'), may hold values from -1.75 to 1.75
- master_up: float32 [768, 3072], P('dp', 'mp'), may hold values from -0.21875 to 0.21875
- master_down: float32 [3072, 768], P('mp', 'dp'), may hold values from -0.109375 to 0.109375
- moment_qkv: float32 [768, 2304], P('dp', 'mp'), may hold values from -28 to 28
- moment_out: float32 [768, 768], P('mp', 'dp'), may hold values from -6 to 6
- moment_up: float32 [768, 3072], P('dp', 'mp'), may hold values from -56 to 56
- moment_down: float32 [3072, 768], P('mp', 'dp'), may hold values from -56 to 56
- average_qkv: float32 [768, 2304], P('dp', 'mp'), may hold values from -0.21875 to 0.21875
- average_out: float32 [768, 768], P('mp', 'dp'), may hold values from -1.75 to 1.75
- average_up: float32 [768, 3072], P('dp', 'mp'), may hold values from -0.21875 to 0.21875
- average_down: float32 [3072, 768], P('mp', 'dp'), may hold values from -0.109375 to 0.109375
- error_qkv: float32 [8, 768, 2304], P('dp', None, 'mp'), may hold values from -112 to 112
- error_out: float32 [8, 768, 768], P('dp', 'mp'), may hold values from -40 to 40
- error_up: float32 [8, 768, 3072], P('dp', None, 'mp'), may hold values from -192 to 192
- error_down: float32 [8, 3072, 768], P('dp', 'mp'), may hold values from -192 to 192
- factor_qkv: float32 [2304, 8], P('mp'), may hold values from -6 to 6
- factor_out: float32 [768, 32], P(None, 'mp'), may hold values from -6 to 6
- factor_up: float32 [3072, 8], P('mp'), may hold values from -6 to 6
- factor_down: float32 [768, 32], P(None, 'mp'), may hold values from -6 to 6
- gain_moment: float32 [2, 768], replicated, may hold values from -56 to 56
Outputs:
- block_out: bfloat16 [16384, 768], P('dp')
- grad_noisy: bfloat16 [16384, 768], P('dp')
- grad_clean: bfloat16 [16384, 768], P('dp')
- gain_grad: float32 [2, 768], replicated
- new_gains: float32 [2, 768], replicated
- new_gain_moment: float32 [2, 768], replicated
- new_master_qkv: float32 [768, 2304], P('dp', 'mp')
- new_master_out: float32 [768, 768], P('mp', 'dp')
- new_master_up: float32 [768, 3072], P('dp', 'mp')
- new_master_down: float32 [3072, 768], P('mp', 'dp')
- new_moment_qkv: float32 [768, 2304], P('dp', 'mp')
- new_moment_out: float32 [768, 768], P('mp', 'dp')
- new_moment_up: float32 [768, 3072], P('dp', 'mp')
- new_moment_down: float32 [3072, 768], P('mp', 'dp')
- new_average_qkv: float32 [768, 2304], P('dp', 'mp')
- new_average_out: float32 [768, 768], P('mp', 'dp')
- new_average_up: float32 [768, 3072], P('dp', 'mp')
- new_average_down: float32 [3072, 768], P('mp', 'dp')
- new_error_qkv: float32 [8, 768, 2304], P('dp', None, 'mp')
- new_error_out: float32 [8, 768, 768], P('dp', 'mp')
- new_error_up: float32 [8, 768, 3072], P('dp', None, 'mp')
- new_error_down: float32 [8, 3072, 768], P('dp', 'mp')
- left_qkv: float32 [768, 32], P(None, 'mp')
- left_out: float32 [768, 8], P('mp')
- left_up: float32 [768, 32], P(None, 'mp')
- left_down: float32 [3072, 8], P('mp')
- right_qkv: float32 [2304, 8], P('mp')
- right_out: float32 [768, 32], P(None, 'mp')
- right_up: float32 [3072, 8], P('mp')
- right_down: float32 [768, 32], P(None, 'mp')
The draws below stay inside these ranges and needn't reach their ends.
Inputs may be any that keep to these rules, and one draw needn't show every extreme that they name: `block_size`: each sequence's block size is 4, 8 or 16; both 4 and 16 occur.
All inputs are finite; a program needn't handle non-finite values.
Results may differ from the reference program's by a relative error of at most 0.017.
The reference program's roundings to bfloat16 on the way count: a program that leaves them out, or rounds other values in their place, can miss the bound.
Values may be sent and summed in bfloat16 or wider, within the bound.
A program may use at most 192 MiB of HBM per device.

```python
import math
import jax
import jax.numpy as jnp
from jax import lax

D = 768
HEADS = 12
HD = 64
FF = 3072
LEN = 1024
SEQ_DEV = 2
RANK = 8
EMA_STEPS = 4
SEQS = 16
TOKENS = 16384
N_DP = 8
N_MP = 4


def draw_block_size(key, part):
    picked = jax.random.randint(key, (SEQS,), 0, 3)
    picked = picked.at[0].set(2).at[1].set(0)
    size_table = jnp.array([4, 8, 16], dtype=jnp.int32)
    return size_table[picked].astype(jnp.int32)


def with_spikes(values, stream_key, source, target, blocks, factor):
    owner, partner = [(jnp.arange(values.shape[axis_at]) // (values.shape[axis_at] // blocks)).reshape([-1 if axis == axis_at else 1 for axis in range(values.ndim)]) for axis_at in (source, target)]
    chosen = jax.random.permutation(stream_key, blocks)[partner]
    strong = (owner == chosen) | (owner == (partner + blocks // 2) % blocks)
    return jnp.where(strong, factor * values, values)


def levels(stream_key, shape, shards, smallest, high):
    loudness = 1.0
    for dim, parts in shards:
        steps = jax.random.uniform(jax.random.fold_in(jax.random.fold_in(stream_key, 6), dim), (parts,), jnp.float32, smallest / len(shards), high / len(shards))
        loudness = loudness * jnp.repeat(jnp.exp(steps), shape[dim] // parts).reshape((-1,) + (1,) * (len(shape) - 1 - dim))
    return loudness


def gaussian(own_key, shape, spread, limit, shards=(), held_as=jnp.bfloat16):
    factor_of = levels(own_key, shape, shards, -0.22, 0.18) if shards else 1.0
    values = jax.random.normal(own_key, shape, jnp.float32) * spread * factor_of
    return jnp.minimum(jnp.maximum(values, -limit), limit).astype(held_as)


def bell_draw_with(own_key, extent, deviation, limit, shards, heavy, kind=jnp.bfloat16):
    values = deviation * jax.random.normal(own_key, extent, jnp.float32)
    if shards:
        values = values * levels(own_key, extent, shards, -0.22, 0.18)
    return jnp.clip(with_spikes(values, jax.random.fold_in(own_key, 3), *heavy), -limit, limit).astype(kind)


def setup_inputs(seed: int = 0) -> dict:
    splits = jax.random.split(jax.random.key(seed), 31)
    return {
        "noisy_rows": gaussian(splits[0], (TOKENS, D), 1.0, 6.0, ((0, 8),)),
        "clean_rows": gaussian(splits[1], (TOKENS, D), 1.0, 6.0, ((0, 8),)),
        "block_size": draw_block_size(jax.random.fold_in(splits[30], 71), 0),
        "cotangent": gaussian(splits[3], (TOKENS, D), 1.0, 6.0, ((0, 8),)),
        "norm_gains": jnp.clip(1.0 + 0.1 * jax.random.normal(splits[4], (2, D), jnp.float32), 0.5, 1.5),
        "weight_qkv": gaussian(splits[5], (D, 3 * HEADS * HD), D ** -0.5, 0.21875, ((1, 4),)),
        "weight_out": gaussian(splits[6], (HEADS * HD, D), (HEADS * HD // 64) ** -0.5, 1.75, ((0, 4),)),
        "weight_up": gaussian(splits[7], (D, FF), D ** -0.5, 0.21875, ((1, 4),)),
        "weight_down": gaussian(splits[8], (FF, D), FF ** -0.5, 0.109375, ((0, 4),)),
        "master_qkv": gaussian(splits[9], (D, 3 * HEADS * HD), D ** -0.5, 0.21875, ((0, 8), (1, 4)), jnp.float32),
        "master_out": gaussian(splits[10], (HEADS * HD, D), (HEADS * HD // 64) ** -0.5, 1.75, ((0, 4), (1, 8)), jnp.float32),
        "master_up": gaussian(splits[11], (D, FF), D ** -0.5, 0.21875, ((0, 8), (1, 4)), jnp.float32),
        "master_down": gaussian(splits[12], (FF, D), FF ** -0.5, 0.109375, ((0, 4), (1, 8)), jnp.float32),
        "moment_qkv": gaussian(splits[13], (D, 3 * HEADS * HD), (0.1 * (SEQ_DEV * LEN) ** 0.5), 28.0, ((0, 8), (1, 4)), jnp.float32),
        "moment_out": gaussian(splits[14], (HEADS * HD, D), (0.05 * (SEQ_DEV * LEN) ** 0.5), 6.0, ((0, 4), (1, 8)), jnp.float32),
        "moment_up": gaussian(splits[15], (D, FF), (0.2 * (SEQ_DEV * LEN) ** 0.5), 56.0, ((0, 8), (1, 4)), jnp.float32),
        "moment_down": gaussian(splits[16], (FF, D), (0.2 * (SEQ_DEV * LEN) ** 0.5), 56.0, ((0, 4), (1, 8)), jnp.float32),
        "average_qkv": gaussian(splits[17], (D, 3 * HEADS * HD), D ** -0.5, 0.21875, ((0, 8), (1, 4)), jnp.float32),
        "average_out": gaussian(splits[18], (HEADS * HD, D), (HEADS * HD // 64) ** -0.5, 1.75, ((0, 4), (1, 8)), jnp.float32),
        "average_up": gaussian(splits[19], (D, FF), D ** -0.5, 0.21875, ((0, 8), (1, 4)), jnp.float32),
        "average_down": gaussian(splits[20], (FF, D), FF ** -0.5, 0.109375, ((0, 4), (1, 8)), jnp.float32),
        "error_qkv": bell_draw_with(splits[21], (N_DP, D, 3 * HEADS * HD), (0.3 * (SEQ_DEV * LEN) ** 0.5), 112.0, ((0, 8), (2, 4)), (0, 1, 8, 2.0), jnp.float32),
        "error_out": bell_draw_with(splits[22], (N_DP, HEADS * HD, D), (0.1 * (SEQ_DEV * LEN) ** 0.5), 40.0, ((0, 8), (1, 4)), (0, 2, 8, 2.0), jnp.float32),
        "error_up": bell_draw_with(splits[23], (N_DP, D, FF), (0.5 * (SEQ_DEV * LEN) ** 0.5), 192.0, ((0, 8), (2, 4)), (0, 1, 8, 2.0), jnp.float32),
        "error_down": bell_draw_with(splits[24], (N_DP, FF, D), (0.5 * (SEQ_DEV * LEN) ** 0.5), 192.0, ((0, 8), (1, 4)), (0, 2, 8, 2.0), jnp.float32),
        "factor_qkv": gaussian(splits[25], (3 * HEADS * HD, RANK), 1.0, 6.0, ((0, 4),), jnp.float32),
        "factor_out": gaussian(splits[26], (D, N_MP * RANK), 1.0, 6.0, ((1, 4),), jnp.float32),
        "factor_up": gaussian(splits[27], (FF, RANK), 1.0, 6.0, ((0, 4),), jnp.float32),
        "factor_down": gaussian(splits[28], (D, N_MP * RANK), 1.0, 6.0, ((1, 4),), jnp.float32),
        "gain_moment": gaussian(splits[29], (2, D), (0.2 * (SEQ_DEV * LEN) ** 0.5), 56.0, (), jnp.float32),
    }


@jax.custom_vjp
def low(v):
    return lax.optimization_barrier(v.astype(jnp.bfloat16)).astype(jnp.float32)

@jax.custom_vjp
def low_back(v):
    return v

def low_keep(v):
    return (low(v), None)

def low_pass(kept, grad):
    return (grad,)

def back_keep(v):
    return (v, None)

def back_low(kept, grad):
    return (low(grad),)
low.defvjp(low_keep, low_pass)
low_back.defvjp(back_keep, back_low)
highest = lax.Precision.HIGHEST
norm_eps = 1e-05
gelu_coef = 0.7978845608028654
masked_score = -1e+30

def layer_norm(values, gain_vector):
    centered = values - lax.optimization_barrier(jnp.mean(values, axis=-1, keepdims=True))
    variance = lax.optimization_barrier(jnp.mean(centered * centered, axis=-1, keepdims=True))
    return centered * lax.rsqrt(variance + norm_eps) * gain_vector

def gelu_tanh(values):
    return 0.5 * values * (1.0 + jnp.tanh(gelu_coef * (values + 0.044715 * values * values * values)))

def rotary_tables(row_count):
    position = (jnp.arange(row_count) % LEN).astype(jnp.float32)
    half_dim = HD // 2
    inverse = jnp.exp(jnp.arange(half_dim).astype(jnp.float32) * (-2.0 * math.log(10000.0) / HD))
    angle = position[:, None] * inverse[None, :]
    return (jnp.cos(angle)[:, None, :], jnp.sin(angle)[:, None, :])

def rotate(values, cosine, sine):
    half_dim = HD // 2
    first_half = values[..., :half_dim]
    second_half = values[..., half_dim:]
    return jnp.concatenate([first_half * cosine - second_half * sine, first_half * sine + second_half * cosine], axis=-1)

def key_mask(block_len):
    place = jnp.arange(LEN, dtype=jnp.int32) // block_len
    same_block = place[:, None] == place[None, :]
    earlier = place[None, :] < place[:, None]
    return jnp.concatenate([same_block, earlier], axis=1)

def attend(mapped):
    query, key_all, value_all, block_len = mapped
    raw_scores = jnp.einsum('qhd,khd->hqk', query, key_all, precision=highest) * (1.0 / math.sqrt(HD))
    scores = jnp.where(key_mask(block_len)[None], low_back(raw_scores), masked_score)
    row_peak = lax.optimization_barrier(jnp.max(scores, axis=-1, keepdims=True))
    exponent = jnp.exp(scores - row_peak)
    softmax_rows = exponent / lax.optimization_barrier(jnp.sum(exponent, axis=-1, keepdims=True))
    return jnp.einsum('hqk,khd->qhd', low(softmax_rows), value_all, precision=highest)

def block_forward(x_noisy, x_clean, gain_pair, weight_qkv, weight_out, weight_up, weight_down, block_sizes):
    row_count = x_noisy.shape[0]
    seq_count = row_count // LEN
    normed_noisy = low(layer_norm(x_noisy, gain_pair[0]))
    normed_clean = low(layer_norm(x_clean, gain_pair[0]))
    split_qkv = weight_qkv.reshape(D, HEADS, 3, HD)
    weight_query = split_qkv[:, :, 0, :].reshape(D, HEADS * HD)
    weight_kv = split_qkv[:, :, 1:, :].reshape(D, HEADS * 2 * HD)
    cosine, sine = rotary_tables(row_count)
    raw_query = low_back(jnp.dot(normed_noisy, weight_query, precision=highest)).reshape(row_count, HEADS, HD)
    query = low(rotate(raw_query, cosine, sine))
    kv_noisy = low_back(jnp.dot(normed_noisy, weight_kv, precision=highest)).reshape(row_count, HEADS, 2, HD)
    kv_clean = low_back(jnp.dot(normed_clean, weight_kv, precision=highest)).reshape(row_count, HEADS, 2, HD)
    key_noisy = low(rotate(kv_noisy[:, :, 0, :], cosine, sine))
    key_clean = low(rotate(kv_clean[:, :, 0, :], cosine, sine))
    value_noisy = low(kv_noisy[:, :, 1, :])
    value_clean = low(kv_clean[:, :, 1, :])
    shape_seq = (seq_count, LEN, HEADS, HD)
    key_all = jnp.concatenate([key_noisy.reshape(shape_seq), key_clean.reshape(shape_seq)], axis=1)
    value_all = jnp.concatenate([value_noisy.reshape(shape_seq), value_clean.reshape(shape_seq)], axis=1)
    attended = lax.map(jax.checkpoint(attend), (query.reshape(shape_seq), key_all, value_all, block_sizes))
    attended = low(low_back(attended.reshape(row_count, HEADS * HD)))
    residual = x_noisy + low_back(jnp.dot(attended, weight_out, precision=highest))
    normed_mid = low(layer_norm(residual, gain_pair[1]))
    hidden = low(gelu_tanh(low_back(jnp.dot(normed_mid, weight_up, precision=highest))))
    return residual + low_back(jnp.dot(hidden, weight_down, precision=highest))

def orthonormal(matrix):
    columns = []
    for position in range(matrix.shape[1]):
        column = matrix[:, position]
        for earlier in columns:
            column = column - jnp.sum(earlier * column) * earlier
        column = column / (jnp.sqrt(jnp.sum(column * column)) + 1e-08)
        columns.append(column)
    return jnp.stack(columns, axis=1)

def power_step(stacked, factors):
    left_side = jnp.einsum('rpmn,pnk->pmk', stacked, factors, precision=highest)
    left_hat = jax.vmap(orthonormal)(left_side)
    right_side = jnp.einsum('rpmn,pmk->pnk', stacked, left_hat, precision=highest) / N_DP
    approx = jnp.einsum('pmk,pnk->pmn', left_hat, right_side, precision=highest)
    return (left_hat, right_side, approx)

def by_columns(gradients, error, factor):
    rows_a = gradients.shape[1]
    cols_b = gradients.shape[2]
    block_width = cols_b // N_MP
    stacked = (gradients + error).reshape(N_DP, rows_a, N_MP, block_width).transpose(0, 2, 1, 3)
    left_hat, right_side, approx = power_step(stacked, factor.reshape(N_MP, block_width, RANK))
    new_error = (stacked - approx[None]).transpose(0, 2, 1, 3).reshape(N_DP, rows_a, cols_b)
    left_full = left_hat.transpose(1, 0, 2).reshape(rows_a, N_MP * RANK)
    right_full = right_side.reshape(cols_b, RANK)
    approx_full = approx.transpose(1, 0, 2).reshape(rows_a, cols_b)
    return (new_error, left_full, right_full, approx_full)

def by_rows(gradients, error, factor):
    rows_a = gradients.shape[1]
    cols_b = gradients.shape[2]
    block_height = rows_a // N_MP
    stacked = (gradients + error).reshape(N_DP, N_MP, block_height, cols_b)
    left_hat, right_side, approx = power_step(stacked, factor.reshape(cols_b, N_MP, RANK).transpose(1, 0, 2))
    new_error = (stacked - approx[None]).reshape(N_DP, rows_a, cols_b)
    left_full = left_hat.reshape(rows_a, RANK)
    right_full = right_side.transpose(1, 0, 2).reshape(cols_b, N_MP * RANK)
    approx_full = approx.reshape(rows_a, cols_b)
    return (new_error, left_full, right_full, approx_full)

def advance(master, moment, average, approx, rate):
    decay = min(0.9999, (1.0 + EMA_STEPS) / (10.0 + EMA_STEPS))
    moment_new = 0.5 * moment + approx
    master_new = master - rate * moment_new
    average_new = decay * average + (1.0 - decay) * master_new
    return (master_new, moment_new, average_new)

def reference(noisy_rows, clean_rows, block_size, cotangent, norm_gains, weight_qkv, weight_out, weight_up, weight_down, master_qkv, master_out, master_up, master_down, moment_qkv, moment_out, moment_up, moment_down, average_qkv, average_out, average_up, average_down, error_qkv, error_out, error_up, error_down, factor_qkv, factor_out, factor_up, factor_down, gain_moment):
    row_count = SEQ_DEV * LEN
    full_qkv = weight_qkv.astype(jnp.float32)
    full_out = weight_out.astype(jnp.float32)
    full_up = weight_up.astype(jnp.float32)
    full_down = weight_down.astype(jnp.float32)

    def replica(mapped):
        part_noisy, part_clean, block_sizes, part_grad = mapped

        def forward(x_noisy, x_clean, gain_pair, w_qkv, w_out, w_up, w_down):
            return block_forward(x_noisy, x_clean, gain_pair, w_qkv, w_out, w_up, w_down, block_sizes)
        result, pullback = jax.vjp(forward, part_noisy.astype(jnp.float32), part_clean.astype(jnp.float32), norm_gains, full_qkv, full_out, full_up, full_down)
        grads_all = pullback(part_grad.astype(jnp.float32))
        return (result.astype(jnp.bfloat16), grads_all[0].astype(jnp.bfloat16), grads_all[1].astype(jnp.bfloat16), grads_all[2], grads_all[3], grads_all[4], grads_all[5], grads_all[6])
    results = lax.map(replica, (noisy_rows.reshape(N_DP, row_count, D), clean_rows.reshape(N_DP, row_count, D), block_size.reshape(N_DP, SEQ_DEV), cotangent.reshape(N_DP, row_count, D)))
    block_out = results[0].reshape(TOKENS, D)
    grad_noisy = results[1].reshape(TOKENS, D)
    grad_clean = results[2].reshape(TOKENS, D)
    gain_grad = lax.optimization_barrier(jnp.sum(results[3], axis=0)) / N_DP
    new_gain_moment = 0.5 * gain_moment + gain_grad
    new_gains = norm_gains - 0.5 / math.sqrt(SEQ_DEV * LEN) * new_gain_moment
    err_qkv, left_qkv, right_qkv, approx_qkv = by_columns(results[4], error_qkv, factor_qkv)
    err_out, left_out, right_out, approx_out = by_rows(results[5], error_out, factor_out)
    err_up, left_up, right_up, approx_up = by_columns(results[6], error_up, factor_up)
    err_down, left_down, right_down, approx_down = by_rows(results[7], error_down, factor_down)
    master_q, moment_q, average_q = advance(master_qkv, moment_qkv, average_qkv, approx_qkv, 3.0 / math.sqrt(D * SEQ_DEV * LEN))
    master_o, moment_o, average_o = advance(master_out, moment_out, average_out, approx_out, 3.0 / math.sqrt(HEADS * HD // 64 * SEQ_DEV * LEN))
    master_u, moment_u, average_u = advance(master_up, moment_up, average_up, approx_up, 3.0 / math.sqrt(D * SEQ_DEV * LEN))
    master_d, moment_d, average_d = advance(master_down, moment_down, average_down, approx_down, 3.0 / math.sqrt(FF * SEQ_DEV * LEN))
    return (block_out, grad_noisy, grad_clean, gain_grad, new_gains, new_gain_moment, master_q, master_o, master_u, master_d, moment_q, moment_o, moment_u, moment_d, average_q, average_o, average_u, average_d, err_qkv, err_out, err_up, err_down, left_qkv, left_out, left_up, left_down, right_qkv, right_out, right_up, right_down)
```

```python
import functools
import math

import jax
import jax.numpy as jnp
import numpy as np
from jax import lax
from jax.experimental import pallas as pl
from jax.experimental.pallas import tpu as pltpu
from jax.sharding import PartitionSpec as P

D = 768
HEADS = 12
HD = 64
FF = 3072
LEN = 1024
RANK = 8
EMA_STEPS = 4
TILE = 256
SLOT = 256

BF = jnp.bfloat16
F32 = jnp.float32
highest = lax.Precision.HIGHEST
norm_eps = 1e-05
gelu_coef = 0.7978845608028654
masked_score = -1e30
MESH_ID = pl.DeviceIdType.MESH


def nt(a, b):
    return lax.dot_general(a, b, (((1,), (1,)), ((), ())), preferred_element_type=F32)


def nn(a, b):
    return lax.dot_general(a, b, (((1,), (0,)), ((), ())), preferred_element_type=F32)


def tn(a, b):
    return lax.dot_general(a, b, (((0,), (0,)), ((), ())), preferred_element_type=F32)


def rotary_tables():
    half = HD // 2
    step = np.float32(-2.0 * math.log(10000.0) / HD)
    inverse = np.exp(np.arange(half, dtype=np.float32) * step).astype(np.float32)
    angle = (np.arange(LEN, dtype=np.float32)[:, None] * inverse[None, :]).astype(np.float32)
    c = np.cos(angle).astype(np.float32)
    s = np.sin(angle).astype(np.float32)
    return np.concatenate([c, c, c, c], 1), np.concatenate([-s, s, -s, s], 1)


def spin(v, cos, sin):
    lane = lax.broadcasted_iota(jnp.int32, v.shape, 1)
    low = lax.rem(lane, HD) < HD // 2
    swapped = jnp.where(low, pltpu.roll(v, 128 - HD // 2, 1), pltpu.roll(v, HD // 2, 1))
    return v * cos + swapped * sin


def block_ids(size, shape, dim):
    shift = 2 + (size >= 8).astype(jnp.int32) + (size >= 16).astype(jnp.int32)
    place = lax.broadcasted_iota(jnp.int32, shape, dim)
    return lax.shift_right_logical(place, jnp.full(shape, shift, jnp.int32))


def fill_bias(size, noisy_bias, clean_bias):
    keys = block_ids(size, (TILE, TILE), 0)
    rows = block_ids(size, (TILE, TILE), 1)
    noisy_bias[...] = jnp.where(rows == keys, 0.0, masked_score)
    clean_bias[...] = jnp.where(keys < rows, 0.0, masked_score)


def attend_kernel(size_ref, xn_ref, xc_ref, w_ref, cos_ref, sin_ref,
                  qn_ref, qc_ref, att_ref, lse_ref, bn_ref, bc_ref, kn_ref, kc_ref, vnt_ref, vct_ref):
    @pl.when(pl.program_id(0) == 0)
    def _():
        fill_bias(size_ref[0], bn_ref, bc_ref)

    w = w_ref[...]
    for src, dst, keys, vals in ((xn_ref, qn_ref, kn_ref, vnt_ref), (xc_ref, qc_ref, kc_ref, vct_ref)):
        a = nn(src[...], w)
        r = spin(a[:, :128], cos_ref[...], sin_ref[...]).astype(BF)
        v = a[:, 128:].astype(BF)
        dst[:, :128] = r
        dst[:, 128:] = v
        keys[...] = r[:, 64:128]
        vals[...] = jnp.transpose(v)[:64]
    for i in range(LEN // TILE):
        lo, hi = i * TILE, (i + 1) * TILE
        q = qn_ref[lo:hi, 0:64] * 0.125
        parts = [nt(kn_ref[lo:hi, :], q) + bn_ref[...], nt(kc_ref[lo:hi, :], q) + bc_ref[...]]
        if i:
            parts.append(nt(kc_ref[0:lo, :], q))
        peak = functools.reduce(jnp.maximum, [jnp.max(s, axis=0, keepdims=True) for s in parts])
        exps = [jnp.exp(s - peak) for s in parts]
        total = functools.reduce(jnp.add, [jnp.sum(e, axis=0, keepdims=True) for e in exps])
        inv = 1.0 / total
        low = [(e * inv).astype(BF) for e in exps]
        o = nn(vnt_ref[:, lo:hi], low[0]) + nn(vct_ref[:, lo:hi], low[1])
        if i:
            o = o + nn(vct_ref[:, 0:lo], low[2])
        att_ref[:, lo:hi] = o.astype(BF)
        lse_ref[0, :, lo:hi] = jnp.broadcast_to(peak + jnp.log(total), (8, TILE))


def fixed2(h):
    return (0, 0)


def lane2(h):
    return (0, h)


def row2(h):
    return (h, 0)


def row3(h):
    return (h, 0, 0)


def attend(size, xn, xc, w, cos, sin):
    heads = w.shape[1] // SLOT
    return pl.pallas_call(
        attend_kernel,
        grid=(heads,),
        in_specs=[
            pl.BlockSpec(memory_space=pltpu.SMEM),
            pl.BlockSpec((LEN, D), fixed2),
            pl.BlockSpec((LEN, D), fixed2),
            pl.BlockSpec((D, SLOT), lane2),
            pl.BlockSpec((LEN, 128), fixed2),
            pl.BlockSpec((LEN, 128), fixed2),
        ],
        out_specs=[
            pl.BlockSpec((LEN, SLOT), lane2),
            pl.BlockSpec((LEN, SLOT), lane2),
            pl.BlockSpec((HD, LEN), row2),
            pl.BlockSpec((1, 8, LEN), row3),
        ],
        out_shape=[
            jax.ShapeDtypeStruct((LEN, SLOT * heads), BF),
            jax.ShapeDtypeStruct((LEN, SLOT * heads), BF),
            jax.ShapeDtypeStruct((HD * heads, LEN), BF),
            jax.ShapeDtypeStruct((heads, 8, LEN), F32),
        ],
        scratch_shapes=[
            pltpu.VMEM((TILE, TILE), F32),
            pltpu.VMEM((TILE, TILE), F32),
            pltpu.VMEM((LEN, HD), BF),
            pltpu.VMEM((LEN, HD), BF),
            pltpu.VMEM((HD, LEN), BF),
            pltpu.VMEM((HD, LEN), BF),
        ],
        compiler_params=pltpu.CompilerParams(vmem_limit_bytes=40 << 20),
        cost_estimate=pl.CostEstimate(flops=6000000000, bytes_accessed=12000000, transcendentals=2800000),
        name="attend",
    )(size, xn, xc, w, cos, sin)


def attend_back_kernel(size_ref, qn_ref, qc_ref, att_ref, lse_ref, g_ref, wo_ref, cos_ref, sin_ref,
                       dn_ref, dc_ref, go_ref, bn_ref, bc_ref, kn_ref, kc_ref, knt_ref, kct_ref,
                       dot_ref, do_ref, dq_ref, dkn_ref, dkc_ref, dvc_ref):
    head = pl.program_id(0)

    @pl.when(head == 0)
    def _():
        fill_bias(size_ref[0], bn_ref, bc_ref)
        dot_ref[...] = nt(wo_ref[...], g_ref[...]).astype(BF)
        go_ref[...] = nn(att_ref[...], g_ref[...])

    do_ref[...] = jnp.transpose(dot_ref[pl.ds(pl.multiple_of(head * HD, HD), HD), :])
    kn_ref[...] = qn_ref[:, 64:128]
    kc_ref[...] = qc_ref[:, 64:128]
    knt_ref[...] = jnp.transpose(qn_ref[:, 0:128])[64:128]
    kct_ref[...] = jnp.transpose(qc_ref[:, 0:128])[64:128]
    dkc_ref[...] = jnp.zeros_like(dkc_ref)
    dvc_ref[...] = jnp.zeros_like(dvc_ref)
    for i in range(LEN // TILE):
        lo, hi = i * TILE, (i + 1) * TILE
        q = qn_ref[lo:hi, 0:64] * 0.125
        do = do_ref[lo:hi, :]
        lse = lse_ref[0, 0:1, lo:hi]
        spans = [(0, lo, hi), (1, lo, hi)] + ([(1, 0, lo)] if i else [])
        probs, grads, inner = [], [], 0.0
        for n, (side, a, b) in enumerate(spans):
            kr = kc_ref if side else kn_ref
            vr = qc_ref if side else qn_ref
            s = nt(kr[a:b, :], q)
            if n == 0:
                s = s + bn_ref[...]
            if n == 1:
                s = s + bc_ref[...]
            p = jnp.exp(s - lse)
            dp = nt(vr[a:b, 128:192], do)
            inner = inner + jnp.sum(p * dp, axis=0, keepdims=True)
            probs.append(p)
            grads.append(dp)
        dqt = 0.0
        for n, (side, a, b) in enumerate(spans):
            ds = (probs[n] * (grads[n] - inner)).astype(BF)
            dv = nn(probs[n].astype(BF), do)
            dk = nn(ds, q)
            ktr = kct_ref if side else knt_ref
            dqt = dqt + nn(ktr[:, a:b], ds)
            if side:
                dkc_ref[a:b, :] += dk
                dvc_ref[a:b, :] += dv
            else:
                dkn_ref[a:b, :] = dk
                dn_ref[a:b, 128:192] = dv.astype(BF)
        dq_ref[lo:hi, :] = jnp.transpose(dqt) * 0.125
    zero = jnp.zeros((LEN, 64), F32)
    sin = -sin_ref[...]
    cos = cos_ref[...]
    dn_ref[:, 0:128] = spin(jnp.concatenate([dq_ref[...], dkn_ref[...]], axis=1), cos, sin).astype(BF)
    dn_ref[:, 192:256] = zero.astype(BF)
    dc_ref[:, 0:128] = spin(jnp.concatenate([zero, dkc_ref[...]], axis=1), cos, sin).astype(BF)
    dc_ref[:, 128:192] = dvc_ref[...].astype(BF)
    dc_ref[:, 192:256] = zero.astype(BF)


def attend_back(size, qn, qc, att, lse, g, wo, cos, sin):
    heads = qn.shape[1] // SLOT
    return pl.pallas_call(
        attend_back_kernel,
        grid=(heads,),
        in_specs=[
            pl.BlockSpec(memory_space=pltpu.SMEM),
            pl.BlockSpec((LEN, SLOT), lane2),
            pl.BlockSpec((LEN, SLOT), lane2),
            pl.BlockSpec((HD * heads, LEN), fixed2),
            pl.BlockSpec((1, 8, LEN), row3),
            pl.BlockSpec((LEN, D), fixed2),
            pl.BlockSpec((HD * heads, D), fixed2),
            pl.BlockSpec((LEN, 128), fixed2),
            pl.BlockSpec((LEN, 128), fixed2),
        ],
        out_specs=[
            pl.BlockSpec((LEN, SLOT), lane2),
            pl.BlockSpec((LEN, SLOT), lane2),
            pl.BlockSpec((HD * heads, D), fixed2),
        ],
        out_shape=[
            jax.ShapeDtypeStruct((LEN, SLOT * heads), BF),
            jax.ShapeDtypeStruct((LEN, SLOT * heads), BF),
            jax.ShapeDtypeStruct((HD * heads, D), F32),
        ],
        scratch_shapes=[
            pltpu.VMEM((TILE, TILE), F32),
            pltpu.VMEM((TILE, TILE), F32),
            pltpu.VMEM((LEN, HD), BF),
            pltpu.VMEM((LEN, HD), BF),
            pltpu.VMEM((HD, LEN), BF),
            pltpu.VMEM((HD, LEN), BF),
            pltpu.VMEM((HD * heads, LEN), BF),
            pltpu.VMEM((LEN, HD), BF),
            pltpu.VMEM((LEN, HD), F32),
            pltpu.VMEM((LEN, HD), F32),
            pltpu.VMEM((LEN, HD), F32),
            pltpu.VMEM((LEN, HD), F32),
        ],
        compiler_params=pltpu.CompilerParams(vmem_limit_bytes=40 << 20),
        cost_estimate=pl.CostEstimate(flops=9000000000, bytes_accessed=12000000, transcendentals=2800000),
        name="attend_back",
    )(size, qn, qc, att, lse, g, wo, cos, sin)


def replica_sum_kernel(count, owners, x_ref, o_ref, in_ref, send_a, recv_a, send_b, recv_b):
    me = lax.axis_index("dp")
    m = lax.axis_index("mp")
    barrier = pltpu.get_barrier_semaphore()
    for k in range(1, count):
        pl.semaphore_signal(barrier, inc=1, device_id=(lax.rem(me + k, count), m), device_id_type=MESH_ID)
    pl.semaphore_wait(barrier, count - 1)

    def piece(j):
        return pl.ds(pl.multiple_of(j * 128, 128), 128)

    def part(j):
        return pltpu.make_async_remote_copy(
            src_ref=x_ref.at[:, piece(j)], dst_ref=in_ref.at[me], send_sem=send_a.at[j], recv_sem=recv_a.at[me],
            device_id=(j, m), device_id_type=MESH_ID)

    def whole(p):
        return pltpu.make_async_remote_copy(
            src_ref=o_ref.at[:, piece(me)], dst_ref=o_ref.at[:, piece(me)], send_sem=send_b.at[p],
            recv_sem=recv_b.at[me], device_id=(p, m), device_id_type=MESH_ID)

    for j in range(owners):
        @pl.when(me != j)
        def _():
            part(j).start()

    @pl.when(me < owners)
    def _():
        in_ref[me] = x_ref[:, piece(me)]
        for s in range(count):
            @pl.when(me != s)
            def _():
                pltpu.make_async_remote_copy(
                    src_ref=x_ref.at[:, piece(0)], dst_ref=in_ref.at[s], send_sem=send_a.at[0], recv_sem=recv_a.at[s],
                    device_id=(s, m), device_id_type=MESH_ID).wait_recv()
        total = in_ref[0]
        for s in range(1, count):
            total = total + in_ref[s]
        o_ref[:, piece(me)] = total
        for p in range(count):
            @pl.when(me != p)
            def _():
                whole(p).start()

    for j in range(owners):
        @pl.when(me != j)
        def _():
            pltpu.make_async_remote_copy(
                src_ref=o_ref.at[:, piece(j)], dst_ref=o_ref.at[:, piece(j)], send_sem=send_b.at[0],
                recv_sem=recv_b.at[j], device_id=(j, m), device_id_type=MESH_ID).wait_recv()
            part(j).wait_send()

    @pl.when(me < owners)
    def _():
        for p in range(count):
            @pl.when(me != p)
            def _():
                whole(p).wait_send()


def replica_sum(x, collective_id):
    count = lax.axis_size("dp")
    owners = x.shape[1] // 128
    if count != 8:
        return lax.psum(x, "dp")
    return pl.pallas_call(
        functools.partial(replica_sum_kernel, count, owners),
        out_shape=jax.ShapeDtypeStruct(x.shape, F32),
        in_specs=[pl.BlockSpec(memory_space=pltpu.VMEM)],
        out_specs=pl.BlockSpec(memory_space=pltpu.VMEM),
        scratch_shapes=[
            pltpu.VMEM((count, x.shape[0], 128), F32),
            pltpu.SemaphoreType.DMA((owners,)),
            pltpu.SemaphoreType.DMA((count,)),
            pltpu.SemaphoreType.DMA((count,)),
            pltpu.SemaphoreType.DMA((owners,)),
        ],
        compiler_params=pltpu.CompilerParams(collective_id=collective_id, has_side_effects=True),
        cost_estimate=pl.CostEstimate(flops=1000000, bytes_accessed=30000000, transcendentals=0),
        name="replica_sum",
    )(x)


def orthonormal_kernel(x_ref, o_ref):
    row = lax.broadcasted_iota(jnp.int32, (RANK, D), 0)
    mats = [x_ref[RANK * t:RANK * (t + 1), :] for t in range(4)]
    for k in range(RANK):
        for t in range(4):
            a = mats[t]
            v = a[k:k + 1, :]
            e = v / (jnp.sqrt(jnp.sum(v * v, axis=1, keepdims=True)) + 1e-08)
            c = jnp.sum(a * e, axis=1, keepdims=True)
            mats[t] = jnp.where(row == k, e, jnp.where(row > k, a - c * e, a))
    for t in range(4):
        o_ref[RANK * t:RANK * (t + 1), :] = mats[t]


def orthonormal(x):
    return pl.pallas_call(
        orthonormal_kernel,
        out_shape=jax.ShapeDtypeStruct((4 * RANK, D), F32),
        in_specs=[pl.BlockSpec(memory_space=pltpu.VMEM)],
        out_specs=pl.BlockSpec(memory_space=pltpu.VMEM),
        name="orthonormal",
    )(x)


def layer_norm(values, gain_vector):
    centered = values - jnp.mean(values, axis=-1, keepdims=True)
    variance = jnp.mean(centered * centered, axis=-1, keepdims=True)
    return centered * lax.rsqrt(variance + norm_eps) * gain_vector


def layer_norm_back(values, gain_vector, grad):
    centered = values - jnp.mean(values, axis=-1, keepdims=True)
    scale = lax.rsqrt(jnp.mean(centered * centered, axis=-1, keepdims=True) + norm_eps)
    unit = centered * scale
    scaled = grad * gain_vector
    inner = jnp.mean(scaled * unit, axis=-1, keepdims=True)
    grad_in = scale * (scaled - jnp.mean(scaled, axis=-1, keepdims=True) - unit * inner)
    return grad_in, jnp.sum(grad * unit, axis=0)


def gelu_tanh(values):
    return 0.5 * values * (1.0 + jnp.tanh(gelu_coef * (values + 0.044715 * values * values * values)))


def gelu_slope(values):
    square = values * values
    bend = jnp.tanh(gelu_coef * (values + 0.044715 * square * values))
    return 0.5 * (1.0 + bend) + 0.5 * values * (1.0 - bend * bend) * (gelu_coef * (1.0 + 3.0 * 0.044715 * square))


def widen(block):
    parts = block.reshape(D, block.shape[1] // (3 * HD), 3 * HD)
    return jnp.pad(parts, ((0, 0), (0, 0), (0, SLOT - 3 * HD))).reshape(D, -1)


def narrow(block):
    parts = block.reshape(D, block.shape[1] // SLOT, SLOT)
    return parts[:, :, : 3 * HD].reshape(D, -1)


def exact(left_side, right_side, left_dim, right_dim):
    return lax.dot_general(
        left_side, right_side, (((left_dim,), (right_dim,)), ((), ())), precision=highest
    )


def refresh(matrix, hat, right_new, master, moment, average, rate, along):
    decay = min(0.9999, (1.0 + EMA_STEPS) / (10.0 + EMA_STEPS))
    approx = exact(hat, right_new, 0, 0)
    share = master.shape[along]
    piece = lax.dynamic_slice_in_dim(approx, lax.axis_index("dp") * share, share, along)
    moment_new = 0.5 * moment + piece
    master_new = master - rate * moment_new
    average_new = decay * average + (1.0 - decay) * master_new
    return ((matrix - approx)[None], master_new, moment_new, average_new)


def local(
    noisy_rows, clean_rows, block_size, cotangent, norm_gains,
    weight_qkv, weight_out, weight_up, weight_down,
    master_qkv, master_out, master_up, master_down,
    moment_qkv, moment_out, moment_up, moment_down,
    average_qkv, average_out, average_up, average_down,
    error_qkv, error_out, error_up, error_down,
    factor_qkv, factor_out, factor_up, factor_down,
    gain_moment,
):
    row_count = noisy_rows.shape[0]
    replicas = lax.axis_size("dp")
    side = lax.axis_index("mp") // 2

    def across(value):
        return lax.ppermute(value, "mp", [(0, 2), (2, 0), (1, 3), (3, 1)])

    def beside(value):
        return lax.ppermute(value, "mp", [(0, 1), (1, 0), (2, 3), (3, 2)])

    def both_sides(value):
        other = across(value)
        first = jnp.where(side == 0, value, other)
        second = jnp.where(side == 0, other, value)
        return jnp.concatenate([first, second], axis=0)

    def mine(value, width=LEN):
        return lax.dynamic_slice_in_dim(value, side * width, width, 0)

    def pair_sum(partial):
        low = partial.astype(BF)
        return low.astype(F32) + beside(low).astype(F32)

    cos, sin = rotary_tables()
    noisy = mine(noisy_rows).astype(F32)
    clean = mine(clean_rows).astype(F32)
    cot = mine(cotangent)
    cot_far = lax.dynamic_slice_in_dim(cotangent, (1 - side) * LEN, LEN, 0)
    size = mine(block_size, 1)
    far_qkv = across(weight_qkv)
    far_out = across(weight_out)
    far_up = across(weight_up)
    far_down = across(weight_down)
    wide_near = widen(weight_qkv)
    wide_far = widen(far_qkv)

    xn = layer_norm(noisy, norm_gains[0]).astype(BF)
    xc = layer_norm(clean, norm_gains[0]).astype(BF)
    qn_near, qc_near, att_near, lse_near = attend(size, xn, xc, wide_near, cos, sin)
    qn_far, qc_far, att_far, lse_far = attend(size, xn, xc, wide_far, cos, sin)
    branch = tn(att_near, weight_out) + tn(att_far, far_out)
    residual = noisy + pair_sum(branch)
    normed_mid = layer_norm(residual, norm_gains[1]).astype(BF)
    normed_far = across(normed_mid)

    def feed(rows, up):
        pre = nn(rows, up)
        return pre, gelu_tanh(pre).astype(BF)

    def feed_back(pre, grad_rows, down):
        return (gelu_slope(pre) * nt(grad_rows, down)).astype(BF)

    pre_near, hidden_near = feed(normed_mid, weight_up)
    pre_far, hidden_far = feed(normed_mid, far_up)
    mlp = pair_sum(nn(hidden_near, weight_down) + nn(hidden_far, far_down))
    block_out = both_sides((residual + mlp).astype(BF))
    gp_near = feed_back(pre_near, cot, weight_down)
    gp_far = feed_back(pre_far, cot, far_down)
    grad_mid = pair_sum(nt(gp_near, weight_up) + nt(gp_far, far_up))
    pre_other, hidden_other = feed(normed_far, weight_up)
    gp_other = feed_back(pre_other, cot_far, weight_down)
    grad_down = tn(hidden_near, cot) + tn(hidden_other, cot_far)
    grad_up = tn(normed_mid, gp_near) + tn(normed_far, gp_other)

    grad_resid_norm, gain_two = layer_norm_back(residual, norm_gains[1], grad_mid)
    grad_resid = cot.astype(F32) + grad_resid_norm
    grad_low = grad_resid.astype(BF)
    dn_far, dc_far, go_far = attend_back(size, qn_far, qc_far, att_far, lse_far, grad_low, far_out, cos, sin)
    dn_near, dc_near, go_near = attend_back(size, qn_near, qc_near, att_near, lse_near, grad_low, weight_out, cos, sin)
    gq_far = narrow(tn(xn, dn_far) + tn(xc, dc_far)).astype(BF)
    gq_near = narrow(tn(xn, dn_near) + tn(xc, dc_near))
    grad_qkv = gq_near + across(gq_far).astype(F32)
    grad_out = go_near + across(go_far.astype(BF)).astype(F32)
    grad_xn = pair_sum(nt(dn_near, wide_near) + nt(dn_far, wide_far))
    grad_xc = pair_sum(nt(dc_near, wide_near) + nt(dc_far, wide_far))
    grad_noisy, gain_noisy = layer_norm_back(noisy, norm_gains[0], grad_xn)
    grad_clean, gain_clean = layer_norm_back(clean, norm_gains[0], grad_xc)
    grad_noisy = both_sides((grad_resid + grad_noisy).astype(BF))
    grad_clean = both_sides(grad_clean.astype(BF))
    gain_part = jnp.stack([gain_noisy + gain_clean, gain_two])
    gain_part = gain_part + across(gain_part)

    matrix_qkv = grad_qkv + error_qkv[0]
    matrix_out = grad_out + error_out[0]
    matrix_up = grad_up + error_up[0]
    matrix_down = grad_down + error_down[0]
    matrices = (matrix_qkv, matrix_out, matrix_up, matrix_down)
    factors = (factor_qkv, factor_out, factor_up, factor_down)

    def padded(value):
        return jnp.pad(value, ((0, 0), (0, D - value.shape[1])))

    lefts = [padded(exact(f, a, 0, 1)) for f, a in zip(factors, matrices)]
    gains_pad = jnp.pad(gain_part, ((0, RANK - 2), (0, 0)))
    left_sum = replica_sum(jnp.concatenate(lefts + [gains_pad], axis=0), 1)
    hats_all = orthonormal(left_sum[: 4 * RANK])
    hats = [hats_all[RANK * t:RANK * (t + 1), : a.shape[0]] for t, a in enumerate(matrices)]
    rights = [padded(exact(h, a, 1, 0)) for h, a in zip(hats, matrices)]
    right_sum = replica_sum(jnp.concatenate(rights, axis=0), 2) / replicas
    rights = [right_sum[RANK * t:RANK * (t + 1), : a.shape[1]] for t, a in enumerate(matrices)]
    rates = [3.0 / math.sqrt(f * row_count) for f in (D, HEADS * HD // 64, D, FF)]
    states = (
        (master_qkv, moment_qkv, average_qkv),
        (master_out, moment_out, average_out),
        (master_up, moment_up, average_up),
        (master_down, moment_down, average_down),
    )
    done = [refresh(a, h, r, *s, rate, along)
            for a, h, r, s, rate, along in zip(matrices, hats, rights, states, rates, (0, 1, 0, 1))]
    errs, masters, moments, averages = zip(*done)
    gain_grad = left_sum[4 * RANK:4 * RANK + 2] / replicas
    new_gain_moment = 0.5 * gain_moment + gain_grad
    new_gains = norm_gains - 0.5 / math.sqrt(row_count) * new_gain_moment
    return (
        block_out, grad_noisy, grad_clean, gain_grad, new_gains, new_gain_moment,
        *masters, *moments, *averages, *errs,
        *[h.T for h in hats], *[r.T for r in rights],
    )


def solution(mesh):
    in_specs = (
        P("dp", None), P("dp", None), P("dp"), P("dp", None), P(),
        P(None, "mp"), P("mp", None), P(None, "mp"), P("mp", None),
        *([P("dp", "mp"), P("mp", "dp")] * 6),
        *([P("dp", None, "mp"), P("dp", "mp", None)] * 2),
        *([P("mp", None), P(None, "mp")] * 2),
        P(),
    )
    out_specs = (
        P("dp", None), P("dp", None), P("dp", None), P(), P(), P(),
        *([P("dp", "mp"), P("mp", "dp")] * 6),
        *([P("dp", None, "mp"), P("dp", "mp", None)] * 2),
        *([P(None, "mp"), P("mp", None)] * 2),
        *([P("mp", None), P(None, "mp")] * 2),
    )
    return jax.shard_map(local, mesh=mesh, in_specs=in_specs, out_specs=out_specs, check_vma=False)
```

```python
import functools
import math

import jax
import jax.numpy as jnp
import numpy as np
from jax import lax
from jax.experimental import pallas as pl
from jax.experimental.pallas import tpu as pltpu
from jax.sharding import PartitionSpec as P

D = 768
HEADS = 12
HD = 64
FF = 3072
LEN = 1024
RANK = 8
EMA_STEPS = 4
TILE = 256
SLOT = 256

BF = jnp.bfloat16
F32 = jnp.float32
highest = lax.Precision.HIGHEST
norm_eps = 1e-05
gelu_coef = 0.7978845608028654
masked_score = -1e30
MESH_ID = pl.DeviceIdType.MESH


def nt(a, b):
    return lax.dot_general(a, b, (((1,), (1,)), ((), ())), preferred_element_type=F32)


def nn(a, b):
    return lax.dot_general(a, b, (((1,), (0,)), ((), ())), preferred_element_type=F32)


def tn(a, b):
    return lax.dot_general(a, b, (((0,), (0,)), ((), ())), preferred_element_type=F32)


def rotary_tables():
    half = HD // 2
    step = np.float32(-2.0 * math.log(10000.0) / HD)
    inverse = np.exp(np.arange(half, dtype=np.float32) * step).astype(np.float32)
    angle = (np.arange(LEN, dtype=np.float32)[:, None] * inverse[None, :]).astype(np.float32)
    c = np.cos(angle).astype(np.float32)
    s = np.sin(angle).astype(np.float32)
    return np.concatenate([c, c, c, c], 1), np.concatenate([-s, s, -s, s], 1)


def spin(v, cos, sin):
    lane = lax.broadcasted_iota(jnp.int32, v.shape, 1)
    low = lax.rem(lane, HD) < HD // 2
    swapped = jnp.where(low, pltpu.roll(v, 128 - HD // 2, 1), pltpu.roll(v, HD // 2, 1))
    return v * cos + swapped * sin


def block_ids(size, shape, dim):
    shift = 2 + (size >= 8).astype(jnp.int32) + (size >= 16).astype(jnp.int32)
    place = lax.broadcasted_iota(jnp.int32, shape, dim)
    return lax.shift_right_logical(place, jnp.full(shape, shift, jnp.int32))


def fill_bias(size, noisy_bias, clean_bias):
    keys = block_ids(size, (TILE, TILE), 0)
    rows = block_ids(size, (TILE, TILE), 1)
    noisy_bias[...] = jnp.where(rows == keys, 0.0, masked_score)
    clean_bias[...] = jnp.where(keys < rows, 0.0, masked_score)


def norm_parts(values):
    centered = values - jnp.mean(values, axis=1, keepdims=True)
    scale = lax.rsqrt(jnp.mean(centered * centered, axis=1, keepdims=True) + norm_eps)
    return centered * scale, scale


def norm_back(values, gain, grad):
    unit, scale = norm_parts(values)
    scaled = grad * gain
    inner = jnp.mean(scaled * unit, axis=1, keepdims=True)
    grad_in = scale * (scaled - jnp.mean(scaled, axis=1, keepdims=True) - unit * inner)
    return grad_in, jnp.sum(grad * unit, axis=0, keepdims=True)


def gelu(u):
    return 0.5 * u * (1.0 + jnp.tanh(gelu_coef * (u + 0.044715 * u * u * u)))


def gelu_slope(u):
    square = u * u
    bend = jnp.tanh(gelu_coef * (u + 0.044715 * square * u))
    return 0.5 * (1.0 + bend) + 0.5 * u * (1.0 - bend * bend) * (gelu_coef * (1.0 + 3.0 * 0.044715 * square))


def whole(shape):
    return pl.BlockSpec(shape, lambda *index: (0,) * len(shape), pipeline_mode=pl.Buffered(1))


def side_rows(h, info, size):
    return (info[0], 0)


def lane2(h, *_):
    return (0, h)


def row3(h, *_):
    return (h, 0, 0)


def attend_head(head, xn_ref, xc_ref, w_ref, cos_ref, sin_ref, qn_ref, qc_ref, att_ref, lse_ref,
                bn_ref, bc_ref, kn_ref, kc_ref, vnt_ref, vct_ref):
    w = w_ref[pl.ds(pl.multiple_of(head * 3 * HD, 3 * HD), 3 * HD), :]
    for src, dst, keys, vals in ((xn_ref, qn_ref, kn_ref, vnt_ref), (xc_ref, qc_ref, kc_ref, vct_ref)):
        a = nt(src[...], w)
        r = spin(a[:, :128], cos_ref[...], sin_ref[...]).astype(BF)
        v = a[:, 128:].astype(BF)
        dst[:, :128] = r
        dst[:, 128:192] = v
        keys[...] = r[:, 64:128]
        vals[...] = jnp.transpose(v)
    here = pl.ds(pl.multiple_of(head * HD, HD), HD)
    for i in range(LEN // TILE):
        lo, hi = i * TILE, (i + 1) * TILE
        q = qn_ref[lo:hi, 0:64] * 0.125
        parts = [nt(kn_ref[lo:hi, :], q) + bn_ref[...], nt(kc_ref[lo:hi, :], q) + bc_ref[...]]
        if i:
            parts.append(nt(kc_ref[0:lo, :], q))
        peak = functools.reduce(jnp.maximum, [jnp.max(s, axis=0, keepdims=True) for s in parts])
        exps = [jnp.exp(s - peak) for s in parts]
        total = functools.reduce(jnp.add, [jnp.sum(e, axis=0, keepdims=True) for e in exps])
        inv = 1.0 / total
        low = [(e * inv).astype(BF) for e in exps]
        o = nn(vnt_ref[:, lo:hi], low[0]) + nn(vct_ref[:, lo:hi], low[1])
        if i:
            o = o + nn(vct_ref[:, 0:lo], low[2])
        att_ref[here, lo:hi] = o.astype(BF)
        lse_ref[0, :, lo:hi] = jnp.broadcast_to(peak + jnp.log(total), (8, TILE))


def attend_near_kernel(info_ref, size_ref, noisy_ref, clean_ref, gain_ref, w_ref, cos_ref, sin_ref,
                       qn_ref, qc_ref, att_ref, lse_ref, xn_ref, xc_ref, *work):
    head = pl.program_id(0)

    @pl.when(head == 0)
    def _():
        fill_bias(size_ref[info_ref[0]], work[0], work[1])
        for src, dst in ((noisy_ref, xn_ref), (clean_ref, xc_ref)):
            for i in range(LEN // TILE):
                lo, hi = i * TILE, (i + 1) * TILE
                dst[lo:hi, :] = (norm_parts(src[lo:hi, :].astype(F32))[0] * gain_ref[0:1, :]).astype(BF)

    attend_head(head, xn_ref, xc_ref, w_ref, cos_ref, sin_ref, qn_ref, qc_ref, att_ref, lse_ref, *work)


def attend_far_kernel(info_ref, size_ref, xn_ref, xc_ref, w_ref, cos_ref, sin_ref,
                      att_near_ref, wo_near_ref, wo_far_ref,
                      qn_ref, qc_ref, att_ref, lse_ref, branch_ref, wo_ref, all_ref, *work):
    head = pl.program_id(0)

    @pl.when(head == 0)
    def _():
        fill_bias(size_ref[info_ref[0]], work[0], work[1])

    attend_head(head, xn_ref, xc_ref, w_ref, cos_ref, sin_ref, qn_ref, qc_ref, att_ref, lse_ref, *work)

    @pl.when(head == 2)
    def _():
        wo_ref[:192, :] = wo_near_ref[...]
        wo_ref[192:, :] = wo_far_ref[...]
        all_ref[:192, :] = att_near_ref[...]
        all_ref[192:, :] = att_ref[...]
        for i in range(LEN // TILE):
            lo, hi = i * TILE, (i + 1) * TILE
            branch_ref[lo:hi, :] = tn(all_ref[:, lo:hi], wo_ref[...]).astype(BF)


attend_work = [
    pltpu.VMEM((TILE, TILE), F32),
    pltpu.VMEM((TILE, TILE), F32),
    pltpu.VMEM((LEN, HD), BF),
    pltpu.VMEM((LEN, HD), BF),
    pltpu.VMEM((HD, LEN), BF),
    pltpu.VMEM((HD, LEN), BF),
]
head_specs = [
    pl.BlockSpec((LEN, SLOT), lane2),
    pl.BlockSpec((LEN, SLOT), lane2),
    whole((3 * HD, LEN)),
    pl.BlockSpec((1, 8, LEN), row3),
]
head_shapes = [
    jax.ShapeDtypeStruct((LEN, SLOT * 3), BF),
    jax.ShapeDtypeStruct((LEN, SLOT * 3), BF),
    jax.ShapeDtypeStruct((3 * HD, LEN), BF),
    jax.ShapeDtypeStruct((3, 8, LEN), F32),
]
rows_shape = jax.ShapeDtypeStruct((LEN, D), BF)


def attend_near(info, size, noisy, clean, gains, w, cos, sin):
    return pl.pallas_call(
        attend_near_kernel,
        grid_spec=pltpu.PrefetchScalarGridSpec(
            num_scalar_prefetch=2,
            grid=(3,),
            in_specs=[
                pl.BlockSpec((LEN, D), side_rows, pipeline_mode=pl.Buffered(1)),
                pl.BlockSpec((LEN, D), side_rows, pipeline_mode=pl.Buffered(1)),
                whole((2, D)),
                whole((9 * HD, D)),
                whole((LEN, 128)),
                whole((LEN, 128)),
            ],
            out_specs=head_specs + [whole((LEN, D)), whole((LEN, D))],
            scratch_shapes=attend_work,
        ),
        out_shape=head_shapes + [rows_shape, rows_shape],
        compiler_params=pltpu.CompilerParams(vmem_limit_bytes=60 << 20),
        name="attend_near",
    )(info, size, noisy, clean, gains, w, cos, sin)


def attend_far(info, size, xn, xc, w, cos, sin, att_near, wo_near, wo_far):
    return pl.pallas_call(
        attend_far_kernel,
        grid_spec=pltpu.PrefetchScalarGridSpec(
            num_scalar_prefetch=2,
            grid=(3,),
            in_specs=[
                whole((LEN, D)),
                whole((LEN, D)),
                whole((9 * HD, D)),
                whole((LEN, 128)),
                whole((LEN, 128)),
                whole((3 * HD, LEN)),
                whole((3 * HD, D)),
                whole((3 * HD, D)),
            ],
            out_specs=head_specs + [whole((LEN, D))],
            scratch_shapes=[pltpu.VMEM((6 * HD, D), BF), pltpu.VMEM((6 * HD, LEN), BF)]
            + attend_work,
        ),
        out_shape=head_shapes + [rows_shape],
        compiler_params=pltpu.CompilerParams(vmem_limit_bytes=60 << 20),
        name="attend_far",
    )(info, size, xn, xc, w, cos, sin, att_near, wo_near, wo_far)


def back_head(head, qn_ref, qc_ref, lse_ref, cos_ref, sin_ref, dn_ref, dc_ref,
              bn_ref, bc_ref, kn_ref, kc_ref, knt_ref, kct_ref, dot_ref, do_ref, dq_ref, dkn_ref, dkc_ref, dvc_ref):
    do_ref[...] = jnp.transpose(dot_ref[pl.ds(pl.multiple_of(head * HD, HD), HD), :])
    kn_ref[...] = qn_ref[:, 64:128]
    kc_ref[...] = qc_ref[:, 64:128]
    knt_ref[...] = jnp.transpose(qn_ref[:, 0:128])[64:128]
    kct_ref[...] = jnp.transpose(qc_ref[:, 0:128])[64:128]
    dkc_ref[...] = jnp.zeros_like(dkc_ref)
    dvc_ref[...] = jnp.zeros_like(dvc_ref)
    slot = pl.multiple_of(head * SLOT, SLOT)
    pair, rest = pl.ds(slot, 128), pl.ds(pl.multiple_of(slot + 128, 128), 128)
    blank = jnp.zeros((TILE, HD), F32)
    for i in range(LEN // TILE):
        lo, hi = i * TILE, (i + 1) * TILE
        q = qn_ref[lo:hi, 0:64] * 0.125
        do = do_ref[lo:hi, :]
        lse = lse_ref[0, 0:1, lo:hi]
        spans = [(0, lo, hi), (1, lo, hi)] + ([(1, 0, lo)] if i else [])
        probs, grads, inner = [], [], 0.0
        for n, (side, a, b) in enumerate(spans):
            kr = kc_ref if side else kn_ref
            vr = qc_ref if side else qn_ref
            s = nt(kr[a:b, :], q)
            if n == 0:
                s = s + bn_ref[...]
            if n == 1:
                s = s + bc_ref[...]
            p = jnp.exp(s - lse)
            dp = nt(vr[a:b, 128:192], do)
            inner = inner + jnp.sum(p * dp, axis=0, keepdims=True)
            probs.append(p)
            grads.append(dp)
        dqt = 0.0
        for n, (side, a, b) in enumerate(spans):
            ds = (probs[n] * (grads[n] - inner)).astype(BF)
            dv = nn(probs[n].astype(BF), do)
            dk = nn(ds, q)
            ktr = kct_ref if side else knt_ref
            dqt = dqt + nn(ktr[:, a:b], ds)
            if side:
                dkc_ref[a:b, :] += dk
                dvc_ref[a:b, :] += dv
            else:
                dkn_ref[a:b, :] = dk
                dn_ref[lo:hi, rest] = jnp.concatenate([dv, blank], axis=1).astype(BF)
        dq_ref[lo:hi, :] = jnp.transpose(dqt) * 0.125
    zero = jnp.zeros((LEN, HD), F32)
    sin = -sin_ref[...]
    cos = cos_ref[...]
    dn_ref[:, pair] = spin(jnp.concatenate([dq_ref[...], dkn_ref[...]], axis=1), cos, sin).astype(BF)
    dc_ref[:, pair] = spin(jnp.concatenate([zero, dkc_ref[...]], axis=1), cos, sin).astype(BF)
    dc_ref[:, rest] = jnp.concatenate([dvc_ref[...], zero], axis=1).astype(BF)


def head_grad(head, xn_ref, xc_ref, dn_ref, dc_ref, gq_ref):
    here = pl.ds(pl.multiple_of(head * SLOT, SLOT), SLOT)
    g = tn(dn_ref[:, here], xn_ref[...]) + tn(dc_ref[:, here], xc_ref[...])
    gq_ref[pl.ds(pl.multiple_of(head * 3 * HD, 3 * HD), 3 * HD), :] = g[:3 * HD].astype(gq_ref.dtype)


def back_far_kernel(info_ref, size_ref, qn_ref, qc_ref, att_ref, lse_ref, g_ref, wo_ref,
                    cos_ref, sin_ref, xn_ref, xc_ref, dn_ref, dc_ref, gq_ref, go_ref, *work):
    head = pl.program_id(0)

    @pl.when(head == 0)
    def _():
        fill_bias(size_ref[info_ref[0]], work[0], work[1])
        work[6][...] = nt(wo_ref[...], g_ref[...]).astype(BF)
        go_ref[...] = nn(att_ref[...], g_ref[...]).astype(BF)

    back_head(head, qn_ref, qc_ref, lse_ref, cos_ref, sin_ref, dn_ref, dc_ref, *work)
    head_grad(head, xn_ref, xc_ref, dn_ref, dc_ref, gq_ref)


def back_near_kernel(info_ref, size_ref, qn_ref, qc_ref, att_ref, lse_ref, g_ref, wo_ref,
                     cos_ref, sin_ref, xn_ref, xc_ref, w_ref, w_far_ref, dn_far_ref, dc_far_ref,
                     gxn_ref, gxc_ref, gq_ref, go_ref, dn_ref, dc_ref, *work):
    head = pl.program_id(0)

    @pl.when(head == 0)
    def _():
        fill_bias(size_ref[info_ref[0]], work[0], work[1])
        work[6][...] = nt(wo_ref[...], g_ref[...]).astype(BF)
        go_ref[...] = nn(att_ref[...], g_ref[...])

    back_head(head, qn_ref, qc_ref, lse_ref, cos_ref, sin_ref, dn_ref, dc_ref, *work)
    head_grad(head, xn_ref, xc_ref, dn_ref, dc_ref, gq_ref)

    @pl.when(head == 2)
    def _():
        for near, far, out in ((dn_ref, dn_far_ref, gxn_ref), (dc_ref, dc_far_ref, gxc_ref)):
            for i in range(LEN // TILE):
                lo, hi = i * TILE, (i + 1) * TILE
                total = 0.0
                for rows, w in ((near, w_ref), (far, w_far_ref)):
                    for j in range(3):
                        total = total + nn(rows[lo:hi, SLOT * j:SLOT * j + 192], w[192 * j:192 * (j + 1), :])
                out[lo:hi, :] = total.astype(BF)


back_work = attend_work[:4] + [
    pltpu.VMEM((HD, LEN), BF),
    pltpu.VMEM((HD, LEN), BF),
    pltpu.VMEM((3 * HD, LEN), BF),
    pltpu.VMEM((LEN, HD), BF),
    pltpu.VMEM((LEN, HD), F32),
    pltpu.VMEM((LEN, HD), F32),
    pltpu.VMEM((LEN, HD), F32),
    pltpu.VMEM((LEN, HD), F32),
]
wide_rows = jax.ShapeDtypeStruct((LEN, 3 * SLOT), BF)


def back_far(info, size, qn, qc, att, lse, g, wo, cos, sin, xn, xc):
    return pl.pallas_call(
        back_far_kernel,
        grid_spec=pltpu.PrefetchScalarGridSpec(
            num_scalar_prefetch=2,
            grid=(3,),
            in_specs=head_specs[:2] + [whole((3 * HD, LEN)), head_specs[3], whole((LEN, D)), whole((3 * HD, D)),
                                       whole((LEN, 128)), whole((LEN, 128)), whole((LEN, D)), whole((LEN, D))],
            out_specs=[whole((LEN, 3 * SLOT)), whole((LEN, 3 * SLOT)), whole((9 * HD, D)), whole((3 * HD, D))],
            scratch_shapes=back_work,
        ),
        out_shape=[wide_rows, wide_rows, jax.ShapeDtypeStruct((9 * HD, D), BF), jax.ShapeDtypeStruct((3 * HD, D), BF)],
        compiler_params=pltpu.CompilerParams(vmem_limit_bytes=60 << 20),
        name="back_far",
    )(info, size, qn, qc, att, lse, g, wo, cos, sin, xn, xc)


def back_near(info, size, qn, qc, att, lse, g, wo, cos, sin, xn, xc, w, w_far, dn_far, dc_far):
    return pl.pallas_call(
        back_near_kernel,
        grid_spec=pltpu.PrefetchScalarGridSpec(
            num_scalar_prefetch=2,
            grid=(3,),
            in_specs=head_specs[:2] + [whole((3 * HD, LEN)), head_specs[3], whole((LEN, D)), whole((3 * HD, D)),
                                       whole((LEN, 128)), whole((LEN, 128)), whole((LEN, D)), whole((LEN, D)),
                                       whole((9 * HD, D)), whole((9 * HD, D)),
                                       whole((LEN, 3 * SLOT)), whole((LEN, 3 * SLOT))],
            out_specs=[whole((LEN, D)), whole((LEN, D)), whole((9 * HD, D)), whole((3 * HD, D))],
            scratch_shapes=[pltpu.VMEM((LEN, 3 * SLOT), BF), pltpu.VMEM((LEN, 3 * SLOT), BF)] + back_work,
        ),
        out_shape=[rows_shape, rows_shape, jax.ShapeDtypeStruct((9 * HD, D), F32), jax.ShapeDtypeStruct((3 * HD, D), F32)],
        compiler_params=pltpu.CompilerParams(vmem_limit_bytes=60 << 20),
        name="back_near",
    )(info, size, qn, qc, att, lse, g, wo, cos, sin, xn, xc, w, w_far, dn_far, dc_far)


def feed_kernel(info_ref, nm_ref, cot_ref, up_ref, down_ref, mlp_ref, gm_ref, hid_ref, gp_ref):
    width = D // 3
    nm = nm_ref[...]
    cot = cot_ref[...]
    for t in range(3):
        lo, hi = t * width, (t + 1) * width
        pre = nn(nm, up_ref[:, lo:hi])
        hid_ref[:, lo:hi] = gelu(pre).astype(BF)
        gp_ref[:, lo:hi] = (gelu_slope(pre) * nt(cot, down_ref[lo:hi, :])).astype(BF)
    for i in range(nm_ref.shape[0] // TILE):
        at = slice(i * TILE, (i + 1) * TILE)
        gm_ref[at, :] = nt(gp_ref[at, :], up_ref[...]).astype(BF)
        mlp_ref[at, :] = nn(hid_ref[at, :], down_ref[...]).astype(BF)


def feed(info, nm, cotangent, up, down, far, chunk):
    rows = nm.shape[0]
    steps = LEN // rows

    def cot_rows(h, at):
        return ((1 - at[0] if far else at[0]) * steps + chunk, 0)

    return pl.pallas_call(
        feed_kernel,
        grid_spec=pltpu.PrefetchScalarGridSpec(
            num_scalar_prefetch=1,
            grid=(1,),
            in_specs=[whole((rows, D)), pl.BlockSpec((rows, D), cot_rows, pipeline_mode=pl.Buffered(1)),
                      whole((D, D)), whole((D, D))],
            out_specs=[whole((rows, D))] * 4,
        ),
        out_shape=[jax.ShapeDtypeStruct((rows, D), BF)] * 4,
        compiler_params=pltpu.CompilerParams(vmem_limit_bytes=60 << 20),
        name="feed",
    )(info, nm, cotangent, up, down)


def exact(left_side, right_side, left_dim, right_dim):
    return lax.dot_general(
        left_side, right_side, (((left_dim,), (right_dim,)), ((), ())), precision=highest, preferred_element_type=F32
    )


def feed_grads_kernel(info_ref, nm_ref, nma_ref, nmb_ref, cot_ref, cot_far_ref, hid_ref, hida_ref, hidb_ref,
                      gp_ref, gpa_ref, gpb_ref, err_up_ref, err_down_ref, fac_up_ref, fac_down_ref,
                      mat_up_ref, mat_down_ref, left_up_ref, left_down_ref, nmt_ref, nmat_ref, nmbt_ref):
    step = pl.program_id(0)

    @pl.when(step == 0)
    def _():
        nmt_ref[...] = jnp.transpose(nm_ref[...])
        nmat_ref[...] = jnp.transpose(nma_ref[...])
        nmbt_ref[...] = jnp.transpose(nmb_ref[...])

    mat_down = (tn(hid_ref[...], cot_ref[...]) + tn(hida_ref[...], cot_far_ref[: LEN // 2, :])
                + tn(hidb_ref[...], cot_far_ref[LEN // 2:, :]) + err_down_ref[0])
    mat_up = (nn(nmt_ref[...], gp_ref[...]) + nn(nmat_ref[...], gpa_ref[...]) + nn(nmbt_ref[...], gpb_ref[...])
              + err_up_ref[0])
    mat_down_ref[...] = mat_down
    mat_up_ref[...] = mat_up
    left_down_ref[...] = exact(fac_down_ref[...], mat_down, 1, 1)
    part = exact(fac_up_ref[...], mat_up, 1, 1)

    @pl.when(step == 0)
    def _():
        left_up_ref[...] = part

    @pl.when(step > 0)
    def _():
        left_up_ref[...] += part


def feed_grads(info, nms, cotangent, hids, gps, err_up, err_down, fac_up, fac_down):
    width = D // 3
    rows = [a.shape[0] for a in nms]

    def near_rows(h, at):
        return (at[0], 0)

    def other_rows(h, at):
        return (1 - at[0], 0)

    return pl.pallas_call(
        feed_grads_kernel,
        grid_spec=pltpu.PrefetchScalarGridSpec(
            num_scalar_prefetch=1,
            grid=(3,),
            in_specs=[
                *[whole((n, D)) for n in rows],
                pl.BlockSpec((LEN, D), near_rows, pipeline_mode=pl.Buffered(1)),
                pl.BlockSpec((LEN, D), other_rows, pipeline_mode=pl.Buffered(1)),
                *[pl.BlockSpec((n, width), lane2) for n in rows],
                *[pl.BlockSpec((n, width), lane2) for n in rows],
                pl.BlockSpec((1, D, width), lambda h, *_: (0, 0, h)),
                pl.BlockSpec((1, width, D), lambda h, *_: (0, h, 0)),
                pl.BlockSpec((RANK, width), lane2),
                whole((RANK, D)),
            ],
            out_specs=[
                pl.BlockSpec((D, width), lane2),
                pl.BlockSpec((width, D), lambda h, *_: (h, 0)),
                whole((RANK, D)),
                pl.BlockSpec((RANK, width), lane2),
            ],
            scratch_shapes=[pltpu.VMEM((D, n), BF) for n in rows],
        ),
        out_shape=[jax.ShapeDtypeStruct((D, D), F32), jax.ShapeDtypeStruct((D, D), F32),
                   jax.ShapeDtypeStruct((RANK, D), F32), jax.ShapeDtypeStruct((RANK, D), F32)],
        compiler_params=pltpu.CompilerParams(vmem_limit_bytes=60 << 20),
        name="feed_grads",
    )(info, *nms, cotangent, cotangent, *hids, *gps, err_up, err_down, fac_up, fac_down)


def greet_neighbour():
    dp = lax.axis_index("dp")
    m = lax.axis_index("mp")
    other = m + 1 - 2 * lax.rem(m, 2)
    barrier = pltpu.get_barrier_semaphore()
    pl.semaphore_signal(barrier, inc=1, device_id=(dp, other), device_id_type=MESH_ID)
    pl.semaphore_wait(barrier, 1)
    return (dp, other)


def chunk(i):
    return slice(i * TILE, (i + 1) * TILE)


def side_chunk(i):
    side = lax.axis_index("mp") // 2
    return pl.ds(pl.multiple_of(side * LEN + i * TILE, TILE), TILE)


CHUNKS = LEN // TILE


def join_kernel(branch_ref, rows_ref, gain_ref, res_ref, nm_ref,
                own_ref, far_ref, x_ref, r_ref, n_ref, sem_own, sem_x, sem_send, sem_recv, sem_r, sem_n):
    def load_own(i):
        return pltpu.make_async_copy(branch_ref.at[chunk(i)], own_ref.at[chunk(i)], sem_own.at[i])

    def load_rows(i):
        return pltpu.make_async_copy(rows_ref.at[side_chunk(i)], x_ref.at[chunk(i)], sem_x.at[i])

    for i in range(CHUNKS):
        load_own(i).start()
        load_rows(i).start()
    peer = greet_neighbour()

    def send(i):
        return pltpu.make_async_remote_copy(
            src_ref=branch_ref.at[chunk(i)], dst_ref=far_ref.at[chunk(i)], send_sem=sem_send.at[i],
            recv_sem=sem_recv.at[i], device_id=peer, device_id_type=MESH_ID)

    def save_res(i):
        return pltpu.make_async_copy(r_ref.at[chunk(i)], res_ref.at[chunk(i)], sem_r.at[i])

    def save_norm(i):
        return pltpu.make_async_copy(n_ref.at[chunk(i)], nm_ref.at[chunk(i)], sem_n.at[i])

    for i in range(CHUNKS):
        send(i).start()
    for i in range(CHUNKS):
        load_own(i).wait()
        load_rows(i).wait()
        send(i).wait_recv()
        r = x_ref[chunk(i), :].astype(F32) + (own_ref[chunk(i), :].astype(F32) + far_ref[chunk(i), :].astype(F32))
        r_ref[chunk(i), :] = r
        n_ref[chunk(i), :] = (norm_parts(r)[0] * gain_ref[1:2, :]).astype(BF)
        save_res(i).start()
        save_norm(i).start()
    for i in range(CHUNKS):
        send(i).wait_send()
        save_res(i).wait()
        save_norm(i).wait()


def anywhere():
    return pl.BlockSpec(memory_space=pl.ANY)


def in_vmem():
    return pl.BlockSpec(memory_space=pltpu.VMEM)


def dma(n=CHUNKS):
    return pltpu.SemaphoreType.DMA((n,))


def join(branch, rows, gains):
    return pl.pallas_call(
        join_kernel,
        in_specs=[anywhere(), anywhere(), in_vmem()],
        out_specs=[anywhere(), anywhere()],
        out_shape=[jax.ShapeDtypeStruct((LEN, D), F32), rows_shape],
        scratch_shapes=[pltpu.VMEM((LEN, D), BF), pltpu.VMEM((LEN, D), BF), pltpu.VMEM((LEN, D), BF),
                        pltpu.VMEM((LEN, D), F32), pltpu.VMEM((LEN, D), BF)] + [dma()] * 6,
        compiler_params=pltpu.CompilerParams(collective_id=3, has_side_effects=True, vmem_limit_bytes=60 << 20),
        name="join",
    )(branch, rows, gains)


def join_back_kernel(own_hbm, ra_hbm, rb_hbm, res_hbm, cot_hbm, gain_ref, grad_hbm, low_hbm, gsum_ref,
                     own_ref, recv_ref, far_ref, res_ref, cot_ref, grad_ref, low_ref,
                     sem_own, sem_r, sem_res, sem_cot, sem_send, sem_recv, sem_g, sem_l):
    half = CHUNKS // 2

    def load_own(i):
        return pltpu.make_async_copy(own_hbm.at[chunk(i)], own_ref.at[chunk(i)], sem_own.at[i])

    def load_recv(i):
        src = ra_hbm if i < half else rb_hbm
        return pltpu.make_async_copy(src.at[chunk(i % half)], recv_ref.at[chunk(i)], sem_r.at[i])

    def load_res(i):
        return pltpu.make_async_copy(res_hbm.at[chunk(i)], res_ref.at[chunk(i)], sem_res.at[i])

    def load_cot(i):
        return pltpu.make_async_copy(cot_hbm.at[side_chunk(i)], cot_ref.at[chunk(i)], sem_cot.at[i])

    for i in range(CHUNKS):
        load_own(i).start()
        load_recv(i).start()
    for i in range(CHUNKS):
        load_res(i).start()
        load_cot(i).start()
    peer = greet_neighbour()

    def send(i):
        return pltpu.make_async_remote_copy(
            src_ref=own_ref.at[chunk(i)], dst_ref=far_ref.at[chunk(i)], send_sem=sem_send.at[i],
            recv_sem=sem_recv.at[i], device_id=peer, device_id_type=MESH_ID)

    def save_grad(i):
        return pltpu.make_async_copy(grad_ref.at[chunk(i)], grad_hbm.at[chunk(i)], sem_g.at[i])

    def save_low(i):
        return pltpu.make_async_copy(low_ref.at[chunk(i)], low_hbm.at[chunk(i)], sem_l.at[i])

    for i in range(CHUNKS):
        load_own(i).wait()
        load_recv(i).wait()
        own_ref[chunk(i), :] = (own_ref[chunk(i), :].astype(F32) + recv_ref[chunk(i), :].astype(F32)).astype(BF)
        send(i).start()
    gsum = 0.0
    for i in range(CHUNKS):
        load_res(i).wait()
        load_cot(i).wait()
        send(i).wait_recv()
        g = own_ref[chunk(i), :].astype(F32) + far_ref[chunk(i), :].astype(F32)
        grad, part = norm_back(res_ref[chunk(i), :], gain_ref[1:2, :], g)
        gsum = gsum + part
        grad = cot_ref[chunk(i), :].astype(F32) + grad
        grad_ref[chunk(i), :] = grad
        low_ref[chunk(i), :] = grad.astype(BF)
        save_grad(i).start()
        save_low(i).start()
    gsum_ref[...] = gsum
    for i in range(CHUNKS):
        send(i).wait_send()
        save_grad(i).wait()
        save_low(i).wait()


def join_back(own, recv_a, recv_b, residual, cotangent, gains):
    return pl.pallas_call(
        join_back_kernel,
        in_specs=[anywhere()] * 5 + [in_vmem()],
        out_specs=[anywhere(), anywhere(), in_vmem()],
        out_shape=[jax.ShapeDtypeStruct((LEN, D), F32), rows_shape, jax.ShapeDtypeStruct((1, D), F32)],
        scratch_shapes=[pltpu.VMEM((LEN, D), BF), pltpu.VMEM((LEN, D), BF), pltpu.VMEM((LEN, D), BF),
                        pltpu.VMEM((LEN, D), F32), pltpu.VMEM((LEN, D), BF), pltpu.VMEM((LEN, D), F32),
                        pltpu.VMEM((LEN, D), BF)] + [dma()] * 8,
        compiler_params=pltpu.CompilerParams(collective_id=4, has_side_effects=True, vmem_limit_bytes=60 << 20),
        name="join_back",
    )(own, recv_a, recv_b, residual, cotangent, gains)


def finish_rows_kernel(gxn_hbm, gxc_hbm, noisy_hbm, clean_hbm, grad_hbm, gain_ref, outn_hbm, outc_hbm, gsum_ref,
                       own_ref, far_ref, x_ref, grad_ref, out_ref,
                       sem_own, sem_x, sem_grad, sem_send, sem_recv, sem_out):
    def pick(i):
        return (gxn_hbm, noisy_hbm, outn_hbm) if i < CHUNKS else (gxc_hbm, clean_hbm, outc_hbm)

    def load_own(i):
        return pltpu.make_async_copy(pick(i)[0].at[chunk(i % CHUNKS)], own_ref.at[chunk(i)], sem_own.at[i])

    def load_rows(i):
        return pltpu.make_async_copy(pick(i)[1].at[side_chunk(i % CHUNKS)], x_ref.at[chunk(i)], sem_x.at[i])

    def load_grad(i):
        return pltpu.make_async_copy(grad_hbm.at[chunk(i)], grad_ref.at[chunk(i)], sem_grad.at[i])

    for i in range(2 * CHUNKS):
        load_own(i).start()
        load_rows(i).start()
        if i < CHUNKS:
            load_grad(i).start()
    peer = greet_neighbour()

    def send(i):
        return pltpu.make_async_remote_copy(
            src_ref=pick(i)[0].at[chunk(i % CHUNKS)], dst_ref=far_ref.at[chunk(i)], send_sem=sem_send.at[i],
            recv_sem=sem_recv.at[i], device_id=peer, device_id_type=MESH_ID)

    def save(i):
        return pltpu.make_async_copy(out_ref.at[chunk(i)], pick(i)[2].at[chunk(i % CHUNKS)], sem_out.at[i])

    for i in range(2 * CHUNKS):
        send(i).start()
    gsum = 0.0
    for i in range(2 * CHUNKS):
        load_own(i).wait()
        load_rows(i).wait()
        if i < CHUNKS:
            load_grad(i).wait()
        send(i).wait_recv()
        g = own_ref[chunk(i), :].astype(F32) + far_ref[chunk(i), :].astype(F32)
        grad, part = norm_back(x_ref[chunk(i), :].astype(F32), gain_ref[0:1, :], g)
        gsum = gsum + part
        if i < CHUNKS:
            grad = grad_ref[chunk(i), :] + grad
        out_ref[chunk(i), :] = grad.astype(BF)
        save(i).start()
    gsum_ref[...] = gsum
    for i in range(2 * CHUNKS):
        send(i).wait_send()
        save(i).wait()


def finish_rows(gxn, gxc, noisy_rows, clean_rows, grad_resid, gains):
    return pl.pallas_call(
        finish_rows_kernel,
        in_specs=[anywhere()] * 5 + [in_vmem()],
        out_specs=[anywhere(), anywhere(), in_vmem()],
        out_shape=[rows_shape, rows_shape, jax.ShapeDtypeStruct((1, D), F32)],
        scratch_shapes=[pltpu.VMEM((2 * LEN, D), BF), pltpu.VMEM((2 * LEN, D), BF), pltpu.VMEM((2 * LEN, D), BF),
                        pltpu.VMEM((LEN, D), F32), pltpu.VMEM((2 * LEN, D), BF)]
        + [dma(2 * CHUNKS), dma(2 * CHUNKS), dma(), dma(2 * CHUNKS), dma(2 * CHUNKS), dma(2 * CHUNKS)],
        compiler_params=pltpu.CompilerParams(collective_id=5, has_side_effects=True, vmem_limit_bytes=60 << 20),
        name="finish_rows",
    )(gxn, gxc, noisy_rows, clean_rows, grad_resid, gains)


def lay_kernel(count, info_ref, *refs):
    sem = refs[-1]
    side = info_ref[0]
    copies = []
    for k in range(count):
        own, other, out = refs[2 * k], refs[2 * k + 1], refs[2 * count + k]
        for n, (src, at) in enumerate(((own, side), (other, 1 - side))):
            copies.append(pltpu.make_async_copy(
                src, out.at[pl.ds(pl.multiple_of(at * LEN, LEN), LEN)], sem.at[2 * k + n]))
    for c in copies:
        c.start()
    for c in copies:
        c.wait()


def lay(info, *pairs):
    count = len(pairs)
    return pl.pallas_call(
        functools.partial(lay_kernel, count),
        in_specs=[pl.BlockSpec(memory_space=pltpu.SMEM)] + [anywhere()] * (2 * count),
        out_specs=[anywhere()] * count,
        out_shape=[jax.ShapeDtypeStruct((2 * LEN, D), BF)] * count,
        scratch_shapes=[dma(2 * count)],
        name="lay",
    )(info, *[v for p in pairs for v in p])


def replica_sum_kernel(count, owners, x_ref, o_ref, in_ref, send_a, recv_a, send_b, recv_b):
    me = lax.axis_index("dp")
    m = lax.axis_index("mp")
    barrier = pltpu.get_barrier_semaphore()
    for k in range(1, count):
        pl.semaphore_signal(barrier, inc=1, device_id=(lax.rem(me + k, count), m), device_id_type=MESH_ID)
    pl.semaphore_wait(barrier, count - 1)

    def piece(j):
        return pl.ds(pl.multiple_of(j * 128, 128), 128)

    def part(j):
        return pltpu.make_async_remote_copy(
            src_ref=x_ref.at[:, piece(j)], dst_ref=in_ref.at[me], send_sem=send_a.at[j], recv_sem=recv_a.at[me],
            device_id=(j, m), device_id_type=MESH_ID)

    def whole(p):
        return pltpu.make_async_remote_copy(
            src_ref=o_ref.at[:, piece(me)], dst_ref=o_ref.at[:, piece(me)], send_sem=send_b.at[p],
            recv_sem=recv_b.at[me], device_id=(p, m), device_id_type=MESH_ID)

    for j in range(owners):
        @pl.when(me != j)
        def _():
            part(j).start()

    @pl.when(me < owners)
    def _():
        in_ref[me] = x_ref[:, piece(me)]
        for s in range(count):
            @pl.when(me != s)
            def _():
                pltpu.make_async_remote_copy(
                    src_ref=x_ref.at[:, piece(0)], dst_ref=in_ref.at[s], send_sem=send_a.at[0], recv_sem=recv_a.at[s],
                    device_id=(s, m), device_id_type=MESH_ID).wait_recv()
        total = in_ref[0]
        for s in range(1, count):
            total = total + in_ref[s]
        o_ref[:, piece(me)] = total
        for p in range(count):
            @pl.when(me != p)
            def _():
                whole(p).start()

    for j in range(owners):
        @pl.when(me != j)
        def _():
            pltpu.make_async_remote_copy(
                src_ref=o_ref.at[:, piece(j)], dst_ref=o_ref.at[:, piece(j)], send_sem=send_b.at[0],
                recv_sem=recv_b.at[j], device_id=(j, m), device_id_type=MESH_ID).wait_recv()
            part(j).wait_send()

    @pl.when(me < owners)
    def _():
        for p in range(count):
            @pl.when(me != p)
            def _():
                whole(p).wait_send()


def replica_sum(x, collective_id):
    count = lax.axis_size("dp")
    owners = x.shape[1] // 128
    if count != 8:
        return lax.psum(x, "dp")
    return pl.pallas_call(
        functools.partial(replica_sum_kernel, count, owners),
        out_shape=jax.ShapeDtypeStruct(x.shape, F32),
        in_specs=[pl.BlockSpec(memory_space=pltpu.VMEM)],
        out_specs=pl.BlockSpec(memory_space=pltpu.VMEM),
        scratch_shapes=[
            pltpu.VMEM((count, x.shape[0], 128), F32),
            pltpu.SemaphoreType.DMA((owners,)),
            pltpu.SemaphoreType.DMA((count,)),
            pltpu.SemaphoreType.DMA((count,)),
            pltpu.SemaphoreType.DMA((owners,)),
        ],
        compiler_params=pltpu.CompilerParams(collective_id=collective_id, has_side_effects=True),
        cost_estimate=pl.CostEstimate(flops=1000000, bytes_accessed=30000000, transcendentals=0),
        name="replica_sum",
    )(x)


def lefts_kernel(gq_ref, gqb_ref, eq_ref, go_ref, gob_ref, eo_ref, fq_ref, fo_ref, lu_ref, ld_ref, g1_ref, g2_ref,
                 mq_ref, mo_ref, pack_ref):
    pack_ref[...] = jnp.zeros_like(pack_ref)
    mq = gq_ref[...] + gqb_ref[...].astype(F32) + eq_ref[0]
    mq_ref[...] = mq
    pack_ref[0:8, :] = exact(fq_ref[...], mq, 1, 0)
    mo = go_ref[...] + gob_ref[...].astype(F32) + eo_ref[0]
    mo_ref[...] = mo
    pack_ref[8:16, 0:192] = exact(fo_ref[...], mo, 1, 1)
    pack_ref[16:24, :] = lu_ref[...]
    pack_ref[24:32, :] = ld_ref[...]
    pack_ref[32:33, :] = g1_ref[...]
    pack_ref[33:34, :] = g2_ref[...]


def lefts(gq, gq_back, err_qkv, go, go_back, err_out, fac_qkv, fac_out, left_up, left_down, gain_one, gain_two):
    args = (gq, gq_back, err_qkv, go, go_back, err_out, fac_qkv, fac_out, left_up, left_down, gain_one, gain_two)
    return pl.pallas_call(
        lefts_kernel,
        grid=(1,),
        in_specs=[whole(v.shape) for v in args],
        out_specs=[whole((9 * HD, D)), whole((3 * HD, D)), whole((5 * RANK, D))],
        out_shape=[jax.ShapeDtypeStruct((9 * HD, D), F32), jax.ShapeDtypeStruct((3 * HD, D), F32),
                   jax.ShapeDtypeStruct((5 * RANK, D), F32)],
        compiler_params=pltpu.CompilerParams(vmem_limit_bytes=40 << 20),
        name="lefts",
    )(*args)


def rights_kernel(sum_ref, mq_ref, mo_ref, mu_ref, md_ref, hq_ref, ho_ref, hu_ref, hd_ref, pack_ref):
    row = lax.broadcasted_iota(jnp.int32, (RANK, D), 0)
    mats = [sum_ref[RANK * t:RANK * (t + 1), :] for t in range(4)]
    for k in range(RANK):
        for t in range(4):
            a = mats[t]
            v = a[k:k + 1, :]
            e = v / (jnp.sqrt(jnp.sum(v * v, axis=1, keepdims=True)) + 1e-08)
            c = jnp.sum(a * e, axis=1, keepdims=True)
            mats[t] = jnp.where(row == k, e, jnp.where(row > k, a - c * e, a))
    hq_ref[...] = mats[0]
    ho_ref[...] = mats[1][:, :192]
    hu_ref[...] = mats[2]
    hd_ref[...] = mats[3]
    pack_ref[...] = jnp.zeros_like(pack_ref)
    pack_ref[0:8, 0:9 * HD] = exact(mats[0], mq_ref[...], 1, 1)
    pack_ref[8:16, :] = exact(mats[1][:, :192], mo_ref[...], 1, 0)
    pack_ref[16:24, :] = exact(mats[2], mu_ref[...], 1, 0)
    pack_ref[24:32, :] = exact(mats[3], md_ref[...], 1, 0)


def rights(left_sum, mats):
    args = (left_sum, *mats)
    shapes = [(RANK, D), (RANK, 3 * HD), (RANK, D), (RANK, D), (4 * RANK, D)]
    return pl.pallas_call(
        rights_kernel,
        grid=(1,),
        in_specs=[whole(v.shape) for v in args],
        out_specs=[whole(s) for s in shapes],
        out_shape=[jax.ShapeDtypeStruct(s, F32) for s in shapes],
        compiler_params=pltpu.CompilerParams(vmem_limit_bytes=40 << 20),
        name="rights",
    )(*args)


def update_kernel(replicas, rates, info_ref, *refs):
    sums, hats, mats, states = refs[0], refs[1:5], refs[5:9], refs[9:21]
    left_sum, gain_ref, gm_ref = refs[21:24]
    errs, news, right_out, gains_out = refs[24:28], refs[28:40], refs[40:44], refs[44:47]
    decay = min(0.9999, (1.0 + EMA_STEPS) / (10.0 + EMA_STEPS))
    share = D // replicas
    shift = lax.rem(D - info_ref[4] * share, D)

    def part(value):
        return pltpu.roll(value, shift, 1)[:, :share]

    for t in range(4):
        hat = hats[t][...]
        right = sums[RANK * t:RANK * (t + 1), :] * (1.0 / replicas)
        right_out[t][...] = right[:, :right_out[t].shape[1]]
        first, second = ((right[:, :9 * HD], hat), (hat, right), (hat, right), (hat, right))[t]
        errs[t][0] = mats[t][...] - exact(first, second, 0, 0)
        first, second = ((part(hat), right[:, :9 * HD]), (hat, part(right)), (part(hat), right), (part(right), hat))[t]
        moment = 0.5 * states[3 * t + 1][...] + exact(first, second, 0, 0)
        master = states[3 * t][...] - rates[t] * moment
        news[3 * t][...] = master
        news[3 * t + 1][...] = moment
        news[3 * t + 2][...] = decay * states[3 * t + 2][...] + (1.0 - decay) * master
    grad = left_sum[32:34, :] * (1.0 / replicas)
    moment = 0.5 * gm_ref[...] + grad
    gains_out[0][...] = grad
    gains_out[1][...] = gain_ref[...] - rates[4] * moment
    gains_out[2][...] = moment


def update(info, replicas, rates, right_sum, hats, mats, states, left_sum, gains, gain_moment):
    args = (right_sum, *hats, *mats, *states, left_sum, gains, gain_moment)
    shapes = [(1, *m.shape) for m in mats] + [s.shape for s in states]
    shapes += [(RANK, 9 * HD), (RANK, D), (RANK, D), (RANK, D)] + [(2, D)] * 3
    return pl.pallas_call(
        functools.partial(update_kernel, replicas, rates),
        grid_spec=pltpu.PrefetchScalarGridSpec(
            num_scalar_prefetch=1,
            grid=(1,),
            in_specs=[whole(v.shape) for v in args],
            out_specs=[whole(s) for s in shapes],
        ),
        out_shape=[jax.ShapeDtypeStruct(s, F32) for s in shapes],
        compiler_params=pltpu.CompilerParams(vmem_limit_bytes=60 << 20),
        name="update",
    )(info, *args)


def local(
    noisy_rows, clean_rows, block_size, cotangent, norm_gains,
    weight_qkv, weight_out, weight_up, weight_down,
    master_qkv, master_out, master_up, master_down,
    moment_qkv, moment_out, moment_up, moment_down,
    average_qkv, average_out, average_up, average_down,
    error_qkv, error_out, error_up, error_down,
    factor_qkv, factor_out, factor_up, factor_down,
    gain_moment,
):
    row_count = noisy_rows.shape[0]
    replicas = lax.axis_size("dp")
    side = lax.axis_index("mp") // 2

    def across(value):
        return lax.ppermute(value, "mp", [(0, 2), (2, 0), (1, 3), (3, 1)])

    def beside(value):
        return lax.ppermute(value, "mp", [(0, 1), (1, 0), (2, 3), (3, 2)])

    def hold(*values):
        return lax.optimization_barrier(values)

    cos, sin = rotary_tables()
    info = jnp.stack([side, 0, 0, 0, lax.axis_index("dp")]).astype(jnp.int32)
    w_near = weight_qkv.T
    w_far, o_far = across(w_near), across(weight_out)
    qn_near, qc_near, att_near, lse_near, xn, xc = attend_near(
        info, block_size, noisy_rows, clean_rows, norm_gains, w_near, cos, sin)
    qn_far, qc_far, att_far, lse_far, branch = attend_far(
        info, block_size, xn, xc, w_far, cos, sin, att_near, weight_out, o_far)
    residual, normed = join(branch, noisy_rows, norm_gains)
    half = LEN // 2
    normed_a, normed_b = across(normed[:half]), across(normed[half:])
    mlp, grad_mid, hidden, grad_pre = feed(info, normed, cotangent, weight_up, weight_down, False, 0)
    mlp_a, grad_a, hidden_a, grad_pre_a = feed(info, normed_a, cotangent, weight_up, weight_down, True, 0)
    grad_a = across(grad_a)
    mlp_b, grad_b, hidden_b, grad_pre_b = feed(info, normed_b, cotangent, weight_up, weight_down, True, 1)
    grad_b = across(grad_b)
    mlp_a, mlp_b = across(mlp_a), across(mlp_b)
    matrix_up, matrix_down, left_up, left_down = feed_grads(
        info, (normed, normed_a, normed_b), cotangent, (hidden, hidden_a, hidden_b), (grad_pre, grad_pre_a, grad_pre_b),
        error_up, error_down, factor_up.T, factor_down.T)
    grad_resid, grad_low, gain_two = join_back(grad_mid, grad_a, grad_b, residual, cotangent, norm_gains)
    mlp = (mlp.astype(F32) + jnp.concatenate([mlp_a, mlp_b], axis=0).astype(F32)).astype(BF)
    out_own = (residual + (mlp.astype(F32) + beside(mlp).astype(F32))).astype(BF)
    out_other = across(out_own)

    dn_far, dc_far, gq_far, go_far = back_far(
        info, block_size, qn_far, qc_far, att_far, lse_far, grad_low, o_far, cos, sin, xn, xc)
    gq_back, go_back = across(gq_far), across(go_far)
    grad_xn, grad_xc, gq_near, go_near = back_near(
        info, block_size, qn_near, qc_near, att_near, lse_near, grad_low, weight_out, cos, sin, xn, xc,
        w_near, w_far, dn_far, dc_far)
    noisy_own, clean_own, gain_one = finish_rows(grad_xn, grad_xc, noisy_rows, clean_rows, grad_resid, norm_gains)
    noisy_other, clean_other = across(noisy_own), across(clean_own)
    gain_part = jnp.concatenate([gain_one, gain_two], axis=0)
    gain_part = gain_part + across(gain_part)
    matrix_qkv, matrix_out, left_pack = lefts(
        gq_near, gq_back, jnp.swapaxes(error_qkv, 1, 2), go_near, go_back, error_out, factor_qkv.T, factor_out.T,
        left_up, left_down, gain_part[0:1], gain_part[1:2])
    left_sum = replica_sum(left_pack, 1)
    mats = (matrix_qkv, matrix_out, matrix_up, matrix_down)
    *hats, right_pack = rights(left_sum, mats)
    right_sum = replica_sum(right_pack, 2)
    rates = [3.0 / math.sqrt(f * row_count) for f in (D, HEADS * HD // 64, D, FF)] + [0.5 / math.sqrt(row_count)]
    states = (
        master_qkv, moment_qkv, average_qkv, master_out, moment_out, average_out,
        master_up, moment_up, average_up, master_down.T, moment_down.T, average_down.T,
    )
    done = update(info, replicas, rates, right_sum, hats, mats, states, left_sum, norm_gains, gain_moment)
    errs, news, right_new, gains_new = done[:4], done[4:16], done[16:20], done[20:23]
    block_out, grad_noisy, grad_clean = lay(
        info, (out_own, out_other), (noisy_own, noisy_other), (clean_own, clean_other))
    fresh = [news[3 * t + k] if t < 3 else news[3 * t + k].T for k in range(3) for t in range(4)]
    return (
        block_out, grad_noisy, grad_clean, *gains_new, *fresh,
        jnp.swapaxes(errs[0], 1, 2), *errs[1:], *[v.T for v in hats], *[v.T for v in right_new],
    )


def solution(mesh):
    in_specs = (
        P("dp", None), P("dp", None), P("dp"), P("dp", None), P(),
        P(None, "mp"), P("mp", None), P(None, "mp"), P("mp", None),
        *([P("dp", "mp"), P("mp", "dp")] * 6),
        *([P("dp", None, "mp"), P("dp", "mp", None)] * 2),
        *([P("mp", None), P(None, "mp")] * 2),
        P(),
    )
    out_specs = (
        P("dp", None), P("dp", None), P("dp", None), P(), P(), P(),
        *([P("dp", "mp"), P("mp", "dp")] * 6),
        *([P("dp", None, "mp"), P("dp", "mp", None)] * 2),
        *([P(None, "mp"), P("mp", None)] * 2),
        *([P("mp", None), P(None, "mp")] * 2),
    )
    return jax.shard_map(local, mesh=mesh, in_specs=in_specs, out_specs=out_specs, check_vma=False)
```

```python
import functools
import math

import jax
import jax.numpy as jnp
import numpy as np
from jax import lax
from jax.experimental import pallas as pl
from jax.experimental.pallas import tpu as pltpu
from jax.sharding import PartitionSpec as P

D = 768
HEADS = 12
HD = 64
FF = 3072
LEN = 1024
RANK = 8
EMA_STEPS = 4
TILE = 256
SLOT = 256

BF = jnp.bfloat16
F32 = jnp.float32
highest = lax.Precision.HIGHEST
norm_eps = 1e-05
gelu_coef = 0.7978845608028654
masked_score = -1e30
MESH_ID = pl.DeviceIdType.MESH


def nt(a, b):
    return lax.dot_general(a, b, (((1,), (1,)), ((), ())), preferred_element_type=F32)


def nn(a, b):
    return lax.dot_general(a, b, (((1,), (0,)), ((), ())), preferred_element_type=F32)


def tn(a, b):
    return lax.dot_general(a, b, (((0,), (0,)), ((), ())), preferred_element_type=F32)


def rotary_tables():
    half = HD // 2
    step = np.float32(-2.0 * math.log(10000.0) / HD)
    inverse = np.exp(np.arange(half, dtype=np.float32) * step).astype(np.float32)
    angle = (np.arange(LEN, dtype=np.float32)[:, None] * inverse[None, :]).astype(np.float32)
    c = np.cos(angle).astype(np.float32)
    s = np.sin(angle).astype(np.float32)
    return np.concatenate([c, c, c, c], 1), np.concatenate([-s, s, -s, s], 1)


def spin(v, cos, sin):
    lane = lax.broadcasted_iota(jnp.int32, v.shape, 1)
    low = lax.rem(lane, HD) < HD // 2
    swapped = jnp.where(low, pltpu.roll(v, 128 - HD // 2, 1), pltpu.roll(v, HD // 2, 1))
    return v * cos + swapped * sin


def block_ids(size, shape, dim):
    shift = 2 + (size >= 8).astype(jnp.int32) + (size >= 16).astype(jnp.int32)
    place = lax.broadcasted_iota(jnp.int32, shape, dim)
    return lax.shift_right_logical(place, jnp.full(shape, shift, jnp.int32))


def fill_bias(size, noisy_bias, clean_bias):
    keys = block_ids(size, (TILE, TILE), 0)
    rows = block_ids(size, (TILE, TILE), 1)
    noisy_bias[...] = jnp.where(rows == keys, 0.0, masked_score)
    clean_bias[...] = jnp.where(keys < rows, 0.0, masked_score)


def norm_parts(values):
    centered = values - jnp.mean(values, axis=1, keepdims=True)
    scale = lax.rsqrt(jnp.mean(centered * centered, axis=1, keepdims=True) + norm_eps)
    return centered * scale, scale


def norm_back(values, gain, grad):
    unit, scale = norm_parts(values)
    scaled = grad * gain
    inner = jnp.mean(scaled * unit, axis=1, keepdims=True)
    grad_in = scale * (scaled - jnp.mean(scaled, axis=1, keepdims=True) - unit * inner)
    return grad_in, jnp.sum(grad * unit, axis=0, keepdims=True)


def gelu_and_slope(u):
    square = u * u
    half = 0.5 + 0.5 * jnp.tanh(u * (gelu_coef + (gelu_coef * 0.044715) * square))
    slope = half + (u * (2.0 * half * (1.0 - half))) * (gelu_coef + (3.0 * 0.044715 * gelu_coef) * square)
    return u * half, slope


def whole(shape):
    return pl.BlockSpec(shape, lambda *index: (0,) * len(shape), pipeline_mode=pl.Buffered(1))


def side_rows(h, info, size):
    return (info[0], 0)


def lane2(h, *_):
    return (0, h)


def row3(h, *_):
    return (h, 0, 0)


def attend_head(head, xn_ref, xc_ref, w_ref, cos_ref, sin_ref, qn_ref, qc_ref, att_ref, lse_ref,
                bn_ref, bc_ref, kn_ref, kc_ref, vnt_ref, vct_ref):
    w = w_ref[pl.ds(pl.multiple_of(head * 3 * HD, 3 * HD), 3 * HD), :]
    for src, dst, keys, vals in ((xn_ref, qn_ref, kn_ref, vnt_ref), (xc_ref, qc_ref, kc_ref, vct_ref)):
        a = nt(src[...], w)
        r = spin(a[:, :128], cos_ref[...], sin_ref[...]).astype(BF)
        v = a[:, 128:].astype(BF)
        dst[:, :128] = r
        dst[:, 128:192] = v
        keys[...] = r[:, 64:128]
        vals[...] = jnp.transpose(v)
    here = pl.ds(pl.multiple_of(head * HD, HD), HD)
    for i in range(LEN // TILE):
        lo, hi = i * TILE, (i + 1) * TILE
        q = qn_ref[lo:hi, 0:64] * 0.125
        parts = [nt(kn_ref[lo:hi, :], q) + bn_ref[...], nt(kc_ref[lo:hi, :], q) + bc_ref[...]]
        if i:
            parts.append(nt(kc_ref[0:lo, :], q))
        peak = functools.reduce(jnp.maximum, [jnp.max(s, axis=0, keepdims=True) for s in parts])
        exps = [jnp.exp(s - peak) for s in parts]
        total = functools.reduce(jnp.add, [jnp.sum(e, axis=0, keepdims=True) for e in exps])
        inv = 1.0 / total
        low = [(e * inv).astype(BF) for e in exps]
        o = nn(vnt_ref[:, lo:hi], low[0]) + nn(vct_ref[:, lo:hi], low[1])
        if i:
            o = o + nn(vct_ref[:, 0:lo], low[2])
        att_ref[here, lo:hi] = o.astype(BF)
        lse_ref[0, :, lo:hi] = jnp.broadcast_to(peak + jnp.log(total), (8, TILE))


def attend_near_kernel(info_ref, size_ref, noisy_hbm, clean_hbm, gain_ref, w_ref, cos_ref, sin_ref,
                       qn_ref, qc_ref, att_ref, lse_ref, xn_hbm, xc_hbm, raw_ref, x_ref, sem_in, sem_out, *work):
    head = pl.program_id(0)
    sides = ((noisy_hbm, xn_hbm), (clean_hbm, xc_hbm))

    def load(s, i):
        at = pl.ds(pl.multiple_of(info_ref[0] * LEN + i * TILE, TILE), TILE)
        return pltpu.make_async_copy(sides[s][0].at[at], raw_ref.at[s, chunk(i)], sem_in.at[CHUNKS * s + i])

    def save(s):
        return pltpu.make_async_copy(x_ref.at[s], sides[s][1], sem_out.at[s])

    @pl.when(head == 0)
    def _():
        for s in range(2):
            for i in range(CHUNKS):
                load(s, i).start()
        fill_bias(size_ref[info_ref[0]], work[0], work[1])
        for s in range(2):
            for i in range(CHUNKS):
                load(s, i).wait()
                x = norm_parts(raw_ref[s, chunk(i), :].astype(F32))[0] * gain_ref[0:1, :]
                x_ref[s, chunk(i), :] = x.astype(BF)
            save(s).start()

    attend_head(head, x_ref.at[0], x_ref.at[1], w_ref, cos_ref, sin_ref, qn_ref, qc_ref, att_ref, lse_ref, *work)

    @pl.when(head == 2)
    def _():
        save(0).wait()
        save(1).wait()


def attend_far_kernel(info_ref, size_ref, xn_ref, xc_ref, w_ref, cos_ref, sin_ref,
                      qn_ref, qc_ref, att_ref, lse_ref, *work):
    head = pl.program_id(0)

    @pl.when(head == 0)
    def _():
        fill_bias(size_ref[info_ref[0]], work[0], work[1])

    attend_head(head, xn_ref, xc_ref, w_ref, cos_ref, sin_ref, qn_ref, qc_ref, att_ref, lse_ref, *work)


CHUNKS = LEN // TILE
HALF = LEN // 2


def chunk(i):
    return slice(i * TILE, (i + 1) * TILE)


def anywhere():
    return pl.BlockSpec(memory_space=pl.ANY)


def in_vmem():
    return pl.BlockSpec(memory_space=pltpu.VMEM)


def dma(n):
    return pltpu.SemaphoreType.DMA((n,))


def rows_of(n):
    return jax.ShapeDtypeStruct((n, D), BF)


attend_work = [
    pltpu.VMEM((TILE, TILE), F32),
    pltpu.VMEM((TILE, TILE), F32),
    pltpu.VMEM((LEN, HD), BF),
    pltpu.VMEM((LEN, HD), BF),
    pltpu.VMEM((HD, LEN), BF),
    pltpu.VMEM((HD, LEN), BF),
]
head_specs = [
    pl.BlockSpec((LEN, SLOT), lane2),
    pl.BlockSpec((LEN, SLOT), lane2),
    whole((3 * HD, LEN)),
    pl.BlockSpec((1, 8, LEN), row3),
]
head_shapes = [
    jax.ShapeDtypeStruct((LEN, SLOT * 3), BF),
    jax.ShapeDtypeStruct((LEN, SLOT * 3), BF),
    jax.ShapeDtypeStruct((3 * HD, LEN), BF),
    jax.ShapeDtypeStruct((3, 8, LEN), F32),
]
rows_shape = jax.ShapeDtypeStruct((LEN, D), BF)


def attend_near(info, size, noisy, clean, gains, w, cos, sin):
    return pl.pallas_call(
        attend_near_kernel,
        grid_spec=pltpu.PrefetchScalarGridSpec(
            num_scalar_prefetch=2,
            grid=(3,),
            in_specs=[
                anywhere(),
                anywhere(),
                whole((2, D)),
                whole((9 * HD, D)),
                whole((LEN, 128)),
                whole((LEN, 128)),
            ],
            out_specs=head_specs + [anywhere(), anywhere()],
            scratch_shapes=[pltpu.VMEM((2, LEN, D), BF), pltpu.VMEM((2, LEN, D), BF), dma(2 * CHUNKS), dma(2)] + attend_work,
        ),
        out_shape=head_shapes + [rows_shape, rows_shape],
        compiler_params=pltpu.CompilerParams(vmem_limit_bytes=60 << 20),
        name="attend_near",
    )(info, size, noisy, clean, gains, w, cos, sin)


def attend_far(info, size, xn, xc, w, cos, sin):
    return pl.pallas_call(
        attend_far_kernel,
        grid_spec=pltpu.PrefetchScalarGridSpec(
            num_scalar_prefetch=2,
            grid=(3,),
            in_specs=[whole((LEN, D)), whole((LEN, D)), whole((9 * HD, D)), whole((LEN, 128)), whole((LEN, 128))],
            out_specs=head_specs,
            scratch_shapes=attend_work,
        ),
        out_shape=head_shapes,
        compiler_params=pltpu.CompilerParams(vmem_limit_bytes=60 << 20),
        name="attend_far",
    )(info, size, xn, xc, w, cos, sin)


def back_head(head, qn_ref, qc_ref, lse_ref, cos_ref, sin_ref, dn_ref, dc_ref,
              bn_ref, bc_ref, kn_ref, kc_ref, knt_ref, kct_ref, dot_ref, do_ref, dq_ref, dkn_ref, dkc_ref, dvc_ref):
    do_ref[...] = jnp.transpose(dot_ref[pl.ds(pl.multiple_of(head * HD, HD), HD), :])
    kn_ref[...] = qn_ref[:, 64:128]
    kc_ref[...] = qc_ref[:, 64:128]
    knt_ref[...] = jnp.transpose(qn_ref[:, 0:128])[64:128]
    kct_ref[...] = jnp.transpose(qc_ref[:, 0:128])[64:128]
    dkc_ref[...] = jnp.zeros_like(dkc_ref)
    dvc_ref[...] = jnp.zeros_like(dvc_ref)
    blank = jnp.zeros((TILE, HD), F32)
    for i in range(LEN // TILE):
        lo, hi = i * TILE, (i + 1) * TILE
        q = qn_ref[lo:hi, 0:64] * 0.125
        do = do_ref[lo:hi, :]
        lse = lse_ref[0, 0:1, lo:hi]
        spans = [(0, lo, hi), (1, lo, hi)] + ([(1, 0, lo)] if i else [])
        probs, grads, inner = [], [], 0.0
        for n, (side, a, b) in enumerate(spans):
            kr = kc_ref if side else kn_ref
            vr = qc_ref if side else qn_ref
            s = nt(kr[a:b, :], q)
            if n == 0:
                s = s + bn_ref[...]
            if n == 1:
                s = s + bc_ref[...]
            p = jnp.exp(s - lse)
            dp = nt(vr[a:b, 128:192], do)
            inner = inner + jnp.sum(p * dp, axis=0, keepdims=True)
            probs.append(p)
            grads.append(dp)
        dqt = 0.0
        for n, (side, a, b) in enumerate(spans):
            ds = (probs[n] * (grads[n] - inner)).astype(BF)
            dv = nn(probs[n].astype(BF), do)
            dk = nn(ds, q)
            ktr = kct_ref if side else knt_ref
            dqt = dqt + nn(ktr[:, a:b], ds)
            if side:
                dkc_ref[a:b, :] += dk
                dvc_ref[a:b, :] += dv
            else:
                dkn_ref[a:b, :] = dk
                dn_ref[lo:hi, 128:256] = jnp.concatenate([dv, blank], axis=1).astype(BF)
        dq_ref[lo:hi, :] = jnp.transpose(dqt) * 0.125
    zero = jnp.zeros((LEN, HD), F32)
    sin = -sin_ref[...]
    cos = cos_ref[...]
    dn_ref[:, 0:128] = spin(jnp.concatenate([dq_ref[...], dkn_ref[...]], axis=1), cos, sin).astype(BF)
    dc_ref[:, 0:128] = spin(jnp.concatenate([zero, dkc_ref[...]], axis=1), cos, sin).astype(BF)
    dc_ref[:, 128:256] = jnp.concatenate([dvc_ref[...], zero], axis=1).astype(BF)


def head_grad(xn_ref, xc_ref, dn_ref, dc_ref, gq_ref):
    g = tn(dn_ref[...], xn_ref[...]) + tn(dc_ref[...], xc_ref[...])
    gq_ref[...] = g[:3 * HD].astype(gq_ref.dtype)


def back_far_kernel(info_ref, size_ref, qn_ref, qc_ref, att_ref, lse_ref, g_ref, wo_ref, cos_ref, sin_ref,
                    xn_hbm, xc_hbm, dn_ref, dc_ref, gq_ref, go_ref, xn_ref, xc_ref, sems, *work):
    head = pl.program_id(0)
    late = [pltpu.make_async_copy(s, d, sems.at[k]) for k, (s, d) in enumerate(((xn_hbm, xn_ref), (xc_hbm, xc_ref)))]

    @pl.when(head == 0)
    def _():
        for c in late:
            c.start()
        fill_bias(size_ref[info_ref[0]], work[0], work[1])
        work[6][...] = nt(wo_ref[...], g_ref[...]).astype(BF)
        go_ref[...] = nn(att_ref[...], g_ref[...]).astype(BF)

    back_head(head, qn_ref, qc_ref, lse_ref, cos_ref, sin_ref, dn_ref, dc_ref, *work)

    @pl.when(head == 0)
    def _():
        for c in late:
            c.wait()

    head_grad(xn_ref, xc_ref, dn_ref, dc_ref, gq_ref)


def back_near_kernel(info_ref, size_ref, qn_ref, qc_ref, att_ref, lse_ref, g_ref, wo_ref, cos_ref, sin_ref,
                     xn_hbm, xc_hbm, w_hbm, w_far_hbm, dnf_hbm, dcf_hbm, gxn_hbm, gxc_hbm, gq_ref, go_ref,
                     xn_ref, xc_ref, w_ref, w_far_ref, dnf_ref, dcf_ref, keep_ref, dn_ref, dc_ref, out_ref,
                     sems, sem_out, *work):
    head = pl.program_id(0)
    late = [pltpu.make_async_copy(s, d, sems.at[k]) for k, (s, d) in enumerate((
        (xn_hbm, xn_ref), (xc_hbm, xc_ref), (w_hbm, w_ref), (w_far_hbm, w_far_ref),
        (dnf_hbm, dnf_ref), (dcf_hbm, dcf_ref)))]

    @pl.when(head == 0)
    def _():
        for c in late:
            c.start()
        fill_bias(size_ref[info_ref[0]], work[0], work[1])
        work[6][...] = nt(wo_ref[...], g_ref[...]).astype(BF)
        go_ref[...] = nn(att_ref[...], g_ref[...])

    back_head(head, qn_ref, qc_ref, lse_ref, cos_ref, sin_ref, dn_ref, dc_ref, *work)

    @pl.when(head == 0)
    def _():
        for c in late:
            c.wait()

    head_grad(xn_ref, xc_ref, dn_ref, dc_ref, gq_ref)
    keep_ref[0, head] = dn_ref[...]
    keep_ref[1, head] = dc_ref[...]

    @pl.when(head == 2)
    def _():
        copies = []
        for s, (far, out) in enumerate(((dnf_ref, gxn_hbm), (dcf_ref, gxc_hbm))):
            for i in range(CHUNKS):
                total = 0.0
                for j in range(3):
                    total = total + nn(keep_ref[s, j, chunk(i), 0:192], w_ref[192 * j:192 * (j + 1), :])
                    total = total + nn(far[chunk(i), SLOT * j:SLOT * j + 192], w_far_ref[192 * j:192 * (j + 1), :])
                out_ref[s, chunk(i), :] = total.astype(BF)
                copies.append(pltpu.make_async_copy(
                    out_ref.at[s, chunk(i)], out.at[chunk(i)], sem_out.at[CHUNKS * s + i]))
                copies[-1].start()
        for c in copies:
            c.wait()


back_work = attend_work[:4] + [
    pltpu.VMEM((HD, LEN), BF),
    pltpu.VMEM((HD, LEN), BF),
    pltpu.VMEM((3 * HD, LEN), BF),
    pltpu.VMEM((LEN, HD), BF),
    pltpu.VMEM((LEN, HD), F32),
    pltpu.VMEM((LEN, HD), F32),
    pltpu.VMEM((LEN, HD), F32),
    pltpu.VMEM((LEN, HD), F32),
]
wide_rows = jax.ShapeDtypeStruct((LEN, 3 * SLOT), BF)


row2_spec = pl.BlockSpec((3 * HD, D), lambda h, *_: (h, 0))


def back_far(info, size, qn, qc, att, lse, g, wo, cos, sin, xn, xc):
    return pl.pallas_call(
        back_far_kernel,
        grid_spec=pltpu.PrefetchScalarGridSpec(
            num_scalar_prefetch=2,
            grid=(3,),
            in_specs=head_specs[:2] + [whole((3 * HD, LEN)), head_specs[3], whole((LEN, D)), whole((3 * HD, D)),
                                       whole((LEN, 128)), whole((LEN, 128)), anywhere(), anywhere()],
            out_specs=head_specs[:2] + [row2_spec, whole((3 * HD, D))],
            scratch_shapes=[pltpu.VMEM((LEN, D), BF), pltpu.VMEM((LEN, D), BF), dma(2)] + back_work,
        ),
        out_shape=[wide_rows, wide_rows, rows_of(9 * HD), rows_of(3 * HD)],
        compiler_params=pltpu.CompilerParams(vmem_limit_bytes=60 << 20),
        name="back_far",
    )(info, size, qn, qc, att, lse, g, wo, cos, sin, xn, xc)


def back_near(info, size, qn, qc, att, lse, g, wo, cos, sin, xn, xc, w, w_far, dn_far, dc_far):
    return pl.pallas_call(
        back_near_kernel,
        grid_spec=pltpu.PrefetchScalarGridSpec(
            num_scalar_prefetch=2,
            grid=(3,),
            in_specs=head_specs[:2] + [whole((3 * HD, LEN)), head_specs[3], whole((LEN, D)), whole((3 * HD, D)),
                                       whole((LEN, 128)), whole((LEN, 128))] + [anywhere()] * 6,
            out_specs=[anywhere(), anywhere(), row2_spec, whole((3 * HD, D))],
            scratch_shapes=[pltpu.VMEM((LEN, D), BF), pltpu.VMEM((LEN, D), BF),
                            pltpu.VMEM((9 * HD, D), BF), pltpu.VMEM((9 * HD, D), BF),
                            pltpu.VMEM((LEN, 3 * SLOT), BF), pltpu.VMEM((LEN, 3 * SLOT), BF),
                            pltpu.VMEM((2, 3, LEN, SLOT), BF), pltpu.VMEM((LEN, SLOT), BF), pltpu.VMEM((LEN, SLOT), BF),
                            pltpu.VMEM((2, LEN, D), BF), dma(6), dma(2 * CHUNKS)] + back_work,
        ),
        out_shape=[rows_shape, rows_shape, jax.ShapeDtypeStruct((9 * HD, D), F32), jax.ShapeDtypeStruct((3 * HD, D), F32)],
        compiler_params=pltpu.CompilerParams(vmem_limit_bytes=60 << 20),
        name="back_near",
    )(info, size, qn, qc, att, lse, g, wo, cos, sin, xn, xc, w, w_far, dn_far, dc_far)


def feed_kernel(mode, info_ref, nm_hbm, cot_hbm, up_hbm, down_hbm, mlp_hbm, gm_hbm, hid_hbm, gp_hbm,
                nm_ref, cot_ref, up_ref, down_ref, mlp_ref, gm_ref, hid_ref, gp_ref, sem_in, sem_tile, sem_row):
    width = D // 3
    rows = nm_ref.shape[0]
    side, half = info_ref[0], info_ref[2]
    start = (side * LEN, (1 - side) * LEN + half * HALF, (1 - side) * LEN + (1 - half) * HALF)[mode]
    cot_rows = cot_hbm.at[pl.ds(pl.multiple_of(start, HALF), rows)]
    loads = [pltpu.make_async_copy(s, d, sem_in.at[k]) for k, (s, d) in enumerate((
        (nm_hbm, nm_ref), (up_hbm, up_ref), (cot_rows, cot_ref), (down_hbm, down_ref)))]
    for c in loads:
        c.start()
    saves = []
    for t in range(3):
        lanes = slice(t * width, (t + 1) * width)
        if t == 0:
            loads[0].wait()
            loads[1].wait()
        pre = nn(nm_ref[...], up_ref[:, lanes])
        hidden, slope = gelu_and_slope(pre)
        hid_ref[:, lanes] = hidden.astype(BF)
        if t == 0:
            loads[2].wait()
            loads[3].wait()
        gp_ref[:, lanes] = (slope * nt(cot_ref[...], down_ref[lanes, :])).astype(BF)
        for k, (v, o) in enumerate(((hid_ref, hid_hbm), (gp_ref, gp_hbm))):
            saves.append(pltpu.make_async_copy(v.at[:, lanes], o.at[:, lanes], sem_tile.at[2 * t + k]))
            saves[-1].start()
    for i in range(rows // TILE):
        at = chunk(i)
        gm_ref[at, :] = nt(gp_ref[at, :], up_ref[...]).astype(BF)
        mlp_ref[at, :] = nn(hid_ref[at, :], down_ref[...]).astype(BF)
        for k, (v, o) in enumerate(((gm_ref, gm_hbm), (mlp_ref, mlp_hbm))):
            saves.append(pltpu.make_async_copy(v.at[at], o.at[at], sem_row.at[2 * i + k]))
            saves[-1].start()
    for c in saves:
        c.wait()


def feed(info, nm, cotangent, up, down, mode):
    rows = nm.shape[0]
    return pl.pallas_call(
        functools.partial(feed_kernel, mode),
        in_specs=[pl.BlockSpec(memory_space=pltpu.SMEM)] + [anywhere()] * 4,
        out_specs=[anywhere()] * 4,
        out_shape=[rows_of(rows)] * 4,
        scratch_shapes=[pltpu.VMEM((rows, D), BF), pltpu.VMEM((rows, D), BF), pltpu.VMEM((D, D), BF), pltpu.VMEM((D, D), BF)]
        + [pltpu.VMEM((rows, D), BF)] * 4 + [dma(4), dma(6), dma(2 * rows // TILE)],
        compiler_params=pltpu.CompilerParams(vmem_limit_bytes=60 << 20),
        name=("feed_near", "feed_a", "feed_b")[mode],
    )(info, nm, cotangent, up, down)


def halves(v):
    high = v.astype(BF)
    return high, (v - high.astype(F32)).astype(BF)


def exact(left_side, right_side, left_dim, right_dim):
    dims = (((left_dim,), (right_dim,)), ((), ()))
    a, b = halves(left_side)
    c, d = halves(right_side)

    def times(x, y):
        return lax.dot_general(x, y, dims, preferred_element_type=F32)

    return times(a, c) + (times(a, d) + times(b, c))


def feed_grads_kernel(info_ref, nm_hbm, nma_hbm, nmb_hbm, cot_ref, cot_far_ref, hid_ref, hida_ref, hidb_ref,
                      gp_ref, gpa_ref, gpb_ref, err_up_ref, err_down_ref, fac_up_ref, fac_down_ref,
                      mat_up_ref, mat_down_ref, left_up_ref, left_down_ref, nm_ref, nmt_ref, sems):
    step = pl.program_id(0)
    late = [pltpu.make_async_copy(s, nm_ref.at[at], sems.at[k]) for k, (s, at) in enumerate((
        (nm_hbm, slice(0, LEN)), (nma_hbm, slice(LEN, LEN + HALF)), (nmb_hbm, slice(LEN + HALF, 2 * LEN))))]

    @pl.when(step == 0)
    def _():
        for c in late:
            c.start()

    half = info_ref[2]
    cot_a = cot_far_ref[pl.ds(pl.multiple_of(half * HALF, HALF), HALF), :]
    cot_b = cot_far_ref[pl.ds(pl.multiple_of((1 - half) * HALF, HALF), HALF), :]
    mat_down = (tn(hid_ref[...], cot_ref[...]) + tn(hida_ref[...], cot_a) + tn(hidb_ref[...], cot_b)) + err_down_ref[0]
    mat_down_ref[...] = mat_down
    left_down_ref[...] = exact(fac_down_ref[...], mat_down, 1, 1)

    @pl.when(step == 0)
    def _():
        for c in late:
            c.wait()
        nmt_ref[...] = jnp.transpose(nm_ref[...])

    mat_up = (nn(nmt_ref[:, :LEN], gp_ref[...]) + nn(nmt_ref[:, LEN:LEN + HALF], gpa_ref[...])
              + nn(nmt_ref[:, LEN + HALF:], gpb_ref[...])) + err_up_ref[0]
    mat_up_ref[...] = mat_up
    part = exact(fac_up_ref[...], mat_up, 1, 1)

    @pl.when(step == 0)
    def _():
        left_up_ref[...] = part

    @pl.when(step > 0)
    def _():
        left_up_ref[...] += part


def feed_grads(info, nms, cotangent, hids, gps, err_up, err_down, fac_up, fac_down):
    width = D // 3
    rows = [a.shape[0] for a in nms]

    def near_rows(h, at):
        return (at[0], 0)

    def other_rows(h, at):
        return (1 - at[0], 0)

    return pl.pallas_call(
        feed_grads_kernel,
        grid_spec=pltpu.PrefetchScalarGridSpec(
            num_scalar_prefetch=1,
            grid=(3,),
            in_specs=[
                *[anywhere() for n in rows],
                pl.BlockSpec((LEN, D), near_rows, pipeline_mode=pl.Buffered(1)),
                pl.BlockSpec((LEN, D), other_rows, pipeline_mode=pl.Buffered(1)),
                *[pl.BlockSpec((n, width), lane2) for n in rows],
                *[pl.BlockSpec((n, width), lane2) for n in rows],
                pl.BlockSpec((1, D, width), lambda h, *_: (0, 0, h)),
                pl.BlockSpec((1, width, D), lambda h, *_: (0, h, 0)),
                pl.BlockSpec((RANK, width), lane2),
                whole((RANK, D)),
            ],
            out_specs=[
                pl.BlockSpec((D, width), lane2),
                pl.BlockSpec((width, D), lambda h, *_: (h, 0)),
                whole((RANK, D)),
                pl.BlockSpec((RANK, width), lane2),
            ],
            scratch_shapes=[pltpu.VMEM((2 * LEN, D), BF), pltpu.VMEM((D, 2 * LEN), BF), dma(3)],
        ),
        out_shape=[jax.ShapeDtypeStruct((D, D), F32), jax.ShapeDtypeStruct((D, D), F32),
                   jax.ShapeDtypeStruct((RANK, D), F32), jax.ShapeDtypeStruct((RANK, D), F32)],
        compiler_params=pltpu.CompilerParams(vmem_limit_bytes=60 << 20),
        name="feed_grads",
    )(info, *nms, cotangent, cotangent, *hids, *gps, err_up, err_down, fac_up, fac_down)


def greet_neighbour():
    dp = lax.axis_index("dp")
    m = lax.axis_index("mp")
    other = m + 1 - 2 * lax.rem(m, 2)
    barrier = pltpu.get_barrier_semaphore()
    pl.semaphore_signal(barrier, inc=1, device_id=(dp, other), device_id_type=MESH_ID)
    pl.semaphore_wait(barrier, 1)
    return (dp, other)


PARTS = HALF // TILE


def own_rows(i):
    half = lax.rem(lax.axis_index("mp"), 2)
    return pl.ds(pl.multiple_of(half * HALF + i * TILE, TILE), TILE)


def peer_rows(i):
    half = lax.rem(lax.axis_index("mp"), 2)
    return pl.ds(pl.multiple_of((1 - half) * HALF + i * TILE, TILE), TILE)


def side_rows_of(i):
    m = lax.axis_index("mp")
    return pl.ds(pl.multiple_of(m * HALF + i * TILE, TILE), TILE)


def copy(src, dst, sem):
    return pltpu.make_async_copy(src, dst, sem)


def push(src, dst, send_sem, recv_sem, peer):
    return pltpu.make_async_remote_copy(
        src_ref=src, dst_ref=dst, send_sem=send_sem, recv_sem=recv_sem, device_id=peer, device_id_type=MESH_ID)


def join_kernel(att_near_hbm, att_far_hbm, wo_near_hbm, wo_far_hbm, rows_hbm, gain_ref, res_hbm, nm_hbm, na_hbm,
                att_ref, wo_ref, x_ref, send_ref, far_ref, r_ref, n_ref,
                sem_in, sem_x, sem_send, sem_recv, sem_send_n, sem_recv_n, sem_out):
    width = 3 * HD
    loads = [copy(att_near_hbm, att_ref.at[0:width], sem_in.at[0]), copy(att_far_hbm, att_ref.at[width:], sem_in.at[1]),
             copy(wo_near_hbm, wo_ref.at[0:width], sem_in.at[2]), copy(wo_far_hbm, wo_ref.at[width:], sem_in.at[3])]
    rows = [copy(rows_hbm.at[side_rows_of(i)], x_ref.at[chunk(i)], sem_x.at[i]) for i in range(PARTS)]
    for c in loads + rows:
        c.start()
    peer = greet_neighbour()
    for c in loads:
        c.wait()
    pushes = []
    for i in range(PARTS):
        send_ref[chunk(i), :] = tn(att_ref[:, peer_rows(i)], wo_ref[...]).astype(BF)
        pushes.append(push(send_ref.at[chunk(i)], far_ref.at[chunk(i)], sem_send.at[i], sem_recv.at[i], peer))
        pushes[-1].start()
    saves = []
    for i in range(PARTS):
        own = tn(att_ref[:, own_rows(i)], wo_ref[...])
        rows[i].wait()
        pushes[i].wait_recv()
        r = x_ref[chunk(i), :].astype(F32) + (own + far_ref[chunk(i), :].astype(F32))
        r_ref[chunk(i), :] = r
        n_ref[chunk(i), :] = (norm_parts(r)[0] * gain_ref[1:2, :]).astype(BF)
        pushes.append(push(n_ref.at[chunk(i)], nm_hbm.at[own_rows(i)], sem_send_n.at[i], sem_recv_n.at[i], peer))
        pushes[-1].start()
        saves += [copy(r_ref.at[chunk(i)], res_hbm.at[chunk(i)], sem_out.at[3 * i]),
                  copy(n_ref.at[chunk(i)], nm_hbm.at[own_rows(i)], sem_out.at[3 * i + 1]),
                  copy(n_ref.at[chunk(i)], na_hbm.at[chunk(i)], sem_out.at[3 * i + 2])]
        for c in saves[-3:]:
            c.start()
    for c in saves:
        c.wait()
    for k, c in enumerate(pushes):
        c.wait_send()
        if k >= PARTS:
            c.wait_recv()


def join(att_near, att_far, wo_near, wo_far, rows, gains):
    return pl.pallas_call(
        join_kernel,
        in_specs=[anywhere()] * 5 + [in_vmem()],
        out_specs=[anywhere()] * 3,
        out_shape=[jax.ShapeDtypeStruct((HALF, D), F32), rows_of(LEN), rows_of(HALF)],
        scratch_shapes=[pltpu.VMEM((6 * HD, LEN), BF), pltpu.VMEM((6 * HD, D), BF), pltpu.VMEM((HALF, D), BF),
                        pltpu.VMEM((HALF, D), BF), pltpu.VMEM((HALF, D), BF), pltpu.VMEM((HALF, D), F32),
                        pltpu.VMEM((HALF, D), BF), dma(4)] + [dma(PARTS)] * 5 + [dma(3 * PARTS)],
        compiler_params=pltpu.CompilerParams(collective_id=3, has_side_effects=True, vmem_limit_bytes=60 << 20),
        name="join",
    )(att_near, att_far, wo_near, wo_far, rows, gains)


def join_back_kernel(gm_hbm, ra_hbm, rb_hbm, res_hbm, cot_hbm, gain_ref, grad_hbm, low_hbm, gsum_ref,
                     own_ref, away_ref, ra_ref, rb_ref, far_ref, res_ref, cot_ref, grad_ref, low_ref,
                     sem_in, sem_send, sem_recv, sem_send_l, sem_recv_l, sem_out):
    first, second = [], []
    for i in range(PARTS):
        first += [copy(gm_hbm.at[peer_rows(i)], away_ref.at[chunk(i)], sem_in.at[6 * i]),
                  copy(rb_hbm.at[chunk(i)], rb_ref.at[chunk(i)], sem_in.at[6 * i + 1])]
        second += [copy(gm_hbm.at[own_rows(i)], own_ref.at[chunk(i)], sem_in.at[6 * i + 2]),
                   copy(ra_hbm.at[chunk(i)], ra_ref.at[chunk(i)], sem_in.at[6 * i + 3]),
                   copy(res_hbm.at[chunk(i)], res_ref.at[chunk(i)], sem_in.at[6 * i + 4]),
                   copy(cot_hbm.at[side_rows_of(i)], cot_ref.at[chunk(i)], sem_in.at[6 * i + 5])]
    for c in first + second:
        c.start()
    peer = greet_neighbour()
    pushes = []
    for i in range(PARTS):
        first[2 * i].wait()
        first[2 * i + 1].wait()
        away_ref[chunk(i), :] = (away_ref[chunk(i), :].astype(F32) + rb_ref[chunk(i), :].astype(F32)).astype(BF)
        pushes.append(push(away_ref.at[chunk(i)], far_ref.at[chunk(i)], sem_send.at[i], sem_recv.at[i], peer))
        pushes[-1].start()
    gsum = 0.0
    saves = []
    for i in range(PARTS):
        for c in second[4 * i:4 * i + 4]:
            c.wait()
        part = own_ref[chunk(i), :].astype(F32) + ra_ref[chunk(i), :].astype(F32)
        pushes[i].wait_recv()
        grad, share = norm_back(res_ref[chunk(i), :], gain_ref[1:2, :], part + far_ref[chunk(i), :].astype(F32))
        gsum = gsum + share
        grad = cot_ref[chunk(i), :].astype(F32) + grad
        grad_ref[chunk(i), :] = grad
        low_ref[chunk(i), :] = grad.astype(BF)
        pushes.append(push(low_ref.at[chunk(i)], low_hbm.at[own_rows(i)], sem_send_l.at[i], sem_recv_l.at[i], peer))
        pushes[-1].start()
        saves += [copy(grad_ref.at[chunk(i)], grad_hbm.at[chunk(i)], sem_out.at[2 * i]),
                  copy(low_ref.at[chunk(i)], low_hbm.at[own_rows(i)], sem_out.at[2 * i + 1])]
        for c in saves[-2:]:
            c.start()
    gsum_ref[...] = gsum
    for c in saves:
        c.wait()
    for k, c in enumerate(pushes):
        c.wait_send()
        if k >= PARTS:
            c.wait_recv()


def join_back(gm, recv_a, recv_b, residual, cotangent, gains):
    half = pltpu.VMEM((HALF, D), BF)
    wide = pltpu.VMEM((HALF, D), F32)
    return pl.pallas_call(
        join_back_kernel,
        in_specs=[anywhere()] * 5 + [in_vmem()],
        out_specs=[anywhere(), anywhere(), in_vmem()],
        out_shape=[jax.ShapeDtypeStruct((HALF, D), F32), rows_shape, jax.ShapeDtypeStruct((1, D), F32)],
        scratch_shapes=[half] * 5 + [wide, half, wide, half, dma(6 * PARTS)] + [dma(PARTS)] * 4 + [dma(2 * PARTS)],
        compiler_params=pltpu.CompilerParams(collective_id=4, has_side_effects=True, vmem_limit_bytes=60 << 20),
        name="join_back",
    )(gm, recv_a, recv_b, residual, cotangent, gains)


def finish_kernel(gxn_hbm, gxc_hbm, mlp_hbm, ra_hbm, rb_hbm, noisy_hbm, clean_hbm, grad_hbm, res_hbm, gain_ref,
                  ends_hbm, gsum_ref,
                  own_ref, away_ref, far_ref, x_ref, wide_ref, ra_ref, rb_ref, out_ref,
                  sem_away, sem_own, sem_x, sem_wide, sem_r, sem_send, sem_recv, sem_out):
    sources = (gxn_hbm, gxc_hbm, mlp_hbm)
    count = 3 * PARTS
    away, own, rows, wide, recv_a, recv_b = [], [], [], [], [], []
    for n in range(count):
        k, i = n // PARTS, n % PARTS
        away.append(copy(sources[k].at[peer_rows(i)], away_ref.at[chunk(n)], sem_away.at[n]))
        own.append(copy(sources[k].at[own_rows(i)], own_ref.at[chunk(n)], sem_own.at[n]))
    for n in range(2 * PARTS):
        k, i = n // PARTS, n % PARTS
        rows.append(copy((noisy_hbm, clean_hbm)[k].at[side_rows_of(i)], x_ref.at[chunk(n)], sem_x.at[n]))
        wide.append(copy((grad_hbm, res_hbm)[k].at[chunk(i)], wide_ref.at[chunk(n)], sem_wide.at[n]))
    for i in range(PARTS):
        recv_a.append(copy(ra_hbm.at[chunk(i)], ra_ref.at[chunk(i)], sem_r.at[i]))
        recv_b.append(copy(rb_hbm.at[chunk(i)], rb_ref.at[chunk(i)], sem_r.at[PARTS + i]))
    for c in away + recv_b + own + rows + wide + recv_a:
        c.start()
    peer = greet_neighbour()
    pushes = []
    for n in range(count):
        away[n].wait()
        if n >= 2 * PARTS:
            i = n - 2 * PARTS
            recv_b[i].wait()
            away_ref[chunk(n), :] = (away_ref[chunk(n), :].astype(F32) + rb_ref[chunk(i), :].astype(F32)).astype(BF)
        pushes.append(push(away_ref.at[chunk(n)], far_ref.at[chunk(n)], sem_send.at[n], sem_recv.at[n], peer))
        pushes[-1].start()
    gsum = 0.0
    saves = []
    for n in range(count):
        k, i = n // PARTS, n % PARTS
        own[n].wait()
        total = own_ref[chunk(n), :].astype(F32)
        if k == 2:
            recv_a[i].wait()
            total = total + ra_ref[chunk(i), :].astype(F32)
        pushes[n].wait_recv()
        total = total + far_ref[chunk(n), :].astype(F32)
        if k < 2:
            rows[n].wait()
            grad, share = norm_back(x_ref[chunk(n), :].astype(F32), gain_ref[0:1, :], total)
            gsum = gsum + share
        else:
            grad = total
        if k != 1:
            w = i if k == 0 else PARTS + i
            wide[w].wait()
            grad = wide_ref[chunk(w), :] + grad
        out_ref[chunk(n), :] = grad.astype(BF)
        saves.append(copy(out_ref.at[chunk(n)], ends_hbm.at[chunk(n)], sem_out.at[n]))
        saves[-1].start()
    gsum_ref[...] = gsum
    for c in saves:
        c.wait()
    for c in pushes:
        c.wait_send()


def finish(gxn, gxc, mlp, recv_a, recv_b, noisy_rows, clean_rows, grad_resid, residual, gains):
    rows = 3 * HALF
    return pl.pallas_call(
        finish_kernel,
        in_specs=[anywhere()] * 9 + [in_vmem()],
        out_specs=[anywhere(), in_vmem()],
        out_shape=[rows_of(rows), jax.ShapeDtypeStruct((1, D), F32)],
        scratch_shapes=[pltpu.VMEM((rows, D), BF), pltpu.VMEM((rows, D), BF), pltpu.VMEM((rows, D), BF),
                        pltpu.VMEM((LEN, D), BF), pltpu.VMEM((LEN, D), F32), pltpu.VMEM((HALF, D), BF),
                        pltpu.VMEM((HALF, D), BF), pltpu.VMEM((rows, D), BF),
                        dma(3 * PARTS), dma(3 * PARTS), dma(2 * PARTS), dma(2 * PARTS), dma(2 * PARTS),
                        dma(3 * PARTS), dma(3 * PARTS), dma(3 * PARTS)],
        compiler_params=pltpu.CompilerParams(collective_id=5, has_side_effects=True, vmem_limit_bytes=60 << 20),
        name="finish",
    )(gxn, gxc, mlp, recv_a, recv_b, noisy_rows, clean_rows, grad_resid, residual, gains)


def place_kernel(info_ref, *refs):
    sources, outs, stage, sem_in, sem_out = refs[:4], refs[4:7], refs[7], refs[8], refs[9]
    order = [3 * n + k for n in range(4) for k in range(3)]
    loads = {j: copy(sources[j // 3].at[pl.ds((j % 3) * HALF, HALF)], stage.at[j], sem_in.at[j]) for j in order}
    for j in order:
        loads[j].start()
    saves = []
    for j in order:
        loads[j].wait()
        at = pl.ds(pl.multiple_of(info_ref[3 + j // 3] * HALF, HALF), HALF)
        saves.append(copy(stage.at[j], outs[j % 3].at[at], sem_out.at[j]))
        saves[-1].start()
    for c in saves:
        c.wait()


def place(info, *ends):
    return pl.pallas_call(
        place_kernel,
        in_specs=[pl.BlockSpec(memory_space=pltpu.SMEM)] + [anywhere()] * 4,
        out_specs=[anywhere()] * 3,
        out_shape=[rows_of(2 * LEN)] * 3,
        scratch_shapes=[pltpu.VMEM((12, HALF, D), BF), dma(12), dma(12)],
        compiler_params=pltpu.CompilerParams(vmem_limit_bytes=60 << 20),
        name="place",
    )(info, *ends)


def replica_sum_kernel(count, owners, x_ref, o_ref, in_ref, send_a, recv_a, send_b, recv_b):
    me = lax.axis_index("dp")
    m = lax.axis_index("mp")
    barrier = pltpu.get_barrier_semaphore()
    for k in range(1, count):
        pl.semaphore_signal(barrier, inc=1, device_id=(lax.rem(me + k, count), m), device_id_type=MESH_ID)
    pl.semaphore_wait(barrier, count - 1)

    def piece(j):
        return pl.ds(pl.multiple_of(j * 128, 128), 128)

    def part(j):
        return pltpu.make_async_remote_copy(
            src_ref=x_ref.at[:, piece(j)], dst_ref=in_ref.at[me], send_sem=send_a.at[j], recv_sem=recv_a.at[me],
            device_id=(j, m), device_id_type=MESH_ID)

    def whole(p):
        return pltpu.make_async_remote_copy(
            src_ref=o_ref.at[:, piece(me)], dst_ref=o_ref.at[:, piece(me)], send_sem=send_b.at[p],
            recv_sem=recv_b.at[me], device_id=(p, m), device_id_type=MESH_ID)

    for j in range(owners):
        @pl.when(me != j)
        def _():
            part(j).start()

    @pl.when(me < owners)
    def _():
        in_ref[me] = x_ref[:, piece(me)]
        for s in range(count):
            @pl.when(me != s)
            def _():
                pltpu.make_async_remote_copy(
                    src_ref=x_ref.at[:, piece(0)], dst_ref=in_ref.at[s], send_sem=send_a.at[0], recv_sem=recv_a.at[s],
                    device_id=(s, m), device_id_type=MESH_ID).wait_recv()
        total = in_ref[0]
        for s in range(1, count):
            total = total + in_ref[s]
        o_ref[:, piece(me)] = total
        for p in range(count):
            @pl.when(me != p)
            def _():
                whole(p).start()

    for j in range(owners):
        @pl.when(me != j)
        def _():
            pltpu.make_async_remote_copy(
                src_ref=o_ref.at[:, piece(j)], dst_ref=o_ref.at[:, piece(j)], send_sem=send_b.at[0],
                recv_sem=recv_b.at[j], device_id=(j, m), device_id_type=MESH_ID).wait_recv()
            part(j).wait_send()

    @pl.when(me < owners)
    def _():
        for p in range(count):
            @pl.when(me != p)
            def _():
                whole(p).wait_send()


def replica_sum(x, collective_id):
    count = lax.axis_size("dp")
    owners = x.shape[1] // 128
    if count != 8:
        return lax.psum(x, "dp")
    return pl.pallas_call(
        functools.partial(replica_sum_kernel, count, owners),
        out_shape=jax.ShapeDtypeStruct(x.shape, F32),
        in_specs=[pl.BlockSpec(memory_space=pltpu.VMEM)],
        out_specs=pl.BlockSpec(memory_space=pltpu.VMEM),
        scratch_shapes=[
            pltpu.VMEM((count, x.shape[0], 128), F32),
            pltpu.SemaphoreType.DMA((owners,)),
            pltpu.SemaphoreType.DMA((count,)),
            pltpu.SemaphoreType.DMA((count,)),
            pltpu.SemaphoreType.DMA((owners,)),
        ],
        compiler_params=pltpu.CompilerParams(collective_id=collective_id, has_side_effects=True),
        cost_estimate=pl.CostEstimate(flops=1000000, bytes_accessed=30000000, transcendentals=0),
        name="replica_sum",
    )(x)


def lefts_kernel(gq_ref, gqb_ref, eq_ref, go_ref, gob_ref, eo_ref, fq_ref, fo_ref, lu_ref, ld_ref, g1_ref, g2_ref,
                 mq_ref, mo_ref, pack_ref):
    pack_ref[...] = jnp.zeros_like(pack_ref)
    mq = gq_ref[...] + gqb_ref[...].astype(F32) + eq_ref[0]
    mq_ref[...] = mq
    pack_ref[0:8, :] = exact(fq_ref[...], mq, 1, 0)
    mo = go_ref[...] + gob_ref[...].astype(F32) + eo_ref[0]
    mo_ref[...] = mo
    pack_ref[8:16, 0:192] = exact(fo_ref[...], mo, 1, 1)
    pack_ref[16:24, :] = lu_ref[...]
    pack_ref[24:32, :] = ld_ref[...]
    pack_ref[32:33, :] = g1_ref[...]
    pack_ref[33:34, :] = g2_ref[...]


def lefts(gq, gq_back, err_qkv, go, go_back, err_out, fac_qkv, fac_out, left_up, left_down, gain_one, gain_two):
    args = (gq, gq_back, err_qkv, go, go_back, err_out, fac_qkv, fac_out, left_up, left_down, gain_one, gain_two)
    return pl.pallas_call(
        lefts_kernel,
        grid=(1,),
        in_specs=[whole(v.shape) for v in args],
        out_specs=[whole((9 * HD, D)), whole((3 * HD, D)), whole((5 * RANK, D))],
        out_shape=[jax.ShapeDtypeStruct((9 * HD, D), F32), jax.ShapeDtypeStruct((3 * HD, D), F32),
                   jax.ShapeDtypeStruct((5 * RANK, D), F32)],
        compiler_params=pltpu.CompilerParams(vmem_limit_bytes=60 << 20),
        name="lefts",
    )(*args)


def rights_kernel(sum_ref, mq_ref, mo_ref, mu_ref, md_ref, hq_ref, ho_ref, hu_ref, hd_ref, pack_ref):
    row = lax.broadcasted_iota(jnp.int32, (RANK, D), 0)
    mats = [sum_ref[RANK * t:RANK * (t + 1), :] for t in range(4)]
    for k in range(RANK):
        for t in range(4):
            a = mats[t]
            v = a[k:k + 1, :]
            e = v / (jnp.sqrt(jnp.sum(v * v, axis=1, keepdims=True)) + 1e-08)
            c = jnp.sum(a * e, axis=1, keepdims=True)
            mats[t] = jnp.where(row == k, e, jnp.where(row > k, a - c * e, a))
    hq_ref[...] = mats[0]
    ho_ref[...] = mats[1][:, :192]
    hu_ref[...] = mats[2]
    hd_ref[...] = mats[3]
    pack_ref[...] = jnp.zeros_like(pack_ref)
    pack_ref[0:8, 0:9 * HD] = exact(mats[0], mq_ref[...], 1, 1)
    pack_ref[8:16, :] = exact(mats[1][:, :192], mo_ref[...], 1, 0)
    pack_ref[16:24, :] = exact(mats[2], mu_ref[...], 1, 0)
    pack_ref[24:32, :] = exact(mats[3], md_ref[...], 1, 0)


def rights(left_sum, mats):
    args = (left_sum, *mats)
    shapes = [(RANK, D), (RANK, 3 * HD), (RANK, D), (RANK, D), (4 * RANK, D)]
    return pl.pallas_call(
        rights_kernel,
        grid=(1,),
        in_specs=[whole(v.shape) for v in args],
        out_specs=[whole(s) for s in shapes],
        out_shape=[jax.ShapeDtypeStruct(s, F32) for s in shapes],
        compiler_params=pltpu.CompilerParams(vmem_limit_bytes=60 << 20),
        name="rights",
    )(*args)


def update_kernel(replicas, rates, info_ref, *refs):
    sums, hats, mats, states = refs[0], refs[1:5], refs[5:9], refs[9:21]
    left_sum, gain_ref, gm_ref = refs[21:24]
    errs, news, right_out, gains_out = refs[24:28], refs[28:40], refs[40:44], refs[44:47]
    decay = min(0.9999, (1.0 + EMA_STEPS) / (10.0 + EMA_STEPS))
    share = D // replicas
    shift = lax.rem(D - info_ref[1] * share, D)

    def part(value):
        return pltpu.roll(value, shift, 1)[:, :share]

    for t in range(4):
        hat = hats[t][...]
        right = sums[RANK * t:RANK * (t + 1), :] * (1.0 / replicas)
        right_out[t][...] = right[:, :right_out[t].shape[1]]
        first, second = ((right[:, :9 * HD], hat), (hat, right), (hat, right), (hat, right))[t]
        errs[t][0] = mats[t][...] - exact(first, second, 0, 0)
        first, second = ((part(hat), right[:, :9 * HD]), (hat, part(right)), (part(hat), right), (part(right), hat))[t]
        moment = 0.5 * states[3 * t + 1][...] + exact(first, second, 0, 0)
        master = states[3 * t][...] - rates[t] * moment
        news[3 * t][...] = master
        news[3 * t + 1][...] = moment
        news[3 * t + 2][...] = decay * states[3 * t + 2][...] + (1.0 - decay) * master
    grad = left_sum[32:34, :] * (1.0 / replicas)
    moment = 0.5 * gm_ref[...] + grad
    gains_out[0][...] = grad
    gains_out[1][...] = gain_ref[...] - rates[4] * moment
    gains_out[2][...] = moment


def update(info, replicas, rates, right_sum, hats, mats, states, left_sum, gains, gain_moment):
    args = (right_sum, *hats, *mats, *states, left_sum, gains, gain_moment)
    shapes = [(1, *m.shape) for m in mats] + [s.shape for s in states]
    shapes += [(RANK, 9 * HD), (RANK, D), (RANK, D), (RANK, D)] + [(2, D)] * 3
    return pl.pallas_call(
        functools.partial(update_kernel, replicas, rates),
        grid_spec=pltpu.PrefetchScalarGridSpec(
            num_scalar_prefetch=1,
            grid=(1,),
            in_specs=[whole(v.shape) for v in args],
            out_specs=[whole(s) for s in shapes],
        ),
        out_shape=[jax.ShapeDtypeStruct(s, F32) for s in shapes],
        compiler_params=pltpu.CompilerParams(vmem_limit_bytes=60 << 20),
        name="update",
    )(info, *args)


def local(
    noisy_rows, clean_rows, block_size, cotangent, norm_gains,
    weight_qkv, weight_out, weight_up, weight_down,
    master_qkv, master_out, master_up, master_down,
    moment_qkv, moment_out, moment_up, moment_down,
    average_qkv, average_out, average_up, average_down,
    error_qkv, error_out, error_up, error_down,
    factor_qkv, factor_out, factor_up, factor_down,
    gain_moment,
):
    row_count = noisy_rows.shape[0]
    replicas = lax.axis_size("dp")
    side = lax.axis_index("mp") // 2

    def across(value):
        return lax.ppermute(value, "mp", [(0, 2), (2, 0), (1, 3), (3, 1)])

    def beside(value):
        return lax.ppermute(value, "mp", [(0, 1), (1, 0), (2, 3), (3, 2)])

    def hold(*values):
        return lax.optimization_barrier(values)

    cos, sin = rotary_tables()
    m = lax.axis_index("mp")
    flip = m + 1 - 2 * (m % 2)
    info = jnp.stack([side, lax.axis_index("dp"), m % 2, m, flip, (m + 2) % 4, (flip + 2) % 4]).astype(jnp.int32)
    w_near = weight_qkv.T
    w_far, o_far = across(w_near), across(weight_out)
    qn_near, qc_near, att_near, lse_near, xn, xc = attend_near(
        info, block_size, noisy_rows, clean_rows, norm_gains, w_near, cos, sin)
    qn_far, qc_far, att_far, lse_far = attend_far(info, block_size, xn, xc, w_far, cos, sin)
    residual, normed, normed_half = join(att_near, att_far, weight_out, o_far, noisy_rows, norm_gains)
    normed_a = across(normed_half)
    mlp, grad_mid, hidden, grad_pre = feed(info, normed, cotangent, weight_up, weight_down, 0)
    normed_a, hidden = hold(normed_a, hidden)
    normed_b = beside(normed_a)
    mlp_a, grad_a, hidden_a, grad_pre_a = feed(info, normed_a, cotangent, weight_up, weight_down, 1)
    normed_b, hidden_a = hold(normed_b, hidden_a)
    mlp_b, grad_b, hidden_b, grad_pre_b = feed(info, normed_b, cotangent, weight_up, weight_down, 2)
    grad_a, grad_b = across(grad_a), across(grad_b)
    matrix_up, matrix_down, left_up, left_down = feed_grads(
        info, (normed, normed_a, normed_b), cotangent, (hidden, hidden_a, hidden_b), (grad_pre, grad_pre_a, grad_pre_b),
        error_up, error_down, factor_up.T, factor_down.T)
    grad_a, grad_b, left_up = hold(grad_a, grad_b, left_up)
    grad_resid, grad_low, gain_two = join_back(grad_mid, grad_a, grad_b, residual, cotangent, norm_gains)

    mlp_a, mlp_b, grad_low = hold(mlp_a, mlp_b, grad_low)
    mlp_a, mlp_b = across(mlp_a), across(mlp_b)
    dn_far, dc_far, gq_far, go_far = back_far(
        info, block_size, qn_far, qc_far, att_far, lse_far, grad_low, o_far, cos, sin, xn, xc)
    mlp_a, mlp_b, dn_far, gq_far, go_far = hold(mlp_a, mlp_b, dn_far, gq_far, go_far)
    gq_back, go_back = across(gq_far), across(go_far)
    grad_xn, grad_xc, gq_near, go_near = back_near(
        info, block_size, qn_near, qc_near, att_near, lse_near, grad_low, weight_out, cos, sin, xn, xc,
        w_near, w_far, dn_far, dc_far)
    ends, gain_one = finish(
        grad_xn, grad_xc, mlp, mlp_a, mlp_b, noisy_rows, clean_rows, grad_resid, residual, norm_gains)
    gain_part = jnp.concatenate([gain_one, gain_two], axis=0)
    gain_part = gain_part + beside(gain_part)
    gain_part = gain_part + across(gain_part)
    ends, gain_part, gq_back, go_back = hold(ends, gain_part, gq_back, go_back)
    ends_side = beside(ends)
    ends_far = across(ends)
    matrix_qkv, matrix_out, left_pack = lefts(
        gq_near, gq_back, jnp.swapaxes(error_qkv, 1, 2), go_near, go_back, error_out, factor_qkv.T, factor_out.T,
        left_up, left_down, gain_part[0:1], gain_part[1:2])
    left_sum = replica_sum(left_pack, 1)
    mats = (matrix_qkv, matrix_out, matrix_up, matrix_down)
    *hats, right_pack = rights(left_sum, mats)
    right_sum = replica_sum(right_pack, 2)
    rates = [3.0 / math.sqrt(f * row_count) for f in (D, HEADS * HD // 64, D, FF)] + [0.5 / math.sqrt(row_count)]
    states = (
        master_qkv, moment_qkv, average_qkv, master_out, moment_out, average_out,
        master_up, moment_up, average_up, master_down.T, moment_down.T, average_down.T,
    )
    done = update(info, replicas, rates, right_sum, hats, mats, states, left_sum, norm_gains, gain_moment)
    errs, news, right_new, gains_new = done[:4], done[4:16], done[16:20], done[20:23]
    ends_far, _ = hold(ends_far, errs[2])
    ends_diag = beside(ends_far)
    block_at, noisy_at, clean_at = 2, 0, 1
    placed = place(info, ends, ends_side, ends_far, ends_diag)
    block_out, grad_noisy, grad_clean = placed[block_at], placed[noisy_at], placed[clean_at]
    fresh = [news[3 * t + k] if t < 3 else news[3 * t + k].T for k in range(3) for t in range(4)]
    return (
        block_out, grad_noisy, grad_clean, *gains_new, *fresh,
        jnp.swapaxes(errs[0], 1, 2), *errs[1:], *[v.T for v in hats], *[v.T for v in right_new],
    )


def solution(mesh):
    in_specs = (
        P("dp", None), P("dp", None), P("dp"), P("dp", None), P(),
        P(None, "mp"), P("mp", None), P(None, "mp"), P("mp", None),
        *([P("dp", "mp"), P("mp", "dp")] * 6),
        *([P("dp", None, "mp"), P("dp", "mp", None)] * 2),
        *([P("mp", None), P(None, "mp")] * 2),
        P(),
    )
    out_specs = (
        P("dp", None), P("dp", None), P("dp", None), P(), P(), P(),
        *([P("dp", "mp"), P("mp", "dp")] * 6),
        *([P("dp", None, "mp"), P("dp", "mp", None)] * 2),
        *([P(None, "mp"), P("mp", None)] * 2),
        *([P("mp", None), P(None, "mp")] * 2),
    )
    return jax.shard_map(local, mesh=mesh, in_specs=in_specs, out_specs=out_specs, check_vma=False)
```

```python
import functools
import math

import jax
import jax.numpy as jnp
import numpy as np
from jax import lax
from jax.experimental import pallas as pl
from jax.experimental.pallas import tpu as pltpu
from jax.sharding import PartitionSpec as P

D = 768
HEADS = 12
HD = 64
FF = 3072
LEN = 1024
RANK = 8
EMA_STEPS = 4
TILE = 256
SLOT = 256

BF = jnp.bfloat16
F32 = jnp.float32
highest = lax.Precision.HIGHEST
norm_eps = 1e-05
gelu_coef = 0.7978845608028654
masked_score = -1e30
MESH_ID = pl.DeviceIdType.MESH


def nt(a, b):
    return lax.dot_general(a, b, (((1,), (1,)), ((), ())), preferred_element_type=F32)


def nn(a, b):
    return lax.dot_general(a, b, (((1,), (0,)), ((), ())), preferred_element_type=F32)


def tn(a, b):
    return lax.dot_general(a, b, (((0,), (0,)), ((), ())), preferred_element_type=F32)


def rotary_tables():
    half = HD // 2
    step = np.float32(-2.0 * math.log(10000.0) / HD)
    inverse = np.exp(np.arange(half, dtype=np.float32) * step).astype(np.float32)
    angle = (np.arange(LEN, dtype=np.float32)[:, None] * inverse[None, :]).astype(np.float32)
    c = np.cos(angle).astype(np.float32)
    s = np.sin(angle).astype(np.float32)
    return np.concatenate([c, c, c, c], 1), np.concatenate([-s, s, -s, s], 1)


def spin(v, cos, sin):
    lane = lax.broadcasted_iota(jnp.int32, v.shape, 1)
    low = lax.rem(lane, HD) < HD // 2
    swapped = jnp.where(low, pltpu.roll(v, 128 - HD // 2, 1), pltpu.roll(v, HD // 2, 1))
    return v * cos + swapped * sin


def block_ids(size, shape, dim):
    shift = 2 + (size >= 8).astype(jnp.int32) + (size >= 16).astype(jnp.int32)
    place = lax.broadcasted_iota(jnp.int32, shape, dim)
    return lax.shift_right_logical(place, jnp.full(shape, shift, jnp.int32))


def fill_bias(size, noisy_bias, clean_bias):
    keys = block_ids(size, (TILE, TILE), 0)
    rows = block_ids(size, (TILE, TILE), 1)
    noisy_bias[...] = jnp.where(rows == keys, 0.0, masked_score)
    clean_bias[...] = jnp.where(keys < rows, 0.0, masked_score)


def norm_parts(values):
    centered = values - jnp.mean(values, axis=1, keepdims=True)
    scale = lax.rsqrt(jnp.mean(centered * centered, axis=1, keepdims=True) + norm_eps)
    return centered * scale, scale


def norm_back(values, gain, grad):
    unit, scale = norm_parts(values)
    scaled = grad * gain
    inner = jnp.mean(scaled * unit, axis=1, keepdims=True)
    grad_in = scale * (scaled - jnp.mean(scaled, axis=1, keepdims=True) - unit * inner)
    return grad_in, jnp.sum(grad * unit, axis=0, keepdims=True)


def gelu_and_slope(u):
    square = u * u
    half = 0.5 + 0.5 * jnp.tanh(u * (gelu_coef + (gelu_coef * 0.044715) * square))
    slope = half + (u * (2.0 * half * (1.0 - half))) * (gelu_coef + (3.0 * 0.044715 * gelu_coef) * square)
    return u * half, slope


def whole(shape):
    return pl.BlockSpec(shape, lambda *index: (0,) * len(shape), pipeline_mode=pl.Buffered(1))


def side_rows(h, info, size):
    return (info[0], 0)


def lane2(h, *_):
    return (0, h)


def row3(h, *_):
    return (h, 0, 0)


def attend_head(head, xn_ref, xc_ref, w_ref, cos_ref, sin_ref, qn_ref, qc_ref, att_ref, lse_ref,
                bn_ref, bc_ref, kn_ref, kc_ref, vnt_ref, vct_ref):
    w = w_ref[pl.ds(pl.multiple_of(head * 3 * HD, 3 * HD), 3 * HD), :]
    for src, dst, keys, vals in ((xn_ref, qn_ref, kn_ref, vnt_ref), (xc_ref, qc_ref, kc_ref, vct_ref)):
        a = nt(src[...], w)
        r = spin(a[:, :128], cos_ref[...], sin_ref[...]).astype(BF)
        v = a[:, 128:].astype(BF)
        dst[:, :128] = r
        dst[:, 128:192] = v
        keys[...] = r[:, 64:128]
        vals[...] = jnp.transpose(v)
    here = pl.ds(pl.multiple_of(head * HD, HD), HD)
    for i in range(LEN // TILE):
        lo, hi = i * TILE, (i + 1) * TILE
        q = qn_ref[lo:hi, 0:64] * 0.125
        parts = [nt(kn_ref[lo:hi, :], q) + bn_ref[...], nt(kc_ref[lo:hi, :], q) + bc_ref[...]]
        if i:
            parts.append(nt(kc_ref[0:lo, :], q))
        peak = functools.reduce(jnp.maximum, [jnp.max(s, axis=0, keepdims=True) for s in parts])
        exps = [jnp.exp(s - peak) for s in parts]
        total = functools.reduce(jnp.add, [jnp.sum(e, axis=0, keepdims=True) for e in exps])
        inv = 1.0 / total
        low = [(e * inv).astype(BF) for e in exps]
        o = nn(vnt_ref[:, lo:hi], low[0]) + nn(vct_ref[:, lo:hi], low[1])
        if i:
            o = o + nn(vct_ref[:, 0:lo], low[2])
        att_ref[here, lo:hi] = o.astype(BF)
        lse_ref[0, :, lo:hi] = jnp.broadcast_to(peak + jnp.log(total), (8, TILE))


def attend_near_kernel(info_ref, size_ref, noisy_hbm, clean_hbm, gain_ref, w_ref, cos_ref, sin_ref,
                       qn_ref, qc_ref, att_ref, lse_ref, xn_hbm, xc_hbm, raw_ref, x_ref, sem_in, sem_out, *work):
    head = pl.program_id(0)
    sides = ((noisy_hbm, xn_hbm), (clean_hbm, xc_hbm))

    def load(s, i):
        at = pl.ds(pl.multiple_of(info_ref[0] * LEN + i * TILE, TILE), TILE)
        return pltpu.make_async_copy(sides[s][0].at[at], raw_ref.at[s, chunk(i)], sem_in.at[CHUNKS * s + i])

    def save(s):
        return pltpu.make_async_copy(x_ref.at[s], sides[s][1], sem_out.at[s])

    @pl.when(head == 0)
    def _():
        for s in range(2):
            for i in range(CHUNKS):
                load(s, i).start()
        fill_bias(size_ref[info_ref[0]], work[0], work[1])
        for s in range(2):
            for i in range(CHUNKS):
                load(s, i).wait()
                x = norm_parts(raw_ref[s, chunk(i), :].astype(F32))[0] * gain_ref[0:1, :]
                x_ref[s, chunk(i), :] = x.astype(BF)
            save(s).start()

    attend_head(head, x_ref.at[0], x_ref.at[1], w_ref, cos_ref, sin_ref, qn_ref, qc_ref, att_ref, lse_ref, *work)

    @pl.when(head == 2)
    def _():
        save(0).wait()
        save(1).wait()


def attend_far_kernel(info_ref, size_ref, xn_ref, xc_ref, w_ref, cos_ref, sin_ref,
                      qn_ref, qc_ref, att_ref, lse_ref, *work):
    head = pl.program_id(0)

    @pl.when(head == 0)
    def _():
        fill_bias(size_ref[info_ref[0]], work[0], work[1])

    attend_head(head, xn_ref, xc_ref, w_ref, cos_ref, sin_ref, qn_ref, qc_ref, att_ref, lse_ref, *work)


CHUNKS = LEN // TILE
HALF = LEN // 2


def chunk(i):
    return slice(i * TILE, (i + 1) * TILE)


def anywhere():
    return pl.BlockSpec(memory_space=pl.ANY)


def in_vmem():
    return pl.BlockSpec(memory_space=pltpu.VMEM)


def dma(n):
    return pltpu.SemaphoreType.DMA((n,))


def rows_of(n):
    return jax.ShapeDtypeStruct((n, D), BF)


attend_work = [
    pltpu.VMEM((TILE, TILE), F32),
    pltpu.VMEM((TILE, TILE), F32),
    pltpu.VMEM((LEN, HD), BF),
    pltpu.VMEM((LEN, HD), BF),
    pltpu.VMEM((HD, LEN), BF),
    pltpu.VMEM((HD, LEN), BF),
]
head_specs = [
    pl.BlockSpec((LEN, SLOT), lane2),
    pl.BlockSpec((LEN, SLOT), lane2),
    whole((3 * HD, LEN)),
    pl.BlockSpec((1, 8, LEN), row3),
]
head_shapes = [
    jax.ShapeDtypeStruct((LEN, SLOT * 3), BF),
    jax.ShapeDtypeStruct((LEN, SLOT * 3), BF),
    jax.ShapeDtypeStruct((3 * HD, LEN), BF),
    jax.ShapeDtypeStruct((3, 8, LEN), F32),
]
rows_shape = jax.ShapeDtypeStruct((LEN, D), BF)


def attend_near(info, size, noisy, clean, gains, w, cos, sin):
    return pl.pallas_call(
        attend_near_kernel,
        grid_spec=pltpu.PrefetchScalarGridSpec(
            num_scalar_prefetch=2,
            grid=(3,),
            in_specs=[
                anywhere(),
                anywhere(),
                whole((2, D)),
                whole((9 * HD, D)),
                whole((LEN, 128)),
                whole((LEN, 128)),
            ],
            out_specs=head_specs + [anywhere(), anywhere()],
            scratch_shapes=[pltpu.VMEM((2, LEN, D), BF), pltpu.VMEM((2, LEN, D), BF), dma(2 * CHUNKS), dma(2)] + attend_work,
        ),
        out_shape=head_shapes + [rows_shape, rows_shape],
        compiler_params=pltpu.CompilerParams(vmem_limit_bytes=60 << 20),
        name="attend_near",
    )(info, size, noisy, clean, gains, w, cos, sin)


def attend_far(info, size, xn, xc, w, cos, sin):
    return pl.pallas_call(
        attend_far_kernel,
        grid_spec=pltpu.PrefetchScalarGridSpec(
            num_scalar_prefetch=2,
            grid=(3,),
            in_specs=[whole((LEN, D)), whole((LEN, D)), whole((9 * HD, D)), whole((LEN, 128)), whole((LEN, 128))],
            out_specs=head_specs,
            scratch_shapes=attend_work,
        ),
        out_shape=head_shapes,
        compiler_params=pltpu.CompilerParams(vmem_limit_bytes=60 << 20),
        name="attend_far",
    )(info, size, xn, xc, w, cos, sin)


def back_head(head, qn_ref, qc_ref, lse_ref, cos_ref, sin_ref, dn_ref, dc_ref,
              bn_ref, bc_ref, kn_ref, kc_ref, knt_ref, kct_ref, dot_ref, do_ref, dq_ref, dkn_ref, dkc_ref, dvc_ref):
    do_ref[...] = jnp.transpose(dot_ref[pl.ds(pl.multiple_of(head * HD, HD), HD), :])
    kn_ref[...] = qn_ref[:, 64:128]
    kc_ref[...] = qc_ref[:, 64:128]
    knt_ref[...] = jnp.transpose(qn_ref[:, 0:128])[64:128]
    kct_ref[...] = jnp.transpose(qc_ref[:, 0:128])[64:128]
    dkc_ref[...] = jnp.zeros_like(dkc_ref)
    dvc_ref[...] = jnp.zeros_like(dvc_ref)
    blank = jnp.zeros((TILE, HD), F32)
    for i in range(LEN // TILE):
        lo, hi = i * TILE, (i + 1) * TILE
        q = qn_ref[lo:hi, 0:64] * 0.125
        do = do_ref[lo:hi, :]
        lse = lse_ref[0, 0:1, lo:hi]
        spans = [(0, lo, hi), (1, lo, hi)] + ([(1, 0, lo)] if i else [])
        probs, grads, inner = [], [], 0.0
        for n, (side, a, b) in enumerate(spans):
            kr = kc_ref if side else kn_ref
            vr = qc_ref if side else qn_ref
            s = nt(kr[a:b, :], q)
            if n == 0:
                s = s + bn_ref[...]
            if n == 1:
                s = s + bc_ref[...]
            p = jnp.exp(s - lse)
            dp = nt(vr[a:b, 128:192], do)
            inner = inner + jnp.sum(p * dp, axis=0, keepdims=True)
            probs.append(p)
            grads.append(dp)
        dqt = 0.0
        for n, (side, a, b) in enumerate(spans):
            ds = (probs[n] * (grads[n] - inner)).astype(BF)
            dv = nn(probs[n].astype(BF), do)
            dk = nn(ds, q)
            ktr = kct_ref if side else knt_ref
            dqt = dqt + nn(ktr[:, a:b], ds)
            if side:
                dkc_ref[a:b, :] += dk
                dvc_ref[a:b, :] += dv
            else:
                dkn_ref[a:b, :] = dk
                dn_ref[lo:hi, 128:256] = jnp.concatenate([dv, blank], axis=1).astype(BF)
        dq_ref[lo:hi, :] = jnp.transpose(dqt) * 0.125
    zero = jnp.zeros((LEN, HD), F32)
    sin = -sin_ref[...]
    cos = cos_ref[...]
    dn_ref[:, 0:128] = spin(jnp.concatenate([dq_ref[...], dkn_ref[...]], axis=1), cos, sin).astype(BF)
    dc_ref[:, 0:128] = spin(jnp.concatenate([zero, dkc_ref[...]], axis=1), cos, sin).astype(BF)
    dc_ref[:, 128:256] = jnp.concatenate([dvc_ref[...], zero], axis=1).astype(BF)


def head_grad(xn_ref, xc_ref, dn_ref, dc_ref, gq_ref):
    g = tn(dn_ref[...], xn_ref[...]) + tn(dc_ref[...], xc_ref[...])
    gq_ref[...] = g[:3 * HD].astype(gq_ref.dtype)


def back_far_kernel(info_ref, size_ref, qn_ref, qc_ref, att_ref, lse_ref, g_ref, wo_ref, cos_ref, sin_ref,
                    xn_hbm, xc_hbm, dn_ref, dc_ref, gq_ref, go_ref, xn_ref, xc_ref, sems, *work):
    head = pl.program_id(0)
    late = [pltpu.make_async_copy(s, d, sems.at[k]) for k, (s, d) in enumerate(((xn_hbm, xn_ref), (xc_hbm, xc_ref)))]

    @pl.when(head == 0)
    def _():
        for c in late:
            c.start()
        fill_bias(size_ref[info_ref[0]], work[0], work[1])
        work[6][...] = nt(wo_ref[...], g_ref[...]).astype(BF)
        go_ref[...] = nn(att_ref[...], g_ref[...]).astype(BF)

    back_head(head, qn_ref, qc_ref, lse_ref, cos_ref, sin_ref, dn_ref, dc_ref, *work)

    @pl.when(head == 0)
    def _():
        for c in late:
            c.wait()

    head_grad(xn_ref, xc_ref, dn_ref, dc_ref, gq_ref)


def back_near_kernel(info_ref, size_ref, qn_ref, qc_ref, att_ref, lse_ref, g_ref, wo_ref, cos_ref, sin_ref,
                     xn_hbm, xc_hbm, w_hbm, w_far_hbm, dnf_hbm, dcf_hbm, gxn_hbm, gxc_hbm, gq_ref, go_ref,
                     xn_ref, xc_ref, w_ref, w_far_ref, dnf_ref, dcf_ref, keep_ref, dn_ref, dc_ref, out_ref,
                     sems, sem_out, *work):
    head = pl.program_id(0)
    late = [pltpu.make_async_copy(s, d, sems.at[k]) for k, (s, d) in enumerate((
        (xn_hbm, xn_ref), (xc_hbm, xc_ref), (w_hbm, w_ref), (w_far_hbm, w_far_ref),
        (dnf_hbm, dnf_ref), (dcf_hbm, dcf_ref)))]

    @pl.when(head == 0)
    def _():
        for c in late:
            c.start()
        fill_bias(size_ref[info_ref[0]], work[0], work[1])
        work[6][...] = nt(wo_ref[...], g_ref[...]).astype(BF)
        go_ref[...] = nn(att_ref[...], g_ref[...])

    back_head(head, qn_ref, qc_ref, lse_ref, cos_ref, sin_ref, dn_ref, dc_ref, *work)

    @pl.when(head == 0)
    def _():
        for c in late:
            c.wait()

    head_grad(xn_ref, xc_ref, dn_ref, dc_ref, gq_ref)
    keep_ref[0, head] = dn_ref[...]
    keep_ref[1, head] = dc_ref[...]

    @pl.when(head == 2)
    def _():
        copies = []
        for s, (far, out) in enumerate(((dnf_ref, gxn_hbm), (dcf_ref, gxc_hbm))):
            for i in range(CHUNKS):
                total = 0.0
                for j in range(3):
                    total = total + nn(keep_ref[s, j, chunk(i), 0:192], w_ref[192 * j:192 * (j + 1), :])
                    total = total + nn(far[chunk(i), SLOT * j:SLOT * j + 192], w_far_ref[192 * j:192 * (j + 1), :])
                out_ref[s, chunk(i), :] = total.astype(BF)
                copies.append(pltpu.make_async_copy(
                    out_ref.at[s, chunk(i)], out.at[chunk(i)], sem_out.at[CHUNKS * s + i]))
                copies[-1].start()
        for c in copies:
            c.wait()


back_work = attend_work[:4] + [
    pltpu.VMEM((HD, LEN), BF),
    pltpu.VMEM((HD, LEN), BF),
    pltpu.VMEM((3 * HD, LEN), BF),
    pltpu.VMEM((LEN, HD), BF),
    pltpu.VMEM((LEN, HD), F32),
    pltpu.VMEM((LEN, HD), F32),
    pltpu.VMEM((LEN, HD), F32),
    pltpu.VMEM((LEN, HD), F32),
]
wide_rows = jax.ShapeDtypeStruct((LEN, 3 * SLOT), BF)


row2_spec = pl.BlockSpec((3 * HD, D), lambda h, *_: (h, 0))


def back_far(info, size, qn, qc, att, lse, g, wo, cos, sin, xn, xc):
    return pl.pallas_call(
        back_far_kernel,
        grid_spec=pltpu.PrefetchScalarGridSpec(
            num_scalar_prefetch=2,
            grid=(3,),
            in_specs=head_specs[:2] + [whole((3 * HD, LEN)), head_specs[3], whole((LEN, D)), whole((3 * HD, D)),
                                       whole((LEN, 128)), whole((LEN, 128)), anywhere(), anywhere()],
            out_specs=head_specs[:2] + [row2_spec, whole((3 * HD, D))],
            scratch_shapes=[pltpu.VMEM((LEN, D), BF), pltpu.VMEM((LEN, D), BF), dma(2)] + back_work,
        ),
        out_shape=[wide_rows, wide_rows, rows_of(9 * HD), rows_of(3 * HD)],
        compiler_params=pltpu.CompilerParams(vmem_limit_bytes=60 << 20),
        name="back_far",
    )(info, size, qn, qc, att, lse, g, wo, cos, sin, xn, xc)


def back_near(info, size, qn, qc, att, lse, g, wo, cos, sin, xn, xc, w, w_far, dn_far, dc_far):
    return pl.pallas_call(
        back_near_kernel,
        grid_spec=pltpu.PrefetchScalarGridSpec(
            num_scalar_prefetch=2,
            grid=(3,),
            in_specs=head_specs[:2] + [whole((3 * HD, LEN)), head_specs[3], whole((LEN, D)), whole((3 * HD, D)),
                                       whole((LEN, 128)), whole((LEN, 128))] + [anywhere()] * 6,
            out_specs=[anywhere(), anywhere(), row2_spec, whole((3 * HD, D))],
            scratch_shapes=[pltpu.VMEM((LEN, D), BF), pltpu.VMEM((LEN, D), BF),
                            pltpu.VMEM((9 * HD, D), BF), pltpu.VMEM((9 * HD, D), BF),
                            pltpu.VMEM((LEN, 3 * SLOT), BF), pltpu.VMEM((LEN, 3 * SLOT), BF),
                            pltpu.VMEM((2, 3, LEN, SLOT), BF), pltpu.VMEM((LEN, SLOT), BF), pltpu.VMEM((LEN, SLOT), BF),
                            pltpu.VMEM((2, LEN, D), BF), dma(6), dma(2 * CHUNKS)] + back_work,
        ),
        out_shape=[rows_shape, rows_shape, jax.ShapeDtypeStruct((9 * HD, D), F32), jax.ShapeDtypeStruct((3 * HD, D), F32)],
        compiler_params=pltpu.CompilerParams(vmem_limit_bytes=60 << 20),
        name="back_near",
    )(info, size, qn, qc, att, lse, g, wo, cos, sin, xn, xc, w, w_far, dn_far, dc_far)


def halves(v):
    high = v.astype(BF)
    return high, (v - high.astype(F32)).astype(BF)


def exact(left_side, right_side, left_dim, right_dim):
    dims = (((left_dim,), (right_dim,)), ((), ()))
    a, b = halves(left_side)
    c, d = halves(right_side)

    def times(x, y):
        return lax.dot_general(x, y, dims, preferred_element_type=F32)

    return times(a, c) + (times(a, d) + times(b, c))


def core_peer():
    m = lax.axis_index("mp")
    return (lax.axis_index("dp"), m + 1 - 2 * lax.rem(m, 2))


def far_peer():
    return (lax.axis_index("dp"), lax.rem(lax.axis_index("mp") + 2, 4))


def greet(*peers):
    barrier = pltpu.get_barrier_semaphore()
    for p in peers:
        pl.semaphore_signal(barrier, inc=1, device_id=p, device_id_type=MESH_ID)
    pl.semaphore_wait(barrier, len(peers))


PARTS = HALF // TILE


def own_rows(i):
    half = lax.rem(lax.axis_index("mp"), 2)
    return pl.ds(pl.multiple_of(half * HALF + i * TILE, TILE), TILE)


def peer_rows(i):
    half = lax.rem(lax.axis_index("mp"), 2)
    return pl.ds(pl.multiple_of((1 - half) * HALF + i * TILE, TILE), TILE)


def side_rows_of(i):
    m = lax.axis_index("mp")
    return pl.ds(pl.multiple_of(m * HALF + i * TILE, TILE), TILE)


def copy(src, dst, sem):
    return pltpu.make_async_copy(src, dst, sem)


def push(src, dst, send_sem, recv_sem, peer):
    return pltpu.make_async_remote_copy(
        src_ref=src, dst_ref=dst, send_sem=send_sem, recv_sem=recv_sem, device_id=peer, device_id_type=MESH_ID)


class Sems:
    def __init__(self, ref):
        self.ref = ref
        self.used = 0

    def take(self):
        self.used += 1
        return self.ref.at[self.used - 1]


def middle_kernel(att_near_hbm, att_far_hbm, wo_near_hbm, wo_far_hbm, rows_hbm, cot_hbm, up_hbm, down_hbm,
                  err_up_hbm, err_down_hbm, fac_up_ref, fac_down_ref, gain_ref,
                  res_hbm, grad_hbm, low_hbm, mlp_hbm, fold_hbm, mat_up_hbm, mat_down_hbm,
                  left_up_ref, left_down_ref, gsum_ref,
                  att_ref, wo_ref, x_ref, send_ref, far_ref, r_ref, nm_ref, cot_ref, up_ref, down_ref, hid_ref, gp_ref,
                  mlp_ref, gm_ref, back_ref, fold_gm_ref, fold_mlp_ref, sum_ref, msum_ref, yet_ref,
                  mat_up_ref, mat_down_ref, nmt_ref, grad_ref, low_ref, sem_ref, send_sem_ref, recv_sem_ref):
    sems, sends, recvs = Sems(sem_ref), Sems(send_sem_ref), Sems(recv_sem_ref)
    m = lax.axis_index("mp")
    side, half = m // 2, lax.rem(m, 2)
    core, far = core_peer(), far_peer()
    width = 3 * HD
    third = D // 3
    pushes, saves = [], []

    def load(src, dst):
        c = pltpu.make_async_copy(src, dst, sems.take())
        c.start()
        return c

    def save(src, dst):
        saves.append(load(src, dst))

    def send(src, dst, peer):
        c = push(src, dst, sends.take(), recvs.take(), peer)
        c.start()
        pushes.append(c)
        return c

    def span(start, n):
        return pl.ds(pl.multiple_of(start, TILE), n)

    own_half, peer_half = half * HALF, (1 - half) * HALF
    first = [load(att_near_hbm, att_ref.at[0:width]), load(att_far_hbm, att_ref.at[width:]),
             load(wo_near_hbm, wo_ref.at[0:width]), load(wo_far_hbm, wo_ref.at[width:])]
    xs = [load(rows_hbm.at[span(m * HALF + i * TILE, TILE)], x_ref.at[chunk(i)]) for i in range(PARTS)]
    up_in, down_in = load(up_hbm, up_ref), load(down_hbm, down_ref)
    cot_in = load(cot_hbm.at[span(side * LEN, LEN)], cot_ref.at[0:LEN])
    cot_far_in = load(cot_hbm.at[span((1 - side) * LEN, LEN)], cot_ref.at[LEN:])
    err_in = [load(err_down_hbm.at[0], mat_down_ref), load(err_up_hbm.at[0], mat_up_ref)]
    greet(core, far)
    for c in first:
        c.wait()
    parts = []
    for i in range(PARTS):
        send_ref[chunk(i), :] = tn(att_ref[:, span(peer_half + i * TILE, TILE)], wo_ref[...]).astype(BF)
        parts.append(send(send_ref.at[chunk(i)], far_ref.at[chunk(i)], core))
    normed, cross = [], []
    for i in range(PARTS):
        at = span(own_half + i * TILE, TILE)
        own = tn(att_ref[:, at], wo_ref[...])
        xs[i].wait()
        parts[i].wait_recv()
        r = x_ref[chunk(i), :].astype(F32) + (own + far_ref[chunk(i), :].astype(F32))
        r_ref[chunk(i), :] = r
        nm_ref[at, :] = (norm_parts(r)[0] * gain_ref[1:2, :]).astype(BF)
        normed.append(send(nm_ref.at[at], nm_ref.at[at], core))
        cross.append(send(nm_ref.at[at], nm_ref.at[span(LEN + own_half + i * TILE, TILE)], far))
        save(r_ref.at[chunk(i)], res_hbm.at[chunk(i)])

    def feed_rows(start, n):
        at = span(start, n)
        for t in range(3):
            lanes = slice(t * third, (t + 1) * third)
            hidden, slope = gelu_and_slope(nn(nm_ref[at, :], up_ref[:, lanes]))
            hid_ref[at, lanes] = hidden.astype(BF)
            gp_ref[at, lanes] = (slope * nt(cot_ref[at, :], down_ref[lanes, :])).astype(BF)
        gm_ref[at, :] = nt(gp_ref[at, :], up_ref[...]).astype(BF)
        mlp_ref[at, :] = nn(hid_ref[at, :], down_ref[...]).astype(BF)

    up_in.wait()
    down_in.wait()
    cot_in.wait()
    feed_rows(own_half, HALF)
    for c in normed:
        c.wait_recv()
    feed_rows(peer_half, HALF)
    save(mlp_ref.at[0:LEN], mlp_hbm)
    swap = [send(gm_ref.at[span(peer_half + i * TILE, TILE)], back_ref.at[chunk(i)], core) for i in range(PARTS)]
    cot_far_in.wait()
    arrived = []
    for i in range(PARTS):
        at = span(LEN + own_half + i * TILE, TILE)
        away = span(LEN + peer_half + i * TILE, TILE)
        cross[i].wait_recv()
        relay = send(nm_ref.at[at], nm_ref.at[at], core)
        feed_rows(LEN + own_half + i * TILE, TILE)
        relay.wait_recv()
        feed_rows(LEN + peer_half + i * TILE, TILE)
        fold = send(gm_ref.at[away], fold_gm_ref.at[chunk(i)], core)
        fold_mlp = send(mlp_ref.at[away], fold_mlp_ref.at[chunk(i)], core)
        fold.wait_recv()
        sum_ref[chunk(i), :] = (gm_ref[at, :].astype(F32) + fold_gm_ref[chunk(i), :].astype(F32)).astype(BF)
        arrived.append(send(sum_ref.at[chunk(i)], yet_ref.at[chunk(i)], far))
        fold_mlp.wait_recv()
        msum_ref[chunk(i), :] = (mlp_ref[at, :].astype(F32) + fold_mlp_ref[chunk(i), :].astype(F32)).astype(BF)
        save(msum_ref.at[chunk(i)], fold_hbm.at[chunk(i)])

    for i in range(8):
        at = slice(i * TILE, (i + 1) * TILE)
        nmt_ref[:, at] = jnp.transpose(nm_ref[at, :])
    for c in err_in:
        c.wait()
    left_up = 0.0
    for t in range(3):
        lanes = slice(t * third, (t + 1) * third)
        mat = tn(hid_ref[:, lanes], cot_ref[...]) + mat_down_ref[lanes, :]
        mat_down_ref[lanes, :] = mat
        save(mat_down_ref.at[lanes], mat_down_hbm.at[lanes])
        left_down_ref[:, lanes] = exact(fac_down_ref[...], mat, 1, 1)
        mat = nn(nmt_ref[...], gp_ref[:, lanes]) + mat_up_ref[:, lanes]
        mat_up_ref[:, lanes] = mat
        save(mat_up_ref.at[:, lanes], mat_up_hbm.at[:, lanes])
        left_up = left_up + exact(fac_up_ref[:, lanes], mat, 1, 1)
    left_up_ref[...] = left_up

    gsum = 0.0
    lows = []
    for i in range(PARTS):
        at = span(own_half + i * TILE, TILE)
        swap[i].wait_recv()
        total = gm_ref[at, :].astype(F32) + back_ref[chunk(i), :].astype(F32)
        arrived[i].wait_recv()
        total = total + yet_ref[chunk(i), :].astype(F32)
        grad, share = norm_back(r_ref[chunk(i), :], gain_ref[1:2, :], total)
        gsum = gsum + share
        grad = cot_ref[at, :].astype(F32) + grad
        grad_ref[chunk(i), :] = grad
        low_ref[chunk(i), :] = grad.astype(BF)
        lows.append(send(low_ref.at[chunk(i)], low_hbm.at[at], core))
        save(low_ref.at[chunk(i)], low_hbm.at[at])
        save(grad_ref.at[chunk(i)], grad_hbm.at[chunk(i)])
    gsum_ref[...] = gsum
    for c in lows:
        c.wait_recv()
    for c in pushes:
        c.wait_send()
    for c in saves:
        c.wait()


def middle(att_near, att_far, wo_near, wo_far, rows, cotangent, up, down, err_up, err_down, fac_up, fac_down, gains):
    def low(n):
        return pltpu.VMEM((n, D), BF)

    def wide(n):
        return pltpu.VMEM((n, D), F32)

    return pl.pallas_call(
        middle_kernel,
        in_specs=[anywhere()] * 10 + [in_vmem()] * 3,
        out_specs=[anywhere()] * 7 + [in_vmem()] * 3,
        out_shape=[jax.ShapeDtypeStruct((HALF, D), F32), jax.ShapeDtypeStruct((HALF, D), F32), rows_of(LEN), rows_of(LEN),
                   rows_of(HALF), jax.ShapeDtypeStruct((D, D), F32), jax.ShapeDtypeStruct((D, D), F32),
                   jax.ShapeDtypeStruct((RANK, D), F32), jax.ShapeDtypeStruct((RANK, D), F32),
                   jax.ShapeDtypeStruct((1, D), F32)],
        scratch_shapes=[pltpu.VMEM((6 * HD, LEN), BF), low(6 * HD), low(HALF), low(HALF), low(HALF), wide(HALF),
                        low(2 * LEN), low(2 * LEN), low(D), low(D), low(2 * LEN), low(2 * LEN),
                        low(2 * LEN), low(2 * LEN), low(HALF), low(HALF), low(HALF), low(HALF), low(HALF), low(HALF),
                        wide(D), wide(D), pltpu.VMEM((D, 2 * LEN), BF), wide(HALF), low(HALF), dma(32), dma(24), dma(24)],
        compiler_params=pltpu.CompilerParams(collective_id=3, has_side_effects=True, vmem_limit_bytes=60 << 20),
        name="middle",
    )(att_near, att_far, wo_near, wo_far, rows, cotangent, up, down, err_up, err_down, fac_up, fac_down, gains)


def settle_kernel(mlp_hbm, far_hbm, res_hbm, out_hbm, own_ref, far_ref, res_ref, core_ref, out_ref,
                  sem_in, sem_send, sem_recv, sem_out):
    peer = core_peer()
    loads = []
    for i in range(PARTS):
        loads += [copy(mlp_hbm.at[own_rows(i)], own_ref.at[chunk(i)], sem_in.at[3 * i]),
                  copy(far_hbm.at[chunk(i)], far_ref.at[chunk(i)], sem_in.at[3 * i + 1]),
                  copy(res_hbm.at[chunk(i)], res_ref.at[chunk(i)], sem_in.at[3 * i + 2])]
    for c in loads:
        c.start()
    greet(peer)
    pushes = [push(mlp_hbm.at[peer_rows(i)], core_ref.at[chunk(i)], sem_send.at[i], sem_recv.at[i], peer)
              for i in range(PARTS)]
    for c in pushes:
        c.start()
    saves = []
    for i in range(PARTS):
        for c in loads[3 * i:3 * i + 3]:
            c.wait()
        pushes[i].wait_recv()
        total = own_ref[chunk(i), :].astype(F32) + core_ref[chunk(i), :].astype(F32) + far_ref[chunk(i), :].astype(F32)
        out_ref[chunk(i), :] = (res_ref[chunk(i), :] + total).astype(BF)
        saves.append(copy(out_ref.at[chunk(i)], out_hbm.at[chunk(i)], sem_out.at[i]))
        saves[-1].start()
    for c in saves:
        c.wait()
    for c in pushes:
        c.wait_send()


def settle(mlp, far, residual):
    half = pltpu.VMEM((HALF, D), BF)
    return pl.pallas_call(
        settle_kernel,
        in_specs=[anywhere()] * 3,
        out_specs=anywhere(),
        out_shape=rows_of(HALF),
        scratch_shapes=[half, half, pltpu.VMEM((HALF, D), F32), half, half, dma(3 * PARTS), dma(PARTS), dma(PARTS), dma(PARTS)],
        compiler_params=pltpu.CompilerParams(collective_id=4, has_side_effects=True, vmem_limit_bytes=60 << 20),
        name="settle",
    )(mlp, far, residual)


def finish_kernel(gxn_hbm, gxc_hbm, noisy_hbm, clean_hbm, grad_hbm, gain_ref, ends_hbm, gsum_ref,
                  own_ref, far_ref, x_ref, wide_ref, out_ref,
                  sem_own, sem_x, sem_wide, sem_send, sem_recv, sem_out):
    sources = (gxn_hbm, gxc_hbm)
    count = 2 * PARTS
    own, rows, wide = [], [], []
    for n in range(count):
        k, i = n // PARTS, n % PARTS
        own.append(copy(sources[k].at[own_rows(i)], own_ref.at[chunk(n)], sem_own.at[n]))
        rows.append(copy((noisy_hbm, clean_hbm)[k].at[side_rows_of(i)], x_ref.at[chunk(n)], sem_x.at[n]))
        if k == 0:
            wide.append(copy(grad_hbm.at[chunk(i)], wide_ref.at[chunk(i)], sem_wide.at[i]))
    for c in own + rows + wide:
        c.start()
    peer = core_peer()
    greet(peer)
    pushes = []
    for n in range(count):
        k, i = n // PARTS, n % PARTS
        pushes.append(push(sources[k].at[peer_rows(i)], far_ref.at[chunk(n)], sem_send.at[n], sem_recv.at[n], peer))
        pushes[-1].start()
    gsum = 0.0
    saves = []
    for n in range(count):
        k, i = n // PARTS, n % PARTS
        own[n].wait()
        rows[n].wait()
        pushes[n].wait_recv()
        total = own_ref[chunk(n), :].astype(F32) + far_ref[chunk(n), :].astype(F32)
        grad, share = norm_back(x_ref[chunk(n), :].astype(F32), gain_ref[0:1, :], total)
        gsum = gsum + share
        if k == 0:
            wide[i].wait()
            grad = wide_ref[chunk(i), :] + grad
        out_ref[chunk(n), :] = grad.astype(BF)
        saves.append(copy(out_ref.at[chunk(n)], ends_hbm.at[chunk(n)], sem_out.at[n]))
        saves[-1].start()
    gsum_ref[...] = gsum
    for c in saves:
        c.wait()
    for c in pushes:
        c.wait_send()


def finish(gxn, gxc, noisy_rows, clean_rows, grad_resid, gains):
    buf = pltpu.VMEM((LEN, D), BF)
    return pl.pallas_call(
        finish_kernel,
        in_specs=[anywhere()] * 5 + [in_vmem()],
        out_specs=[anywhere(), in_vmem()],
        out_shape=[rows_of(LEN), jax.ShapeDtypeStruct((1, D), F32)],
        scratch_shapes=[buf, buf, buf, pltpu.VMEM((HALF, D), F32), buf,
                        dma(2 * PARTS), dma(2 * PARTS), dma(PARTS), dma(2 * PARTS), dma(2 * PARTS), dma(2 * PARTS)],
        compiler_params=pltpu.CompilerParams(collective_id=5, has_side_effects=True, vmem_limit_bytes=60 << 20),
        name="finish",
    )(gxn, gxc, noisy_rows, clean_rows, grad_resid, gains)


def place_kernel(count, info_ref, *refs):
    sources, outs, stage, sem_in, sem_out = refs[:4], refs[4:4 + count], refs[4 + count], refs[5 + count], refs[6 + count]
    loads = [copy(sources[j // count].at[pl.ds((j % count) * HALF, HALF)], stage.at[j], sem_in.at[j])
             for j in range(4 * count)]
    for c in loads:
        c.start()
    saves = []
    for j, c in enumerate(loads):
        c.wait()
        at = pl.ds(pl.multiple_of(info_ref[3 + j // count] * HALF, HALF), HALF)
        saves.append(copy(stage.at[j], outs[j % count].at[at], sem_out.at[j]))
        saves[-1].start()
    for c in saves:
        c.wait()


def place(info, *ends):
    count = ends[0].shape[0] // HALF
    return pl.pallas_call(
        functools.partial(place_kernel, count),
        in_specs=[pl.BlockSpec(memory_space=pltpu.SMEM)] + [anywhere()] * 4,
        out_specs=[anywhere()] * count,
        out_shape=[rows_of(2 * LEN)] * count,
        scratch_shapes=[pltpu.VMEM((4 * count, HALF, D), BF), dma(4 * count), dma(4 * count)],
        compiler_params=pltpu.CompilerParams(vmem_limit_bytes=60 << 20),
        name="place",
    )(info, *ends)


def replica_sum_kernel(count, owners, gains, *refs):
    x_ref, refs = refs[0], refs[1:]
    if gains:
        gain_ref, o_ref, gsum_ref, in_ref, slot_ref, send_a, recv_a, send_b, recv_b, send_g, recv_g = refs
    else:
        o_ref, in_ref, send_a, recv_a, send_b, recv_b = refs
    me = lax.axis_index("dp")
    m = lax.axis_index("mp")
    barrier = pltpu.get_barrier_semaphore()
    for k in range(1, count):
        pl.semaphore_signal(barrier, inc=1, device_id=(lax.rem(me + k, count), m), device_id_type=MESH_ID)
    if gains:
        for k in range(1, 4):
            pl.semaphore_signal(barrier, inc=1, device_id=(me, lax.rem(m + k, 4)), device_id_type=MESH_ID)
    pl.semaphore_wait(barrier, count - 1 + (3 if gains else 0))

    def piece(j):
        return pl.ds(pl.multiple_of(j * 128, 128), 128)

    def part(j):
        return pltpu.make_async_remote_copy(
            src_ref=x_ref.at[:, piece(j)], dst_ref=in_ref.at[me], send_sem=send_a.at[j], recv_sem=recv_a.at[me],
            device_id=(j, m), device_id_type=MESH_ID)

    def whole(p):
        return pltpu.make_async_remote_copy(
            src_ref=o_ref.at[:, piece(me)], dst_ref=o_ref.at[:, piece(me)], send_sem=send_b.at[p],
            recv_sem=recv_b.at[me], device_id=(p, m), device_id_type=MESH_ID)

    for j in range(owners):
        @pl.when(me != j)
        def _():
            part(j).start()

    shares = []
    if gains:
        for k in range(1, 4):
            shares.append(push(gain_ref, slot_ref.at[k], send_g.at[k - 1], recv_g.at[k - 1], (me, lax.rem(m + k, 4))))
            shares[-1].start()

    @pl.when(me < owners)
    def _():
        in_ref[me] = x_ref[:, piece(me)]
        for s in range(count):
            @pl.when(me != s)
            def _():
                pltpu.make_async_remote_copy(
                    src_ref=x_ref.at[:, piece(0)], dst_ref=in_ref.at[s], send_sem=send_a.at[0], recv_sem=recv_a.at[s],
                    device_id=(s, m), device_id_type=MESH_ID).wait_recv()
        total = in_ref[0]
        for s in range(1, count):
            total = total + in_ref[s]
        o_ref[:, piece(me)] = total
        for p in range(count):
            @pl.when(me != p)
            def _():
                whole(p).start()

    for j in range(owners):
        @pl.when(me != j)
        def _():
            pltpu.make_async_remote_copy(
                src_ref=o_ref.at[:, piece(j)], dst_ref=o_ref.at[:, piece(j)], send_sem=send_b.at[0],
                recv_sem=recv_b.at[j], device_id=(j, m), device_id_type=MESH_ID).wait_recv()
            part(j).wait_send()

    @pl.when(me < owners)
    def _():
        for p in range(count):
            @pl.when(me != p)
            def _():
                whole(p).wait_send()


    for c in shares:
        c.wait()
    if gains:
        slot_ref[0] = gain_ref[...]
        parts = [slot_ref[lax.rem(m - k + 4, 4)] for k in range(4)]
        gsum_ref[...] = (parts[0] + parts[1]) + (parts[2] + parts[3])


def replica_sum(x, collective_id, gains=None):
    count = lax.axis_size("dp")
    owners = x.shape[1] // 128
    if count != 8:
        total = lax.psum(x, "dp")
        return total if gains is None else (total, lax.psum(gains, "mp"))
    args, outs, slots, tail = (x,), [jax.ShapeDtypeStruct(x.shape, F32)], [], []
    if gains is not None:
        args, outs = (x, gains), outs + [jax.ShapeDtypeStruct(gains.shape, F32)]
        slots, tail = [pltpu.VMEM((4, *gains.shape), F32)], [dma(3), dma(3)]
    done = pl.pallas_call(
        functools.partial(replica_sum_kernel, count, owners, gains is not None),
        out_shape=outs,
        in_specs=[in_vmem()] * len(args),
        out_specs=[in_vmem()] * len(outs),
        scratch_shapes=[pltpu.VMEM((count, x.shape[0], 128), F32)] + slots
        + [dma(owners), dma(count), dma(count), dma(owners)] + tail,
        compiler_params=pltpu.CompilerParams(collective_id=collective_id, has_side_effects=True),
        name="replica_sum",
    )(*args)
    return done[0] if gains is None else done


def lefts_kernel(gq_ref, gqb_ref, eq_ref, go_ref, gob_ref, eo_ref, fq_ref, fo_ref, lu_ref, ld_ref, g1_ref, g2_ref,
                 mq_ref, mo_ref, pack_ref):
    pack_ref[...] = jnp.zeros_like(pack_ref)
    mq = gq_ref[...] + gqb_ref[...].astype(F32) + eq_ref[0]
    mq_ref[...] = mq
    pack_ref[0:8, :] = exact(fq_ref[...], mq, 1, 0)
    mo = go_ref[...] + gob_ref[...].astype(F32) + eo_ref[0]
    mo_ref[...] = mo
    pack_ref[8:16, 0:192] = exact(fo_ref[...], mo, 1, 1)
    pack_ref[16:24, :] = lu_ref[...]
    pack_ref[24:32, :] = ld_ref[...]
    pack_ref[32:33, :] = g1_ref[...]
    pack_ref[33:34, :] = g2_ref[...]


def lefts(gq, gq_back, err_qkv, go, go_back, err_out, fac_qkv, fac_out, left_up, left_down, gain_one, gain_two):
    args = (gq, gq_back, err_qkv, go, go_back, err_out, fac_qkv, fac_out, left_up, left_down, gain_one, gain_two)
    return pl.pallas_call(
        lefts_kernel,
        grid=(1,),
        in_specs=[whole(v.shape) for v in args],
        out_specs=[whole((9 * HD, D)), whole((3 * HD, D)), whole((5 * RANK, D))],
        out_shape=[jax.ShapeDtypeStruct((9 * HD, D), F32), jax.ShapeDtypeStruct((3 * HD, D), F32),
                   jax.ShapeDtypeStruct((5 * RANK, D), F32)],
        compiler_params=pltpu.CompilerParams(vmem_limit_bytes=60 << 20),
        name="lefts",
    )(*args)


def rights_kernel(sum_ref, mq_ref, mo_ref, mu_ref, md_ref, hq_ref, ho_ref, hu_ref, hd_ref, pack_ref):
    row = lax.broadcasted_iota(jnp.int32, (RANK, D), 0)
    mats = [sum_ref[RANK * t:RANK * (t + 1), :] for t in range(4)]
    for k in range(RANK):
        for t in range(4):
            a = mats[t]
            v = a[k:k + 1, :]
            e = v / (jnp.sqrt(jnp.sum(v * v, axis=1, keepdims=True)) + 1e-08)
            c = jnp.sum(a * e, axis=1, keepdims=True)
            mats[t] = jnp.where(row == k, e, jnp.where(row > k, a - c * e, a))
    hq_ref[...] = mats[0]
    ho_ref[...] = mats[1][:, :192]
    hu_ref[...] = mats[2]
    hd_ref[...] = mats[3]
    pack_ref[...] = jnp.zeros_like(pack_ref)
    pack_ref[0:8, 0:9 * HD] = exact(mats[0], mq_ref[...], 1, 1)
    pack_ref[8:16, :] = exact(mats[1][:, :192], mo_ref[...], 1, 0)
    pack_ref[16:24, :] = exact(mats[2], mu_ref[...], 1, 0)
    pack_ref[24:32, :] = exact(mats[3], md_ref[...], 1, 0)


def rights(left_sum, mats):
    args = (left_sum, *mats)
    shapes = [(RANK, D), (RANK, 3 * HD), (RANK, D), (RANK, D), (4 * RANK, D)]
    return pl.pallas_call(
        rights_kernel,
        grid=(1,),
        in_specs=[whole(v.shape) for v in args],
        out_specs=[whole(s) for s in shapes],
        out_shape=[jax.ShapeDtypeStruct(s, F32) for s in shapes],
        compiler_params=pltpu.CompilerParams(vmem_limit_bytes=60 << 20),
        name="rights",
    )(*args)


def update_kernel(replicas, rates, info_ref, *refs):
    sums, hats, mats, states = refs[0], refs[1:5], refs[5:9], refs[9:21]
    total_ref, gain_ref, gm_ref = refs[21:24]
    errs, news, right_out, gains_out = refs[24:28], refs[28:40], refs[40:44], refs[44:47]
    decay = min(0.9999, (1.0 + EMA_STEPS) / (10.0 + EMA_STEPS))
    share = D // replicas
    shift = lax.rem(D - info_ref[1] * share, D)

    def part(value):
        return pltpu.roll(value, shift, 1)[:, :share]

    for t in range(4):
        hat = hats[t][...]
        right = sums[RANK * t:RANK * (t + 1), :] * (1.0 / replicas)
        right_out[t][...] = right[:, :right_out[t].shape[1]]
        first, second = ((right[:, :9 * HD], hat), (hat, right), (hat, right), (hat, right))[t]
        errs[t][0] = mats[t][...] - exact(first, second, 0, 0)
        first, second = ((part(hat), right[:, :9 * HD]), (hat, part(right)), (part(hat), right), (part(right), hat))[t]
        moment = 0.5 * states[3 * t + 1][...] + exact(first, second, 0, 0)
        master = states[3 * t][...] - rates[t] * moment
        news[3 * t][...] = master
        news[3 * t + 1][...] = moment
        news[3 * t + 2][...] = decay * states[3 * t + 2][...] + (1.0 - decay) * master
    grad = total_ref[0:2, :] * (1.0 / replicas)
    moment = 0.5 * gm_ref[...] + grad
    gains_out[0][...] = grad
    gains_out[1][...] = gain_ref[...] - rates[4] * moment
    gains_out[2][...] = moment


def update(info, replicas, rates, right_sum, hats, mats, states, gain_sum, gains, gain_moment):
    args = (right_sum, *hats, *mats, *states, gain_sum, gains, gain_moment)
    shapes = [(1, *m.shape) for m in mats] + [s.shape for s in states]
    shapes += [(RANK, 9 * HD), (RANK, D), (RANK, D), (RANK, D)] + [(2, D)] * 3
    return pl.pallas_call(
        functools.partial(update_kernel, replicas, rates),
        grid_spec=pltpu.PrefetchScalarGridSpec(
            num_scalar_prefetch=1,
            grid=(1,),
            in_specs=[whole(v.shape) for v in args],
            out_specs=[whole(s) for s in shapes],
        ),
        out_shape=[jax.ShapeDtypeStruct(s, F32) for s in shapes],
        compiler_params=pltpu.CompilerParams(vmem_limit_bytes=60 << 20),
        name="update",
    )(info, *args)


def local(
    noisy_rows, clean_rows, block_size, cotangent, norm_gains,
    weight_qkv, weight_out, weight_up, weight_down,
    master_qkv, master_out, master_up, master_down,
    moment_qkv, moment_out, moment_up, moment_down,
    average_qkv, average_out, average_up, average_down,
    error_qkv, error_out, error_up, error_down,
    factor_qkv, factor_out, factor_up, factor_down,
    gain_moment,
):
    row_count = noisy_rows.shape[0]
    replicas = lax.axis_size("dp")
    side = lax.axis_index("mp") // 2

    def across(value):
        return lax.ppermute(value, "mp", [(0, 2), (2, 0), (1, 3), (3, 1)])

    def beside(value):
        return lax.ppermute(value, "mp", [(0, 1), (1, 0), (2, 3), (3, 2)])

    def hold(*values):
        return lax.optimization_barrier(values)

    cos, sin = rotary_tables()
    m = lax.axis_index("mp")
    flip = m + 1 - 2 * (m % 2)
    info = jnp.stack([side, lax.axis_index("dp"), m % 2, m, flip, (m + 2) % 4, (flip + 2) % 4]).astype(jnp.int32)
    w_near = weight_qkv.T
    w_far, o_far = across(w_near), across(weight_out)
    qn_near, qc_near, att_near, lse_near, xn, xc = attend_near(
        info, block_size, noisy_rows, clean_rows, norm_gains, w_near, cos, sin)
    qn_far, qc_far, att_far, lse_far = attend_far(info, block_size, xn, xc, w_far, cos, sin)
    residual, grad_resid, grad_low, mlp, mlp_fold, matrix_up, matrix_down, left_up, left_down, gain_two = middle(
        att_near, att_far, weight_out, o_far, noisy_rows, cotangent, weight_up, weight_down,
        error_up, error_down, factor_up.T, factor_down.T, norm_gains)
    mlp_far = across(mlp_fold)
    dn_far, dc_far, gq_far, go_far = back_far(
        info, block_size, qn_far, qc_far, att_far, lse_far, grad_low, o_far, cos, sin, xn, xc)
    mlp_far, dn_far, gq_far, go_far = hold(mlp_far, dn_far, gq_far, go_far)
    gq_back, go_back = across(gq_far), across(go_far)
    out_half = settle(mlp, mlp_far, residual)
    out_half, dn_far = hold(out_half, dn_far)
    out_far, out_side = across(out_half), beside(out_half)
    grad_xn, grad_xc, gq_near, go_near = back_near(
        info, block_size, qn_near, qc_near, att_near, lse_near, grad_low, weight_out, cos, sin, xn, xc,
        w_near, w_far, dn_far, dc_far)
    ends, gain_one = finish(grad_xn, grad_xc, noisy_rows, clean_rows, grad_resid, norm_gains)
    ends, gq_back, go_back = hold(ends, gq_back, go_back)
    ends_far = across(ends)
    ends_side = beside(ends)
    matrix_qkv, matrix_out, left_pack = lefts(
        gq_near, gq_back, jnp.swapaxes(error_qkv, 1, 2), go_near, go_back, error_out, factor_qkv.T, factor_out.T,
        left_up, left_down, gain_one, gain_two)
    left_sum = replica_sum(left_pack, 1)
    mats = (matrix_qkv, matrix_out, matrix_up, matrix_down)
    *hats, right_pack = rights(left_sum, mats)
    right_sum, gain_sum = replica_sum(right_pack, 2, left_sum[4 * RANK:])
    rates = [3.0 / math.sqrt(f * row_count) for f in (D, HEADS * HD // 64, D, FF)] + [0.5 / math.sqrt(row_count)]
    states = (
        master_qkv, moment_qkv, average_qkv, master_out, moment_out, average_out,
        master_up, moment_up, average_up, master_down.T, moment_down.T, average_down.T,
    )
    done = update(info, replicas, rates, right_sum, hats, mats, states, gain_sum, norm_gains, gain_moment)
    errs, news, right_new, gains_new = done[:4], done[4:16], done[16:20], done[20:23]
    out_far, out_half = hold(out_far, out_half)
    out_diag = beside(out_far)
    block_out, = place(info, out_half, out_side, out_far, out_diag)
    ends_far, _, block_out = hold(ends_far, errs[2], block_out)
    ends_diag = beside(ends_far)
    grad_noisy, grad_clean = place(info, ends, ends_side, ends_far, ends_diag)
    fresh = [news[3 * t + k] if t < 3 else news[3 * t + k].T for k in range(3) for t in range(4)]
    return (
        block_out, grad_noisy, grad_clean, *gains_new, *fresh,
        jnp.swapaxes(errs[0], 1, 2), *errs[1:], *[v.T for v in hats], *[v.T for v in right_new],
    )


def solution(mesh):
    in_specs = (
        P("dp", None), P("dp", None), P("dp"), P("dp", None), P(),
        P(None, "mp"), P("mp", None), P(None, "mp"), P("mp", None),
        *([P("dp", "mp"), P("mp", "dp")] * 6),
        *([P("dp", None, "mp"), P("dp", "mp", None)] * 2),
        *([P("mp", None), P(None, "mp")] * 2),
        P(),
    )
    out_specs = (
        P("dp", None), P("dp", None), P("dp", None), P(), P(), P(),
        *([P("dp", "mp"), P("mp", "dp")] * 6),
        *([P("dp", None, "mp"), P("dp", "mp", None)] * 2),
        *([P(None, "mp"), P("mp", None)] * 2),
        *([P("mp", None), P(None, "mp")] * 2),
    )
    return jax.shard_map(local, mesh=mesh, in_specs=in_specs, out_specs=out_specs, check_vma=False)
```

```python
import functools
import math

import jax
import jax.numpy as jnp
import numpy as np
from jax import lax
from jax.experimental import pallas as pl
from jax.experimental.pallas import tpu as pltpu
from jax.sharding import PartitionSpec as P

D = 768
HEADS = 12
HD = 64
FF = 3072
LEN = 1024
RANK = 8
EMA_STEPS = 4
TILE = 256
SLOT = 256

BF = jnp.bfloat16
F32 = jnp.float32
highest = lax.Precision.HIGHEST
norm_eps = 1e-05
gelu_coef = 0.7978845608028654
masked_score = -1e30
MESH_ID = pl.DeviceIdType.MESH


def nt(a, b):
    return lax.dot_general(a, b, (((1,), (1,)), ((), ())), preferred_element_type=F32)


def nn(a, b):
    return lax.dot_general(a, b, (((1,), (0,)), ((), ())), preferred_element_type=F32)


def tn(a, b):
    return lax.dot_general(a, b, (((0,), (0,)), ((), ())), preferred_element_type=F32)


def rotary_tables():
    half = HD // 2
    step = np.float32(-2.0 * math.log(10000.0) / HD)
    inverse = np.exp(np.arange(half, dtype=np.float32) * step).astype(np.float32)
    angle = (np.arange(LEN, dtype=np.float32)[:, None] * inverse[None, :]).astype(np.float32)
    c = np.cos(angle).astype(np.float32)
    s = np.sin(angle).astype(np.float32)
    return np.concatenate([c, c, c, c], 1), np.concatenate([-s, s, -s, s], 1)


def spin(v, cos, sin):
    lane = lax.broadcasted_iota(jnp.int32, v.shape, 1)
    low = lax.rem(lane, HD) < HD // 2
    swapped = jnp.where(low, pltpu.roll(v, 128 - HD // 2, 1), pltpu.roll(v, HD // 2, 1))
    return v * cos + swapped * sin


def block_ids(size, shape, dim):
    shift = 2 + (size >= 8).astype(jnp.int32) + (size >= 16).astype(jnp.int32)
    place = lax.broadcasted_iota(jnp.int32, shape, dim)
    return lax.shift_right_logical(place, jnp.full(shape, shift, jnp.int32))


def fill_bias(size, noisy_bias, clean_bias):
    keys = block_ids(size, (TILE, TILE), 0)
    rows = block_ids(size, (TILE, TILE), 1)
    noisy_bias[...] = jnp.where(rows == keys, 0.0, masked_score)
    clean_bias[...] = jnp.where(keys < rows, 0.0, masked_score)


def norm_parts(values):
    centered = values - jnp.mean(values, axis=1, keepdims=True)
    scale = lax.rsqrt(jnp.mean(centered * centered, axis=1, keepdims=True) + norm_eps)
    return centered * scale, scale


def norm_back(values, gain, grad):
    unit, scale = norm_parts(values)
    scaled = grad * gain
    inner = jnp.mean(scaled * unit, axis=1, keepdims=True)
    grad_in = scale * (scaled - jnp.mean(scaled, axis=1, keepdims=True) - unit * inner)
    return grad_in, jnp.sum(grad * unit, axis=0, keepdims=True)


def gelu_and_slope(u):
    square = u * u
    half = 0.5 + 0.5 * jnp.tanh(u * (gelu_coef + (gelu_coef * 0.044715) * square))
    slope = half + (u * (2.0 * half * (1.0 - half))) * (gelu_coef + (3.0 * 0.044715 * gelu_coef) * square)
    return u * half, slope


def whole(shape):
    return pl.BlockSpec(shape, lambda *index: (0,) * len(shape), pipeline_mode=pl.Buffered(1))


def side_rows(h, info, size):
    return (info[0], 0)


def lane2(h, *_):
    return (0, h)


def row3(h, *_):
    return (h, 0, 0)


def attend_head(head, xn_ref, xc_ref, w_ref, cos_ref, sin_ref, qn_ref, qc_ref, att_ref, lse_ref,
                bn_ref, bc_ref, kn_ref, kc_ref, vnt_ref, vct_ref):
    w = w_ref[pl.ds(pl.multiple_of(head * 3 * HD, 3 * HD), 3 * HD), :]
    for src, dst, keys, vals in ((xn_ref, qn_ref, kn_ref, vnt_ref), (xc_ref, qc_ref, kc_ref, vct_ref)):
        a = nt(src[...], w)
        r = spin(a[:, :128], cos_ref[...], sin_ref[...]).astype(BF)
        v = a[:, 128:].astype(BF)
        dst[:, :128] = r
        dst[:, 128:192] = v
        keys[...] = r[:, 64:128]
        vals[...] = jnp.transpose(v)
    here = pl.ds(pl.multiple_of(head * HD, HD), HD)
    for i in range(LEN // TILE):
        lo, hi = i * TILE, (i + 1) * TILE
        q = qn_ref[lo:hi, 0:64] * 0.125
        parts = [nt(kn_ref[lo:hi, :], q) + bn_ref[...], nt(kc_ref[lo:hi, :], q) + bc_ref[...]]
        if i:
            parts.append(nt(kc_ref[0:lo, :], q))
        peak = functools.reduce(jnp.maximum, [jnp.max(s, axis=0, keepdims=True) for s in parts])
        exps = [jnp.exp(s - peak) for s in parts]
        total = functools.reduce(jnp.add, [jnp.sum(e, axis=0, keepdims=True) for e in exps])
        inv = 1.0 / total
        low = [(e * inv).astype(BF) for e in exps]
        o = nn(vnt_ref[:, lo:hi], low[0]) + nn(vct_ref[:, lo:hi], low[1])
        if i:
            o = o + nn(vct_ref[:, 0:lo], low[2])
        att_ref[here, lo:hi] = o.astype(BF)
        lse_ref[0, :, lo:hi] = jnp.broadcast_to(peak + jnp.log(total), (8, TILE))


def attend_kernel(size_ref, noisy_hbm, clean_hbm, w_hbm, wo_hbm, gain_ref, cos_ref, sin_ref,
                  qn_ref, qc_ref, att_ref, lse_ref, xn_hbm, xc_hbm, w_far_hbm, o_far_hbm,
                  raw_ref, x_ref, w_ref, sem_in, sem_out, sem_send, sem_recv, *work):
    head = pl.program_id(0)
    side = lax.axis_index("mp") // 2
    peer = far_peer()
    sides = ((noisy_hbm, xn_hbm), (clean_hbm, xc_hbm))
    width = 3 * HD

    def load(s, i):
        at = pl.ds(pl.multiple_of(side * LEN + i * TILE, TILE), TILE)
        return pltpu.make_async_copy(sides[s][0].at[at], raw_ref.at[s, chunk(i)], sem_in.at[CHUNKS * s + i])

    def save(s):
        return pltpu.make_async_copy(x_ref.at[s], sides[s][1], sem_out.at[s])

    def give(j):
        at = slice(width * j, width * (j + 1))
        return push(w_hbm.at[at], w_ref.at[slice(width * (3 + j), width * (4 + j))], sem_send.at[j], sem_recv.at[j], peer)

    near_w = pltpu.make_async_copy(w_hbm, w_ref.at[0:3 * width], sem_in.at[2 * CHUNKS])
    give_out = push(wo_hbm, o_far_hbm, sem_send.at[3], sem_recv.at[3], peer)
    keep_w = pltpu.make_async_copy(w_ref.at[3 * width:], w_far_hbm, sem_out.at[2])

    @pl.when(head == 0)
    def _():
        for s in range(2):
            for i in range(CHUNKS):
                load(s, i).start()
        near_w.start()
        greet(peer)
        for j in range(3):
            give(j).start()
        give_out.start()
        fill_bias(size_ref[side], work[0], work[1])
        for s in range(2):
            for i in range(CHUNKS):
                load(s, i).wait()
                x = norm_parts(raw_ref[s, chunk(i), :].astype(F32))[0] * gain_ref[0:1, :]
                x_ref[s, chunk(i), :] = x.astype(BF)
            save(s).start()
        near_w.wait()

    for j in range(3):
        @pl.when(head == 3 + j)
        def _():
            give(j).wait_recv()

    @pl.when(head == 5)
    def _():
        keep_w.start()

    attend_head(head, x_ref.at[0], x_ref.at[1], w_ref, cos_ref, sin_ref, qn_ref, qc_ref, att_ref, lse_ref, *work)

    @pl.when(head == 5)
    def _():
        save(0).wait()
        save(1).wait()
        keep_w.wait()
        for j in range(3):
            give(j).wait_send()
        give_out.wait()


CHUNKS = LEN // TILE
HALF = LEN // 2


def chunk(i):
    return slice(i * TILE, (i + 1) * TILE)


def anywhere():
    return pl.BlockSpec(memory_space=pl.ANY)


def in_vmem():
    return pl.BlockSpec(memory_space=pltpu.VMEM)


def dma(n):
    return pltpu.SemaphoreType.DMA((n,))


def rows_of(n):
    return jax.ShapeDtypeStruct((n, D), BF)


attend_work = [
    pltpu.VMEM((TILE, TILE), F32),
    pltpu.VMEM((TILE, TILE), F32),
    pltpu.VMEM((LEN, HD), BF),
    pltpu.VMEM((LEN, HD), BF),
    pltpu.VMEM((HD, LEN), BF),
    pltpu.VMEM((HD, LEN), BF),
]
rows_shape = jax.ShapeDtypeStruct((LEN, D), BF)


def attend(size, noisy, clean, w, wo, gains, cos, sin):
    return pl.pallas_call(
        attend_kernel,
        grid=(6,),
        in_specs=[pl.BlockSpec(memory_space=pltpu.SMEM)] + [anywhere()] * 4
        + [whole((2, D)), whole((LEN, 128)), whole((LEN, 128))],
        out_specs=[pl.BlockSpec((LEN, SLOT), lane2), pl.BlockSpec((LEN, SLOT), lane2), whole((6 * HD, LEN)),
                   pl.BlockSpec((1, 8, LEN), row3)] + [anywhere()] * 4,
        out_shape=[jax.ShapeDtypeStruct((LEN, SLOT * 6), BF), jax.ShapeDtypeStruct((LEN, SLOT * 6), BF),
                   jax.ShapeDtypeStruct((6 * HD, LEN), BF), jax.ShapeDtypeStruct((6, 8, LEN), F32),
                   rows_shape, rows_shape, rows_of(9 * HD), rows_of(3 * HD)],
        scratch_shapes=[pltpu.VMEM((2, LEN, D), BF), pltpu.VMEM((2, LEN, D), BF), pltpu.VMEM((18 * HD, D), BF),
                        dma(2 * CHUNKS + 1), dma(3), dma(4), dma(4)] + attend_work,
        compiler_params=pltpu.CompilerParams(collective_id=6, has_side_effects=True, vmem_limit_bytes=60 << 20),
        name="attend",
    )(size, noisy, clean, w, wo, gains, cos, sin)


def back_head(head, qn_ref, qc_ref, lse_ref, cos_ref, sin_ref, dn_ref, dc_ref,
              bn_ref, bc_ref, kn_ref, kc_ref, knt_ref, kct_ref, dot_ref, do_ref, dq_ref, dkn_ref, dkc_ref, dvc_ref):
    do_ref[...] = jnp.transpose(dot_ref[pl.ds(pl.multiple_of(head * HD, HD), HD), :])
    kn_ref[...] = qn_ref[:, 64:128]
    kc_ref[...] = qc_ref[:, 64:128]
    knt_ref[...] = jnp.transpose(qn_ref[:, 0:128])[64:128]
    kct_ref[...] = jnp.transpose(qc_ref[:, 0:128])[64:128]
    dkc_ref[...] = jnp.zeros_like(dkc_ref)
    dvc_ref[...] = jnp.zeros_like(dvc_ref)
    blank = jnp.zeros((TILE, HD), F32)
    for i in range(LEN // TILE):
        lo, hi = i * TILE, (i + 1) * TILE
        q = qn_ref[lo:hi, 0:64] * 0.125
        do = do_ref[lo:hi, :]
        lse = lse_ref[0, 0:1, lo:hi]
        spans = [(0, lo, hi), (1, lo, hi)] + ([(1, 0, lo)] if i else [])
        probs, grads, inner = [], [], 0.0
        for n, (side, a, b) in enumerate(spans):
            kr = kc_ref if side else kn_ref
            vr = qc_ref if side else qn_ref
            s = nt(kr[a:b, :], q)
            if n == 0:
                s = s + bn_ref[...]
            if n == 1:
                s = s + bc_ref[...]
            p = jnp.exp(s - lse)
            dp = nt(vr[a:b, 128:192], do)
            inner = inner + jnp.sum(p * dp, axis=0, keepdims=True)
            probs.append(p)
            grads.append(dp)
        dqt = 0.0
        for n, (side, a, b) in enumerate(spans):
            ds = (probs[n] * (grads[n] - inner)).astype(BF)
            dv = nn(probs[n].astype(BF), do)
            dk = nn(ds, q)
            ktr = kct_ref if side else knt_ref
            dqt = dqt + nn(ktr[:, a:b], ds)
            if side:
                dkc_ref[a:b, :] += dk
                dvc_ref[a:b, :] += dv
            else:
                dkn_ref[a:b, :] = dk
                dn_ref[lo:hi, 128:256] = jnp.concatenate([dv, blank], axis=1).astype(BF)
        dq_ref[lo:hi, :] = jnp.transpose(dqt) * 0.125
    zero = jnp.zeros((LEN, HD), F32)
    sin = -sin_ref[...]
    cos = cos_ref[...]
    dn_ref[:, 0:128] = spin(jnp.concatenate([dq_ref[...], dkn_ref[...]], axis=1), cos, sin).astype(BF)
    dc_ref[:, 0:128] = spin(jnp.concatenate([zero, dkc_ref[...]], axis=1), cos, sin).astype(BF)
    dc_ref[:, 128:256] = jnp.concatenate([dvc_ref[...], zero], axis=1).astype(BF)


def head_grad(xn_ref, xc_ref, dn_ref, dc_ref, gq_ref):
    g = tn(dn_ref[...], xn_ref[...]) + tn(dc_ref[...], xc_ref[...])
    gq_ref[...] = g[:3 * HD].astype(gq_ref.dtype)


def back_far_kernel(info_ref, size_ref, qn_ref, qc_ref, att_ref, lse_ref, g_ref, wo_ref, cos_ref, sin_ref,
                    xn_hbm, xc_hbm, dn_ref, dc_ref, gq_ref, go_ref, xn_ref, xc_ref, sems, *work):
    head = pl.program_id(0)
    late = [pltpu.make_async_copy(s, d, sems.at[k]) for k, (s, d) in enumerate(((xn_hbm, xn_ref), (xc_hbm, xc_ref)))]

    @pl.when(head == 0)
    def _():
        for c in late:
            c.start()
        fill_bias(size_ref[info_ref[0]], work[0], work[1])
        work[6][...] = nt(wo_ref[...], g_ref[...]).astype(BF)
        go_ref[...] = nn(att_ref[...], g_ref[...]).astype(BF)

    back_head(head, qn_ref, qc_ref, lse_ref, cos_ref, sin_ref, dn_ref, dc_ref, *work)

    @pl.when(head == 0)
    def _():
        for c in late:
            c.wait()

    head_grad(xn_ref, xc_ref, dn_ref, dc_ref, gq_ref)


def back_near_kernel(info_ref, size_ref, qn_ref, qc_ref, att_ref, lse_ref, g_ref, wo_ref, cos_ref, sin_ref,
                     xn_hbm, xc_hbm, w_hbm, w_far_hbm, dnf_hbm, dcf_hbm, gxn_hbm, gxc_hbm, gq_ref, go_ref,
                     xn_ref, xc_ref, w_ref, w_far_ref, dnf_ref, dcf_ref, keep_ref, dn_ref, dc_ref, out_ref,
                     sems, sem_out, *work):
    head = pl.program_id(0)
    late = [pltpu.make_async_copy(s, d, sems.at[k]) for k, (s, d) in enumerate((
        (xn_hbm, xn_ref), (xc_hbm, xc_ref), (w_hbm, w_ref), (w_far_hbm, w_far_ref),
        (dnf_hbm, dnf_ref), (dcf_hbm, dcf_ref)))]

    @pl.when(head == 0)
    def _():
        for c in late:
            c.start()
        fill_bias(size_ref[info_ref[0]], work[0], work[1])
        work[6][...] = nt(wo_ref[...], g_ref[...]).astype(BF)
        go_ref[...] = nn(att_ref[...], g_ref[...])

    back_head(head, qn_ref, qc_ref, lse_ref, cos_ref, sin_ref, dn_ref, dc_ref, *work)

    @pl.when(head == 0)
    def _():
        for c in late:
            c.wait()

    head_grad(xn_ref, xc_ref, dn_ref, dc_ref, gq_ref)
    keep_ref[0, head] = dn_ref[...]
    keep_ref[1, head] = dc_ref[...]

    @pl.when(head == 2)
    def _():
        copies = []
        for s, (far, out) in enumerate(((dnf_ref, gxn_hbm), (dcf_ref, gxc_hbm))):
            for i in range(CHUNKS):
                total = 0.0
                for j in range(3):
                    total = total + nn(keep_ref[s, j, chunk(i), 0:192], w_ref[192 * j:192 * (j + 1), :])
                    total = total + nn(far[chunk(i), SLOT * j:SLOT * j + 192], w_far_ref[192 * j:192 * (j + 1), :])
                out_ref[s, chunk(i), :] = total.astype(BF)
                copies.append(pltpu.make_async_copy(
                    out_ref.at[s, chunk(i)], out.at[chunk(i)], sem_out.at[CHUNKS * s + i]))
                copies[-1].start()
        for c in copies:
            c.wait()


back_work = attend_work[:4] + [
    pltpu.VMEM((HD, LEN), BF),
    pltpu.VMEM((HD, LEN), BF),
    pltpu.VMEM((3 * HD, LEN), BF),
    pltpu.VMEM((LEN, HD), BF),
    pltpu.VMEM((LEN, HD), F32),
    pltpu.VMEM((LEN, HD), F32),
    pltpu.VMEM((LEN, HD), F32),
    pltpu.VMEM((LEN, HD), F32),
]
wide_rows = jax.ShapeDtypeStruct((LEN, 3 * SLOT), BF)


def head_inputs(first):
    return [pl.BlockSpec((LEN, SLOT), lambda h, *_: (0, h + first)), pl.BlockSpec((LEN, SLOT), lambda h, *_: (0, h + first)),
            pl.BlockSpec((3 * HD, LEN), lambda h, *_: (first // 3, 0), pipeline_mode=pl.Buffered(1)),
            pl.BlockSpec((1, 8, LEN), lambda h, *_: (h + first, 0, 0))]


row2_spec = pl.BlockSpec((3 * HD, D), lambda h, *_: (h, 0))


def back_far(info, size, qn, qc, att, lse, g, wo, cos, sin, xn, xc):
    return pl.pallas_call(
        back_far_kernel,
        grid_spec=pltpu.PrefetchScalarGridSpec(
            num_scalar_prefetch=2,
            grid=(3,),
            in_specs=head_inputs(3) + [whole((LEN, D)), whole((3 * HD, D)),
                                       whole((LEN, 128)), whole((LEN, 128)), anywhere(), anywhere()],
            out_specs=[pl.BlockSpec((LEN, SLOT), lane2), pl.BlockSpec((LEN, SLOT), lane2), row2_spec, whole((3 * HD, D))],
            scratch_shapes=[pltpu.VMEM((LEN, D), BF), pltpu.VMEM((LEN, D), BF), dma(2)] + back_work,
        ),
        out_shape=[wide_rows, wide_rows, rows_of(9 * HD), rows_of(3 * HD)],
        compiler_params=pltpu.CompilerParams(vmem_limit_bytes=60 << 20),
        name="back_far",
    )(info, size, qn, qc, att, lse, g, wo, cos, sin, xn, xc)


def back_near(info, size, qn, qc, att, lse, g, wo, cos, sin, xn, xc, w, w_far, dn_far, dc_far):
    return pl.pallas_call(
        back_near_kernel,
        grid_spec=pltpu.PrefetchScalarGridSpec(
            num_scalar_prefetch=2,
            grid=(3,),
            in_specs=head_inputs(0) + [whole((LEN, D)), whole((3 * HD, D)),
                                       whole((LEN, 128)), whole((LEN, 128))] + [anywhere()] * 6,
            out_specs=[anywhere(), anywhere(), row2_spec, whole((3 * HD, D))],
            scratch_shapes=[pltpu.VMEM((LEN, D), BF), pltpu.VMEM((LEN, D), BF),
                            pltpu.VMEM((9 * HD, D), BF), pltpu.VMEM((9 * HD, D), BF),
                            pltpu.VMEM((LEN, 3 * SLOT), BF), pltpu.VMEM((LEN, 3 * SLOT), BF),
                            pltpu.VMEM((2, 3, LEN, SLOT), BF), pltpu.VMEM((LEN, SLOT), BF), pltpu.VMEM((LEN, SLOT), BF),
                            pltpu.VMEM((2, LEN, D), BF), dma(6), dma(2 * CHUNKS)] + back_work,
        ),
        out_shape=[rows_shape, rows_shape, jax.ShapeDtypeStruct((9 * HD, D), F32), jax.ShapeDtypeStruct((3 * HD, D), F32)],
        compiler_params=pltpu.CompilerParams(vmem_limit_bytes=60 << 20),
        name="back_near",
    )(info, size, qn, qc, att, lse, g, wo, cos, sin, xn, xc, w, w_far, dn_far, dc_far)


def halves(v):
    high = v.astype(BF)
    return high, (v - high.astype(F32)).astype(BF)


def exact(left_side, right_side, left_dim, right_dim):
    dims = (((left_dim,), (right_dim,)), ((), ()))
    a, b = halves(left_side)
    c, d = halves(right_side)

    def times(x, y):
        return lax.dot_general(x, y, dims, preferred_element_type=F32)

    return times(a, c) + (times(a, d) + times(b, c))


def core_peer():
    m = lax.axis_index("mp")
    return (lax.axis_index("dp"), m + 1 - 2 * lax.rem(m, 2))


def far_peer():
    return (lax.axis_index("dp"), lax.rem(lax.axis_index("mp") + 2, 4))


def greet(*peers):
    barrier = pltpu.get_barrier_semaphore()
    for p in peers:
        pl.semaphore_signal(barrier, inc=1, device_id=p, device_id_type=MESH_ID)
    pl.semaphore_wait(barrier, len(peers))


PARTS = HALF // TILE


def own_rows(i):
    half = lax.rem(lax.axis_index("mp"), 2)
    return pl.ds(pl.multiple_of(half * HALF + i * TILE, TILE), TILE)


def peer_rows(i):
    half = lax.rem(lax.axis_index("mp"), 2)
    return pl.ds(pl.multiple_of((1 - half) * HALF + i * TILE, TILE), TILE)


def side_rows_of(i):
    m = lax.axis_index("mp")
    return pl.ds(pl.multiple_of(m * HALF + i * TILE, TILE), TILE)


def copy(src, dst, sem):
    return pltpu.make_async_copy(src, dst, sem)


def push(src, dst, send_sem, recv_sem, peer):
    return pltpu.make_async_remote_copy(
        src_ref=src, dst_ref=dst, send_sem=send_sem, recv_sem=recv_sem, device_id=peer, device_id_type=MESH_ID)


class Sems:
    def __init__(self, ref):
        self.ref = ref
        self.used = 0

    def take(self):
        self.used += 1
        return self.ref.at[self.used - 1]


def middle_kernel(att_hbm, wo_near_hbm, wo_far_hbm, rows_hbm, cot_hbm, up_hbm, down_hbm,
                  err_up_hbm, err_down_hbm, fac_up_ref, fac_down_ref, gain_ref,
                  res_hbm, grad_hbm, low_hbm, mlp_hbm, fold_hbm, mat_up_hbm, mat_down_hbm,
                  left_up_ref, left_down_ref, gsum_ref,
                  att_ref, wo_ref, x_ref, send_ref, far_ref, r_ref, nm_ref, cot_ref, up_ref, down_ref, hid_ref, gp_ref,
                  mlp_ref, gm_ref, back_ref, fold_gm_ref, fold_mlp_ref, sum_ref, msum_ref, yet_ref,
                  mat_up_ref, mat_down_ref, nmt_ref, grad_ref, low_ref, sem_ref, send_sem_ref, recv_sem_ref):
    sems, sends, recvs = Sems(sem_ref), Sems(send_sem_ref), Sems(recv_sem_ref)
    m = lax.axis_index("mp")
    side, half = m // 2, lax.rem(m, 2)
    core, far = core_peer(), far_peer()
    width = 3 * HD
    third = D // 3
    pushes, saves = [], []

    def load(src, dst):
        c = pltpu.make_async_copy(src, dst, sems.take())
        c.start()
        return c

    def save(src, dst):
        saves.append(load(src, dst))

    def send(src, dst, peer):
        c = push(src, dst, sends.take(), recvs.take(), peer)
        c.start()
        pushes.append(c)
        return c

    def span(start, n):
        return pl.ds(pl.multiple_of(start, TILE), n)

    own_half, peer_half = half * HALF, (1 - half) * HALF
    first = [load(att_hbm, att_ref), load(wo_near_hbm, wo_ref.at[0:width]), load(wo_far_hbm, wo_ref.at[width:])]
    xs = [load(rows_hbm.at[span(m * HALF + i * TILE, TILE)], x_ref.at[chunk(i)]) for i in range(PARTS)]
    up_in, down_in = load(up_hbm, up_ref), load(down_hbm, down_ref)
    cot_in = load(cot_hbm.at[span(side * LEN, LEN)], cot_ref.at[0:LEN])
    cot_far_in = load(cot_hbm.at[span((1 - side) * LEN, LEN)], cot_ref.at[LEN:])
    err_in = [load(err_down_hbm.at[0], mat_down_ref), load(err_up_hbm.at[0], mat_up_ref)]
    greet(core, far)
    for c in first:
        c.wait()
    parts = []
    for i in range(PARTS):
        send_ref[chunk(i), :] = tn(att_ref[:, span(peer_half + i * TILE, TILE)], wo_ref[...]).astype(BF)
        parts.append(send(send_ref.at[chunk(i)], far_ref.at[chunk(i)], core))
    normed, cross = [], []
    for i in range(PARTS):
        at = span(own_half + i * TILE, TILE)
        own = tn(att_ref[:, at], wo_ref[...])
        xs[i].wait()
        parts[i].wait_recv()
        r = x_ref[chunk(i), :].astype(F32) + (own + far_ref[chunk(i), :].astype(F32))
        r_ref[chunk(i), :] = r
        nm_ref[at, :] = (norm_parts(r)[0] * gain_ref[1:2, :]).astype(BF)
        normed.append(send(nm_ref.at[at], nm_ref.at[at], core))
        cross.append(send(nm_ref.at[at], nm_ref.at[span(LEN + own_half + i * TILE, TILE)], far))
        save(r_ref.at[chunk(i)], res_hbm.at[chunk(i)])

    def feed_rows(start, n):
        at = span(start, n)
        for t in range(3):
            lanes = slice(t * third, (t + 1) * third)
            hidden, slope = gelu_and_slope(nn(nm_ref[at, :], up_ref[:, lanes]))
            hid_ref[at, lanes] = hidden.astype(BF)
            gp_ref[at, lanes] = (slope * nt(cot_ref[at, :], down_ref[lanes, :])).astype(BF)
        gm_ref[at, :] = nt(gp_ref[at, :], up_ref[...]).astype(BF)
        mlp_ref[at, :] = nn(hid_ref[at, :], down_ref[...]).astype(BF)

    up_in.wait()
    down_in.wait()
    cot_in.wait()
    feed_rows(own_half, HALF)
    for c in normed:
        c.wait_recv()
    feed_rows(peer_half, HALF)
    save(mlp_ref.at[0:LEN], mlp_hbm)
    swap = [send(gm_ref.at[span(peer_half + i * TILE, TILE)], back_ref.at[chunk(i)], core) for i in range(PARTS)]
    cot_far_in.wait()
    arrived = []
    for i in range(PARTS):
        at = span(LEN + own_half + i * TILE, TILE)
        away = span(LEN + peer_half + i * TILE, TILE)
        cross[i].wait_recv()
        relay = send(nm_ref.at[at], nm_ref.at[at], core)
        feed_rows(LEN + own_half + i * TILE, TILE)
        relay.wait_recv()
        feed_rows(LEN + peer_half + i * TILE, TILE)
        fold = send(gm_ref.at[away], fold_gm_ref.at[chunk(i)], core)
        fold_mlp = send(mlp_ref.at[away], fold_mlp_ref.at[chunk(i)], core)
        fold.wait_recv()
        sum_ref[chunk(i), :] = (gm_ref[at, :].astype(F32) + fold_gm_ref[chunk(i), :].astype(F32)).astype(BF)
        arrived.append(send(sum_ref.at[chunk(i)], yet_ref.at[chunk(i)], far))
        fold_mlp.wait_recv()
        msum_ref[chunk(i), :] = (mlp_ref[at, :].astype(F32) + fold_mlp_ref[chunk(i), :].astype(F32)).astype(BF)
        save(msum_ref.at[chunk(i)], fold_hbm.at[chunk(i)])

    for i in range(8):
        at = slice(i * TILE, (i + 1) * TILE)
        nmt_ref[:, at] = jnp.transpose(nm_ref[at, :])
    for c in err_in:
        c.wait()
    left_up = 0.0
    for t in range(3):
        lanes = slice(t * third, (t + 1) * third)
        mat = tn(hid_ref[:, lanes], cot_ref[...]) + mat_down_ref[lanes, :]
        mat_down_ref[lanes, :] = mat
        save(mat_down_ref.at[lanes], mat_down_hbm.at[lanes])
        left_down_ref[:, lanes] = exact(fac_down_ref[...], mat, 1, 1)
        mat = nn(nmt_ref[...], gp_ref[:, lanes]) + mat_up_ref[:, lanes]
        mat_up_ref[:, lanes] = mat
        save(mat_up_ref.at[:, lanes], mat_up_hbm.at[:, lanes])
        left_up = left_up + exact(fac_up_ref[:, lanes], mat, 1, 1)
    left_up_ref[...] = left_up

    gsum = 0.0
    lows = []
    for i in range(PARTS):
        at = span(own_half + i * TILE, TILE)
        swap[i].wait_recv()
        total = gm_ref[at, :].astype(F32) + back_ref[chunk(i), :].astype(F32)
        arrived[i].wait_recv()
        total = total + yet_ref[chunk(i), :].astype(F32)
        grad, share = norm_back(r_ref[chunk(i), :], gain_ref[1:2, :], total)
        gsum = gsum + share
        grad = cot_ref[at, :].astype(F32) + grad
        grad_ref[chunk(i), :] = grad
        low_ref[chunk(i), :] = grad.astype(BF)
        lows.append(send(low_ref.at[chunk(i)], low_hbm.at[at], core))
        save(low_ref.at[chunk(i)], low_hbm.at[at])
        save(grad_ref.at[chunk(i)], grad_hbm.at[chunk(i)])
    gsum_ref[...] = gsum
    for c in lows:
        c.wait_recv()
    for c in pushes:
        c.wait_send()
    for c in saves:
        c.wait()


def middle(att, wo_near, wo_far, rows, cotangent, up, down, err_up, err_down, fac_up, fac_down, gains):
    def low(n):
        return pltpu.VMEM((n, D), BF)

    def wide(n):
        return pltpu.VMEM((n, D), F32)

    return pl.pallas_call(
        middle_kernel,
        in_specs=[anywhere()] * 9 + [in_vmem()] * 3,
        out_specs=[anywhere()] * 7 + [in_vmem()] * 3,
        out_shape=[jax.ShapeDtypeStruct((HALF, D), F32), jax.ShapeDtypeStruct((HALF, D), F32), rows_of(LEN), rows_of(LEN),
                   rows_of(HALF), jax.ShapeDtypeStruct((D, D), F32), jax.ShapeDtypeStruct((D, D), F32),
                   jax.ShapeDtypeStruct((RANK, D), F32), jax.ShapeDtypeStruct((RANK, D), F32),
                   jax.ShapeDtypeStruct((1, D), F32)],
        scratch_shapes=[pltpu.VMEM((6 * HD, LEN), BF), low(6 * HD), low(HALF), low(HALF), low(HALF), wide(HALF),
                        low(2 * LEN), low(2 * LEN), low(D), low(D), low(2 * LEN), low(2 * LEN),
                        low(2 * LEN), low(2 * LEN), low(HALF), low(HALF), low(HALF), low(HALF), low(HALF), low(HALF),
                        wide(D), wide(D), pltpu.VMEM((D, 2 * LEN), BF), wide(HALF), low(HALF), dma(32), dma(24), dma(24)],
        compiler_params=pltpu.CompilerParams(collective_id=3, has_side_effects=True, vmem_limit_bytes=60 << 20),
        name="middle",
    )(att, wo_near, wo_far, rows, cotangent, up, down, err_up, err_down, fac_up, fac_down, gains)


def settle_kernel(mlp_hbm, far_hbm, res_hbm, out_hbm, own_ref, far_ref, res_ref, core_ref, out_ref,
                  sem_in, sem_send, sem_recv, sem_out):
    peer = core_peer()
    loads = []
    for i in range(PARTS):
        loads += [copy(mlp_hbm.at[own_rows(i)], own_ref.at[chunk(i)], sem_in.at[3 * i]),
                  copy(far_hbm.at[chunk(i)], far_ref.at[chunk(i)], sem_in.at[3 * i + 1]),
                  copy(res_hbm.at[chunk(i)], res_ref.at[chunk(i)], sem_in.at[3 * i + 2])]
    for c in loads:
        c.start()
    greet(peer)
    pushes = [push(mlp_hbm.at[peer_rows(i)], core_ref.at[chunk(i)], sem_send.at[i], sem_recv.at[i], peer)
              for i in range(PARTS)]
    for c in pushes:
        c.start()
    saves = []
    for i in range(PARTS):
        for c in loads[3 * i:3 * i + 3]:
            c.wait()
        pushes[i].wait_recv()
        total = own_ref[chunk(i), :].astype(F32) + core_ref[chunk(i), :].astype(F32) + far_ref[chunk(i), :].astype(F32)
        out_ref[chunk(i), :] = (res_ref[chunk(i), :] + total).astype(BF)
        saves.append(copy(out_ref.at[chunk(i)], out_hbm.at[chunk(i)], sem_out.at[i]))
        saves[-1].start()
    for c in saves:
        c.wait()
    for c in pushes:
        c.wait_send()


def settle(mlp, far, residual):
    half = pltpu.VMEM((HALF, D), BF)
    return pl.pallas_call(
        settle_kernel,
        in_specs=[anywhere()] * 3,
        out_specs=anywhere(),
        out_shape=rows_of(HALF),
        scratch_shapes=[half, half, pltpu.VMEM((HALF, D), F32), half, half, dma(3 * PARTS), dma(PARTS), dma(PARTS), dma(PARTS)],
        compiler_params=pltpu.CompilerParams(collective_id=4, has_side_effects=True, vmem_limit_bytes=60 << 20),
        name="settle",
    )(mlp, far, residual)


def finish_kernel(gxn_hbm, gxc_hbm, noisy_hbm, clean_hbm, grad_hbm, gain_ref, ends_hbm, gsum_ref,
                  own_ref, far_ref, x_ref, wide_ref, out_ref,
                  sem_own, sem_x, sem_wide, sem_send, sem_recv, sem_out):
    sources = (gxn_hbm, gxc_hbm)
    count = 2 * PARTS
    own, rows, wide = [], [], []
    for n in range(count):
        k, i = n // PARTS, n % PARTS
        own.append(copy(sources[k].at[own_rows(i)], own_ref.at[chunk(n)], sem_own.at[n]))
        rows.append(copy((noisy_hbm, clean_hbm)[k].at[side_rows_of(i)], x_ref.at[chunk(n)], sem_x.at[n]))
        if k == 0:
            wide.append(copy(grad_hbm.at[chunk(i)], wide_ref.at[chunk(i)], sem_wide.at[i]))
    for c in own + rows + wide:
        c.start()
    peer = core_peer()
    greet(peer)
    pushes = []
    for n in range(count):
        k, i = n // PARTS, n % PARTS
        pushes.append(push(sources[k].at[peer_rows(i)], far_ref.at[chunk(n)], sem_send.at[n], sem_recv.at[n], peer))
        pushes[-1].start()
    gsum = 0.0
    saves = []
    for n in range(count):
        k, i = n // PARTS, n % PARTS
        own[n].wait()
        rows[n].wait()
        pushes[n].wait_recv()
        total = own_ref[chunk(n), :].astype(F32) + far_ref[chunk(n), :].astype(F32)
        grad, share = norm_back(x_ref[chunk(n), :].astype(F32), gain_ref[0:1, :], total)
        gsum = gsum + share
        if k == 0:
            wide[i].wait()
            grad = wide_ref[chunk(i), :] + grad
        out_ref[chunk(n), :] = grad.astype(BF)
        saves.append(copy(out_ref.at[chunk(n)], ends_hbm.at[chunk(n)], sem_out.at[n]))
        saves[-1].start()
    gsum_ref[...] = gsum
    for c in saves:
        c.wait()
    for c in pushes:
        c.wait_send()


def finish(gxn, gxc, noisy_rows, clean_rows, grad_resid, gains):
    buf = pltpu.VMEM((LEN, D), BF)
    return pl.pallas_call(
        finish_kernel,
        in_specs=[anywhere()] * 5 + [in_vmem()],
        out_specs=[anywhere(), in_vmem()],
        out_shape=[rows_of(LEN), jax.ShapeDtypeStruct((1, D), F32)],
        scratch_shapes=[buf, buf, buf, pltpu.VMEM((HALF, D), F32), buf,
                        dma(2 * PARTS), dma(2 * PARTS), dma(PARTS), dma(2 * PARTS), dma(2 * PARTS), dma(2 * PARTS)],
        compiler_params=pltpu.CompilerParams(collective_id=5, has_side_effects=True, vmem_limit_bytes=60 << 20),
        name="finish",
    )(gxn, gxc, noisy_rows, clean_rows, grad_resid, gains)


def place_kernel(count, info_ref, *refs):
    sources, outs, stage, sem_in, sem_out = refs[:4], refs[4:4 + count], refs[4 + count], refs[5 + count], refs[6 + count]
    loads = [copy(sources[j // count].at[pl.ds((j % count) * HALF, HALF)], stage.at[j], sem_in.at[j])
             for j in range(4 * count)]
    for c in loads:
        c.start()
    saves = []
    for j, c in enumerate(loads):
        c.wait()
        at = pl.ds(pl.multiple_of(info_ref[3 + j // count] * HALF, HALF), HALF)
        saves.append(copy(stage.at[j], outs[j % count].at[at], sem_out.at[j]))
        saves[-1].start()
    for c in saves:
        c.wait()


def place(info, *ends):
    count = ends[0].shape[0] // HALF
    return pl.pallas_call(
        functools.partial(place_kernel, count),
        in_specs=[pl.BlockSpec(memory_space=pltpu.SMEM)] + [anywhere()] * 4,
        out_specs=[anywhere()] * count,
        out_shape=[rows_of(2 * LEN)] * count,
        scratch_shapes=[pltpu.VMEM((4 * count, HALF, D), BF), dma(4 * count), dma(4 * count)],
        compiler_params=pltpu.CompilerParams(vmem_limit_bytes=60 << 20),
        name="place",
    )(info, *ends)


def lefts_kernel(gq_ref, gqb_ref, eq_ref, go_ref, gob_ref, eo_ref, fq_ref, fo_ref, lu_ref, ld_ref, g1_ref, g2_ref,
                 mq_ref, mo_ref, pack_ref):
    pack_ref[...] = jnp.zeros_like(pack_ref)
    mq = gq_ref[...] + gqb_ref[...].astype(F32) + eq_ref[0]
    mq_ref[...] = mq
    pack_ref[0:8, :] = exact(fq_ref[...], mq, 1, 0)
    mo = go_ref[...] + gob_ref[...].astype(F32) + eo_ref[0]
    mo_ref[...] = mo
    pack_ref[8:16, 0:192] = exact(fo_ref[...], mo, 1, 1)
    pack_ref[16:24, :] = lu_ref[...]
    pack_ref[24:32, :] = ld_ref[...]
    pack_ref[32:33, :] = g1_ref[...]
    pack_ref[33:34, :] = g2_ref[...]


def lefts(gq, gq_back, err_qkv, go, go_back, err_out, fac_qkv, fac_out, left_up, left_down, gain_one, gain_two):
    args = (gq, gq_back, err_qkv, go, go_back, err_out, fac_qkv, fac_out, left_up, left_down, gain_one, gain_two)
    return pl.pallas_call(
        lefts_kernel,
        grid=(1,),
        in_specs=[whole(v.shape) for v in args],
        out_specs=[whole((9 * HD, D)), whole((3 * HD, D)), whole((5 * RANK, D))],
        out_shape=[jax.ShapeDtypeStruct((9 * HD, D), F32), jax.ShapeDtypeStruct((3 * HD, D), F32),
                   jax.ShapeDtypeStruct((5 * RANK, D), F32)],
        compiler_params=pltpu.CompilerParams(vmem_limit_bytes=60 << 20),
        name="lefts",
    )(*args)


def rights_kernel(sum_ref, mq_ref, mo_ref, mu_ref, md_ref, hq_ref, ho_ref, hu_ref, hd_ref, pack_ref):
    mats = orthonormalize(sum_ref)
    hq_ref[...] = mats[0]
    ho_ref[...] = mats[1][:, :192]
    hu_ref[...] = mats[2]
    hd_ref[...] = mats[3]
    pack_ref[...] = jnp.zeros_like(pack_ref)
    pack_ref[0:8, 0:9 * HD] = exact(mats[0], mq_ref[...], 1, 1)
    pack_ref[8:16, :] = exact(mats[1][:, :192], mo_ref[...], 1, 0)
    pack_ref[16:24, :] = exact(mats[2], mu_ref[...], 1, 0)
    pack_ref[24:32, :] = exact(mats[3], md_ref[...], 1, 0)


def rights(left_sum, mats):
    args = (left_sum, *mats)
    shapes = [(RANK, D), (RANK, 3 * HD), (RANK, D), (RANK, D), (4 * RANK, D)]
    return pl.pallas_call(
        rights_kernel,
        grid=(1,),
        in_specs=[whole(v.shape) for v in args],
        out_specs=[whole(s) for s in shapes],
        out_shape=[jax.ShapeDtypeStruct(s, F32) for s in shapes],
        compiler_params=pltpu.CompilerParams(vmem_limit_bytes=60 << 20),
        name="rights",
    )(*args)


def orthonormalize(sum_ref):
    row = lax.broadcasted_iota(jnp.int32, (RANK, D), 0)
    mats = [sum_ref[RANK * t:RANK * (t + 1), :] for t in range(4)]
    for k in range(RANK):
        for t in range(4):
            a = mats[t]
            v = a[k:k + 1, :]
            e = v / (jnp.sqrt(jnp.sum(v * v, axis=1, keepdims=True)) + 1e-08)
            c = jnp.sum(a * e, axis=1, keepdims=True)
            mats[t] = jnp.where(row == k, e, jnp.where(row > k, a - c * e, a))
    return mats


def reduce_kernel(count, gq_hbm, gqb_hbm, eq_hbm, go_hbm, gob_hbm, eo_hbm, mu_hbm, md_hbm,
                  fq_ref, fo_ref, lu_ref, ld_ref, g1_ref, g2_ref,
                  mq_hbm, mo_hbm, hat_ref, right_ref, gsum_ref,
                  gq_ref, gqb_ref, mq_ref, go_ref, gob_ref, mo_ref, mu_ref, md_ref, x_ref, sum_ref, in_a, y_ref, in_b, slot_ref,
                  sem_ref, send_ref, recv_ref):
    me = lax.axis_index("dp")
    m = lax.axis_index("mp")
    sems, sends, recvs = Sems(sem_ref), Sems(send_ref), Sems(recv_ref)
    owners = D // 128

    def load(src, dst):
        c = copy(src, dst, sems.take())
        c.start()
        return c

    loads = [load(gq_hbm, gq_ref), load(eq_hbm.at[0], mq_ref), load(gqb_hbm, gqb_ref),
             load(go_hbm, go_ref), load(eo_hbm.at[0], mo_ref), load(gob_hbm, gob_ref)]
    late = [load(mu_hbm, mu_ref), load(md_hbm, md_ref)]
    barrier = pltpu.get_barrier_semaphore()
    for k in range(1, count):
        pl.semaphore_signal(barrier, inc=1, device_id=(lax.rem(me + k, count), m), device_id_type=MESH_ID)
    for k in range(1, 4):
        pl.semaphore_signal(barrier, inc=1, device_id=(me, lax.rem(m + k, 4)), device_id_type=MESH_ID)
    pl.semaphore_wait(barrier, count + 2)

    def spread_sum(src_ref, box_ref, out_ref):
        send_a, recv_a = [sends.take() for _ in range(owners)], [recvs.take() for _ in range(count)]
        send_b, recv_b = [sends.take() for _ in range(count)], [recvs.take() for _ in range(owners)]

        def lanes(j):
            return slice(128 * j, 128 * (j + 1))

        for j in range(owners):
            for s in range(count):
                if s != j:
                    @pl.when(me == s)
                    def _():
                        push(src_ref.at[:, lanes(j)], box_ref.at[s], send_a[j], recv_a[s], (j, m)).start()
        for j in range(owners):
            @pl.when(me == j)
            def _():
                box_ref[j] = src_ref[:, lanes(j)]
                for s in range(count):
                    if s != j:
                        push(src_ref.at[:, lanes(j)], box_ref.at[s], send_a[j], recv_a[s], (s, m)).wait_recv()
                total = box_ref[0]
                for s in range(1, count):
                    total = total + box_ref[s]
                out_ref[:, lanes(j)] = total
                for p in range(count):
                    if p != j:
                        push(out_ref.at[:, lanes(j)], out_ref.at[:, lanes(j)], send_b[p], recv_b[j], (p, m)).start()
        for j in range(owners):
            @pl.when(me != j)
            def _():
                push(out_ref.at[:, lanes(j)], out_ref.at[:, lanes(j)], send_b[0], recv_b[j], (j, m)).wait_recv()

        def settle_sends():
            for j in range(owners):
                @pl.when(me != j)
                def _():
                    push(src_ref.at[:, lanes(j)], box_ref.at[0], send_a[j], recv_a[0], (j, m)).wait_send()

                @pl.when(me == j)
                def _():
                    for p in range(count):
                        if p != j:
                            push(out_ref.at[:, lanes(j)], out_ref.at[:, lanes(j)], send_b[p], recv_b[j], (p, m)).wait_send()

        return settle_sends

    x_ref[...] = jnp.zeros_like(x_ref)
    x_ref[16:24, :] = lu_ref[...]
    x_ref[24:32, :] = ld_ref[...]
    x_ref[32:33, :] = g1_ref[...]
    x_ref[33:34, :] = g2_ref[...]
    for c in loads[:3]:
        c.wait()
    mq = gq_ref[...] + gqb_ref[...].astype(F32) + mq_ref[...]
    mq_ref[...] = mq
    saves = [load(mq_ref, mq_hbm)]
    x_ref[0:8, :] = exact(fq_ref[...], mq, 1, 0)
    for c in loads[3:]:
        c.wait()
    mo = go_ref[...] + gob_ref[...].astype(F32) + mo_ref[...]
    mo_ref[...] = mo
    saves.append(load(mo_ref, mo_hbm))
    x_ref[8:16, 0:192] = exact(fo_ref[...], mo, 1, 1)
    finish_a = spread_sum(x_ref, in_a, sum_ref)
    shares = []
    for k in range(1, 4):
        shares.append(push(sum_ref.at[4 * RANK:5 * RANK], slot_ref.at[k], sends.take(), recvs.take(), (me, lax.rem(m + k, 4))))
        shares[-1].start()
    hats = orthonormalize(sum_ref)
    for t in range(4):
        hat_ref[RANK * t:RANK * (t + 1), :] = hats[t]
    for c in late:
        c.wait()
    y_ref[...] = jnp.zeros_like(y_ref)
    y_ref[0:8, 0:9 * HD] = exact(hats[0], mq_ref[...], 1, 1)
    y_ref[8:16, :] = exact(hats[1][:, :192], mo_ref[...], 1, 0)
    y_ref[16:24, :] = exact(hats[2], mu_ref[...], 1, 0)
    y_ref[24:32, :] = exact(hats[3], md_ref[...], 1, 0)
    finish_b = spread_sum(y_ref, in_b, right_ref)
    for c in shares:
        c.wait()
    slot_ref[0] = sum_ref[4 * RANK:5 * RANK, :]
    parts = [slot_ref[lax.rem(m - k + 4, 4)] for k in range(4)]
    gsum_ref[...] = (parts[0] + parts[1]) + (parts[2] + parts[3])
    finish_a()
    finish_b()
    for c in saves:
        c.wait()


def reduce_factors(gq, gq_back, err_qkv, go, go_back, err_out, mat_up, mat_down, fac_qkv, fac_out, left_up, left_down,
                   gain_one, gain_two):
    count = lax.axis_size("dp")
    args = (gq, gq_back, err_qkv, go, go_back, err_out, mat_up, mat_down,
            fac_qkv, fac_out, left_up, left_down, gain_one, gain_two)
    if count != 8:
        mq, mo, pack = lefts(*args[:6], *args[8:])
        total = lax.psum(pack, "dp")
        *hats, pack = rights(total, (mq, mo, mat_up, mat_down))
        hats[1] = jnp.pad(hats[1], ((0, 0), (0, D - 3 * HD)))
        return mq, mo, jnp.concatenate(hats, axis=0), lax.psum(pack, "dp"), lax.psum(total[4 * RANK:], "mp")

    def wide(n):
        return pltpu.VMEM((n, D), F32)

    owners = D // 128
    links = 2 * (owners + count) + 3
    return pl.pallas_call(
        functools.partial(reduce_kernel, count),
        in_specs=[anywhere()] * 8 + [in_vmem()] * 6,
        out_specs=[anywhere()] * 2 + [in_vmem()] * 3,
        out_shape=[jax.ShapeDtypeStruct(s, F32) for s in ((9 * HD, D), (3 * HD, D), (4 * RANK, D), (4 * RANK, D), (RANK, D))],
        scratch_shapes=[wide(9 * HD), pltpu.VMEM((9 * HD, D), BF), wide(9 * HD), wide(3 * HD), pltpu.VMEM((3 * HD, D), BF),
                        wide(3 * HD), wide(D), wide(D), wide(5 * RANK), wide(5 * RANK),
                        pltpu.VMEM((count, 5 * RANK, 128), F32), wide(4 * RANK), pltpu.VMEM((count, 4 * RANK, 128), F32),
                        pltpu.VMEM((4, RANK, D), F32), dma(10), dma(links), dma(links)],
        compiler_params=pltpu.CompilerParams(collective_id=1, has_side_effects=True, vmem_limit_bytes=60 << 20),
        name="reduce_factors",
    )(*args)


def update_kernel(replicas, rates, info_ref, *refs):
    sums, hats, mats, states = refs[0], refs[1], refs[2:6], refs[6:18]
    total_ref, gain_ref, gm_ref = refs[18:21]
    errs, news, right_out, hat_out, gains_out = refs[21:25], refs[25:37], refs[37:41], refs[41:45], refs[45:48]
    decay = min(0.9999, (1.0 + EMA_STEPS) / (10.0 + EMA_STEPS))
    share = D // replicas
    shift = lax.rem(D - info_ref[1] * share, D)

    def part(value):
        return pltpu.roll(value, shift, 1)[:, :share]

    for t in range(4):
        hat = hats[RANK * t:RANK * (t + 1), :hat_out[t].shape[1]]
        hat_out[t][...] = hat
        right = sums[RANK * t:RANK * (t + 1), :] * (1.0 / replicas)
        right_out[t][...] = right[:, :right_out[t].shape[1]]
        first, second = ((right[:, :9 * HD], hat), (hat, right), (hat, right), (hat, right))[t]
        errs[t][0] = mats[t][...] - exact(first, second, 0, 0)
        first, second = ((part(hat), right[:, :9 * HD]), (hat, part(right)), (part(hat), right), (part(right), hat))[t]
        moment = 0.5 * states[3 * t + 1][...] + exact(first, second, 0, 0)
        master = states[3 * t][...] - rates[t] * moment
        news[3 * t][...] = master
        news[3 * t + 1][...] = moment
        news[3 * t + 2][...] = decay * states[3 * t + 2][...] + (1.0 - decay) * master
    grad = total_ref[0:2, :] * (1.0 / replicas)
    moment = 0.5 * gm_ref[...] + grad
    gains_out[0][...] = grad
    gains_out[1][...] = gain_ref[...] - rates[4] * moment
    gains_out[2][...] = moment


def update(info, replicas, rates, right_sum, hats, mats, states, gain_sum, gains, gain_moment):
    args = (right_sum, hats, *mats, *states, gain_sum, gains, gain_moment)
    shapes = [(1, *m.shape) for m in mats] + [s.shape for s in states]
    shapes += [(RANK, 9 * HD), (RANK, D), (RANK, D), (RANK, D)]
    shapes += [(RANK, D), (RANK, 3 * HD), (RANK, D), (RANK, D)] + [(2, D)] * 3
    return pl.pallas_call(
        functools.partial(update_kernel, replicas, rates),
        grid_spec=pltpu.PrefetchScalarGridSpec(
            num_scalar_prefetch=1,
            grid=(1,),
            in_specs=[whole(v.shape) for v in args],
            out_specs=[whole(s) for s in shapes],
        ),
        out_shape=[jax.ShapeDtypeStruct(s, F32) for s in shapes],
        compiler_params=pltpu.CompilerParams(vmem_limit_bytes=60 << 20),
        name="update",
    )(info, *args)


def local(
    noisy_rows, clean_rows, block_size, cotangent, norm_gains,
    weight_qkv, weight_out, weight_up, weight_down,
    master_qkv, master_out, master_up, master_down,
    moment_qkv, moment_out, moment_up, moment_down,
    average_qkv, average_out, average_up, average_down,
    error_qkv, error_out, error_up, error_down,
    factor_qkv, factor_out, factor_up, factor_down,
    gain_moment,
):
    row_count = noisy_rows.shape[0]
    replicas = lax.axis_size("dp")
    side = lax.axis_index("mp") // 2

    def across(value):
        return lax.ppermute(value, "mp", [(0, 2), (2, 0), (1, 3), (3, 1)])

    def beside(value):
        return lax.ppermute(value, "mp", [(0, 1), (1, 0), (2, 3), (3, 2)])

    def hold(*values):
        return lax.optimization_barrier(values)

    cos, sin = rotary_tables()
    m = lax.axis_index("mp")
    flip = m + 1 - 2 * (m % 2)
    info = jnp.stack([side, lax.axis_index("dp"), m % 2, m, flip, (m + 2) % 4, (flip + 2) % 4]).astype(jnp.int32)
    w_near = weight_qkv.T
    qn, qc, att, lse, xn, xc, w_far, o_far = attend(
        block_size, noisy_rows, clean_rows, w_near, weight_out, norm_gains, cos, sin)
    residual, grad_resid, grad_low, mlp, mlp_fold, matrix_up, matrix_down, left_up, left_down, gain_two = middle(
        att, weight_out, o_far, noisy_rows, cotangent, weight_up, weight_down,
        error_up, error_down, factor_up.T, factor_down.T, norm_gains)
    mlp_far = across(mlp_fold)
    dn_far, dc_far, gq_far, go_far = back_far(
        info, block_size, qn, qc, att, lse, grad_low, o_far, cos, sin, xn, xc)
    mlp_far, dn_far, gq_far, go_far = hold(mlp_far, dn_far, gq_far, go_far)
    gq_back, go_back = across(gq_far), across(go_far)
    out_half = settle(mlp, mlp_far, residual)
    out_half, dn_far = hold(out_half, dn_far)
    out_far, out_side = across(out_half), beside(out_half)
    grad_xn, grad_xc, gq_near, go_near = back_near(
        info, block_size, qn, qc, att, lse, grad_low, weight_out, cos, sin, xn, xc,
        w_near, w_far, dn_far, dc_far)
    ends, gain_one = finish(grad_xn, grad_xc, noisy_rows, clean_rows, grad_resid, norm_gains)
    ends, gq_back, go_back = hold(ends, gq_back, go_back)
    ends_far = across(ends)
    ends_side = beside(ends)
    matrix_qkv, matrix_out, hats, right_sum, gain_sum = reduce_factors(
        gq_near, gq_back, jnp.swapaxes(error_qkv, 1, 2), go_near, go_back, error_out, matrix_up, matrix_down,
        factor_qkv.T, factor_out.T, left_up, left_down, gain_one, gain_two)
    mats = (matrix_qkv, matrix_out, matrix_up, matrix_down)
    rates = [3.0 / math.sqrt(f * row_count) for f in (D, HEADS * HD // 64, D, FF)] + [0.5 / math.sqrt(row_count)]
    states = (
        master_qkv, moment_qkv, average_qkv, master_out, moment_out, average_out,
        master_up, moment_up, average_up, master_down.T, moment_down.T, average_down.T,
    )
    done = update(info, replicas, rates, right_sum, hats, mats, states, gain_sum, norm_gains, gain_moment)
    errs, news, right_new, left_new, gains_new = done[:4], done[4:16], done[16:20], done[20:24], done[24:27]
    out_far, out_half = hold(out_far, out_half)
    out_diag = beside(out_far)
    block_out, = place(info, out_half, out_side, out_far, out_diag)
    ends_far, _, block_out = hold(ends_far, errs[2], block_out)
    ends_diag = beside(ends_far)
    grad_noisy, grad_clean = place(info, ends, ends_side, ends_far, ends_diag)
    fresh = [news[3 * t + k] if t < 3 else news[3 * t + k].T for k in range(3) for t in range(4)]
    return (
        block_out, grad_noisy, grad_clean, *gains_new, *fresh,
        jnp.swapaxes(errs[0], 1, 2), *errs[1:], *[v.T for v in left_new], *[v.T for v in right_new],
    )


def solution(mesh):
    in_specs = (
        P("dp", None), P("dp", None), P("dp"), P("dp", None), P(),
        P(None, "mp"), P("mp", None), P(None, "mp"), P("mp", None),
        *([P("dp", "mp"), P("mp", "dp")] * 6),
        *([P("dp", None, "mp"), P("dp", "mp", None)] * 2),
        *([P("mp", None), P(None, "mp")] * 2),
        P(),
    )
    out_specs = (
        P("dp", None), P("dp", None), P("dp", None), P(), P(), P(),
        *([P("dp", "mp"), P("mp", "dp")] * 6),
        *([P("dp", None, "mp"), P("dp", "mp", None)] * 2),
        *([P(None, "mp"), P("mp", None)] * 2),
        *([P("mp", None), P(None, "mp")] * 2),
    )
    return jax.shard_map(local, mesh=mesh, in_specs=in_specs, out_specs=out_specs, check_vma=False)
```

```python
import functools
import math

import jax
import jax.numpy as jnp
import numpy as np
from jax import lax
from jax.experimental import pallas as pl
from jax.experimental.pallas import tpu as pltpu
from jax.sharding import PartitionSpec as P

D = 768
HEADS = 12
HD = 64
FF = 3072
LEN = 1024
RANK = 8
EMA_STEPS = 4
TILE = 256
SLOT = 256

BF = jnp.bfloat16
F32 = jnp.float32
highest = lax.Precision.HIGHEST
norm_eps = 1e-05
gelu_coef = 0.7978845608028654
masked_score = -1e30
MESH_ID = pl.DeviceIdType.MESH


def nt(a, b):
    return lax.dot_general(a, b, (((1,), (1,)), ((), ())), preferred_element_type=F32)


def nn(a, b):
    return lax.dot_general(a, b, (((1,), (0,)), ((), ())), preferred_element_type=F32)


def tn(a, b):
    return lax.dot_general(a, b, (((0,), (0,)), ((), ())), preferred_element_type=F32)


def rotary_tables():
    half = HD // 2
    step = np.float32(-2.0 * math.log(10000.0) / HD)
    inverse = np.exp(np.arange(half, dtype=np.float32) * step).astype(np.float32)
    angle = (np.arange(LEN, dtype=np.float32)[:, None] * inverse[None, :]).astype(np.float32)
    c = np.cos(angle).astype(np.float32)
    s = np.sin(angle).astype(np.float32)
    return np.concatenate([c, c, c, c], 1), np.concatenate([-s, s, -s, s], 1)


def spin(v, cos, sin):
    lane = lax.broadcasted_iota(jnp.int32, v.shape, 1)
    low = lax.rem(lane, HD) < HD // 2
    swapped = jnp.where(low, pltpu.roll(v, 128 - HD // 2, 1), pltpu.roll(v, HD // 2, 1))
    return v * cos + swapped * sin


def block_ids(size, shape, dim):
    shift = 2 + (size >= 8).astype(jnp.int32) + (size >= 16).astype(jnp.int32)
    place = lax.broadcasted_iota(jnp.int32, shape, dim)
    return lax.shift_right_logical(place, jnp.full(shape, shift, jnp.int32))


def fill_bias(size, noisy_bias, clean_bias):
    keys = block_ids(size, (TILE, TILE), 0)
    rows = block_ids(size, (TILE, TILE), 1)
    noisy_bias[...] = jnp.where(rows == keys, 0.0, masked_score)
    clean_bias[...] = jnp.where(keys < rows, 0.0, masked_score)


def norm_parts(values):
    centered = values - jnp.mean(values, axis=1, keepdims=True)
    scale = lax.rsqrt(jnp.mean(centered * centered, axis=1, keepdims=True) + norm_eps)
    return centered * scale, scale


def norm_back(values, gain, grad):
    unit, scale = norm_parts(values)
    scaled = grad * gain
    inner = jnp.mean(scaled * unit, axis=1, keepdims=True)
    grad_in = scale * (scaled - jnp.mean(scaled, axis=1, keepdims=True) - unit * inner)
    return grad_in, jnp.sum(grad * unit, axis=0, keepdims=True)


def gelu_and_slope(u):
    square = u * u
    half = 0.5 + 0.5 * jnp.tanh(u * (gelu_coef + (gelu_coef * 0.044715) * square))
    slope = half + (u * (2.0 * half * (1.0 - half))) * (gelu_coef + (3.0 * 0.044715 * gelu_coef) * square)
    return u * half, slope


def whole(shape):
    return pl.BlockSpec(shape, lambda *index: (0,) * len(shape), pipeline_mode=pl.Buffered(1))


def side_rows(h, info, size):
    return (info[0], 0)


def lane2(h, *_):
    return (0, h)


def row3(h, *_):
    return (h, 0, 0)


def attend_head(head, xn_ref, xc_ref, w_ref, cos_ref, sin_ref, qn_ref, qc_ref, att_ref, lse_ref,
                bn_ref, bc_ref, kn_ref, kc_ref, vnt_ref, vct_ref):
    w = w_ref[pl.ds(pl.multiple_of(head * 3 * HD, 3 * HD), 3 * HD), :]
    for src, dst, keys, vals in ((xn_ref, qn_ref, kn_ref, vnt_ref), (xc_ref, qc_ref, kc_ref, vct_ref)):
        a = nt(src[...], w)
        r = spin(a[:, :128], cos_ref[...], sin_ref[...]).astype(BF)
        v = a[:, 128:].astype(BF)
        dst[:, :128] = r
        dst[:, 128:192] = v
        keys[...] = r[:, 64:128]
        vals[...] = jnp.transpose(v)
    here = pl.ds(pl.multiple_of(head * HD, HD), HD)
    for i in range(LEN // TILE):
        lo, hi = i * TILE, (i + 1) * TILE
        q = qn_ref[lo:hi, 0:64] * 0.125
        parts = [nt(kn_ref[lo:hi, :], q) + bn_ref[...], nt(kc_ref[lo:hi, :], q) + bc_ref[...]]
        if i:
            parts.append(nt(kc_ref[0:lo, :], q))
        peak = functools.reduce(jnp.maximum, [jnp.max(s, axis=0, keepdims=True) for s in parts])
        exps = [jnp.exp(s - peak) for s in parts]
        total = functools.reduce(jnp.add, [jnp.sum(e, axis=0, keepdims=True) for e in exps])
        inv = 1.0 / total
        low = [(e * inv).astype(BF) for e in exps]
        o = nn(vnt_ref[:, lo:hi], low[0]) + nn(vct_ref[:, lo:hi], low[1])
        if i:
            o = o + nn(vct_ref[:, 0:lo], low[2])
        att_ref[here, lo:hi] = o.astype(BF)
        lse_ref[0, :, lo:hi] = jnp.broadcast_to(peak + jnp.log(total), (8, TILE))


def attend_kernel(size_ref, noisy_hbm, clean_hbm, w_hbm, wo_hbm, gain_ref, cos_ref, sin_ref,
                  qn_ref, qc_ref, att_ref, lse_ref, xn_hbm, xc_hbm, w_far_hbm, o_far_hbm,
                  raw_ref, x_ref, w_ref, sem_in, sem_out, sem_send, sem_recv, *work):
    head = pl.program_id(0)
    side = lax.axis_index("mp") // 2
    peer = far_peer()
    sides = ((noisy_hbm, xn_hbm), (clean_hbm, xc_hbm))
    width = 3 * HD

    def load(s, i):
        at = pl.ds(pl.multiple_of(side * LEN + i * TILE, TILE), TILE)
        return pltpu.make_async_copy(sides[s][0].at[at], raw_ref.at[s, chunk(i)], sem_in.at[CHUNKS * s + i])

    def save(s):
        return pltpu.make_async_copy(x_ref.at[s], sides[s][1], sem_out.at[s])

    def give(j):
        at = slice(width * j, width * (j + 1))
        return push(w_hbm.at[at], w_ref.at[slice(width * (3 + j), width * (4 + j))], sem_send.at[j], sem_recv.at[j], peer)

    near_w = pltpu.make_async_copy(w_hbm, w_ref.at[0:3 * width], sem_in.at[2 * CHUNKS])
    give_out = push(wo_hbm, o_far_hbm, sem_send.at[3], sem_recv.at[3], peer)
    keep_w = pltpu.make_async_copy(w_ref.at[3 * width:], w_far_hbm, sem_out.at[2])

    @pl.when(head == 0)
    def _():
        for s in range(2):
            for i in range(CHUNKS):
                load(s, i).start()
        near_w.start()
        greet(peer)
        for j in range(3):
            give(j).start()
        give_out.start()
        fill_bias(size_ref[side], work[0], work[1])
        for s in range(2):
            for i in range(CHUNKS):
                load(s, i).wait()
                x = norm_parts(raw_ref[s, chunk(i), :].astype(F32))[0] * gain_ref[0:1, :]
                x_ref[s, chunk(i), :] = x.astype(BF)
            save(s).start()
        near_w.wait()

    for j in range(3):
        @pl.when(head == 3 + j)
        def _():
            give(j).wait_recv()

    @pl.when(head == 5)
    def _():
        keep_w.start()

    attend_head(head, x_ref.at[0], x_ref.at[1], w_ref, cos_ref, sin_ref, qn_ref, qc_ref, att_ref, lse_ref, *work)

    @pl.when(head == 5)
    def _():
        save(0).wait()
        save(1).wait()
        keep_w.wait()
        for j in range(3):
            give(j).wait_send()
        give_out.wait()


CHUNKS = LEN // TILE
HALF = LEN // 2


def chunk(i):
    return slice(i * TILE, (i + 1) * TILE)


def anywhere():
    return pl.BlockSpec(memory_space=pl.ANY)


def in_vmem():
    return pl.BlockSpec(memory_space=pltpu.VMEM)


def dma(n):
    return pltpu.SemaphoreType.DMA((n,))


def rows_of(n):
    return jax.ShapeDtypeStruct((n, D), BF)


attend_work = [
    pltpu.VMEM((TILE, TILE), F32),
    pltpu.VMEM((TILE, TILE), F32),
    pltpu.VMEM((LEN, HD), BF),
    pltpu.VMEM((LEN, HD), BF),
    pltpu.VMEM((HD, LEN), BF),
    pltpu.VMEM((HD, LEN), BF),
]
rows_shape = jax.ShapeDtypeStruct((LEN, D), BF)


def attend(size, noisy, clean, w, wo, gains, cos, sin):
    return pl.pallas_call(
        attend_kernel,
        grid=(6,),
        in_specs=[pl.BlockSpec(memory_space=pltpu.SMEM)] + [anywhere()] * 4
        + [whole((2, D)), whole((LEN, 128)), whole((LEN, 128))],
        out_specs=[pl.BlockSpec((LEN, SLOT), lane2), pl.BlockSpec((LEN, SLOT), lane2), whole((6 * HD, LEN)),
                   pl.BlockSpec((1, 8, LEN), row3)] + [anywhere()] * 4,
        out_shape=[jax.ShapeDtypeStruct((LEN, SLOT * 6), BF), jax.ShapeDtypeStruct((LEN, SLOT * 6), BF),
                   jax.ShapeDtypeStruct((6 * HD, LEN), BF), jax.ShapeDtypeStruct((6, 8, LEN), F32),
                   rows_shape, rows_shape, rows_of(9 * HD), rows_of(3 * HD)],
        scratch_shapes=[pltpu.VMEM((2, LEN, D), BF), pltpu.VMEM((2, LEN, D), BF), pltpu.VMEM((18 * HD, D), BF),
                        dma(2 * CHUNKS + 1), dma(3), dma(4), dma(4)] + attend_work,
        compiler_params=pltpu.CompilerParams(collective_id=6, has_side_effects=True, vmem_limit_bytes=60 << 20),
        name="attend",
    )(size, noisy, clean, w, wo, gains, cos, sin)


WIDE = 5 * 128


def back_head(head, qn_ref, qc_ref, lse_ref, cos_ref, sin_ref, av_ref, c_ref,
              bn_ref, bc_ref, kn_ref, kc_ref, knt_ref, kct_ref, dot_ref, do_ref, dq_ref, dkn_ref, dkc_ref, dvc_ref, dvn_ref):
    do_ref[...] = jnp.transpose(dot_ref[pl.ds(pl.multiple_of(head * HD, HD), HD), :])
    kn_ref[...] = qn_ref[:, 64:128]
    kc_ref[...] = qc_ref[:, 64:128]
    knt_ref[...] = jnp.transpose(qn_ref[:, 0:128])[64:128]
    kct_ref[...] = jnp.transpose(qc_ref[:, 0:128])[64:128]
    for i in reversed(range(LEN // TILE)):
        lo, hi = i * TILE, (i + 1) * TILE
        last = i == LEN // TILE - 1
        q = qn_ref[lo:hi, 0:64] * 0.125
        do = do_ref[lo:hi, :]
        lse = lse_ref[0, 0:1, lo:hi]
        spans = [(0, lo, hi), (1, lo, hi)] + ([(1, 0, lo)] if i else [])
        probs, grads, inner = [], [], 0.0
        for n, (side, a, b) in enumerate(spans):
            kr = kc_ref if side else kn_ref
            vr = qc_ref if side else qn_ref
            s = nt(kr[a:b, :], q)
            if n == 0:
                s = s + bn_ref[...]
            if n == 1:
                s = s + bc_ref[...]
            p = jnp.exp(s - lse)
            dp = nt(vr[a:b, 128:192], do)
            inner = inner + jnp.sum(p * dp, axis=0, keepdims=True)
            probs.append(p)
            grads.append(dp)
        dqt = 0.0
        for n, (side, a, b) in enumerate(spans):
            ds = (probs[n] * (grads[n] - inner)).astype(BF)
            dv = nn(probs[n].astype(BF), do)
            dk = nn(ds, q)
            ktr = kct_ref if side else knt_ref
            dqt = dqt + nn(ktr[:, a:b], ds)
            if side and last:
                dkc_ref[a:b, :] = dk
                dvc_ref[a:b, :] = dv
            elif side:
                dkc_ref[a:b, :] += dk
                dvc_ref[a:b, :] += dv
            else:
                dkn_ref[a:b, :] = dk
                dvn_ref[a:b, :] = dv.astype(BF)
        dq_ref[lo:hi, :] = jnp.transpose(dqt) * 0.125
    sin = -sin_ref[...]
    cos = cos_ref[...]
    pair = pl.ds(pl.multiple_of(head * 128, 128), 128)
    av_ref[:, pair] = spin(jnp.concatenate([dq_ref[...], dkn_ref[...]], axis=1), cos, sin).astype(BF)
    both = jnp.concatenate([dkc_ref[...], dvc_ref[...]], axis=1)
    lane = lax.broadcasted_iota(jnp.int32, both.shape, 1)
    c_ref[:, pair] = jnp.where(lane < HD, spin(both, cos, sin), both).astype(BF)
    for j in range(3):
        @pl.when(head == j)
        def _():
            av_ref[:, 384 + HD * j:384 + HD * (j + 1)] = dvn_ref[...]


def group_grad(xn_ref, xc_ref, av, c, gq_ref):
    g = tn(av, xn_ref[...])
    e = tn(c, xc_ref[...])
    for j in range(3):
        row = 3 * HD * j
        gq_ref[row:row + HD, :] = g[128 * j:128 * j + HD].astype(gq_ref.dtype)
        gq_ref[row + HD:row + 2 * HD, :] = (g[128 * j + HD:128 * (j + 1)] + e[128 * j:128 * j + HD]).astype(gq_ref.dtype)
        gq_ref[row + 2 * HD:row + 3 * HD, :] = (
            g[384 + HD * j:384 + HD * (j + 1)] + e[128 * j + HD:128 * (j + 1)]).astype(gq_ref.dtype)


def back_start(size_ref, att_ref, g_ref, wo_ref, go_ref, av_ref, work):
    fill_bias(size_ref[lax.axis_index("mp") // 2], work[0], work[1])
    work[6][...] = nt(wo_ref[...], g_ref[...]).astype(BF)
    go_ref[...] = nn(att_ref[...], g_ref[...]).astype(go_ref.dtype)
    av_ref[:, 576:WIDE] = jnp.zeros((LEN, WIDE - 576), BF)


def back_far_kernel(size_ref, qn_ref, qc_ref, att_ref, lse_ref, g_ref, wo_ref, cos_ref, sin_ref,
                    xn_hbm, xc_hbm, av_ref, c_ref, both_ref, xn_ref, xc_ref, sems, *work):
    head = pl.program_id(0)
    late = [pltpu.make_async_copy(s, d, sems.at[k]) for k, (s, d) in enumerate(((xn_hbm, xn_ref), (xc_hbm, xc_ref)))]

    @pl.when(head == 0)
    def _():
        for c in late:
            c.start()
        back_start(size_ref, att_ref, g_ref, wo_ref, both_ref.at[9 * HD:], av_ref, work)

    back_head(head, qn_ref, qc_ref, lse_ref, cos_ref, sin_ref, av_ref, c_ref, *work)

    @pl.when(head == 2)
    def _():
        for c in late:
            c.wait()
        group_grad(xn_ref, xc_ref, av_ref[...], c_ref[...], both_ref)


def back_near_kernel(size_ref, qn_ref, qc_ref, att_ref, lse_ref, g_ref, wo_ref, cos_ref, sin_ref,
                     xn_hbm, xc_hbm, w_hbm, w_far_hbm, avf_hbm, cf_hbm, gxn_hbm, gxc_hbm, gq_ref, go_ref,
                     xn_ref, xc_ref, wav_ref, wc_ref, av_ref, c_ref, out_ref, sems, sem_w, sem_out, *work):
    head = pl.program_id(0)
    late = [pltpu.make_async_copy(s, d, sems.at[k]) for k, (s, d) in enumerate((
        (xn_hbm, xn_ref), (xc_hbm, xc_ref), (avf_hbm, av_ref.at[:, WIDE:]), (cf_hbm, c_ref.at[:, 384:])))]
    for n, src in enumerate((w_hbm, w_far_hbm)):
        for j in range(3):
            row, base, k = 192 * j, WIDE * n, 3 * (3 * n + j)
            late.append(pltpu.make_async_copy(
                src.at[row:row + 128], wav_ref.at[base + 128 * j:base + 128 * (j + 1)], sem_w.at[k]))
            late.append(pltpu.make_async_copy(
                src.at[row + 128:row + 192], wav_ref.at[base + 384 + 64 * j:base + 448 + 64 * j], sem_w.at[k + 1]))
            late.append(pltpu.make_async_copy(
                src.at[row + 64:row + 192], wc_ref.at[384 * n + 128 * j:384 * n + 128 * (j + 1)], sem_w.at[k + 2]))

    @pl.when(head == 0)
    def _():
        for c in late:
            c.start()
        for n in range(2):
            wav_ref[WIDE * n + 576:WIDE * (n + 1), :] = jnp.zeros((WIDE - 576, D), BF)
        back_start(size_ref, att_ref, g_ref, wo_ref, go_ref, av_ref, work)

    back_head(head, qn_ref, qc_ref, lse_ref, cos_ref, sin_ref, av_ref, c_ref, *work)

    @pl.when(head == 2)
    def _():
        for c in late:
            c.wait()
        copies = []
        for s, (rows, w, out) in enumerate(((av_ref, wav_ref, gxn_hbm), (c_ref, wc_ref, gxc_hbm))):
            for i in range(CHUNKS):
                out_ref[s, chunk(i), :] = nn(rows[chunk(i), :], w[...]).astype(BF)
                copies.append(pltpu.make_async_copy(
                    out_ref.at[s, chunk(i)], out.at[chunk(i)], sem_out.at[CHUNKS * s + i]))
                copies[-1].start()
        group_grad(xn_ref, xc_ref, av_ref[:, :WIDE], c_ref[:, :384], gq_ref)
        for c in copies:
            c.wait()


back_work = attend_work[:4] + [
    pltpu.VMEM((HD, LEN), BF),
    pltpu.VMEM((HD, LEN), BF),
    pltpu.VMEM((3 * HD, LEN), BF),
    pltpu.VMEM((LEN, HD), BF),
    pltpu.VMEM((LEN, HD), F32),
    pltpu.VMEM((LEN, HD), F32),
    pltpu.VMEM((LEN, HD), F32),
    pltpu.VMEM((LEN, HD), F32),
    pltpu.VMEM((LEN, HD), BF),
]
def head_inputs(first):
    return [pl.BlockSpec((LEN, SLOT), lambda h, *_: (0, h + first)), pl.BlockSpec((LEN, SLOT), lambda h, *_: (0, h + first)),
            pl.BlockSpec((3 * HD, LEN), lambda h, *_: (first // 3, 0), pipeline_mode=pl.Buffered(1)),
            pl.BlockSpec((1, 8, LEN), lambda h, *_: (h + first, 0, 0))]


def back_far(size, qn, qc, att, lse, g, wo, cos, sin, xn, xc):
    return pl.pallas_call(
        back_far_kernel,
        grid=(3,),
        in_specs=[pl.BlockSpec(memory_space=pltpu.SMEM)] + head_inputs(3)
        + [whole((LEN, D)), whole((3 * HD, D)), whole((LEN, 128)), whole((LEN, 128)), anywhere(), anywhere()],
        out_specs=[whole((LEN, WIDE)), whole((LEN, 384)), whole((D, D))],
        out_shape=[jax.ShapeDtypeStruct((LEN, WIDE), BF), jax.ShapeDtypeStruct((LEN, 384), BF), rows_of(D)],
        scratch_shapes=[pltpu.VMEM((LEN, D), BF), pltpu.VMEM((LEN, D), BF), dma(2)] + back_work,
        compiler_params=pltpu.CompilerParams(vmem_limit_bytes=60 << 20),
        name="back_far",
    )(size, qn, qc, att, lse, g, wo, cos, sin, xn, xc)


def back_near(size, qn, qc, att, lse, g, wo, cos, sin, xn, xc, w, w_far, av_far, c_far):
    return pl.pallas_call(
        back_near_kernel,
        grid=(3,),
        in_specs=[pl.BlockSpec(memory_space=pltpu.SMEM)] + head_inputs(0)
        + [whole((LEN, D)), whole((3 * HD, D)), whole((LEN, 128)), whole((LEN, 128))] + [anywhere()] * 6,
        out_specs=[anywhere(), anywhere(), whole((9 * HD, D)), whole((3 * HD, D))],
        out_shape=[rows_shape, rows_shape, jax.ShapeDtypeStruct((9 * HD, D), F32), jax.ShapeDtypeStruct((3 * HD, D), F32)],
        scratch_shapes=[pltpu.VMEM((LEN, D), BF), pltpu.VMEM((LEN, D), BF), pltpu.VMEM((2 * WIDE, D), BF), pltpu.VMEM((D, D), BF),
                        pltpu.VMEM((LEN, 2 * WIDE), BF), pltpu.VMEM((LEN, D), BF), pltpu.VMEM((2, LEN, D), BF),
                        dma(4), dma(18), dma(2 * CHUNKS)] + back_work,
        compiler_params=pltpu.CompilerParams(vmem_limit_bytes=60 << 20),
        name="back_near",
    )(size, qn, qc, att, lse, g, wo, cos, sin, xn, xc, w, w_far, av_far, c_far)


def halves(v):
    high = v.astype(BF)
    return high, (v - high.astype(F32)).astype(BF)


def exact(left_side, right_side, left_dim, right_dim):
    dims = (((left_dim,), (right_dim,)), ((), ()))
    a, b = halves(left_side)
    c, d = halves(right_side)

    def times(x, y):
        return lax.dot_general(x, y, dims, preferred_element_type=F32)

    return times(a, c) + (times(a, d) + times(b, c))


def core_peer():
    m = lax.axis_index("mp")
    return (lax.axis_index("dp"), m + 1 - 2 * lax.rem(m, 2))


def far_peer():
    return (lax.axis_index("dp"), lax.rem(lax.axis_index("mp") + 2, 4))


def greet(*peers):
    barrier = pltpu.get_barrier_semaphore()
    for p in peers:
        pl.semaphore_signal(barrier, inc=1, device_id=p, device_id_type=MESH_ID)
    pl.semaphore_wait(barrier, len(peers))


PARTS = HALF // TILE


def own_rows(i):
    half = lax.rem(lax.axis_index("mp"), 2)
    return pl.ds(pl.multiple_of(half * HALF + i * TILE, TILE), TILE)


def peer_rows(i):
    half = lax.rem(lax.axis_index("mp"), 2)
    return pl.ds(pl.multiple_of((1 - half) * HALF + i * TILE, TILE), TILE)


def side_rows_of(i):
    m = lax.axis_index("mp")
    return pl.ds(pl.multiple_of(m * HALF + i * TILE, TILE), TILE)


def copy(src, dst, sem):
    return pltpu.make_async_copy(src, dst, sem)


def push(src, dst, send_sem, recv_sem, peer):
    return pltpu.make_async_remote_copy(
        src_ref=src, dst_ref=dst, send_sem=send_sem, recv_sem=recv_sem, device_id=peer, device_id_type=MESH_ID)


class Sems:
    def __init__(self, ref):
        self.ref = ref
        self.used = 0

    def take(self):
        self.used += 1
        return self.ref.at[self.used - 1]


def middle_kernel(att_hbm, wo_near_hbm, wo_far_hbm, rows_hbm, cot_hbm, up_hbm, down_hbm,
                  err_up_hbm, err_down_hbm, fac_up_ref, fac_down_ref, gain_ref,
                  res_hbm, grad_hbm, low_hbm, mlp_hbm, fold_hbm, mat_up_hbm, mat_down_hbm,
                  left_up_ref, left_down_ref, gsum_ref,
                  att_ref, wo_ref, x_ref, send_ref, far_ref, r_ref, nm_ref, cot_ref, up_ref, down_ref, hid_ref, gp_ref,
                  mlp_ref, gm_ref, back_ref, fold_gm_ref, fold_mlp_ref, sum_ref, msum_ref, yet_ref,
                  mat_up_ref, mat_down_ref, nmt_ref, grad_ref, low_ref, sem_ref, send_sem_ref, recv_sem_ref):
    sems, sends, recvs = Sems(sem_ref), Sems(send_sem_ref), Sems(recv_sem_ref)
    m = lax.axis_index("mp")
    side, half = m // 2, lax.rem(m, 2)
    core, far = core_peer(), far_peer()
    width = 3 * HD
    third = D // 3
    pushes, saves = [], []

    def load(src, dst):
        c = pltpu.make_async_copy(src, dst, sems.take())
        c.start()
        return c

    def save(src, dst):
        saves.append(load(src, dst))

    def send(src, dst, peer):
        c = push(src, dst, sends.take(), recvs.take(), peer)
        c.start()
        pushes.append(c)
        return c

    def span(start, n):
        return pl.ds(pl.multiple_of(start, TILE), n)

    own_half, peer_half = half * HALF, (1 - half) * HALF
    first = [load(att_hbm, att_ref), load(wo_near_hbm, wo_ref.at[0:width]), load(wo_far_hbm, wo_ref.at[width:])]
    xs = [load(rows_hbm.at[span(m * HALF + i * TILE, TILE)], x_ref.at[chunk(i)]) for i in range(PARTS)]
    up_in, down_in = load(up_hbm, up_ref), load(down_hbm, down_ref)
    cot_in = load(cot_hbm.at[span(side * LEN, LEN)], cot_ref.at[0:LEN])
    cot_far_in = load(cot_hbm.at[span((1 - side) * LEN, LEN)], cot_ref.at[LEN:])
    err_in = [load(err_down_hbm.at[0], mat_down_ref), load(err_up_hbm.at[0], mat_up_ref)]
    greet(core, far)
    for c in first:
        c.wait()
    parts = []
    for i in range(PARTS):
        send_ref[chunk(i), :] = tn(att_ref[:, span(peer_half + i * TILE, TILE)], wo_ref[...]).astype(BF)
        parts.append(send(send_ref.at[chunk(i)], far_ref.at[chunk(i)], core))
    normed, cross = [], []
    for i in range(PARTS):
        at = span(own_half + i * TILE, TILE)
        own = tn(att_ref[:, at], wo_ref[...])
        xs[i].wait()
        parts[i].wait_recv()
        r = x_ref[chunk(i), :].astype(F32) + (own + far_ref[chunk(i), :].astype(F32))
        r_ref[chunk(i), :] = r
        nm_ref[at, :] = (norm_parts(r)[0] * gain_ref[1:2, :]).astype(BF)
        normed.append(send(nm_ref.at[at], nm_ref.at[at], core))
        cross.append(send(nm_ref.at[at], nm_ref.at[span(LEN + own_half + i * TILE, TILE)], far))
        save(r_ref.at[chunk(i)], res_hbm.at[chunk(i)])

    def feed_rows(start, n):
        at = span(start, n)
        for t in range(3):
            lanes = slice(t * third, (t + 1) * third)
            hidden, slope = gelu_and_slope(nn(nm_ref[at, :], up_ref[:, lanes]))
            hid_ref[at, lanes] = hidden.astype(BF)
            gp_ref[at, lanes] = (slope * nt(cot_ref[at, :], down_ref[lanes, :])).astype(BF)
        gm_ref[at, :] = nt(gp_ref[at, :], up_ref[...]).astype(BF)
        mlp_ref[at, :] = nn(hid_ref[at, :], down_ref[...]).astype(BF)

    up_in.wait()
    down_in.wait()
    cot_in.wait()
    feed_rows(own_half, HALF)
    for c in normed:
        c.wait_recv()
    feed_rows(peer_half, HALF)
    save(mlp_ref.at[0:LEN], mlp_hbm)
    swap = [send(gm_ref.at[span(peer_half + i * TILE, TILE)], back_ref.at[chunk(i)], core) for i in range(PARTS)]
    cot_far_in.wait()
    arrived = []
    for i in range(PARTS):
        at = span(LEN + own_half + i * TILE, TILE)
        away = span(LEN + peer_half + i * TILE, TILE)
        cross[i].wait_recv()
        relay = send(nm_ref.at[at], nm_ref.at[at], core)
        feed_rows(LEN + own_half + i * TILE, TILE)
        relay.wait_recv()
        feed_rows(LEN + peer_half + i * TILE, TILE)
        fold = send(gm_ref.at[away], fold_gm_ref.at[chunk(i)], core)
        fold_mlp = send(mlp_ref.at[away], fold_mlp_ref.at[chunk(i)], core)
        fold.wait_recv()
        sum_ref[chunk(i), :] = (gm_ref[at, :].astype(F32) + fold_gm_ref[chunk(i), :].astype(F32)).astype(BF)
        arrived.append(send(sum_ref.at[chunk(i)], yet_ref.at[chunk(i)], far))
        fold_mlp.wait_recv()
        msum_ref[chunk(i), :] = (mlp_ref[at, :].astype(F32) + fold_mlp_ref[chunk(i), :].astype(F32)).astype(BF)
        save(msum_ref.at[chunk(i)], fold_hbm.at[chunk(i)])

    for i in range(8):
        at = slice(i * TILE, (i + 1) * TILE)
        nmt_ref[:, at] = jnp.transpose(nm_ref[at, :])
    for c in err_in:
        c.wait()
    left_up = 0.0
    for t in range(3):
        lanes = slice(t * third, (t + 1) * third)
        mat = tn(hid_ref[:, lanes], cot_ref[...]) + mat_down_ref[lanes, :]
        mat_down_ref[lanes, :] = mat
        save(mat_down_ref.at[lanes], mat_down_hbm.at[lanes])
        left_down_ref[:, lanes] = exact(fac_down_ref[...], mat, 1, 1)
        mat = nn(nmt_ref[...], gp_ref[:, lanes]) + mat_up_ref[:, lanes]
        mat_up_ref[:, lanes] = mat
        save(mat_up_ref.at[:, lanes], mat_up_hbm.at[:, lanes])
        left_up = left_up + exact(fac_up_ref[:, lanes], mat, 1, 1)
    left_up_ref[...] = left_up

    gsum = 0.0
    lows = []
    for i in range(PARTS):
        at = span(own_half + i * TILE, TILE)
        swap[i].wait_recv()
        total = gm_ref[at, :].astype(F32) + back_ref[chunk(i), :].astype(F32)
        arrived[i].wait_recv()
        total = total + yet_ref[chunk(i), :].astype(F32)
        grad, share = norm_back(r_ref[chunk(i), :], gain_ref[1:2, :], total)
        gsum = gsum + share
        grad = cot_ref[at, :].astype(F32) + grad
        grad_ref[chunk(i), :] = grad
        low_ref[chunk(i), :] = grad.astype(BF)
        lows.append(send(low_ref.at[chunk(i)], low_hbm.at[at], core))
        save(low_ref.at[chunk(i)], low_hbm.at[at])
        save(grad_ref.at[chunk(i)], grad_hbm.at[chunk(i)])
    gsum_ref[...] = gsum
    for c in lows:
        c.wait_recv()
    for c in pushes:
        c.wait_send()
    for c in saves:
        c.wait()


def middle(att, wo_near, wo_far, rows, cotangent, up, down, err_up, err_down, fac_up, fac_down, gains):
    def low(n):
        return pltpu.VMEM((n, D), BF)

    def wide(n):
        return pltpu.VMEM((n, D), F32)

    return pl.pallas_call(
        middle_kernel,
        in_specs=[anywhere()] * 9 + [in_vmem()] * 3,
        out_specs=[anywhere()] * 7 + [in_vmem()] * 3,
        out_shape=[jax.ShapeDtypeStruct((HALF, D), F32), jax.ShapeDtypeStruct((HALF, D), F32), rows_of(LEN), rows_of(LEN),
                   rows_of(HALF), jax.ShapeDtypeStruct((D, D), F32), jax.ShapeDtypeStruct((D, D), F32),
                   jax.ShapeDtypeStruct((RANK, D), F32), jax.ShapeDtypeStruct((RANK, D), F32),
                   jax.ShapeDtypeStruct((1, D), F32)],
        scratch_shapes=[pltpu.VMEM((6 * HD, LEN), BF), low(6 * HD), low(HALF), low(HALF), low(HALF), wide(HALF),
                        low(2 * LEN), low(2 * LEN), low(D), low(D), low(2 * LEN), low(2 * LEN),
                        low(2 * LEN), low(2 * LEN), low(HALF), low(HALF), low(HALF), low(HALF), low(HALF), low(HALF),
                        wide(D), wide(D), pltpu.VMEM((D, 2 * LEN), BF), wide(HALF), low(HALF), dma(32), dma(24), dma(24)],
        compiler_params=pltpu.CompilerParams(collective_id=3, has_side_effects=True, vmem_limit_bytes=60 << 20),
        name="middle",
    )(att, wo_near, wo_far, rows, cotangent, up, down, err_up, err_down, fac_up, fac_down, gains)


def settle_kernel(mlp_hbm, far_hbm, res_hbm, out_hbm, own_ref, far_ref, res_ref, core_ref, out_ref,
                  sem_in, sem_send, sem_recv, sem_out):
    peer = core_peer()
    loads = []
    for i in range(PARTS):
        loads += [copy(mlp_hbm.at[own_rows(i)], own_ref.at[chunk(i)], sem_in.at[3 * i]),
                  copy(far_hbm.at[chunk(i)], far_ref.at[chunk(i)], sem_in.at[3 * i + 1]),
                  copy(res_hbm.at[chunk(i)], res_ref.at[chunk(i)], sem_in.at[3 * i + 2])]
    for c in loads:
        c.start()
    greet(peer)
    pushes = [push(mlp_hbm.at[peer_rows(i)], core_ref.at[chunk(i)], sem_send.at[i], sem_recv.at[i], peer)
              for i in range(PARTS)]
    for c in pushes:
        c.start()
    saves = []
    for i in range(PARTS):
        for c in loads[3 * i:3 * i + 3]:
            c.wait()
        pushes[i].wait_recv()
        total = own_ref[chunk(i), :].astype(F32) + core_ref[chunk(i), :].astype(F32) + far_ref[chunk(i), :].astype(F32)
        out_ref[chunk(i), :] = (res_ref[chunk(i), :] + total).astype(BF)
        saves.append(copy(out_ref.at[chunk(i)], out_hbm.at[chunk(i)], sem_out.at[i]))
        saves[-1].start()
    for c in saves:
        c.wait()
    for c in pushes:
        c.wait_send()


def settle(mlp, far, residual):
    half = pltpu.VMEM((HALF, D), BF)
    return pl.pallas_call(
        settle_kernel,
        in_specs=[anywhere()] * 3,
        out_specs=anywhere(),
        out_shape=rows_of(HALF),
        scratch_shapes=[half, half, pltpu.VMEM((HALF, D), F32), half, half, dma(3 * PARTS), dma(PARTS), dma(PARTS), dma(PARTS)],
        compiler_params=pltpu.CompilerParams(collective_id=4, has_side_effects=True, vmem_limit_bytes=60 << 20),
        name="settle",
    )(mlp, far, residual)


def finish_kernel(gxn_hbm, gxc_hbm, noisy_hbm, clean_hbm, grad_hbm, gain_ref, gain_two_ref, noisy_out_hbm, clean_out_hbm, gsum_ref,
                  own_ref, far_ref, x_ref, wide_ref, out_ref,
                  sem_own, sem_x, sem_wide, sem_send, sem_recv, sem_out):
    sources = (gxn_hbm, gxc_hbm)
    count = 2 * PARTS
    own, rows, wide = [], [], []
    for n in range(count):
        k, i = n // PARTS, n % PARTS
        own.append(copy(sources[k].at[own_rows(i)], own_ref.at[chunk(n)], sem_own.at[n]))
        rows.append(copy((noisy_hbm, clean_hbm)[k].at[side_rows_of(i)], x_ref.at[chunk(n)], sem_x.at[n]))
        if k == 0:
            wide.append(copy(grad_hbm.at[chunk(i)], wide_ref.at[chunk(i)], sem_wide.at[i]))
    for c in own + rows + wide:
        c.start()
    peer = core_peer()
    greet(peer)
    pushes = []
    for n in range(count):
        k, i = n // PARTS, n % PARTS
        pushes.append(push(sources[k].at[peer_rows(i)], far_ref.at[chunk(n)], sem_send.at[n], sem_recv.at[n], peer))
        pushes[-1].start()
    gsum = 0.0
    saves = []
    for n in range(count):
        k, i = n // PARTS, n % PARTS
        own[n].wait()
        rows[n].wait()
        pushes[n].wait_recv()
        total = own_ref[chunk(n), :].astype(F32) + far_ref[chunk(n), :].astype(F32)
        grad, share = norm_back(x_ref[chunk(n), :].astype(F32), gain_ref[0:1, :], total)
        gsum = gsum + share
        if k == 0:
            wide[i].wait()
            grad = wide_ref[chunk(i), :] + grad
        out_ref[chunk(n), :] = grad.astype(BF)
        target = (noisy_out_hbm, clean_out_hbm)[k]
        saves.append(copy(out_ref.at[chunk(n)], target.at[chunk(i)], sem_out.at[n]))
        saves[-1].start()
    gsum_ref[0:1, :] = gsum
    gsum_ref[1:2, :] = gain_two_ref[...]
    gsum_ref[2:8, :] = jnp.zeros((6, D), F32)
    for c in saves:
        c.wait()
    for c in pushes:
        c.wait_send()


def finish(gxn, gxc, noisy_rows, clean_rows, grad_resid, gains, gain_two):
    buf = pltpu.VMEM((LEN, D), BF)
    return pl.pallas_call(
        finish_kernel,
        in_specs=[anywhere()] * 5 + [in_vmem()] * 2,
        out_specs=[anywhere(), anywhere(), in_vmem()],
        out_shape=[rows_of(HALF), rows_of(HALF), jax.ShapeDtypeStruct((RANK, D), F32)],
        scratch_shapes=[buf, buf, buf, pltpu.VMEM((HALF, D), F32), buf,
                        dma(2 * PARTS), dma(2 * PARTS), dma(PARTS), dma(2 * PARTS), dma(2 * PARTS), dma(2 * PARTS)],
        compiler_params=pltpu.CompilerParams(collective_id=5, has_side_effects=True, vmem_limit_bytes=60 << 20),
        name="finish",
    )(gxn, gxc, noisy_rows, clean_rows, grad_resid, gains, gain_two)


def place_kernel(count, *refs):
    sources, outs = refs[:4 * count], refs[4 * count:5 * count]
    stage, sem_in, sem_out = refs[5 * count:]
    m = lax.axis_index("mp")
    beside = m + 1 - 2 * lax.rem(m, 2)
    spots = (m, beside, lax.rem(m + 2, 4), lax.rem(beside + 2, 4))
    loads = [copy(sources[j], stage.at[j], sem_in.at[j]) for j in range(4 * count)]
    for c in loads:
        c.start()
    saves = []
    for j, c in enumerate(loads):
        c.wait()
        at = pl.ds(pl.multiple_of(spots[j % 4] * HALF, HALF), HALF)
        saves.append(copy(stage.at[j], outs[j // 4].at[at], sem_out.at[j]))
        saves[-1].start()
    for c in saves:
        c.wait()


def place(*ends):
    count = len(ends) // 4
    return pl.pallas_call(
        functools.partial(place_kernel, count),
        in_specs=[anywhere()] * (4 * count),
        out_specs=[anywhere()] * count,
        out_shape=[rows_of(2 * LEN)] * count,
        scratch_shapes=[pltpu.VMEM((4 * count, HALF, D), BF), dma(4 * count), dma(4 * count)],
        compiler_params=pltpu.CompilerParams(vmem_limit_bytes=60 << 20),
        name="place",
    )(*ends)


PACK = 1024


def lefts_kernel(gq_ref, both_ref, eq_ref, go_ref, eo_ref, fq_ref, fo_ref, lu_ref, ld_ref, gain_ref,
                 mq_ref, mo_ref, pack_ref):
    pack_ref[...] = jnp.zeros_like(pack_ref)
    mq = gq_ref[...] + both_ref[:9 * HD, :].astype(F32) + eq_ref[0]
    mq_ref[...] = mq
    pack_ref[0:8, 0:D] = exact(fq_ref[...], mq, 1, 0)
    mo = go_ref[...] + both_ref[9 * HD:, :].astype(F32) + eo_ref[0]
    mo_ref[...] = mo
    pack_ref[0:8, D:D + 3 * HD] = exact(fo_ref[...], mo, 1, 1)
    pack_ref[8:16, 0:D] = lu_ref[...]
    pack_ref[16:24, 0:D] = ld_ref[...]
    for k in range(6):
        pack_ref[8 + k:9 + k, D:PACK] = gain_ref[k // 3:k // 3 + 1, 256 * (k % 3):256 * (k % 3 + 1)]


def lefts(*args):
    return pl.pallas_call(
        lefts_kernel,
        grid=(1,),
        in_specs=[whole(v.shape) for v in args],
        out_specs=[whole((9 * HD, D)), whole((3 * HD, D)), whole((3 * RANK, PACK))],
        out_shape=[jax.ShapeDtypeStruct((9 * HD, D), F32), jax.ShapeDtypeStruct((3 * HD, D), F32),
                   jax.ShapeDtypeStruct((3 * RANK, PACK), F32)],
        compiler_params=pltpu.CompilerParams(vmem_limit_bytes=60 << 20),
        name="lefts",
    )(*args)


def orthonormalize(sum_ref):
    mats = [sum_ref[0:8, 0:D], sum_ref[0:8, D:PACK], sum_ref[8:16, 0:D], sum_ref[16:24, 0:D]]
    for k in range(RANK):
        for t in range(4):
            a = mats[t]
            row = lax.broadcasted_iota(jnp.int32, a.shape, 0)
            v = a[k:k + 1, :]
            e = v / (jnp.sqrt(jnp.sum(v * v, axis=1, keepdims=True)) + 1e-08)
            c = jnp.sum(a * e, axis=1, keepdims=True)
            mats[t] = jnp.where(row == k, e, jnp.where(row > k, a - c * e, a))
    mats[1] = mats[1][:, :3 * HD]
    return mats


def right_products(hats, mq_ref, mo_ref, mu_ref, md_ref, pack_ref):
    out = exact(hats[1], mo_ref[...], 1, 0)
    pack_ref[0:8, 0:D] = exact(hats[2], mu_ref[...], 1, 0)
    pack_ref[8:16, 0:D] = exact(hats[3], md_ref[...], 1, 0)
    pack_ref[16:24, 0:D] = jnp.zeros((RANK, D), F32)
    pack_ref[16:24, 0:9 * HD] = exact(hats[0], mq_ref[...], 1, 1)
    for k in range(3):
        pack_ref[8 * k:8 * k + 8, D:PACK] = out[:, 256 * k:256 * (k + 1)]


def unpack_rights(pack_ref):
    out = jnp.concatenate([pack_ref[8 * k:8 * k + 8, D:PACK] for k in range(3)], axis=1)
    return [pack_ref[16:24, 0:9 * HD], out, pack_ref[0:8, 0:D], pack_ref[8:16, 0:D]]


def rights_kernel(sum_ref, mq_ref, mo_ref, mu_ref, md_ref, hq_ref, ho_ref, hu_ref, hd_ref, pack_ref):
    hats = orthonormalize(sum_ref)
    for hat, ref in zip(hats, (hq_ref, ho_ref, hu_ref, hd_ref)):
        ref[...] = hat
    right_products(hats, mq_ref, mo_ref, mu_ref, md_ref, pack_ref)


def rights(left_sum, mats):
    args = (left_sum, *mats)
    shapes = [(RANK, D), (RANK, 3 * HD), (RANK, D), (RANK, D), (3 * RANK, PACK)]
    return pl.pallas_call(
        rights_kernel,
        grid=(1,),
        in_specs=[whole(v.shape) for v in args],
        out_specs=[whole(s) for s in shapes],
        out_shape=[jax.ShapeDtypeStruct(s, F32) for s in shapes],
        compiler_params=pltpu.CompilerParams(vmem_limit_bytes=60 << 20),
        name="rights",
    )(*args)


def reduce_kernel(count, x_ref, mq_hbm, mo_hbm, mu_hbm, md_hbm, hat_ref, right_ref, gsum_ref,
                  mq_ref, mo_ref, mu_ref, md_ref, sum_ref, in_a, y_ref, in_b, slot_ref, sem_ref, send_ref, recv_ref):
    me = lax.axis_index("dp")
    m = lax.axis_index("mp")
    sends, recvs = Sems(send_ref), Sems(recv_ref)
    late = [copy(s, d, sem_ref.at[k]) for k, (s, d) in enumerate((
        (mq_hbm, mq_ref), (mo_hbm, mo_ref), (mu_hbm, mu_ref), (md_hbm, md_ref)))]
    for c in late:
        c.start()
    barrier = pltpu.get_barrier_semaphore()
    for k in range(1, count):
        pl.semaphore_signal(barrier, inc=1, device_id=(lax.rem(me + k, count), m), device_id_type=MESH_ID)
    pl.semaphore_signal(barrier, inc=1, device_id=core_peer(), device_id_type=MESH_ID)
    pl.semaphore_wait(barrier, count)

    def lanes(j):
        return pl.ds(pl.multiple_of(j * 128, 128), 128)

    def spread_sum(src_ref, box_ref, out_ref):
        gather, scatter = [], []
        for k in range(1, count):
            j = lax.rem(me + k, count)
            gather.append(push(src_ref.at[:, lanes(j)], box_ref.at[k], sends.take(), recvs.take(), (j, m)))
        for c in gather:
            c.start()
        total = src_ref[:, lanes(me)]
        for k in range(1, count):
            gather[k - 1].wait_recv()
            total = total + box_ref[k]
        out_ref[:, lanes(me)] = total
        for k in range(1, count):
            j = lax.rem(me + k, count)
            scatter.append(push(out_ref.at[:, lanes(me)], out_ref.at[:, lanes(me)], sends.take(), recvs.take(), (j, m)))
            scatter[-1].start()
        for k in range(1, count):
            scatter[k - 1].wait_recv()
        return gather + scatter

    sent = spread_sum(x_ref, in_a, sum_ref)
    share = push(sum_ref.at[8:16, D:PACK], slot_ref, sends.take(), recvs.take(), core_peer())
    share.start()
    hats = orthonormalize(sum_ref)
    hat_ref[...] = jnp.zeros_like(hat_ref)
    for t in range(4):
        hat_ref[RANK * t:RANK * (t + 1), 0:hats[t].shape[1]] = hats[t]
    for c in late:
        c.wait()
    right_products(hats, mq_ref, mo_ref, mu_ref, md_ref, y_ref)
    sent += spread_sum(y_ref, in_b, right_ref)
    share.wait()
    gsum_ref[...] = sum_ref[8:16, D:PACK] + slot_ref[...]
    for c in sent:
        c.wait_send()


def reduce_factors(pack, mats):
    count = lax.axis_size("dp")
    if count != 8:
        total = lax.psum(pack, "dp")
        *hats, pack = rights(total, mats)
        hats[1] = jnp.pad(hats[1], ((0, 0), (0, D - 3 * HD)))
        share = total[8:16, D:PACK]
        share = share + lax.ppermute(share, "mp", [(0, 1), (1, 0), (2, 3), (3, 2)])
        return jnp.concatenate(hats, axis=0), lax.psum(pack, "dp"), share

    def wide(n):
        return pltpu.VMEM((n, D), F32)

    links = 4 * (count - 1) + 1
    return pl.pallas_call(
        functools.partial(reduce_kernel, count),
        in_specs=[in_vmem()] + [anywhere()] * 4,
        out_specs=[in_vmem()] * 3,
        out_shape=[jax.ShapeDtypeStruct(s, F32) for s in ((4 * RANK, D), (3 * RANK, PACK), (RANK, PACK - D))],
        scratch_shapes=[wide(9 * HD), wide(3 * HD), wide(D), wide(D), pltpu.VMEM((3 * RANK, PACK), F32),
                        pltpu.VMEM((count, 3 * RANK, 128), F32), pltpu.VMEM((3 * RANK, PACK), F32),
                        pltpu.VMEM((count, 3 * RANK, 128), F32), pltpu.VMEM((RANK, PACK - D), F32),
                        dma(4), dma(links), dma(links)],
        compiler_params=pltpu.CompilerParams(collective_id=1, has_side_effects=True, vmem_limit_bytes=60 << 20),
        name="reduce_factors",
    )(pack, *mats)


def update_kernel(replicas, rates, *refs):
    sums, hats, mats, states = refs[0], refs[1], refs[2:6], refs[6:18]
    errs, news, right_out, hat_out = refs[18:22], refs[22:34], refs[34:38], refs[38:42]
    decay = min(0.9999, (1.0 + EMA_STEPS) / (10.0 + EMA_STEPS))
    share = D // replicas
    shift = lax.rem(D - lax.axis_index("dp") * share, D)

    def part(value):
        return pltpu.roll(value, shift, 1)[:, :share]

    rights_all = unpack_rights(sums)
    for t in range(4):
        hat = hats[RANK * t:RANK * (t + 1), :hat_out[t].shape[1]]
        hat_out[t][...] = hat
        right = rights_all[t] * (1.0 / replicas)
        right_out[t][...] = right
        first, second = ((right, hat), (hat, right), (hat, right), (hat, right))[t]
        errs[t][0] = mats[t][...] - exact(first, second, 0, 0)
        first, second = ((part(hat), right), (hat, part(right)), (part(hat), right), (part(right), hat))[t]
        moment = 0.5 * states[3 * t + 1][...] + exact(first, second, 0, 0)
        master = states[3 * t][...] - rates[t] * moment
        news[3 * t][...] = master
        news[3 * t + 1][...] = moment
        news[3 * t + 2][...] = decay * states[3 * t + 2][...] + (1.0 - decay) * master


def update(replicas, rates, right_sum, hats, mats, states):
    args = (right_sum, hats, *mats, *states)
    shapes = [(1, *m.shape) for m in mats] + [s.shape for s in states]
    shapes += [(RANK, 9 * HD), (RANK, D), (RANK, D), (RANK, D)]
    shapes += [(RANK, D), (RANK, 3 * HD), (RANK, D), (RANK, D)]
    return pl.pallas_call(
        functools.partial(update_kernel, replicas, rates),
        grid=(1,),
        in_specs=[whole(v.shape) for v in args],
        out_specs=[whole(s) for s in shapes],
        out_shape=[jax.ShapeDtypeStruct(s, F32) for s in shapes],
        compiler_params=pltpu.CompilerParams(vmem_limit_bytes=60 << 20),
        name="update",
    )(*args)


def local(
    noisy_rows, clean_rows, block_size, cotangent, norm_gains,
    weight_qkv, weight_out, weight_up, weight_down,
    master_qkv, master_out, master_up, master_down,
    moment_qkv, moment_out, moment_up, moment_down,
    average_qkv, average_out, average_up, average_down,
    error_qkv, error_out, error_up, error_down,
    factor_qkv, factor_out, factor_up, factor_down,
    gain_moment,
):
    row_count = noisy_rows.shape[0]
    replicas = lax.axis_size("dp")

    def across(value):
        return lax.ppermute(value, "mp", [(0, 2), (2, 0), (1, 3), (3, 1)])

    def beside(value):
        return lax.ppermute(value, "mp", [(0, 1), (1, 0), (2, 3), (3, 2)])

    def hold(*values):
        return lax.optimization_barrier(values)

    cos, sin = rotary_tables()
    w_near = weight_qkv.T
    qn, qc, att, lse, xn, xc, w_far, o_far = attend(
        block_size, noisy_rows, clean_rows, w_near, weight_out, norm_gains, cos, sin)
    residual, grad_resid, grad_low, mlp, mlp_fold, matrix_up, matrix_down, left_up, left_down, gain_two = middle(
        att, weight_out, o_far, noisy_rows, cotangent, weight_up, weight_down,
        error_up, error_down, factor_up.T, factor_down.T, norm_gains)
    mlp_far = across(mlp_fold)
    av_far, c_far, grads_far = back_far(block_size, qn, qc, att, lse, grad_low, o_far, cos, sin, xn, xc)
    mlp_far, av_far, grads_far = hold(mlp_far, av_far, grads_far)
    grads_back = across(grads_far)
    out_half = settle(mlp, mlp_far, residual)
    out_half, av_far = hold(out_half, av_far)
    out_far, out_side = across(out_half), beside(out_half)
    grad_xn, grad_xc, gq_near, go_near = back_near(
        block_size, qn, qc, att, lse, grad_low, weight_out, cos, sin, xn, xc, w_near, w_far, av_far, c_far)
    noisy_half, clean_half, gain_pair = finish(
        grad_xn, grad_xc, noisy_rows, clean_rows, grad_resid, norm_gains, gain_two)
    noisy_half, clean_half, grads_back = hold(noisy_half, clean_half, grads_back)
    matrix_qkv, matrix_out, pack = lefts(
        gq_near, grads_back, jnp.swapaxes(error_qkv, 1, 2), go_near, error_out,
        factor_qkv.T, factor_out.T, left_up, left_down, gain_pair)
    noisy_half, clean_half, pack, out_far = hold(noisy_half, clean_half, pack, out_far)
    noisy_far, clean_far = across(noisy_half), across(clean_half)
    noisy_side, clean_side = beside(noisy_half), beside(clean_half)
    mats = (matrix_qkv, matrix_out, matrix_up, matrix_down)
    hats, right_sum, gain_sum = reduce_factors(pack, mats)
    rates = [3.0 / math.sqrt(f * row_count) for f in (D, HEADS * HD // 64, D, FF)] + [0.5 / math.sqrt(row_count)]
    states = (
        master_qkv, moment_qkv, average_qkv, master_out, moment_out, average_out,
        master_up, moment_up, average_up, master_down.T, moment_down.T, average_down.T,
    )
    done = update(replicas, rates, right_sum, hats, mats, states)
    errs, news, right_new, left_new = done[:4], done[4:16], done[16:20], done[20:24]
    noisy_far, _ = hold(noisy_far, hats)
    out_diag, noisy_diag = beside(out_far), beside(noisy_far)
    clean_far, out_diag, noisy_diag, _ = hold(clean_far, out_diag, noisy_diag, errs[2])
    clean_diag = beside(clean_far)
    block_out, grad_noisy = place(
        out_half, out_side, out_far, out_diag, noisy_half, noisy_side, noisy_far, noisy_diag)
    grad_noisy, clean_diag = hold(grad_noisy, clean_diag)
    grad_clean, = place(clean_half, clean_side, clean_far, clean_diag)
    clean_far, gain_sum = hold(clean_far, gain_sum)
    gain_grad = (gain_sum + across(gain_sum))[:6].reshape(2, D) / replicas
    gain_step = 0.5 * gain_moment + gain_grad
    gains_new = (gain_grad, norm_gains - rates[4] * gain_step, gain_step)
    fresh = [news[3 * t + k] if t < 3 else news[3 * t + k].T for k in range(3) for t in range(4)]
    return (
        block_out, grad_noisy, grad_clean, *gains_new, *fresh,
        jnp.swapaxes(errs[0], 1, 2), *errs[1:], *[v.T for v in left_new], *[v.T for v in right_new],
    )


def solution(mesh):
    in_specs = (
        P("dp", None), P("dp", None), P("dp"), P("dp", None), P(),
        P(None, "mp"), P("mp", None), P(None, "mp"), P("mp", None),
        *([P("dp", "mp"), P("mp", "dp")] * 6),
        *([P("dp", None, "mp"), P("dp", "mp", None)] * 2),
        *([P("mp", None), P(None, "mp")] * 2),
        P(),
    )
    out_specs = (
        P("dp", None), P("dp", None), P("dp", None), P(), P(), P(),
        *([P("dp", "mp"), P("mp", "dp")] * 6),
        *([P("dp", None, "mp"), P("dp", "mp", None)] * 2),
        *([P(None, "mp"), P("mp", None)] * 2),
        *([P("mp", None), P(None, "mp")] * 2),
    )
    return jax.shard_map(local, mesh=mesh, in_specs=in_specs, out_specs=out_specs, check_vma=False)
```

```python
import functools
import math

import jax
import jax.numpy as jnp
import numpy as np
from jax import lax
from jax.experimental import pallas as pl
from jax.experimental.pallas import tpu as pltpu
from jax.sharding import PartitionSpec as P

D = 768
HEADS = 12
HD = 64
FF = 3072
LEN = 1024
RANK = 8
EMA_STEPS = 4
TILE = 256
SLOT = 256

BF = jnp.bfloat16
F32 = jnp.float32
highest = lax.Precision.HIGHEST
norm_eps = 1e-05
gelu_coef = 0.7978845608028654
masked_score = -1e30
MESH_ID = pl.DeviceIdType.MESH


def nt(a, b):
    return lax.dot_general(a, b, (((1,), (1,)), ((), ())), preferred_element_type=F32)


def nn(a, b):
    return lax.dot_general(a, b, (((1,), (0,)), ((), ())), preferred_element_type=F32)


def tn(a, b):
    return lax.dot_general(a, b, (((0,), (0,)), ((), ())), preferred_element_type=F32)


def rotary_tables():
    half = HD // 2
    step = np.float32(-2.0 * math.log(10000.0) / HD)
    inverse = np.exp(np.arange(half, dtype=np.float32) * step).astype(np.float32)
    angle = (np.arange(LEN, dtype=np.float32)[:, None] * inverse[None, :]).astype(np.float32)
    c = np.cos(angle).astype(np.float32)
    s = np.sin(angle).astype(np.float32)
    return np.concatenate([c, c, c, c], 1), np.concatenate([-s, s, -s, s], 1)


def spin(v, cos, sin):
    lane = lax.broadcasted_iota(jnp.int32, v.shape, 1)
    low = lax.rem(lane, HD) < HD // 2
    swapped = jnp.where(low, pltpu.roll(v, 128 - HD // 2, 1), pltpu.roll(v, HD // 2, 1))
    return v * cos + swapped * sin


def block_ids(size, shape, dim):
    shift = 2 + (size >= 8).astype(jnp.int32) + (size >= 16).astype(jnp.int32)
    place = lax.broadcasted_iota(jnp.int32, shape, dim)
    return lax.shift_right_logical(place, jnp.full(shape, shift, jnp.int32))


def fill_bias(size, noisy_bias, clean_bias):
    keys = block_ids(size, (TILE, TILE), 0)
    rows = block_ids(size, (TILE, TILE), 1)
    noisy_bias[...] = jnp.where(rows == keys, 0.0, masked_score)
    clean_bias[...] = jnp.where(keys < rows, 0.0, masked_score)


def norm_parts(values):
    centered = values - jnp.mean(values, axis=1, keepdims=True)
    scale = lax.rsqrt(jnp.mean(centered * centered, axis=1, keepdims=True) + norm_eps)
    return centered * scale, scale


def norm_back(values, gain, grad):
    unit, scale = norm_parts(values)
    scaled = grad * gain
    inner = jnp.mean(scaled * unit, axis=1, keepdims=True)
    grad_in = scale * (scaled - jnp.mean(scaled, axis=1, keepdims=True) - unit * inner)
    return grad_in, jnp.sum(grad * unit, axis=0, keepdims=True)


def gelu_and_slope(u):
    square = u * u
    half = 0.5 + 0.5 * jnp.tanh(u * (gelu_coef + (gelu_coef * 0.044715) * square))
    slope = half + (u * (2.0 * half * (1.0 - half))) * (gelu_coef + (3.0 * 0.044715 * gelu_coef) * square)
    return u * half, slope


def whole(shape):
    return pl.BlockSpec(shape, lambda *index: (0,) * len(shape), pipeline_mode=pl.Buffered(1))


def side_rows(h, info, size):
    return (info[0], 0)


def lane2(h, *_):
    return (0, h)


def row3(h, *_):
    return (h, 0, 0)


def attend_head(head, xn_ref, xc_ref, w_ref, cos_ref, sin_ref, qn_ref, qc_ref, att_ref, lse_ref,
                bn_ref, bc_ref, kn_ref, kc_ref, vnt_ref, vct_ref):
    w = w_ref[pl.ds(pl.multiple_of(head * 3 * HD, 3 * HD), 3 * HD), :]
    for src, dst, keys, vals in ((xn_ref, qn_ref, kn_ref, vnt_ref), (xc_ref, qc_ref, kc_ref, vct_ref)):
        a = nt(src[...], w)
        r = spin(a[:, :128], cos_ref[...], sin_ref[...]).astype(BF)
        v = a[:, 128:].astype(BF)
        dst[:, :128] = r
        dst[:, 128:192] = v
        keys[...] = r[:, 64:128]
        vals[...] = jnp.transpose(v)
    here = pl.ds(pl.multiple_of(head * HD, HD), HD)
    for i in range(LEN // TILE):
        lo, hi = i * TILE, (i + 1) * TILE
        q = qn_ref[lo:hi, 0:64] * 0.125
        parts = [nt(kn_ref[lo:hi, :], q) + bn_ref[...], nt(kc_ref[lo:hi, :], q) + bc_ref[...]]
        if i:
            parts.append(nt(kc_ref[0:lo, :], q))
        peak = functools.reduce(jnp.maximum, [jnp.max(s, axis=0, keepdims=True) for s in parts])
        exps = [jnp.exp(s - peak) for s in parts]
        total = functools.reduce(jnp.add, [jnp.sum(e, axis=0, keepdims=True) for e in exps])
        inv = 1.0 / total
        low = [(e * inv).astype(BF) for e in exps]
        o = nn(vnt_ref[:, lo:hi], low[0]) + nn(vct_ref[:, lo:hi], low[1])
        if i:
            o = o + nn(vct_ref[:, 0:lo], low[2])
        att_ref[here, lo:hi] = o.astype(BF)
        lse_ref[0, :, lo:hi] = jnp.broadcast_to(peak + jnp.log(total), (8, TILE))


def attend_kernel(size_ref, noisy_hbm, clean_hbm, w_hbm, wo_hbm, gain_ref, cos_ref, sin_ref,
                  qn_ref, qc_ref, att_ref, lse_ref, xn_hbm, xc_hbm, w_far_hbm, o_far_hbm,
                  raw_ref, x_ref, w_ref, sem_in, sem_out, sem_send, sem_recv, *work):
    head = pl.program_id(0)
    side = lax.axis_index("mp") // 2
    peer = far_peer()
    sides = ((noisy_hbm, xn_hbm), (clean_hbm, xc_hbm))
    width = 3 * HD

    def load(s, i):
        at = pl.ds(pl.multiple_of(side * LEN + i * TILE, TILE), TILE)
        return pltpu.make_async_copy(sides[s][0].at[at], raw_ref.at[s, chunk(i)], sem_in.at[CHUNKS * s + i])

    def save(s):
        return pltpu.make_async_copy(x_ref.at[s], sides[s][1], sem_out.at[s])

    def give(j):
        at = slice(width * j, width * (j + 1))
        return push(w_hbm.at[at], w_ref.at[slice(width * (3 + j), width * (4 + j))], sem_send.at[j], sem_recv.at[j], peer)

    near_w = pltpu.make_async_copy(w_hbm, w_ref.at[0:3 * width], sem_in.at[2 * CHUNKS])
    give_out = push(wo_hbm, o_far_hbm, sem_send.at[3], sem_recv.at[3], peer)
    keep_w = pltpu.make_async_copy(w_ref.at[3 * width:], w_far_hbm, sem_out.at[2])

    @pl.when(head == 0)
    def _():
        for s in range(2):
            for i in range(CHUNKS):
                load(s, i).start()
        near_w.start()
        greet(peer)
        for j in range(3):
            give(j).start()
        give_out.start()
        fill_bias(size_ref[side], work[0], work[1])
        for s in range(2):
            for i in range(CHUNKS):
                load(s, i).wait()
                x = norm_parts(raw_ref[s, chunk(i), :].astype(F32))[0] * gain_ref[0:1, :]
                x_ref[s, chunk(i), :] = x.astype(BF)
            save(s).start()
        near_w.wait()

    for j in range(3):
        @pl.when(head == 3 + j)
        def _():
            give(j).wait_recv()

    @pl.when(head == 5)
    def _():
        keep_w.start()

    attend_head(head, x_ref.at[0], x_ref.at[1], w_ref, cos_ref, sin_ref, qn_ref, qc_ref, att_ref, lse_ref, *work)

    @pl.when(head == 5)
    def _():
        save(0).wait()
        save(1).wait()
        keep_w.wait()
        for j in range(3):
            give(j).wait_send()
        give_out.wait()


CHUNKS = LEN // TILE
HALF = LEN // 2


def chunk(i):
    return slice(i * TILE, (i + 1) * TILE)


def anywhere():
    return pl.BlockSpec(memory_space=pl.ANY)


def in_vmem():
    return pl.BlockSpec(memory_space=pltpu.VMEM)


def dma(n):
    return pltpu.SemaphoreType.DMA((n,))


def rows_of(n):
    return jax.ShapeDtypeStruct((n, D), BF)


attend_work = [
    pltpu.VMEM((TILE, TILE), F32),
    pltpu.VMEM((TILE, TILE), F32),
    pltpu.VMEM((LEN, HD), BF),
    pltpu.VMEM((LEN, HD), BF),
    pltpu.VMEM((HD, LEN), BF),
    pltpu.VMEM((HD, LEN), BF),
]
rows_shape = jax.ShapeDtypeStruct((LEN, D), BF)


def attend(size, noisy, clean, w, wo, gains, cos, sin):
    return pl.pallas_call(
        attend_kernel,
        grid=(6,),
        in_specs=[pl.BlockSpec(memory_space=pltpu.SMEM)] + [anywhere()] * 4
        + [whole((2, D)), whole((LEN, 128)), whole((LEN, 128))],
        out_specs=[pl.BlockSpec((LEN, SLOT), lane2), pl.BlockSpec((LEN, SLOT), lane2), whole((6 * HD, LEN)),
                   pl.BlockSpec((1, 8, LEN), row3)] + [anywhere()] * 4,
        out_shape=[jax.ShapeDtypeStruct((LEN, SLOT * 6), BF), jax.ShapeDtypeStruct((LEN, SLOT * 6), BF),
                   jax.ShapeDtypeStruct((6 * HD, LEN), BF), jax.ShapeDtypeStruct((6, 8, LEN), F32),
                   rows_shape, rows_shape, rows_of(9 * HD), rows_of(3 * HD)],
        scratch_shapes=[pltpu.VMEM((2, LEN, D), BF), pltpu.VMEM((2, LEN, D), BF), pltpu.VMEM((18 * HD, D), BF),
                        dma(2 * CHUNKS + 1), dma(3), dma(4), dma(4)] + attend_work,
        compiler_params=pltpu.CompilerParams(collective_id=6, has_side_effects=True, vmem_limit_bytes=60 << 20),
        name="attend",
    )(size, noisy, clean, w, wo, gains, cos, sin)


WIDE = 5 * 128


def back_head(head, qn_ref, qc_ref, lse_ref, cos_ref, sin_ref, av_ref, c_ref,
              bn_ref, bc_ref, kn_ref, kc_ref, knt_ref, kct_ref, dot_ref, do_ref, dq_ref, dkn_ref, dkc_ref, dvc_ref, dvn_ref):
    do_ref[...] = jnp.transpose(dot_ref[pl.ds(pl.multiple_of(head * HD, HD), HD), :])
    kn_ref[...] = qn_ref[:, 64:128]
    kc_ref[...] = qc_ref[:, 64:128]
    knt_ref[...] = jnp.transpose(qn_ref[:, 0:128])[64:128]
    kct_ref[...] = jnp.transpose(qc_ref[:, 0:128])[64:128]
    for i in reversed(range(LEN // TILE)):
        lo, hi = i * TILE, (i + 1) * TILE
        last = i == LEN // TILE - 1
        q = qn_ref[lo:hi, 0:64] * 0.125
        do = do_ref[lo:hi, :]
        lse = lse_ref[0, 0:1, lo:hi]
        spans = [(0, lo, hi), (1, lo, hi)] + ([(1, 0, lo)] if i else [])
        probs, grads, inner = [], [], 0.0
        for n, (side, a, b) in enumerate(spans):
            kr = kc_ref if side else kn_ref
            vr = qc_ref if side else qn_ref
            s = nt(kr[a:b, :], q)
            if n == 0:
                s = s + bn_ref[...]
            if n == 1:
                s = s + bc_ref[...]
            p = jnp.exp(s - lse)
            dp = nt(vr[a:b, 128:192], do)
            inner = inner + jnp.sum(p * dp, axis=0, keepdims=True)
            probs.append(p)
            grads.append(dp)
        dqt = 0.0
        for n, (side, a, b) in enumerate(spans):
            ds = (probs[n] * (grads[n] - inner)).astype(BF)
            dv = nn(probs[n].astype(BF), do)
            dk = nn(ds, q)
            ktr = kct_ref if side else knt_ref
            dqt = dqt + nn(ktr[:, a:b], ds)
            if side and last:
                dkc_ref[a:b, :] = dk
                dvc_ref[a:b, :] = dv
            elif side:
                dkc_ref[a:b, :] += dk
                dvc_ref[a:b, :] += dv
            else:
                dkn_ref[a:b, :] = dk
                dvn_ref[a:b, :] = dv.astype(BF)
        dq_ref[lo:hi, :] = jnp.transpose(dqt) * 0.125
    sin = -sin_ref[...]
    cos = cos_ref[...]
    pair = pl.ds(pl.multiple_of(head * 128, 128), 128)
    av_ref[:, pair] = spin(jnp.concatenate([dq_ref[...], dkn_ref[...]], axis=1), cos, sin).astype(BF)
    both = jnp.concatenate([dkc_ref[...], dvc_ref[...]], axis=1)
    lane = lax.broadcasted_iota(jnp.int32, both.shape, 1)
    c_ref[:, pair] = jnp.where(lane < HD, spin(both, cos, sin), both).astype(BF)
    for j in range(3):
        @pl.when(head == j)
        def _():
            av_ref[:, 384 + HD * j:384 + HD * (j + 1)] = dvn_ref[...]


def group_grad(xn_ref, xc_ref, av, c, gq_ref):
    g = tn(av, xn_ref[...])
    e = tn(c, xc_ref[...])
    for j in range(3):
        row = 3 * HD * j
        gq_ref[row:row + HD, :] = g[128 * j:128 * j + HD].astype(gq_ref.dtype)
        gq_ref[row + HD:row + 2 * HD, :] = (g[128 * j + HD:128 * (j + 1)] + e[128 * j:128 * j + HD]).astype(gq_ref.dtype)
        gq_ref[row + 2 * HD:row + 3 * HD, :] = (
            g[384 + HD * j:384 + HD * (j + 1)] + e[128 * j + HD:128 * (j + 1)]).astype(gq_ref.dtype)


def back_start(size_ref, att_ref, g_ref, wo_ref, go_ref, av_ref, work):
    fill_bias(size_ref[lax.axis_index("mp") // 2], work[0], work[1])
    work[6][...] = nt(wo_ref[...], g_ref[...]).astype(BF)
    go_ref[...] = nn(att_ref[...], g_ref[...]).astype(go_ref.dtype)
    av_ref[:, 576:WIDE] = jnp.zeros((LEN, WIDE - 576), BF)


def back_far_kernel(size_ref, qn_ref, qc_ref, att_ref, lse_ref, g_ref, wo_ref, cos_ref, sin_ref,
                    xn_hbm, xc_hbm, av_ref, c_ref, both_ref, xn_ref, xc_ref, sems, *work):
    head = pl.program_id(0)
    late = [pltpu.make_async_copy(s, d, sems.at[k]) for k, (s, d) in enumerate(((xn_hbm, xn_ref), (xc_hbm, xc_ref)))]

    @pl.when(head == 0)
    def _():
        for c in late:
            c.start()
        back_start(size_ref, att_ref, g_ref, wo_ref, both_ref.at[9 * HD:], av_ref, work)

    back_head(head, qn_ref, qc_ref, lse_ref, cos_ref, sin_ref, av_ref, c_ref, *work)

    @pl.when(head == 2)
    def _():
        for c in late:
            c.wait()
        group_grad(xn_ref, xc_ref, av_ref[...], c_ref[...], both_ref)


def back_near_kernel(size_ref, qn_ref, qc_ref, att_ref, lse_ref, g_ref, wo_ref, cos_ref, sin_ref,
                     xn_hbm, xc_hbm, w_hbm, w_far_hbm, avf_hbm, cf_hbm, gxn_hbm, gxc_hbm, gq_ref, go_ref,
                     xn_ref, xc_ref, wav_ref, wc_ref, av_ref, c_ref, out_ref, sems, sem_w, sem_out, *work):
    head = pl.program_id(0)
    late = [pltpu.make_async_copy(s, d, sems.at[k]) for k, (s, d) in enumerate((
        (xn_hbm, xn_ref), (xc_hbm, xc_ref), (avf_hbm, av_ref.at[:, WIDE:]), (cf_hbm, c_ref.at[:, 384:])))]
    for n, src in enumerate((w_hbm, w_far_hbm)):
        for j in range(3):
            row, base, k = 192 * j, WIDE * n, 3 * (3 * n + j)
            late.append(pltpu.make_async_copy(
                src.at[row:row + 128], wav_ref.at[base + 128 * j:base + 128 * (j + 1)], sem_w.at[k]))
            late.append(pltpu.make_async_copy(
                src.at[row + 128:row + 192], wav_ref.at[base + 384 + 64 * j:base + 448 + 64 * j], sem_w.at[k + 1]))
            late.append(pltpu.make_async_copy(
                src.at[row + 64:row + 192], wc_ref.at[384 * n + 128 * j:384 * n + 128 * (j + 1)], sem_w.at[k + 2]))

    @pl.when(head == 0)
    def _():
        for c in late:
            c.start()
        for n in range(2):
            wav_ref[WIDE * n + 576:WIDE * (n + 1), :] = jnp.zeros((WIDE - 576, D), BF)
        back_start(size_ref, att_ref, g_ref, wo_ref, go_ref, av_ref, work)

    back_head(head, qn_ref, qc_ref, lse_ref, cos_ref, sin_ref, av_ref, c_ref, *work)

    @pl.when(head == 2)
    def _():
        for c in late:
            c.wait()
        copies = []
        for s, (rows, w, out) in enumerate(((av_ref, wav_ref, gxn_hbm), (c_ref, wc_ref, gxc_hbm))):
            for i in range(CHUNKS):
                out_ref[s, chunk(i), :] = nn(rows[chunk(i), :], w[...]).astype(BF)
                copies.append(pltpu.make_async_copy(
                    out_ref.at[s, chunk(i)], out.at[chunk(i)], sem_out.at[CHUNKS * s + i]))
                copies[-1].start()
        group_grad(xn_ref, xc_ref, av_ref[:, :WIDE], c_ref[:, :384], gq_ref)
        for c in copies:
            c.wait()


back_work = attend_work[:4] + [
    pltpu.VMEM((HD, LEN), BF),
    pltpu.VMEM((HD, LEN), BF),
    pltpu.VMEM((3 * HD, LEN), BF),
    pltpu.VMEM((LEN, HD), BF),
    pltpu.VMEM((LEN, HD), F32),
    pltpu.VMEM((LEN, HD), F32),
    pltpu.VMEM((LEN, HD), F32),
    pltpu.VMEM((LEN, HD), F32),
    pltpu.VMEM((LEN, HD), BF),
]
def head_inputs(first):
    return [pl.BlockSpec((LEN, SLOT), lambda h, *_: (0, h + first)), pl.BlockSpec((LEN, SLOT), lambda h, *_: (0, h + first)),
            pl.BlockSpec((3 * HD, LEN), lambda h, *_: (first // 3, 0), pipeline_mode=pl.Buffered(1)),
            pl.BlockSpec((1, 8, LEN), lambda h, *_: (h + first, 0, 0))]


def back_far(size, qn, qc, att, lse, g, wo, cos, sin, xn, xc):
    return pl.pallas_call(
        back_far_kernel,
        grid=(3,),
        in_specs=[pl.BlockSpec(memory_space=pltpu.SMEM)] + head_inputs(3)
        + [whole((LEN, D)), whole((3 * HD, D)), whole((LEN, 128)), whole((LEN, 128)), anywhere(), anywhere()],
        out_specs=[whole((LEN, WIDE)), whole((LEN, 384)), whole((D, D))],
        out_shape=[jax.ShapeDtypeStruct((LEN, WIDE), BF), jax.ShapeDtypeStruct((LEN, 384), BF), rows_of(D)],
        scratch_shapes=[pltpu.VMEM((LEN, D), BF), pltpu.VMEM((LEN, D), BF), dma(2)] + back_work,
        compiler_params=pltpu.CompilerParams(vmem_limit_bytes=60 << 20),
        name="back_far",
    )(size, qn, qc, att, lse, g, wo, cos, sin, xn, xc)


def back_near(size, qn, qc, att, lse, g, wo, cos, sin, xn, xc, w, w_far, av_far, c_far):
    return pl.pallas_call(
        back_near_kernel,
        grid=(3,),
        in_specs=[pl.BlockSpec(memory_space=pltpu.SMEM)] + head_inputs(0)
        + [whole((LEN, D)), whole((3 * HD, D)), whole((LEN, 128)), whole((LEN, 128))] + [anywhere()] * 6,
        out_specs=[anywhere(), anywhere(), whole((9 * HD, D)), whole((3 * HD, D))],
        out_shape=[rows_shape, rows_shape, jax.ShapeDtypeStruct((9 * HD, D), F32), jax.ShapeDtypeStruct((3 * HD, D), F32)],
        scratch_shapes=[pltpu.VMEM((LEN, D), BF), pltpu.VMEM((LEN, D), BF), pltpu.VMEM((2 * WIDE, D), BF), pltpu.VMEM((D, D), BF),
                        pltpu.VMEM((LEN, 2 * WIDE), BF), pltpu.VMEM((LEN, D), BF), pltpu.VMEM((2, LEN, D), BF),
                        dma(4), dma(18), dma(2 * CHUNKS)] + back_work,
        compiler_params=pltpu.CompilerParams(vmem_limit_bytes=60 << 20),
        name="back_near",
    )(size, qn, qc, att, lse, g, wo, cos, sin, xn, xc, w, w_far, av_far, c_far)


def halves(v):
    high = v.astype(BF)
    return high, (v - high.astype(F32)).astype(BF)


def exact(left_side, right_side, left_dim, right_dim):
    dims = (((left_dim,), (right_dim,)), ((), ()))
    a, b = halves(left_side)
    c, d = halves(right_side)

    def times(x, y):
        return lax.dot_general(x, y, dims, preferred_element_type=F32)

    return times(a, c) + (times(a, d) + times(b, c))


def core_peer():
    m = lax.axis_index("mp")
    return (lax.axis_index("dp"), m + 1 - 2 * lax.rem(m, 2))


def far_peer():
    return (lax.axis_index("dp"), lax.rem(lax.axis_index("mp") + 2, 4))


def greet(*peers):
    barrier = pltpu.get_barrier_semaphore()
    for p in peers:
        pl.semaphore_signal(barrier, inc=1, device_id=p, device_id_type=MESH_ID)
    pl.semaphore_wait(barrier, len(peers))


PARTS = HALF // TILE


def own_rows(i):
    half = lax.rem(lax.axis_index("mp"), 2)
    return pl.ds(pl.multiple_of(half * HALF + i * TILE, TILE), TILE)


def peer_rows(i):
    half = lax.rem(lax.axis_index("mp"), 2)
    return pl.ds(pl.multiple_of((1 - half) * HALF + i * TILE, TILE), TILE)


def side_rows_of(i):
    m = lax.axis_index("mp")
    return pl.ds(pl.multiple_of(m * HALF + i * TILE, TILE), TILE)


def copy(src, dst, sem):
    return pltpu.make_async_copy(src, dst, sem)


def push(src, dst, send_sem, recv_sem, peer):
    return pltpu.make_async_remote_copy(
        src_ref=src, dst_ref=dst, send_sem=send_sem, recv_sem=recv_sem, device_id=peer, device_id_type=MESH_ID)


class Sems:
    def __init__(self, ref):
        self.ref = ref
        self.used = 0

    def take(self):
        self.used += 1
        return self.ref.at[self.used - 1]


def middle_kernel(att_hbm, wo_near_hbm, wo_far_hbm, rows_hbm, cot_hbm, up_hbm, down_hbm,
                  err_up_hbm, err_down_hbm, fac_up_ref, fac_down_ref, gain_ref,
                  res_hbm, grad_hbm, low_hbm, mlp_hbm, fold_hbm, mat_up_hbm, mat_down_hbm,
                  left_up_ref, left_down_ref, gsum_ref,
                  att_ref, wo_ref, x_ref, send_ref, far_ref, r_ref, nm_ref, cot_ref, up_ref, down_ref, hid_ref, gp_ref,
                  mlp_ref, gm_ref, back_ref, fold_gm_ref, fold_mlp_ref, sum_ref, msum_ref, yet_ref,
                  mat_up_ref, mat_down_ref, nmt_ref, grad_ref, low_ref, sem_ref, send_sem_ref, recv_sem_ref):
    sems, sends, recvs = Sems(sem_ref), Sems(send_sem_ref), Sems(recv_sem_ref)
    m = lax.axis_index("mp")
    side, half = m // 2, lax.rem(m, 2)
    core, far = core_peer(), far_peer()
    width = 3 * HD
    third = D // 3
    pushes, saves = [], []

    def load(src, dst):
        c = pltpu.make_async_copy(src, dst, sems.take())
        c.start()
        return c

    def save(src, dst):
        saves.append(load(src, dst))

    def send(src, dst, peer):
        c = push(src, dst, sends.take(), recvs.take(), peer)
        c.start()
        pushes.append(c)
        return c

    def span(start, n):
        return pl.ds(pl.multiple_of(start, TILE), n)

    own_half, peer_half = half * HALF, (1 - half) * HALF
    first = [load(att_hbm, att_ref), load(wo_near_hbm, wo_ref.at[0:width]), load(wo_far_hbm, wo_ref.at[width:])]
    xs = [load(rows_hbm.at[span(m * HALF + i * TILE, TILE)], x_ref.at[chunk(i)]) for i in range(PARTS)]
    up_in, down_in = load(up_hbm, up_ref), load(down_hbm, down_ref)
    cot_in = load(cot_hbm.at[span(side * LEN, LEN)], cot_ref.at[0:LEN])
    cot_far_in = load(cot_hbm.at[span((1 - side) * LEN, LEN)], cot_ref.at[LEN:])
    err_in = [load(err_down_hbm.at[0], mat_down_ref), load(err_up_hbm.at[0], mat_up_ref)]
    greet(core, far)
    for c in first:
        c.wait()
    parts = []
    for i in range(PARTS):
        send_ref[chunk(i), :] = tn(att_ref[:, span(peer_half + i * TILE, TILE)], wo_ref[...]).astype(BF)
        parts.append(send(send_ref.at[chunk(i)], far_ref.at[chunk(i)], core))
    normed, cross = [], []
    for i in range(PARTS):
        at = span(own_half + i * TILE, TILE)
        own = tn(att_ref[:, at], wo_ref[...])
        xs[i].wait()
        parts[i].wait_recv()
        r = x_ref[chunk(i), :].astype(F32) + (own + far_ref[chunk(i), :].astype(F32))
        r_ref[chunk(i), :] = r
        nm_ref[at, :] = (norm_parts(r)[0] * gain_ref[1:2, :]).astype(BF)
        normed.append(send(nm_ref.at[at], nm_ref.at[at], core))
        cross.append(send(nm_ref.at[at], nm_ref.at[span(LEN + own_half + i * TILE, TILE)], far))
        save(r_ref.at[chunk(i)], res_hbm.at[chunk(i)])

    def feed_rows(start, n):
        at = span(start, n)
        for t in range(3):
            lanes = slice(t * third, (t + 1) * third)
            hidden, slope = gelu_and_slope(nn(nm_ref[at, :], up_ref[:, lanes]))
            hid_ref[at, lanes] = hidden.astype(BF)
            gp_ref[at, lanes] = (slope * nt(cot_ref[at, :], down_ref[lanes, :])).astype(BF)
        gm_ref[at, :] = nt(gp_ref[at, :], up_ref[...]).astype(BF)
        mlp_ref[at, :] = nn(hid_ref[at, :], down_ref[...]).astype(BF)

    up_in.wait()
    down_in.wait()
    cot_in.wait()
    feed_rows(own_half, HALF)
    for c in normed:
        c.wait_recv()
    feed_rows(peer_half, HALF)
    save(mlp_ref.at[0:LEN], mlp_hbm)
    swap = [send(gm_ref.at[span(peer_half + i * TILE, TILE)], back_ref.at[chunk(i)], core) for i in range(PARTS)]
    cot_far_in.wait()
    arrived = []
    for i in range(PARTS):
        at = span(LEN + own_half + i * TILE, TILE)
        away = span(LEN + peer_half + i * TILE, TILE)
        cross[i].wait_recv()
        relay = send(nm_ref.at[at], nm_ref.at[at], core)
        feed_rows(LEN + own_half + i * TILE, TILE)
        relay.wait_recv()
        feed_rows(LEN + peer_half + i * TILE, TILE)
        fold = send(gm_ref.at[away], fold_gm_ref.at[chunk(i)], core)
        fold_mlp = send(mlp_ref.at[away], fold_mlp_ref.at[chunk(i)], core)
        fold.wait_recv()
        sum_ref[chunk(i), :] = (gm_ref[at, :].astype(F32) + fold_gm_ref[chunk(i), :].astype(F32)).astype(BF)
        arrived.append(send(sum_ref.at[chunk(i)], yet_ref.at[chunk(i)], far))
        fold_mlp.wait_recv()
        msum_ref[chunk(i), :] = (mlp_ref[at, :].astype(F32) + fold_mlp_ref[chunk(i), :].astype(F32)).astype(BF)
        save(msum_ref.at[chunk(i)], fold_hbm.at[chunk(i)])

    for i in range(8):
        at = slice(i * TILE, (i + 1) * TILE)
        nmt_ref[:, at] = jnp.transpose(nm_ref[at, :])
    for c in err_in:
        c.wait()
    left_up = 0.0
    for t in range(3):
        lanes = slice(t * third, (t + 1) * third)
        mat = tn(hid_ref[:, lanes], cot_ref[...]) + mat_down_ref[lanes, :]
        mat_down_ref[lanes, :] = mat
        save(mat_down_ref.at[lanes], mat_down_hbm.at[lanes])
        left_down_ref[:, lanes] = exact(fac_down_ref[...], mat, 1, 1)
        mat = nn(nmt_ref[...], gp_ref[:, lanes]) + mat_up_ref[:, lanes]
        mat_up_ref[:, lanes] = mat
        save(mat_up_ref.at[:, lanes], mat_up_hbm.at[:, lanes])
        left_up = left_up + exact(fac_up_ref[:, lanes], mat, 1, 1)
    left_up_ref[...] = left_up

    gsum = 0.0
    lows = []
    for i in range(PARTS):
        at = span(own_half + i * TILE, TILE)
        swap[i].wait_recv()
        total = gm_ref[at, :].astype(F32) + back_ref[chunk(i), :].astype(F32)
        arrived[i].wait_recv()
        total = total + yet_ref[chunk(i), :].astype(F32)
        grad, share = norm_back(r_ref[chunk(i), :], gain_ref[1:2, :], total)
        gsum = gsum + share
        grad = cot_ref[at, :].astype(F32) + grad
        grad_ref[chunk(i), :] = grad
        low_ref[chunk(i), :] = grad.astype(BF)
        lows.append(send(low_ref.at[chunk(i)], low_hbm.at[at], core))
        save(low_ref.at[chunk(i)], low_hbm.at[at])
        save(grad_ref.at[chunk(i)], grad_hbm.at[chunk(i)])
    gsum_ref[...] = gsum
    for c in lows:
        c.wait_recv()
    for c in pushes:
        c.wait_send()
    for c in saves:
        c.wait()


def middle(att, wo_near, wo_far, rows, cotangent, up, down, err_up, err_down, fac_up, fac_down, gains):
    def low(n):
        return pltpu.VMEM((n, D), BF)

    def wide(n):
        return pltpu.VMEM((n, D), F32)

    return pl.pallas_call(
        middle_kernel,
        in_specs=[anywhere()] * 9 + [in_vmem()] * 3,
        out_specs=[anywhere()] * 7 + [in_vmem()] * 3,
        out_shape=[jax.ShapeDtypeStruct((HALF, D), F32), jax.ShapeDtypeStruct((HALF, D), F32), rows_of(LEN), rows_of(LEN),
                   rows_of(HALF), jax.ShapeDtypeStruct((D, D), F32), jax.ShapeDtypeStruct((D, D), F32),
                   jax.ShapeDtypeStruct((RANK, D), F32), jax.ShapeDtypeStruct((RANK, D), F32),
                   jax.ShapeDtypeStruct((1, D), F32)],
        scratch_shapes=[pltpu.VMEM((6 * HD, LEN), BF), low(6 * HD), low(HALF), low(HALF), low(HALF), wide(HALF),
                        low(2 * LEN), low(2 * LEN), low(D), low(D), low(2 * LEN), low(2 * LEN),
                        low(2 * LEN), low(2 * LEN), low(HALF), low(HALF), low(HALF), low(HALF), low(HALF), low(HALF),
                        wide(D), wide(D), pltpu.VMEM((D, 2 * LEN), BF), wide(HALF), low(HALF), dma(32), dma(24), dma(24)],
        compiler_params=pltpu.CompilerParams(collective_id=3, has_side_effects=True, vmem_limit_bytes=60 << 20),
        name="middle",
    )(att, wo_near, wo_far, rows, cotangent, up, down, err_up, err_down, fac_up, fac_down, gains)


def settle_kernel(mlp_hbm, far_hbm, res_hbm, out_hbm, own_ref, far_ref, res_ref, core_ref, out_ref,
                  sem_in, sem_send, sem_recv, sem_out):
    peer = core_peer()
    loads = []
    for i in range(PARTS):
        loads += [copy(mlp_hbm.at[own_rows(i)], own_ref.at[chunk(i)], sem_in.at[3 * i]),
                  copy(far_hbm.at[chunk(i)], far_ref.at[chunk(i)], sem_in.at[3 * i + 1]),
                  copy(res_hbm.at[chunk(i)], res_ref.at[chunk(i)], sem_in.at[3 * i + 2])]
    for c in loads:
        c.start()
    greet(peer)
    pushes = [push(mlp_hbm.at[peer_rows(i)], core_ref.at[chunk(i)], sem_send.at[i], sem_recv.at[i], peer)
              for i in range(PARTS)]
    for c in pushes:
        c.start()
    saves = []
    for i in range(PARTS):
        for c in loads[3 * i:3 * i + 3]:
            c.wait()
        pushes[i].wait_recv()
        total = own_ref[chunk(i), :].astype(F32) + core_ref[chunk(i), :].astype(F32) + far_ref[chunk(i), :].astype(F32)
        out_ref[chunk(i), :] = (res_ref[chunk(i), :] + total).astype(BF)
        saves.append(copy(out_ref.at[chunk(i)], out_hbm.at[chunk(i)], sem_out.at[i]))
        saves[-1].start()
    for c in saves:
        c.wait()
    for c in pushes:
        c.wait_send()


def settle(mlp, far, residual):
    half = pltpu.VMEM((HALF, D), BF)
    return pl.pallas_call(
        settle_kernel,
        in_specs=[anywhere()] * 3,
        out_specs=anywhere(),
        out_shape=rows_of(HALF),
        scratch_shapes=[half, half, pltpu.VMEM((HALF, D), F32), half, half, dma(3 * PARTS), dma(PARTS), dma(PARTS), dma(PARTS)],
        compiler_params=pltpu.CompilerParams(collective_id=4, has_side_effects=True, vmem_limit_bytes=60 << 20),
        name="settle",
    )(mlp, far, residual)


def finish_kernel(gxn_hbm, gxc_hbm, noisy_hbm, clean_hbm, grad_hbm, gain_ref, gain_two_ref, ends_hbm, gsum_ref,
                  own_ref, far_ref, x_ref, wide_ref, out_ref,
                  sem_own, sem_x, sem_wide, sem_send, sem_recv, sem_out):
    sources = (gxn_hbm, gxc_hbm)
    count = 2 * PARTS
    own, rows, wide = [], [], []
    for n in range(count):
        k, i = n // PARTS, n % PARTS
        own.append(copy(sources[k].at[own_rows(i)], own_ref.at[chunk(n)], sem_own.at[n]))
        rows.append(copy((noisy_hbm, clean_hbm)[k].at[side_rows_of(i)], x_ref.at[chunk(n)], sem_x.at[n]))
        if k == 0:
            wide.append(copy(grad_hbm.at[chunk(i)], wide_ref.at[chunk(i)], sem_wide.at[i]))
    for c in own + rows + wide:
        c.start()
    peer = core_peer()
    greet(peer)
    pushes = []
    for n in range(count):
        k, i = n // PARTS, n % PARTS
        pushes.append(push(sources[k].at[peer_rows(i)], far_ref.at[chunk(n)], sem_send.at[n], sem_recv.at[n], peer))
        pushes[-1].start()
    gsum = 0.0
    saves = []
    for n in range(count):
        k, i = n // PARTS, n % PARTS
        own[n].wait()
        rows[n].wait()
        pushes[n].wait_recv()
        total = own_ref[chunk(n), :].astype(F32) + far_ref[chunk(n), :].astype(F32)
        grad, share = norm_back(x_ref[chunk(n), :].astype(F32), gain_ref[0:1, :], total)
        gsum = gsum + share
        if k == 0:
            wide[i].wait()
            grad = wide_ref[chunk(i), :] + grad
        out_ref[chunk(n), :] = grad.astype(BF)
        saves.append(copy(out_ref.at[chunk(n)], ends_hbm.at[chunk(n)], sem_out.at[n]))
        saves[-1].start()
    gsum_ref[0:1, :] = gsum
    gsum_ref[1:2, :] = gain_two_ref[...]
    gsum_ref[2:8, :] = jnp.zeros((6, D), F32)
    for c in saves:
        c.wait()
    for c in pushes:
        c.wait_send()


def finish(gxn, gxc, noisy_rows, clean_rows, grad_resid, gains, gain_two):
    buf = pltpu.VMEM((LEN, D), BF)
    return pl.pallas_call(
        finish_kernel,
        in_specs=[anywhere()] * 5 + [in_vmem()] * 2,
        out_specs=[anywhere(), in_vmem()],
        out_shape=[rows_of(LEN), jax.ShapeDtypeStruct((RANK, D), F32)],
        scratch_shapes=[buf, buf, buf, pltpu.VMEM((HALF, D), F32), buf,
                        dma(2 * PARTS), dma(2 * PARTS), dma(PARTS), dma(2 * PARTS), dma(2 * PARTS), dma(2 * PARTS)],
        compiler_params=pltpu.CompilerParams(collective_id=5, has_side_effects=True, vmem_limit_bytes=60 << 20),
        name="finish",
    )(gxn, gxc, noisy_rows, clean_rows, grad_resid, gains, gain_two)


def place_kernel(plan, given, count, *refs):
    sources, outs = refs[:given], refs[len(refs) - 3 - count:len(refs) - 3]
    stage, sem_in, sem_out = refs[len(refs) - 3:]
    m = lax.axis_index("mp")
    beside = m + 1 - 2 * lax.rem(m, 2)
    spots = (m, beside, lax.rem(m + 2, 4), lax.rem(beside + 2, 4))
    loads = [copy(sources[s].at[part * HALF:(part + 1) * HALF], stage.at[j], sem_in.at[j])
             for j, (s, part, _, _) in enumerate(plan)]
    for c in loads:
        c.start()
    saves = []
    for j, (_, _, target, spot) in enumerate(plan):
        loads[j].wait()
        at = pl.ds(pl.multiple_of(spots[spot] * HALF, HALF), HALF)
        saves.append(copy(stage.at[j], outs[target].at[at], sem_out.at[j]))
        saves[-1].start()
    for c in saves:
        c.wait()


def place(plan, count, *pieces, onto=()):
    total, given = len(plan), len(pieces)
    return pl.pallas_call(
        functools.partial(place_kernel, plan, given, count),
        in_specs=[anywhere()] * (given + len(onto)),
        out_specs=[anywhere()] * count,
        out_shape=[rows_of(2 * LEN)] * count,
        scratch_shapes=[pltpu.VMEM((total, HALF, D), BF), dma(total), dma(total)],
        input_output_aliases={given + k: k for k in range(len(onto))},
        compiler_params=pltpu.CompilerParams(vmem_limit_bytes=14 << 20),
        name="place",
    )(*pieces, *onto)


PACK = 1024


def left_products(gq, both_ref, eq, go, eo, fq_ref, fo_ref, lu_ref, ld_ref, gain_ref, mq_ref, mo_ref, pack_ref):
    pack_ref[...] = jnp.zeros_like(pack_ref)
    mq = gq + both_ref[:9 * HD, :].astype(F32) + eq
    mq_ref[...] = mq
    pack_ref[0:8, 0:D] = exact(fq_ref[...], mq, 1, 0)
    mo = go + both_ref[9 * HD:, :].astype(F32) + eo
    mo_ref[...] = mo
    pack_ref[0:8, D:D + 3 * HD] = exact(fo_ref[...], mo, 1, 1)
    pack_ref[8:16, 0:D] = lu_ref[...]
    pack_ref[16:24, 0:D] = ld_ref[...]
    for k in range(6):
        pack_ref[8 + k:9 + k, D:PACK] = gain_ref[k // 3:k // 3 + 1, 256 * (k % 3):256 * (k % 3 + 1)]


def lefts_kernel(gq_ref, both_ref, eq_ref, go_ref, eo_ref, fq_ref, fo_ref, lu_ref, ld_ref, gain_ref,
                 mq_ref, mo_ref, pack_ref):
    left_products(gq_ref[...], both_ref, eq_ref[0], go_ref[...], eo_ref[0], fq_ref, fo_ref, lu_ref, ld_ref, gain_ref,
                  mq_ref, mo_ref, pack_ref)


def lefts(*args):
    return pl.pallas_call(
        lefts_kernel,
        grid=(1,),
        in_specs=[whole(v.shape) for v in args],
        out_specs=[whole((9 * HD, D)), whole((3 * HD, D)), whole((3 * RANK, PACK))],
        out_shape=[jax.ShapeDtypeStruct((9 * HD, D), F32), jax.ShapeDtypeStruct((3 * HD, D), F32),
                   jax.ShapeDtypeStruct((3 * RANK, PACK), F32)],
        compiler_params=pltpu.CompilerParams(vmem_limit_bytes=60 << 20),
        name="lefts",
    )(*args)


def orthonormalize(sum_ref):
    mats = [sum_ref[0:8, 0:D], sum_ref[0:8, D:PACK], sum_ref[8:16, 0:D], sum_ref[16:24, 0:D]]
    for k in range(RANK):
        for t in range(4):
            a = mats[t]
            row = lax.broadcasted_iota(jnp.int32, a.shape, 0)
            v = a[k:k + 1, :]
            e = v / (jnp.sqrt(jnp.sum(v * v, axis=1, keepdims=True)) + 1e-08)
            c = jnp.sum(a * e, axis=1, keepdims=True)
            mats[t] = jnp.where(row == k, e, jnp.where(row > k, a - c * e, a))
    mats[1] = mats[1][:, :3 * HD]
    return mats


def right_products(hats, mq_ref, mo_ref, mu_ref, md_ref, pack_ref):
    out = exact(hats[1], mo_ref[...], 1, 0)
    pack_ref[0:8, 0:D] = exact(hats[2], mu_ref[...], 1, 0)
    pack_ref[8:16, 0:D] = exact(hats[3], md_ref[...], 1, 0)
    pack_ref[16:24, 0:D] = jnp.zeros((RANK, D), F32)
    pack_ref[16:24, 0:9 * HD] = exact(hats[0], mq_ref[...], 1, 1)
    for k in range(3):
        pack_ref[8 * k:8 * k + 8, D:PACK] = out[:, 256 * k:256 * (k + 1)]


def unpack_rights(pack_ref):
    out = jnp.concatenate([pack_ref[8 * k:8 * k + 8, D:PACK] for k in range(3)], axis=1)
    return [pack_ref[16:24, 0:9 * HD], out, pack_ref[0:8, 0:D], pack_ref[8:16, 0:D]]


def rights_kernel(sum_ref, mq_ref, mo_ref, mu_ref, md_ref, hq_ref, ho_ref, hu_ref, hd_ref, pack_ref):
    hats = orthonormalize(sum_ref)
    for hat, ref in zip(hats, (hq_ref, ho_ref, hu_ref, hd_ref)):
        ref[...] = hat
    right_products(hats, mq_ref, mo_ref, mu_ref, md_ref, pack_ref)


def rights(left_sum, mats):
    args = (left_sum, *mats)
    shapes = [(RANK, D), (RANK, 3 * HD), (RANK, D), (RANK, D), (3 * RANK, PACK)]
    return pl.pallas_call(
        rights_kernel,
        grid=(1,),
        in_specs=[whole(v.shape) for v in args],
        out_specs=[whole(s) for s in shapes],
        out_shape=[jax.ShapeDtypeStruct(s, F32) for s in shapes],
        compiler_params=pltpu.CompilerParams(vmem_limit_bytes=60 << 20),
        name="rights",
    )(*args)


def reduce_kernel(count, gq_hbm, both_hbm, eq_hbm, go_hbm, eo_hbm, mu_hbm, md_hbm, fq_ref, fo_ref, lu_ref, ld_ref, gain_ref,
                  mq_hbm, mo_hbm, hat_ref, right_ref, gsum_ref,
                  gq_ref, both_ref, mq_ref, go_ref, mo_ref, mu_ref, md_ref, x_ref, sum_ref, in_a, y_ref, in_b, slot_ref,
                  sem_ref, send_ref, recv_ref):
    me = lax.axis_index("dp")
    m = lax.axis_index("mp")
    sends, recvs = Sems(send_ref), Sems(recv_ref)
    loads = [copy(s, d, sem_ref.at[k]) for k, (s, d) in enumerate((
        (gq_hbm, gq_ref), (both_hbm, both_ref), (eq_hbm.at[0], mq_ref), (go_hbm, go_ref), (eo_hbm.at[0], mo_ref),
        (mu_hbm, mu_ref), (md_hbm, md_ref)))]
    for c in loads:
        c.start()
    barrier = pltpu.get_barrier_semaphore()
    for k in range(1, count):
        pl.semaphore_signal(barrier, inc=1, device_id=(lax.rem(me + k, count), m), device_id_type=MESH_ID)
    pl.semaphore_signal(barrier, inc=1, device_id=core_peer(), device_id_type=MESH_ID)
    pl.semaphore_wait(barrier, count)

    def lanes(j):
        return pl.ds(pl.multiple_of(j * 128, 128), 128)

    def spread_sum(src_ref, box_ref, out_ref):
        gather, scatter = [], []
        for k in range(1, count):
            j = lax.rem(me + k, count)
            gather.append(push(src_ref.at[:, lanes(j)], box_ref.at[k], sends.take(), recvs.take(), (j, m)))
        for c in gather:
            c.start()
        total = src_ref[:, lanes(me)]
        for k in range(1, count):
            gather[k - 1].wait_recv()
            total = total + box_ref[k]
        out_ref[:, lanes(me)] = total
        for k in range(1, count):
            j = lax.rem(me + k, count)
            scatter.append(push(out_ref.at[:, lanes(me)], out_ref.at[:, lanes(me)], sends.take(), recvs.take(), (j, m)))
            scatter[-1].start()
        for k in range(1, count):
            scatter[k - 1].wait_recv()
        return gather + scatter

    for c in loads[:5]:
        c.wait()
    left_products(gq_ref[...], both_ref, mq_ref[...], go_ref[...], mo_ref[...], fq_ref, fo_ref, lu_ref, ld_ref, gain_ref,
                  mq_ref, mo_ref, x_ref)
    saves = [copy(mq_ref, mq_hbm, sem_ref.at[7]), copy(mo_ref, mo_hbm, sem_ref.at[8])]
    for c in saves:
        c.start()
    sent = spread_sum(x_ref, in_a, sum_ref)
    share = push(sum_ref.at[8:16, D:PACK], slot_ref, sends.take(), recvs.take(), core_peer())
    share.start()
    hats = orthonormalize(sum_ref)
    hat_ref[...] = jnp.zeros_like(hat_ref)
    for t in range(4):
        hat_ref[RANK * t:RANK * (t + 1), 0:hats[t].shape[1]] = hats[t]
    for c in loads[5:]:
        c.wait()
    right_products(hats, mq_ref, mo_ref, mu_ref, md_ref, y_ref)
    sent += spread_sum(y_ref, in_b, right_ref)
    share.wait()
    gsum_ref[...] = sum_ref[8:16, D:PACK] + slot_ref[...]
    for c in sent:
        c.wait_send()
    for c in saves:
        c.wait()


def reduce_factors(gq, both, err_qkv, go, err_out, mat_up, mat_down, *small):
    count = lax.axis_size("dp")
    if count != 8:
        mq, mo, pack = lefts(gq, both, err_qkv, go, err_out, *small)
        total = lax.psum(pack, "dp")
        *hats, pack = rights(total, (mq, mo, mat_up, mat_down))
        hats[1] = jnp.pad(hats[1], ((0, 0), (0, D - 3 * HD)))
        share = total[8:16, D:PACK]
        share = share + lax.ppermute(share, "mp", [(0, 1), (1, 0), (2, 3), (3, 2)])
        return mq, mo, jnp.concatenate(hats, axis=0), lax.psum(pack, "dp"), share

    def wide(n):
        return pltpu.VMEM((n, D), F32)

    links = 4 * (count - 1) + 1
    return pl.pallas_call(
        functools.partial(reduce_kernel, count),
        in_specs=[anywhere()] * 7 + [in_vmem()] * 5,
        out_specs=[anywhere()] * 2 + [in_vmem()] * 3,
        out_shape=[jax.ShapeDtypeStruct(s, F32) for s in ((9 * HD, D), (3 * HD, D), (4 * RANK, D), (3 * RANK, PACK), (RANK, PACK - D))],
        scratch_shapes=[wide(9 * HD), pltpu.VMEM((D, D), BF), wide(9 * HD), wide(3 * HD), wide(3 * HD), wide(D), wide(D),
                        pltpu.VMEM((3 * RANK, PACK), F32), pltpu.VMEM((3 * RANK, PACK), F32),
                        pltpu.VMEM((count, 3 * RANK, 128), F32), pltpu.VMEM((3 * RANK, PACK), F32),
                        pltpu.VMEM((count, 3 * RANK, 128), F32), pltpu.VMEM((RANK, PACK - D), F32),
                        dma(9), dma(links), dma(links)],
        compiler_params=pltpu.CompilerParams(collective_id=1, has_side_effects=True, vmem_limit_bytes=60 << 20),
        name="reduce_factors",
    )(gq, both, err_qkv, go, err_out, mat_up, mat_down, *small)


def update_kernel(replicas, rates, *refs):
    sums, hats, mats, states = refs[0], refs[1], refs[2:6], refs[6:18]
    errs, news, right_out, hat_out = refs[18:22], refs[22:34], refs[34:38], refs[38:42]
    decay = min(0.9999, (1.0 + EMA_STEPS) / (10.0 + EMA_STEPS))
    share = D // replicas
    shift = lax.rem(D - lax.axis_index("dp") * share, D)

    def part(value):
        return pltpu.roll(value, shift, 1)[:, :share]

    rights_all = unpack_rights(sums)
    for t in range(4):
        hat = hats[RANK * t:RANK * (t + 1), :hat_out[t].shape[1]]
        hat_out[t][...] = hat
        right = rights_all[t] * (1.0 / replicas)
        right_out[t][...] = right
        first, second = ((right, hat), (hat, right), (hat, right), (hat, right))[t]
        errs[t][0] = mats[t][...] - exact(first, second, 0, 0)
        first, second = ((part(hat), right), (hat, part(right)), (part(hat), right), (part(right), hat))[t]
        moment = 0.5 * states[3 * t + 1][...] + exact(first, second, 0, 0)
        master = states[3 * t][...] - rates[t] * moment
        news[3 * t][...] = master
        news[3 * t + 1][...] = moment
        news[3 * t + 2][...] = decay * states[3 * t + 2][...] + (1.0 - decay) * master


def update(replicas, rates, right_sum, hats, mats, states):
    args = (right_sum, hats, *mats, *states)
    shapes = [(1, *m.shape) for m in mats] + [s.shape for s in states]
    shapes += [(RANK, 9 * HD), (RANK, D), (RANK, D), (RANK, D)]
    shapes += [(RANK, D), (RANK, 3 * HD), (RANK, D), (RANK, D)]
    return pl.pallas_call(
        functools.partial(update_kernel, replicas, rates),
        grid=(1,),
        in_specs=[whole(v.shape) for v in args],
        out_specs=[whole(s) for s in shapes],
        out_shape=[jax.ShapeDtypeStruct(s, F32) for s in shapes],
        compiler_params=pltpu.CompilerParams(vmem_limit_bytes=60 << 20),
        name="update",
    )(*args)


def local(
    noisy_rows, clean_rows, block_size, cotangent, norm_gains,
    weight_qkv, weight_out, weight_up, weight_down,
    master_qkv, master_out, master_up, master_down,
    moment_qkv, moment_out, moment_up, moment_down,
    average_qkv, average_out, average_up, average_down,
    error_qkv, error_out, error_up, error_down,
    factor_qkv, factor_out, factor_up, factor_down,
    gain_moment,
):
    row_count = noisy_rows.shape[0]
    replicas = lax.axis_size("dp")

    def across(value):
        return lax.ppermute(value, "mp", [(0, 2), (2, 0), (1, 3), (3, 1)])

    def beside(value):
        return lax.ppermute(value, "mp", [(0, 1), (1, 0), (2, 3), (3, 2)])

    def hold(*values):
        return lax.optimization_barrier(values)

    cos, sin = rotary_tables()
    w_near = weight_qkv.T
    qn, qc, att, lse, xn, xc, w_far, o_far = attend(
        block_size, noisy_rows, clean_rows, w_near, weight_out, norm_gains, cos, sin)
    residual, grad_resid, grad_low, mlp, mlp_fold, matrix_up, matrix_down, left_up, left_down, gain_two = middle(
        att, weight_out, o_far, noisy_rows, cotangent, weight_up, weight_down,
        error_up, error_down, factor_up.T, factor_down.T, norm_gains)
    mlp_far = across(mlp_fold)
    av_far, c_far, grads_far = back_far(block_size, qn, qc, att, lse, grad_low, o_far, cos, sin, xn, xc)
    mlp_far, av_far, grads_far = hold(mlp_far, av_far, grads_far)
    grads_back = across(grads_far)
    out_half = settle(mlp, mlp_far, residual)
    out_half, av_far = hold(out_half, av_far)
    out_far, out_side = across(out_half), beside(out_half)
    grad_xn, grad_xc, gq_near, go_near = back_near(
        block_size, qn, qc, att, lse, grad_low, weight_out, cos, sin, xn, xc, w_near, w_far, av_far, c_far)
    ends, gain_pair = finish(
        grad_xn, grad_xc, noisy_rows, clean_rows, grad_resid, norm_gains, gain_two)
    ends, grads_back = hold(ends, grads_back)
    ends_far = across(ends)
    ends_side = beside(ends)
    matrix_qkv, matrix_out, hats, right_sum, gain_sum = reduce_factors(
        gq_near, grads_back, jnp.swapaxes(error_qkv, 1, 2), go_near, error_out, matrix_up, matrix_down,
        factor_qkv.T, factor_out.T, left_up, left_down, gain_pair)
    mats = (matrix_qkv, matrix_out, matrix_up, matrix_down)
    rates = [3.0 / math.sqrt(f * row_count) for f in (D, HEADS * HD // 64, D, FF)] + [0.5 / math.sqrt(row_count)]
    states = (
        master_qkv, moment_qkv, average_qkv, master_out, moment_out, average_out,
        master_up, moment_up, average_up, master_down.T, moment_down.T, average_down.T,
    )
    done = update(replicas, rates, right_sum, hats, mats, states)
    errs, news, right_new, left_new = done[:4], done[4:16], done[16:20], done[20:24]
    out_far, _ = hold(out_far, hats)
    out_diag = beside(out_far)
    out_diag, _ = hold(out_diag, errs[2])
    block_out, grad_noisy, grad_clean = place(
        [(0, 0, 0, 0), (1, 0, 0, 1), (2, 0, 0, 2), (3, 0, 0, 3), (4, 0, 1, 0), (4, 1, 2, 0), (5, 0, 1, 1), (5, 1, 2, 1)], 3,
        out_half, out_side, out_far, out_diag, ends, ends_side)
    ends_far, grad_noisy, grad_clean = hold(ends_far, grad_noisy, grad_clean)
    ends_diag = beside(ends_far)
    grad_noisy, grad_clean = place(
        [(0, 0, 0, 2), (0, 1, 1, 2), (1, 0, 0, 3), (1, 1, 1, 3)], 2, ends_far, ends_diag, onto=(grad_noisy, grad_clean))
    ends_far, gain_sum = hold(ends_far, gain_sum)
    gain_grad = (gain_sum + across(gain_sum))[:6].reshape(2, D) / replicas
    gain_step = 0.5 * gain_moment + gain_grad
    gains_new = (gain_grad, norm_gains - rates[4] * gain_step, gain_step)
    fresh = [news[3 * t + k] if t < 3 else news[3 * t + k].T for k in range(3) for t in range(4)]
    return (
        block_out, grad_noisy, grad_clean, *gains_new, *fresh,
        jnp.swapaxes(errs[0], 1, 2), *errs[1:], *[v.T for v in left_new], *[v.T for v in right_new],
    )


def solution(mesh):
    in_specs = (
        P("dp", None), P("dp", None), P("dp"), P("dp", None), P(),
        P(None, "mp"), P("mp", None), P(None, "mp"), P("mp", None),
        *([P("dp", "mp"), P("mp", "dp")] * 6),
        *([P("dp", None, "mp"), P("dp", "mp", None)] * 2),
        *([P("mp", None), P(None, "mp")] * 2),
        P(),
    )
    out_specs = (
        P("dp", None), P("dp", None), P("dp", None), P(), P(), P(),
        *([P("dp", "mp"), P("mp", "dp")] * 6),
        *([P("dp", None, "mp"), P("dp", "mp", None)] * 2),
        *([P(None, "mp"), P("mp", None)] * 2),
        *([P("mp", None), P(None, "mp")] * 2),
    )
    return jax.shard_map(local, mesh=mesh, in_specs=in_specs, out_specs=out_specs, check_vma=False)
```

```python
import functools
import math

import jax
import jax.numpy as jnp
import numpy as np
from jax import lax
from jax.experimental import pallas as pl
from jax.experimental.pallas import tpu as pltpu
from jax.sharding import PartitionSpec as P

D = 768
HEADS = 12
HD = 64
FF = 3072
LEN = 1024
RANK = 8
EMA_STEPS = 4
TILE = 256
SLOT = 256

BF = jnp.bfloat16
F32 = jnp.float32
highest = lax.Precision.HIGHEST
norm_eps = 1e-05
gelu_coef = 0.7978845608028654
masked_score = -1e30
MESH_ID = pl.DeviceIdType.MESH


def nt(a, b):
    return lax.dot_general(a, b, (((1,), (1,)), ((), ())), preferred_element_type=F32)


def nn(a, b):
    return lax.dot_general(a, b, (((1,), (0,)), ((), ())), preferred_element_type=F32)


def tn(a, b):
    return lax.dot_general(a, b, (((0,), (0,)), ((), ())), preferred_element_type=F32)


def rotary_tables():
    half = HD // 2
    step = np.float32(-2.0 * math.log(10000.0) / HD)
    inverse = np.exp(np.arange(half, dtype=np.float32) * step).astype(np.float32)
    angle = (np.arange(LEN, dtype=np.float32)[:, None] * inverse[None, :]).astype(np.float32)
    c = np.cos(angle).astype(np.float32)
    s = np.sin(angle).astype(np.float32)
    return np.concatenate([c, c, c, c], 1), np.concatenate([-s, s, -s, s], 1)


def spin(v, cos, sin):
    lane = lax.broadcasted_iota(jnp.int32, v.shape, 1)
    low = lax.rem(lane, HD) < HD // 2
    swapped = jnp.where(low, pltpu.roll(v, 128 - HD // 2, 1), pltpu.roll(v, HD // 2, 1))
    return v * cos + swapped * sin


def block_ids(size, shape, dim):
    shift = 2 + (size >= 8).astype(jnp.int32) + (size >= 16).astype(jnp.int32)
    place = lax.broadcasted_iota(jnp.int32, shape, dim)
    return lax.shift_right_logical(place, jnp.full(shape, shift, jnp.int32))


def fill_bias(size, noisy_bias, clean_bias):
    keys = block_ids(size, (TILE, TILE), 0)
    rows = block_ids(size, (TILE, TILE), 1)
    noisy_bias[...] = jnp.where(rows == keys, 0.0, masked_score)
    clean_bias[...] = jnp.where(keys < rows, 0.0, masked_score)


def norm_parts(values):
    centered = values - jnp.mean(values, axis=1, keepdims=True)
    scale = lax.rsqrt(jnp.mean(centered * centered, axis=1, keepdims=True) + norm_eps)
    return centered * scale, scale


def norm_back(values, gain, grad):
    unit, scale = norm_parts(values)
    scaled = grad * gain
    inner = jnp.mean(scaled * unit, axis=1, keepdims=True)
    grad_in = scale * (scaled - jnp.mean(scaled, axis=1, keepdims=True) - unit * inner)
    return grad_in, jnp.sum(grad * unit, axis=0, keepdims=True)


def gelu_and_slope(u):
    square = u * u
    half = 0.5 + 0.5 * jnp.tanh(u * (gelu_coef + (gelu_coef * 0.044715) * square))
    slope = half + (u * (2.0 * half * (1.0 - half))) * (gelu_coef + (3.0 * 0.044715 * gelu_coef) * square)
    return u * half, slope


def whole(shape):
    return pl.BlockSpec(shape, lambda *index: (0,) * len(shape), pipeline_mode=pl.Buffered(1))


def side_rows(h, info, size):
    return (info[0], 0)


def lane2(h, *_):
    return (0, h)


def row3(h, *_):
    return (h, 0, 0)


def attend_head(head, xn_ref, xc_ref, w_ref, cos_ref, sin_ref, qn_ref, qc_ref, att_ref, lse_ref,
                bn_ref, bc_ref, kn_ref, kc_ref, vnt_ref, vct_ref):
    w = w_ref[pl.ds(pl.multiple_of(head * 3 * HD, 3 * HD), 3 * HD), :]
    for src, dst, keys, vals in ((xn_ref, qn_ref, kn_ref, vnt_ref), (xc_ref, qc_ref, kc_ref, vct_ref)):
        a = nt(src[...], w)
        r = spin(a[:, :128], cos_ref[...], sin_ref[...]).astype(BF)
        v = a[:, 128:].astype(BF)
        dst[:, :128] = r
        dst[:, 128:192] = v
        keys[...] = r[:, 64:128]
        vals[...] = jnp.transpose(v)
    here = pl.ds(pl.multiple_of(head * HD, HD), HD)
    for i in range(LEN // TILE):
        lo, hi = i * TILE, (i + 1) * TILE
        q = qn_ref[lo:hi, 0:64] * 0.125
        parts = [nt(kn_ref[lo:hi, :], q) + bn_ref[...], nt(kc_ref[lo:hi, :], q) + bc_ref[...]]
        if i:
            parts.append(nt(kc_ref[0:lo, :], q))
        peak = functools.reduce(jnp.maximum, [jnp.max(s, axis=0, keepdims=True) for s in parts])
        exps = [jnp.exp(s - peak) for s in parts]
        total = functools.reduce(jnp.add, [jnp.sum(e, axis=0, keepdims=True) for e in exps])
        inv = 1.0 / total
        low = [(e * inv).astype(BF) for e in exps]
        o = nn(vnt_ref[:, lo:hi], low[0]) + nn(vct_ref[:, lo:hi], low[1])
        if i:
            o = o + nn(vct_ref[:, 0:lo], low[2])
        att_ref[here, lo:hi] = o.astype(BF)
        lse_ref[0, :, lo:hi] = jnp.broadcast_to(peak + jnp.log(total), (8, TILE))


def attend_kernel(size_ref, noisy_hbm, clean_hbm, w_hbm, wo_hbm, gain_ref, cos_ref, sin_ref,
                  qn_ref, qc_ref, att_ref, lse_ref, xn_hbm, xc_hbm, w_far_hbm, o_far_hbm,
                  raw_ref, x_ref, w_ref, o_ref, sem_in, sem_out, sem_send, sem_recv, *work):
    head = pl.program_id(0)
    side = lax.axis_index("mp") // 2
    peer = far_peer()
    sides = ((noisy_hbm, xn_hbm), (clean_hbm, xc_hbm))
    width = 3 * HD

    def load(s, i):
        at = pl.ds(pl.multiple_of(side * LEN + i * TILE, TILE), TILE)
        return pltpu.make_async_copy(sides[s][0].at[at], raw_ref.at[s, chunk(i)], sem_in.at[CHUNKS * s + i])

    def save(s):
        return pltpu.make_async_copy(x_ref.at[s], sides[s][1], sem_out.at[s])

    dp = lax.axis_index("dp")
    odd = lax.rem(dp, 2)
    mate = (dp + 1 - 2 * odd, lax.axis_index("mp"))
    part = width // 2

    def pick(j, which):
        return pl.ds(pl.multiple_of(width * j + part * which, part), part)

    def give(j):
        return push(w_hbm.at[pick(j, odd)], w_ref.at[pick(3 + j, odd)], sem_send.at[j], sem_recv.at[j], peer)

    def relay(j):
        return push(w_ref.at[pick(3 + j, odd)], w_ref.at[pick(3 + j, odd)], sem_send.at[4 + j], sem_recv.at[4 + j], mate)

    near_w = pltpu.make_async_copy(w_hbm, w_ref.at[0:3 * width], sem_in.at[2 * CHUNKS])
    give_out = push(wo_hbm.at[pick(0, odd)], o_ref.at[pick(0, odd)], sem_send.at[3], sem_recv.at[3], peer)
    relay_out = push(o_ref.at[pick(0, odd)], o_ref.at[pick(0, odd)], sem_send.at[7], sem_recv.at[7], mate)
    keep_w = pltpu.make_async_copy(w_ref.at[3 * width:], w_far_hbm, sem_out.at[2])
    keep_o = pltpu.make_async_copy(o_ref, o_far_hbm, sem_out.at[3])

    @pl.when(head == 0)
    def _():
        for s in range(2):
            for i in range(CHUNKS):
                load(s, i).start()
        near_w.start()
        greet(peer, mate)
        for j in range(3):
            give(j).start()
        give_out.start()
        fill_bias(size_ref[side], work[0], work[1])
        for s in range(2):
            for i in range(CHUNKS):
                load(s, i).wait()
                x = norm_parts(raw_ref[s, chunk(i), :].astype(F32))[0] * gain_ref[0:1, :]
                x_ref[s, chunk(i), :] = x.astype(BF)
            save(s).start()
        near_w.wait()

    for j in range(3):
        @pl.when(head == 1 + j)
        def _():
            give(j).wait_recv()
            relay(j).start()

    @pl.when(head == 3)
    def _():
        give_out.wait_recv()
        relay_out.start()

    for j in range(3):
        @pl.when(head == 3 + j)
        def _():
            relay(j).wait_recv()

    @pl.when(head == 5)
    def _():
        keep_w.start()
        relay_out.wait_recv()
        keep_o.start()

    attend_head(head, x_ref.at[0], x_ref.at[1], w_ref, cos_ref, sin_ref, qn_ref, qc_ref, att_ref, lse_ref, *work)

    @pl.when(head == 5)
    def _():
        save(0).wait()
        save(1).wait()
        keep_w.wait()
        keep_o.wait()
        for j in range(3):
            give(j).wait_send()
            relay(j).wait_send()
        give_out.wait_send()
        relay_out.wait_send()


CHUNKS = LEN // TILE
HALF = LEN // 2


def chunk(i):
    return slice(i * TILE, (i + 1) * TILE)


def anywhere():
    return pl.BlockSpec(memory_space=pl.ANY)


def in_vmem():
    return pl.BlockSpec(memory_space=pltpu.VMEM)


def dma(n):
    return pltpu.SemaphoreType.DMA((n,))


def rows_of(n):
    return jax.ShapeDtypeStruct((n, D), BF)


attend_work = [
    pltpu.VMEM((TILE, TILE), F32),
    pltpu.VMEM((TILE, TILE), F32),
    pltpu.VMEM((LEN, HD), BF),
    pltpu.VMEM((LEN, HD), BF),
    pltpu.VMEM((HD, LEN), BF),
    pltpu.VMEM((HD, LEN), BF),
]
rows_shape = jax.ShapeDtypeStruct((LEN, D), BF)


def attend(size, noisy, clean, w, wo, gains, cos, sin):
    return pl.pallas_call(
        attend_kernel,
        grid=(6,),
        in_specs=[pl.BlockSpec(memory_space=pltpu.SMEM)] + [anywhere()] * 4
        + [whole((2, D)), whole((LEN, 128)), whole((LEN, 128))],
        out_specs=[pl.BlockSpec((LEN, SLOT), lane2), pl.BlockSpec((LEN, SLOT), lane2), whole((6 * HD, LEN)),
                   pl.BlockSpec((1, 8, LEN), row3)] + [anywhere()] * 4,
        out_shape=[jax.ShapeDtypeStruct((LEN, SLOT * 6), BF), jax.ShapeDtypeStruct((LEN, SLOT * 6), BF),
                   jax.ShapeDtypeStruct((6 * HD, LEN), BF), jax.ShapeDtypeStruct((6, 8, LEN), F32),
                   rows_shape, rows_shape, rows_of(9 * HD), rows_of(3 * HD)],
        scratch_shapes=[pltpu.VMEM((2, LEN, D), BF), pltpu.VMEM((2, LEN, D), BF), pltpu.VMEM((18 * HD, D), BF),
                        pltpu.VMEM((3 * HD, D), BF), dma(2 * CHUNKS + 1), dma(4), dma(8), dma(8)] + attend_work,
        compiler_params=pltpu.CompilerParams(collective_id=6, has_side_effects=True, vmem_limit_bytes=60 << 20),
        name="attend",
    )(size, noisy, clean, w, wo, gains, cos, sin)


WIDE = 5 * 128


def back_head(head, qn_ref, qc_ref, lse_ref, cos_ref, sin_ref, av_ref, c_ref,
              bn_ref, bc_ref, kn_ref, kc_ref, knt_ref, kct_ref, dot_ref, do_ref, dq_ref, dkn_ref, dkc_ref, dvc_ref, dvn_ref):
    do_ref[...] = jnp.transpose(dot_ref[pl.ds(pl.multiple_of(head * HD, HD), HD), :])
    kn_ref[...] = qn_ref[:, 64:128]
    kc_ref[...] = qc_ref[:, 64:128]
    knt_ref[...] = jnp.transpose(qn_ref[:, 0:128])[64:128]
    kct_ref[...] = jnp.transpose(qc_ref[:, 0:128])[64:128]
    for i in reversed(range(LEN // TILE)):
        lo, hi = i * TILE, (i + 1) * TILE
        last = i == LEN // TILE - 1
        q = qn_ref[lo:hi, 0:64] * 0.125
        do = do_ref[lo:hi, :]
        lse = lse_ref[0, 0:1, lo:hi]
        spans = [(0, lo, hi), (1, lo, hi)] + ([(1, 0, lo)] if i else [])
        probs, grads, inner = [], [], 0.0
        for n, (side, a, b) in enumerate(spans):
            kr = kc_ref if side else kn_ref
            vr = qc_ref if side else qn_ref
            s = nt(kr[a:b, :], q)
            if n == 0:
                s = s + bn_ref[...]
            if n == 1:
                s = s + bc_ref[...]
            p = jnp.exp(s - lse)
            dp = nt(vr[a:b, 128:192], do)
            inner = inner + jnp.sum(p * dp, axis=0, keepdims=True)
            probs.append(p)
            grads.append(dp)
        dqt = 0.0
        for n, (side, a, b) in enumerate(spans):
            ds = (probs[n] * (grads[n] - inner)).astype(BF)
            dv = nn(probs[n].astype(BF), do)
            dk = nn(ds, q)
            ktr = kct_ref if side else knt_ref
            dqt = dqt + nn(ktr[:, a:b], ds)
            if side and last:
                dkc_ref[a:b, :] = dk
                dvc_ref[a:b, :] = dv
            elif side:
                dkc_ref[a:b, :] += dk
                dvc_ref[a:b, :] += dv
            else:
                dkn_ref[a:b, :] = dk
                dvn_ref[a:b, :] = dv.astype(BF)
        dq_ref[lo:hi, :] = jnp.transpose(dqt) * 0.125
    sin = -sin_ref[...]
    cos = cos_ref[...]
    pair = pl.ds(pl.multiple_of(head * 128, 128), 128)
    av_ref[:, pair] = spin(jnp.concatenate([dq_ref[...], dkn_ref[...]], axis=1), cos, sin).astype(BF)
    both = jnp.concatenate([dkc_ref[...], dvc_ref[...]], axis=1)
    lane = lax.broadcasted_iota(jnp.int32, both.shape, 1)
    c_ref[:, pair] = jnp.where(lane < HD, spin(both, cos, sin), both).astype(BF)
    for j in range(3):
        @pl.when(head == j)
        def _():
            av_ref[:, 384 + HD * j:384 + HD * (j + 1)] = dvn_ref[...]


def group_grad(xn_ref, xc_ref, av, c, gq_ref):
    g = tn(av, xn_ref[...])
    e = tn(c, xc_ref[...])
    for j in range(3):
        row = 3 * HD * j
        gq_ref[row:row + HD, :] = g[128 * j:128 * j + HD].astype(gq_ref.dtype)
        gq_ref[row + HD:row + 2 * HD, :] = (g[128 * j + HD:128 * (j + 1)] + e[128 * j:128 * j + HD]).astype(gq_ref.dtype)
        gq_ref[row + 2 * HD:row + 3 * HD, :] = (
            g[384 + HD * j:384 + HD * (j + 1)] + e[128 * j + HD:128 * (j + 1)]).astype(gq_ref.dtype)


def back_start(size_ref, att_ref, g_ref, wo_ref, go_ref, av_ref, work):
    fill_bias(size_ref[lax.axis_index("mp") // 2], work[0], work[1])
    work[6][...] = nt(wo_ref[...], g_ref[...]).astype(BF)
    go_ref[...] = nn(att_ref[...], g_ref[...]).astype(go_ref.dtype)
    av_ref[:, 576:WIDE] = jnp.zeros((LEN, WIDE - 576), BF)


def back_far_kernel(size_ref, qn_ref, qc_ref, att_ref, lse_ref, g_ref, wo_ref, cos_ref, sin_ref,
                    xn_hbm, xc_hbm, av_ref, c_ref, both_ref, xn_ref, xc_ref, sems, *work):
    head = pl.program_id(0)
    late = [pltpu.make_async_copy(s, d, sems.at[k]) for k, (s, d) in enumerate(((xn_hbm, xn_ref), (xc_hbm, xc_ref)))]

    @pl.when(head == 0)
    def _():
        for c in late:
            c.start()
        back_start(size_ref, att_ref, g_ref, wo_ref, both_ref.at[9 * HD:], av_ref, work)

    back_head(head, qn_ref, qc_ref, lse_ref, cos_ref, sin_ref, av_ref, c_ref, *work)

    @pl.when(head == 2)
    def _():
        for c in late:
            c.wait()
        group_grad(xn_ref, xc_ref, av_ref[...], c_ref[...], both_ref)


def back_near_kernel(size_ref, qn_ref, qc_ref, att_ref, lse_ref, g_ref, wo_ref, cos_ref, sin_ref,
                     xn_hbm, xc_hbm, w_hbm, w_far_hbm, avf_hbm, cf_hbm, gxn_hbm, gxc_hbm, gq_ref, go_ref,
                     xn_ref, xc_ref, wav_ref, wc_ref, av_ref, c_ref, out_ref, sems, sem_w, sem_out, *work):
    head = pl.program_id(0)
    late = [pltpu.make_async_copy(s, d, sems.at[k]) for k, (s, d) in enumerate((
        (xn_hbm, xn_ref), (xc_hbm, xc_ref), (avf_hbm, av_ref.at[:, WIDE:]), (cf_hbm, c_ref.at[:, 384:])))]
    for n, src in enumerate((w_hbm, w_far_hbm)):
        for j in range(3):
            row, base, k = 192 * j, WIDE * n, 3 * (3 * n + j)
            late.append(pltpu.make_async_copy(
                src.at[row:row + 128], wav_ref.at[base + 128 * j:base + 128 * (j + 1)], sem_w.at[k]))
            late.append(pltpu.make_async_copy(
                src.at[row + 128:row + 192], wav_ref.at[base + 384 + 64 * j:base + 448 + 64 * j], sem_w.at[k + 1]))
            late.append(pltpu.make_async_copy(
                src.at[row + 64:row + 192], wc_ref.at[384 * n + 128 * j:384 * n + 128 * (j + 1)], sem_w.at[k + 2]))

    @pl.when(head == 0)
    def _():
        for c in late:
            c.start()
        for n in range(2):
            wav_ref[WIDE * n + 576:WIDE * (n + 1), :] = jnp.zeros((WIDE - 576, D), BF)
        back_start(size_ref, att_ref, g_ref, wo_ref, go_ref, av_ref, work)

    back_head(head, qn_ref, qc_ref, lse_ref, cos_ref, sin_ref, av_ref, c_ref, *work)

    @pl.when(head == 2)
    def _():
        for c in late:
            c.wait()
        copies = []
        for s, (rows, w, out) in enumerate(((av_ref, wav_ref, gxn_hbm), (c_ref, wc_ref, gxc_hbm))):
            for i in range(CHUNKS):
                out_ref[s, chunk(i), :] = nn(rows[chunk(i), :], w[...]).astype(BF)
                copies.append(pltpu.make_async_copy(
                    out_ref.at[s, chunk(i)], out.at[chunk(i)], sem_out.at[CHUNKS * s + i]))
                copies[-1].start()
        group_grad(xn_ref, xc_ref, av_ref[:, :WIDE], c_ref[:, :384], gq_ref)
        for c in copies:
            c.wait()


back_work = attend_work[:4] + [
    pltpu.VMEM((HD, LEN), BF),
    pltpu.VMEM((HD, LEN), BF),
    pltpu.VMEM((3 * HD, LEN), BF),
    pltpu.VMEM((LEN, HD), BF),
    pltpu.VMEM((LEN, HD), F32),
    pltpu.VMEM((LEN, HD), F32),
    pltpu.VMEM((LEN, HD), F32),
    pltpu.VMEM((LEN, HD), F32),
    pltpu.VMEM((LEN, HD), BF),
]
def head_inputs(first):
    return [pl.BlockSpec((LEN, SLOT), lambda h, *_: (0, h + first)), pl.BlockSpec((LEN, SLOT), lambda h, *_: (0, h + first)),
            pl.BlockSpec((3 * HD, LEN), lambda h, *_: (first // 3, 0), pipeline_mode=pl.Buffered(1)),
            pl.BlockSpec((1, 8, LEN), lambda h, *_: (h + first, 0, 0))]


def back_far(size, qn, qc, att, lse, g, wo, cos, sin, xn, xc):
    return pl.pallas_call(
        back_far_kernel,
        grid=(3,),
        in_specs=[pl.BlockSpec(memory_space=pltpu.SMEM)] + head_inputs(3)
        + [whole((LEN, D)), whole((3 * HD, D)), whole((LEN, 128)), whole((LEN, 128)), anywhere(), anywhere()],
        out_specs=[whole((LEN, WIDE)), whole((LEN, 384)), whole((D, D))],
        out_shape=[jax.ShapeDtypeStruct((LEN, WIDE), BF), jax.ShapeDtypeStruct((LEN, 384), BF), rows_of(D)],
        scratch_shapes=[pltpu.VMEM((LEN, D), BF), pltpu.VMEM((LEN, D), BF), dma(2)] + back_work,
        compiler_params=pltpu.CompilerParams(vmem_limit_bytes=60 << 20),
        name="back_far",
    )(size, qn, qc, att, lse, g, wo, cos, sin, xn, xc)


def back_near(size, qn, qc, att, lse, g, wo, cos, sin, xn, xc, w, w_far, av_far, c_far):
    return pl.pallas_call(
        back_near_kernel,
        grid=(3,),
        in_specs=[pl.BlockSpec(memory_space=pltpu.SMEM)] + head_inputs(0)
        + [whole((LEN, D)), whole((3 * HD, D)), whole((LEN, 128)), whole((LEN, 128))] + [anywhere()] * 6,
        out_specs=[anywhere(), anywhere(), whole((9 * HD, D)), whole((3 * HD, D))],
        out_shape=[rows_shape, rows_shape, jax.ShapeDtypeStruct((9 * HD, D), F32), jax.ShapeDtypeStruct((3 * HD, D), F32)],
        scratch_shapes=[pltpu.VMEM((LEN, D), BF), pltpu.VMEM((LEN, D), BF), pltpu.VMEM((2 * WIDE, D), BF), pltpu.VMEM((D, D), BF),
                        pltpu.VMEM((LEN, 2 * WIDE), BF), pltpu.VMEM((LEN, D), BF), pltpu.VMEM((2, LEN, D), BF),
                        dma(4), dma(18), dma(2 * CHUNKS)] + back_work,
        compiler_params=pltpu.CompilerParams(vmem_limit_bytes=60 << 20),
        name="back_near",
    )(size, qn, qc, att, lse, g, wo, cos, sin, xn, xc, w, w_far, av_far, c_far)


def halves(v):
    high = v.astype(BF)
    return high, (v - high.astype(F32)).astype(BF)


def exact(left_side, right_side, left_dim, right_dim):
    dims = (((left_dim,), (right_dim,)), ((), ()))
    a, b = halves(left_side)
    c, d = halves(right_side)

    def times(x, y):
        return lax.dot_general(x, y, dims, preferred_element_type=F32)

    return times(a, c) + (times(a, d) + times(b, c))


def core_peer():
    m = lax.axis_index("mp")
    return (lax.axis_index("dp"), m + 1 - 2 * lax.rem(m, 2))


def far_peer():
    return (lax.axis_index("dp"), lax.rem(lax.axis_index("mp") + 2, 4))


def greet(*peers):
    barrier = pltpu.get_barrier_semaphore()
    for p in peers:
        pl.semaphore_signal(barrier, inc=1, device_id=p, device_id_type=MESH_ID)
    pl.semaphore_wait(barrier, len(peers))


PARTS = HALF // TILE


def own_rows(i):
    half = lax.rem(lax.axis_index("mp"), 2)
    return pl.ds(pl.multiple_of(half * HALF + i * TILE, TILE), TILE)


def peer_rows(i):
    half = lax.rem(lax.axis_index("mp"), 2)
    return pl.ds(pl.multiple_of((1 - half) * HALF + i * TILE, TILE), TILE)


def side_rows_of(i):
    m = lax.axis_index("mp")
    return pl.ds(pl.multiple_of(m * HALF + i * TILE, TILE), TILE)


def copy(src, dst, sem):
    return pltpu.make_async_copy(src, dst, sem)


def push(src, dst, send_sem, recv_sem, peer):
    return pltpu.make_async_remote_copy(
        src_ref=src, dst_ref=dst, send_sem=send_sem, recv_sem=recv_sem, device_id=peer, device_id_type=MESH_ID)


class Sems:
    def __init__(self, ref):
        self.ref = ref
        self.used = 0

    def take(self):
        self.used += 1
        return self.ref.at[self.used - 1]


def middle_kernel(att_hbm, wo_near_hbm, wo_far_hbm, rows_hbm, cot_hbm, up_hbm, down_hbm,
                  err_up_hbm, err_down_hbm, fac_up_ref, fac_down_ref, gain_ref,
                  res_hbm, grad_hbm, low_hbm, mlp_hbm, fold_hbm, mat_up_hbm, mat_down_hbm,
                  left_up_ref, left_down_ref, gsum_ref,
                  att_ref, wo_ref, x_ref, send_ref, far_ref, r_ref, nm_ref, cot_ref, up_ref, down_ref, hid_ref, gp_ref,
                  mlp_ref, gm_ref, back_ref, fold_gm_ref, fold_mlp_ref, sum_ref, msum_ref, yet_ref,
                  mat_up_ref, mat_down_ref, nmt_ref, grad_ref, low_ref, sem_ref, send_sem_ref, recv_sem_ref):
    sems, sends, recvs = Sems(sem_ref), Sems(send_sem_ref), Sems(recv_sem_ref)
    m = lax.axis_index("mp")
    side, half = m // 2, lax.rem(m, 2)
    core, far = core_peer(), far_peer()
    width = 3 * HD
    third = D // 3
    pushes, saves = [], []

    def load(src, dst):
        c = pltpu.make_async_copy(src, dst, sems.take())
        c.start()
        return c

    def save(src, dst):
        saves.append(load(src, dst))

    def send(src, dst, peer):
        c = push(src, dst, sends.take(), recvs.take(), peer)
        c.start()
        pushes.append(c)
        return c

    def span(start, n):
        return pl.ds(pl.multiple_of(start, TILE), n)

    own_half, peer_half = half * HALF, (1 - half) * HALF
    first = [load(att_hbm, att_ref), load(wo_near_hbm, wo_ref.at[0:width]), load(wo_far_hbm, wo_ref.at[width:])]
    xs = [load(rows_hbm.at[span(m * HALF + i * TILE, TILE)], x_ref.at[chunk(i)]) for i in range(PARTS)]
    up_in, down_in = load(up_hbm, up_ref), load(down_hbm, down_ref)
    cot_in = load(cot_hbm.at[span(side * LEN, LEN)], cot_ref.at[0:LEN])
    cot_far_in = load(cot_hbm.at[span((1 - side) * LEN, LEN)], cot_ref.at[LEN:])
    err_in = [load(err_down_hbm.at[0], mat_down_ref), load(err_up_hbm.at[0], mat_up_ref)]
    greet(core, far)
    for c in first:
        c.wait()
    normed, cross = [], []
    for i in range(PARTS):
        send_ref[chunk(i), :] = tn(att_ref[:, span(peer_half + i * TILE, TILE)], wo_ref[...]).astype(BF)
        handed = send(send_ref.at[chunk(i)], far_ref.at[chunk(i)], core)
        at = span(own_half + i * TILE, TILE)
        own = tn(att_ref[:, at], wo_ref[...])
        xs[i].wait()
        handed.wait_recv()
        r = x_ref[chunk(i), :].astype(F32) + (own + far_ref[chunk(i), :].astype(F32))
        r_ref[chunk(i), :] = r
        nm_ref[at, :] = (norm_parts(r)[0] * gain_ref[1:2, :]).astype(BF)
        normed.append(send(nm_ref.at[at], nm_ref.at[at], core))
        cross.append(send(nm_ref.at[at], nm_ref.at[span(LEN + own_half + i * TILE, TILE)], far))
        save(r_ref.at[chunk(i)], res_hbm.at[chunk(i)])

    def feed_rows(start, n):
        at = span(start, n)
        for t in range(3):
            lanes = slice(t * third, (t + 1) * third)
            hidden, slope = gelu_and_slope(nn(nm_ref[at, :], up_ref[:, lanes]))
            hid_ref[at, lanes] = hidden.astype(BF)
            gp_ref[at, lanes] = (slope * nt(cot_ref[at, :], down_ref[lanes, :])).astype(BF)
        gm_ref[at, :] = nt(gp_ref[at, :], up_ref[...]).astype(BF)
        mlp_ref[at, :] = nn(hid_ref[at, :], down_ref[...]).astype(BF)

    up_in.wait()
    down_in.wait()
    cot_in.wait()
    feed_rows(own_half, HALF)
    for c in normed:
        c.wait_recv()
    feed_rows(peer_half, HALF)
    save(mlp_ref.at[0:LEN], mlp_hbm)
    swap = [send(gm_ref.at[span(peer_half + i * TILE, TILE)], back_ref.at[chunk(i)], core) for i in range(PARTS)]
    cot_far_in.wait()
    arrived = []
    for i in range(PARTS):
        at = span(LEN + own_half + i * TILE, TILE)
        away = span(LEN + peer_half + i * TILE, TILE)
        cross[i].wait_recv()
        relay = send(nm_ref.at[at], nm_ref.at[at], core)
        feed_rows(LEN + own_half + i * TILE, TILE)
        relay.wait_recv()
        feed_rows(LEN + peer_half + i * TILE, TILE)
        fold = send(gm_ref.at[away], fold_gm_ref.at[chunk(i)], core)
        fold_mlp = send(mlp_ref.at[away], fold_mlp_ref.at[chunk(i)], core)
        fold.wait_recv()
        sum_ref[chunk(i), :] = (gm_ref[at, :].astype(F32) + fold_gm_ref[chunk(i), :].astype(F32)).astype(BF)
        arrived.append(send(sum_ref.at[chunk(i)], yet_ref.at[chunk(i)], far))
        fold_mlp.wait_recv()
        msum_ref[chunk(i), :] = (mlp_ref[at, :].astype(F32) + fold_mlp_ref[chunk(i), :].astype(F32)).astype(BF)
        save(msum_ref.at[chunk(i)], fold_hbm.at[chunk(i)])

    for i in range(8):
        at = slice(i * TILE, (i + 1) * TILE)
        nmt_ref[:, at] = jnp.transpose(nm_ref[at, :])
    for c in err_in:
        c.wait()
    left_up = 0.0
    for t in range(3):
        lanes = slice(t * third, (t + 1) * third)
        mat = tn(hid_ref[:, lanes], cot_ref[...]) + mat_down_ref[lanes, :]
        mat_down_ref[lanes, :] = mat
        save(mat_down_ref.at[lanes], mat_down_hbm.at[lanes])
        left_down_ref[:, lanes] = exact(fac_down_ref[...], mat, 1, 1)
        mat = nn(nmt_ref[...], gp_ref[:, lanes]) + mat_up_ref[:, lanes]
        mat_up_ref[:, lanes] = mat
        save(mat_up_ref.at[:, lanes], mat_up_hbm.at[:, lanes])
        left_up = left_up + exact(fac_up_ref[:, lanes], mat, 1, 1)
    left_up_ref[...] = left_up

    gsum = 0.0
    lows = []
    for i in range(PARTS):
        at = span(own_half + i * TILE, TILE)
        swap[i].wait_recv()
        total = gm_ref[at, :].astype(F32) + back_ref[chunk(i), :].astype(F32)
        arrived[i].wait_recv()
        total = total + yet_ref[chunk(i), :].astype(F32)
        grad, share = norm_back(r_ref[chunk(i), :], gain_ref[1:2, :], total)
        gsum = gsum + share
        grad = cot_ref[at, :].astype(F32) + grad
        grad_ref[chunk(i), :] = grad
        low_ref[chunk(i), :] = grad.astype(BF)
        lows.append(send(low_ref.at[chunk(i)], low_hbm.at[at], core))
        save(low_ref.at[chunk(i)], low_hbm.at[at])
        save(grad_ref.at[chunk(i)], grad_hbm.at[chunk(i)])
    gsum_ref[...] = gsum
    for c in lows:
        c.wait_recv()
    for c in pushes:
        c.wait_send()
    for c in saves:
        c.wait()


def middle(att, wo_near, wo_far, rows, cotangent, up, down, err_up, err_down, fac_up, fac_down, gains):
    def low(n):
        return pltpu.VMEM((n, D), BF)

    def wide(n):
        return pltpu.VMEM((n, D), F32)

    return pl.pallas_call(
        middle_kernel,
        in_specs=[anywhere()] * 9 + [in_vmem()] * 3,
        out_specs=[anywhere()] * 7 + [in_vmem()] * 3,
        out_shape=[jax.ShapeDtypeStruct((HALF, D), F32), jax.ShapeDtypeStruct((HALF, D), F32), rows_of(LEN), rows_of(LEN),
                   rows_of(HALF), jax.ShapeDtypeStruct((D, D), F32), jax.ShapeDtypeStruct((D, D), F32),
                   jax.ShapeDtypeStruct((RANK, D), F32), jax.ShapeDtypeStruct((RANK, D), F32),
                   jax.ShapeDtypeStruct((1, D), F32)],
        scratch_shapes=[pltpu.VMEM((6 * HD, LEN), BF), low(6 * HD), low(HALF), low(HALF), low(HALF), wide(HALF),
                        low(2 * LEN), low(2 * LEN), low(D), low(D), low(2 * LEN), low(2 * LEN),
                        low(2 * LEN), low(2 * LEN), low(HALF), low(HALF), low(HALF), low(HALF), low(HALF), low(HALF),
                        wide(D), wide(D), pltpu.VMEM((D, 2 * LEN), BF), wide(HALF), low(HALF), dma(32), dma(24), dma(24)],
        compiler_params=pltpu.CompilerParams(collective_id=3, has_side_effects=True, vmem_limit_bytes=60 << 20),
        name="middle",
    )(att, wo_near, wo_far, rows, cotangent, up, down, err_up, err_down, fac_up, fac_down, gains)


def settle_kernel(mlp_hbm, far_hbm, res_hbm, out_hbm, own_ref, far_ref, res_ref, core_ref, out_ref,
                  sem_in, sem_send, sem_recv, sem_out):
    peer = core_peer()
    loads = []
    for i in range(PARTS):
        loads += [copy(mlp_hbm.at[own_rows(i)], own_ref.at[chunk(i)], sem_in.at[3 * i]),
                  copy(far_hbm.at[chunk(i)], far_ref.at[chunk(i)], sem_in.at[3 * i + 1]),
                  copy(res_hbm.at[chunk(i)], res_ref.at[chunk(i)], sem_in.at[3 * i + 2])]
    for c in loads:
        c.start()
    greet(peer)
    pushes = [push(mlp_hbm.at[peer_rows(i)], core_ref.at[chunk(i)], sem_send.at[i], sem_recv.at[i], peer)
              for i in range(PARTS)]
    for c in pushes:
        c.start()
    saves = []
    for i in range(PARTS):
        for c in loads[3 * i:3 * i + 3]:
            c.wait()
        pushes[i].wait_recv()
        total = own_ref[chunk(i), :].astype(F32) + core_ref[chunk(i), :].astype(F32) + far_ref[chunk(i), :].astype(F32)
        out_ref[chunk(i), :] = (res_ref[chunk(i), :] + total).astype(BF)
        saves.append(copy(out_ref.at[chunk(i)], out_hbm.at[chunk(i)], sem_out.at[i]))
        saves[-1].start()
    for c in saves:
        c.wait()
    for c in pushes:
        c.wait_send()


def settle(mlp, far, residual):
    half = pltpu.VMEM((HALF, D), BF)
    return pl.pallas_call(
        settle_kernel,
        in_specs=[anywhere()] * 3,
        out_specs=anywhere(),
        out_shape=rows_of(HALF),
        scratch_shapes=[half, half, pltpu.VMEM((HALF, D), F32), half, half, dma(3 * PARTS), dma(PARTS), dma(PARTS), dma(PARTS)],
        compiler_params=pltpu.CompilerParams(collective_id=4, has_side_effects=True, vmem_limit_bytes=60 << 20),
        name="settle",
    )(mlp, far, residual)


def finish_kernel(gxn_hbm, gxc_hbm, noisy_hbm, clean_hbm, grad_hbm, gain_ref, gain_two_ref, ends_hbm, gsum_ref,
                  own_ref, far_ref, x_ref, wide_ref, out_ref,
                  sem_own, sem_x, sem_wide, sem_send, sem_recv, sem_out):
    sources = (gxn_hbm, gxc_hbm)
    count = 2 * PARTS
    own, rows, wide = [], [], []
    for n in range(count):
        k, i = n // PARTS, n % PARTS
        own.append(copy(sources[k].at[own_rows(i)], own_ref.at[chunk(n)], sem_own.at[n]))
        rows.append(copy((noisy_hbm, clean_hbm)[k].at[side_rows_of(i)], x_ref.at[chunk(n)], sem_x.at[n]))
        if k == 0:
            wide.append(copy(grad_hbm.at[chunk(i)], wide_ref.at[chunk(i)], sem_wide.at[i]))
    for c in own + rows + wide:
        c.start()
    peer = core_peer()
    greet(peer)
    pushes = []
    for n in range(count):
        k, i = n // PARTS, n % PARTS
        pushes.append(push(sources[k].at[peer_rows(i)], far_ref.at[chunk(n)], sem_send.at[n], sem_recv.at[n], peer))
        pushes[-1].start()
    gsum = 0.0
    saves = []
    for n in range(count):
        k, i = n // PARTS, n % PARTS
        own[n].wait()
        rows[n].wait()
        pushes[n].wait_recv()
        total = own_ref[chunk(n), :].astype(F32) + far_ref[chunk(n), :].astype(F32)
        grad, share = norm_back(x_ref[chunk(n), :].astype(F32), gain_ref[0:1, :], total)
        gsum = gsum + share
        if k == 0:
            wide[i].wait()
            grad = wide_ref[chunk(i), :] + grad
        out_ref[chunk(n), :] = grad.astype(BF)
        saves.append(copy(out_ref.at[chunk(n)], ends_hbm.at[chunk(n)], sem_out.at[n]))
        saves[-1].start()
    gsum_ref[0:1, :] = gsum
    gsum_ref[1:2, :] = gain_two_ref[...]
    gsum_ref[2:8, :] = jnp.zeros((6, D), F32)
    for c in saves:
        c.wait()
    for c in pushes:
        c.wait_send()


def finish(gxn, gxc, noisy_rows, clean_rows, grad_resid, gains, gain_two):
    buf = pltpu.VMEM((LEN, D), BF)
    return pl.pallas_call(
        finish_kernel,
        in_specs=[anywhere()] * 5 + [in_vmem()] * 2,
        out_specs=[anywhere(), in_vmem()],
        out_shape=[rows_of(LEN), jax.ShapeDtypeStruct((RANK, D), F32)],
        scratch_shapes=[buf, buf, buf, pltpu.VMEM((HALF, D), F32), buf,
                        dma(2 * PARTS), dma(2 * PARTS), dma(PARTS), dma(2 * PARTS), dma(2 * PARTS), dma(2 * PARTS)],
        compiler_params=pltpu.CompilerParams(collective_id=5, has_side_effects=True, vmem_limit_bytes=60 << 20),
        name="finish",
    )(gxn, gxc, noisy_rows, clean_rows, grad_resid, gains, gain_two)


def place_kernel(plan, given, count, *refs):
    sources, outs = refs[:given], refs[len(refs) - 3 - count:len(refs) - 3]
    stage, sem_in, sem_out = refs[len(refs) - 3:]
    m = lax.axis_index("mp")
    beside = m + 1 - 2 * lax.rem(m, 2)
    spots = (m, beside, lax.rem(m + 2, 4), lax.rem(beside + 2, 4))
    loads = [copy(sources[s].at[part * HALF:(part + 1) * HALF], stage.at[j], sem_in.at[j])
             for j, (s, part, _, _) in enumerate(plan)]
    for c in loads:
        c.start()
    saves = []
    for j, (_, _, target, spot) in enumerate(plan):
        loads[j].wait()
        at = pl.ds(pl.multiple_of(spots[spot] * HALF, HALF), HALF)
        saves.append(copy(stage.at[j], outs[target].at[at], sem_out.at[j]))
        saves[-1].start()
    for c in saves:
        c.wait()


def place(plan, count, *pieces, onto=()):
    total, given = len(plan), len(pieces)
    return pl.pallas_call(
        functools.partial(place_kernel, plan, given, count),
        in_specs=[anywhere()] * (given + len(onto)),
        out_specs=[anywhere()] * count,
        out_shape=[rows_of(2 * LEN)] * count,
        scratch_shapes=[pltpu.VMEM((total, HALF, D), BF), dma(total), dma(total)],
        input_output_aliases={given + k: k for k in range(len(onto))},
        compiler_params=pltpu.CompilerParams(vmem_limit_bytes=14 << 20),
        name="place",
    )(*pieces, *onto)


PACK = 1024


def left_products(gq, both_ref, eq, go, eo, fq_ref, fo_ref, lu_ref, ld_ref, gain_ref, mq_ref, mo_ref, pack_ref):
    pack_ref[...] = jnp.zeros_like(pack_ref)
    mq = gq + both_ref[:9 * HD, :].astype(F32) + eq
    mq_ref[...] = mq
    pack_ref[0:8, 0:D] = exact(fq_ref[...], mq, 1, 0)
    mo = go + both_ref[9 * HD:, :].astype(F32) + eo
    mo_ref[...] = mo
    pack_ref[0:8, D:D + 3 * HD] = exact(fo_ref[...], mo, 1, 1)
    pack_ref[8:16, 0:D] = lu_ref[...]
    pack_ref[16:24, 0:D] = ld_ref[...]
    for k in range(6):
        pack_ref[8 + k:9 + k, D:PACK] = gain_ref[k // 3:k // 3 + 1, 256 * (k % 3):256 * (k % 3 + 1)]


def lefts_kernel(gq_ref, both_ref, eq_ref, go_ref, eo_ref, fq_ref, fo_ref, lu_ref, ld_ref, gain_ref,
                 mq_ref, mo_ref, pack_ref):
    left_products(gq_ref[...], both_ref, eq_ref[0], go_ref[...], eo_ref[0], fq_ref, fo_ref, lu_ref, ld_ref, gain_ref,
                  mq_ref, mo_ref, pack_ref)


def lefts(*args):
    return pl.pallas_call(
        lefts_kernel,
        grid=(1,),
        in_specs=[whole(v.shape) for v in args],
        out_specs=[whole((9 * HD, D)), whole((3 * HD, D)), whole((3 * RANK, PACK))],
        out_shape=[jax.ShapeDtypeStruct((9 * HD, D), F32), jax.ShapeDtypeStruct((3 * HD, D), F32),
                   jax.ShapeDtypeStruct((3 * RANK, PACK), F32)],
        compiler_params=pltpu.CompilerParams(vmem_limit_bytes=60 << 20),
        name="lefts",
    )(*args)


def orthonormalize(sum_ref):
    mats = [sum_ref[0:8, 0:D], sum_ref[0:8, D:PACK], sum_ref[8:16, 0:D], sum_ref[16:24, 0:D]]
    for k in range(RANK):
        for t in range(4):
            a = mats[t]
            row = lax.broadcasted_iota(jnp.int32, a.shape, 0)
            v = a[k:k + 1, :]
            e = v / (jnp.sqrt(jnp.sum(v * v, axis=1, keepdims=True)) + 1e-08)
            c = jnp.sum(a * e, axis=1, keepdims=True)
            mats[t] = jnp.where(row == k, e, jnp.where(row > k, a - c * e, a))
    mats[1] = mats[1][:, :3 * HD]
    return mats


def right_products(hats, mq_ref, mo_ref, mu_ref, md_ref, pack_ref):
    out = exact(hats[1], mo_ref[...], 1, 0)
    pack_ref[0:8, 0:D] = exact(hats[2], mu_ref[...], 1, 0)
    pack_ref[8:16, 0:D] = exact(hats[3], md_ref[...], 1, 0)
    pack_ref[16:24, 0:D] = jnp.zeros((RANK, D), F32)
    pack_ref[16:24, 0:9 * HD] = exact(hats[0], mq_ref[...], 1, 1)
    for k in range(3):
        pack_ref[8 * k:8 * k + 8, D:PACK] = out[:, 256 * k:256 * (k + 1)]


def unpack_rights(pack_ref):
    out = jnp.concatenate([pack_ref[8 * k:8 * k + 8, D:PACK] for k in range(3)], axis=1)
    return [pack_ref[16:24, 0:9 * HD], out, pack_ref[0:8, 0:D], pack_ref[8:16, 0:D]]


def rights_kernel(sum_ref, mq_ref, mo_ref, mu_ref, md_ref, hq_ref, ho_ref, hu_ref, hd_ref, pack_ref):
    hats = orthonormalize(sum_ref)
    for hat, ref in zip(hats, (hq_ref, ho_ref, hu_ref, hd_ref)):
        ref[...] = hat
    right_products(hats, mq_ref, mo_ref, mu_ref, md_ref, pack_ref)


def rights(left_sum, mats):
    args = (left_sum, *mats)
    shapes = [(RANK, D), (RANK, 3 * HD), (RANK, D), (RANK, D), (3 * RANK, PACK)]
    return pl.pallas_call(
        rights_kernel,
        grid=(1,),
        in_specs=[whole(v.shape) for v in args],
        out_specs=[whole(s) for s in shapes],
        out_shape=[jax.ShapeDtypeStruct(s, F32) for s in shapes],
        compiler_params=pltpu.CompilerParams(vmem_limit_bytes=60 << 20),
        name="rights",
    )(*args)


def reduce_kernel(count, gq_hbm, both_hbm, eq_hbm, go_hbm, eo_hbm, mu_hbm, md_hbm, fq_ref, fo_ref, lu_ref, ld_ref, gain_ref,
                  mq_hbm, mo_hbm, hat_ref, right_ref, gsum_ref,
                  gq_ref, both_ref, mq_ref, go_ref, mo_ref, mu_ref, md_ref, x_ref, sum_ref, in_a, y_ref, in_b, slot_ref,
                  sem_ref, send_ref, recv_ref):
    me = lax.axis_index("dp")
    m = lax.axis_index("mp")
    sends, recvs = Sems(send_ref), Sems(recv_ref)
    loads = [copy(s, d, sem_ref.at[k]) for k, (s, d) in enumerate((
        (gq_hbm, gq_ref), (both_hbm, both_ref), (eq_hbm.at[0], mq_ref), (go_hbm, go_ref), (eo_hbm.at[0], mo_ref),
        (mu_hbm, mu_ref), (md_hbm, md_ref)))]
    for c in loads:
        c.start()
    barrier = pltpu.get_barrier_semaphore()
    for k in range(1, count):
        pl.semaphore_signal(barrier, inc=1, device_id=(lax.rem(me + k, count), m), device_id_type=MESH_ID)
    pl.semaphore_signal(barrier, inc=1, device_id=core_peer(), device_id_type=MESH_ID)
    pl.semaphore_wait(barrier, count)

    def lanes(j):
        return pl.ds(pl.multiple_of(j * 128, 128), 128)

    def spread_sum(src_ref, box_ref, out_ref):
        gather, scatter = [], []
        for k in range(1, count):
            j = lax.rem(me + k, count)
            gather.append(push(src_ref.at[:, lanes(j)], box_ref.at[k], sends.take(), recvs.take(), (j, m)))
        for c in gather:
            c.start()
        total = src_ref[:, lanes(me)]
        for k in range(1, count):
            gather[k - 1].wait_recv()
            total = total + box_ref[k]
        out_ref[:, lanes(me)] = total
        for k in range(1, count):
            j = lax.rem(me + k, count)
            scatter.append(push(out_ref.at[:, lanes(me)], out_ref.at[:, lanes(me)], sends.take(), recvs.take(), (j, m)))
            scatter[-1].start()
        for k in range(1, count):
            scatter[k - 1].wait_recv()
        return gather + scatter

    for c in loads[:5]:
        c.wait()
    left_products(gq_ref[...], both_ref, mq_ref[...], go_ref[...], mo_ref[...], fq_ref, fo_ref, lu_ref, ld_ref, gain_ref,
                  mq_ref, mo_ref, x_ref)
    saves = [copy(mq_ref, mq_hbm, sem_ref.at[7]), copy(mo_ref, mo_hbm, sem_ref.at[8])]
    for c in saves:
        c.start()
    sent = spread_sum(x_ref, in_a, sum_ref)
    share = push(sum_ref.at[8:16, D:PACK], slot_ref, sends.take(), recvs.take(), core_peer())
    share.start()
    hats = orthonormalize(sum_ref)
    hat_ref[...] = jnp.zeros_like(hat_ref)
    for t in range(4):
        hat_ref[RANK * t:RANK * (t + 1), 0:hats[t].shape[1]] = hats[t]
    for c in loads[5:]:
        c.wait()
    right_products(hats, mq_ref, mo_ref, mu_ref, md_ref, y_ref)
    sent += spread_sum(y_ref, in_b, right_ref)
    share.wait()
    gsum_ref[...] = sum_ref[8:16, D:PACK] + slot_ref[...]
    for c in sent:
        c.wait_send()
    for c in saves:
        c.wait()


def reduce_factors(gq, both, err_qkv, go, err_out, mat_up, mat_down, *small):
    count = lax.axis_size("dp")
    if count != 8:
        mq, mo, pack = lefts(gq, both, err_qkv, go, err_out, *small)
        total = lax.psum(pack, "dp")
        *hats, pack = rights(total, (mq, mo, mat_up, mat_down))
        hats[1] = jnp.pad(hats[1], ((0, 0), (0, D - 3 * HD)))
        share = total[8:16, D:PACK]
        share = share + lax.ppermute(share, "mp", [(0, 1), (1, 0), (2, 3), (3, 2)])
        return mq, mo, jnp.concatenate(hats, axis=0), lax.psum(pack, "dp"), share

    def wide(n):
        return pltpu.VMEM((n, D), F32)

    links = 4 * (count - 1) + 1
    return pl.pallas_call(
        functools.partial(reduce_kernel, count),
        in_specs=[anywhere()] * 7 + [in_vmem()] * 5,
        out_specs=[anywhere()] * 2 + [in_vmem()] * 3,
        out_shape=[jax.ShapeDtypeStruct(s, F32) for s in ((9 * HD, D), (3 * HD, D), (4 * RANK, D), (3 * RANK, PACK), (RANK, PACK - D))],
        scratch_shapes=[wide(9 * HD), pltpu.VMEM((D, D), BF), wide(9 * HD), wide(3 * HD), wide(3 * HD), wide(D), wide(D),
                        pltpu.VMEM((3 * RANK, PACK), F32), pltpu.VMEM((3 * RANK, PACK), F32),
                        pltpu.VMEM((count, 3 * RANK, 128), F32), pltpu.VMEM((3 * RANK, PACK), F32),
                        pltpu.VMEM((count, 3 * RANK, 128), F32), pltpu.VMEM((RANK, PACK - D), F32),
                        dma(9), dma(links), dma(links)],
        compiler_params=pltpu.CompilerParams(collective_id=1, has_side_effects=True, vmem_limit_bytes=60 << 20),
        name="reduce_factors",
    )(gq, both, err_qkv, go, err_out, mat_up, mat_down, *small)


def update_kernel(replicas, rates, *refs):
    sums, hats, mats, states = refs[0], refs[1], refs[2:6], refs[6:18]
    errs, news, right_out, hat_out = refs[18:22], refs[22:34], refs[34:38], refs[38:42]
    decay = min(0.9999, (1.0 + EMA_STEPS) / (10.0 + EMA_STEPS))
    share = D // replicas
    shift = lax.rem(D - lax.axis_index("dp") * share, D)

    def part(value):
        return pltpu.roll(value, shift, 1)[:, :share]

    rights_all = unpack_rights(sums)
    for t in range(4):
        hat = hats[RANK * t:RANK * (t + 1), :hat_out[t].shape[1]]
        hat_out[t][...] = hat
        right = rights_all[t] * (1.0 / replicas)
        right_out[t][...] = right
        first, second = ((right, hat), (hat, right), (hat, right), (hat, right))[t]
        errs[t][0] = mats[t][...] - exact(first, second, 0, 0)
        first, second = ((part(hat), right), (hat, part(right)), (part(hat), right), (part(right), hat))[t]
        moment = 0.5 * states[3 * t + 1][...] + exact(first, second, 0, 0)
        master = states[3 * t][...] - rates[t] * moment
        news[3 * t][...] = master
        news[3 * t + 1][...] = moment
        news[3 * t + 2][...] = decay * states[3 * t + 2][...] + (1.0 - decay) * master


def update(replicas, rates, right_sum, hats, mats, states):
    args = (right_sum, hats, *mats, *states)
    shapes = [(1, *m.shape) for m in mats] + [s.shape for s in states]
    shapes += [(RANK, 9 * HD), (RANK, D), (RANK, D), (RANK, D)]
    shapes += [(RANK, D), (RANK, 3 * HD), (RANK, D), (RANK, D)]
    return pl.pallas_call(
        functools.partial(update_kernel, replicas, rates),
        grid=(1,),
        in_specs=[whole(v.shape) for v in args],
        out_specs=[whole(s) for s in shapes],
        out_shape=[jax.ShapeDtypeStruct(s, F32) for s in shapes],
        compiler_params=pltpu.CompilerParams(vmem_limit_bytes=60 << 20),
        name="update",
    )(*args)


def local(
    noisy_rows, clean_rows, block_size, cotangent, norm_gains,
    weight_qkv, weight_out, weight_up, weight_down,
    master_qkv, master_out, master_up, master_down,
    moment_qkv, moment_out, moment_up, moment_down,
    average_qkv, average_out, average_up, average_down,
    error_qkv, error_out, error_up, error_down,
    factor_qkv, factor_out, factor_up, factor_down,
    gain_moment,
):
    row_count = noisy_rows.shape[0]
    replicas = lax.axis_size("dp")

    def across(value):
        return lax.ppermute(value, "mp", [(0, 2), (2, 0), (1, 3), (3, 1)])

    def beside(value):
        return lax.ppermute(value, "mp", [(0, 1), (1, 0), (2, 3), (3, 2)])

    def hold(*values):
        return lax.optimization_barrier(values)

    cos, sin = rotary_tables()
    w_near = weight_qkv.T
    qn, qc, att, lse, xn, xc, w_far, o_far = attend(
        block_size, noisy_rows, clean_rows, w_near, weight_out, norm_gains, cos, sin)
    residual, grad_resid, grad_low, mlp, mlp_fold, matrix_up, matrix_down, left_up, left_down, gain_two = middle(
        att, weight_out, o_far, noisy_rows, cotangent, weight_up, weight_down,
        error_up, error_down, factor_up.T, factor_down.T, norm_gains)
    mlp_far = across(mlp_fold)
    av_far, c_far, grads_far = back_far(block_size, qn, qc, att, lse, grad_low, o_far, cos, sin, xn, xc)
    mlp_far, av_far, grads_far = hold(mlp_far, av_far, grads_far)
    grads_back = across(grads_far)
    out_half = settle(mlp, mlp_far, residual)
    out_half, av_far = hold(out_half, av_far)
    out_far, out_side = across(out_half), beside(out_half)
    grad_xn, grad_xc, gq_near, go_near = back_near(
        block_size, qn, qc, att, lse, grad_low, weight_out, cos, sin, xn, xc, w_near, w_far, av_far, c_far)
    ends, gain_pair = finish(
        grad_xn, grad_xc, noisy_rows, clean_rows, grad_resid, norm_gains, gain_two)
    ends, grads_back = hold(ends, grads_back)
    ends_far = across(ends)
    ends_side = beside(ends)
    matrix_qkv, matrix_out, hats, right_sum, gain_sum = reduce_factors(
        gq_near, grads_back, jnp.swapaxes(error_qkv, 1, 2), go_near, error_out, matrix_up, matrix_down,
        factor_qkv.T, factor_out.T, left_up, left_down, gain_pair)
    mats = (matrix_qkv, matrix_out, matrix_up, matrix_down)
    rates = [3.0 / math.sqrt(f * row_count) for f in (D, HEADS * HD // 64, D, FF)] + [0.5 / math.sqrt(row_count)]
    states = (
        master_qkv, moment_qkv, average_qkv, master_out, moment_out, average_out,
        master_up, moment_up, average_up, master_down.T, moment_down.T, average_down.T,
    )
    done = update(replicas, rates, right_sum, hats, mats, states)
    errs, news, right_new, left_new = done[:4], done[4:16], done[16:20], done[20:24]
    out_far, _ = hold(out_far, hats)
    out_diag = beside(out_far)
    out_diag, _ = hold(out_diag, errs[2])
    block_out, grad_noisy, grad_clean = place(
        [(0, 0, 0, 0), (1, 0, 0, 1), (2, 0, 0, 2), (3, 0, 0, 3), (4, 0, 1, 0), (4, 1, 2, 0), (5, 0, 1, 1), (5, 1, 2, 1)], 3,
        out_half, out_side, out_far, out_diag, ends, ends_side)
    ends_far, grad_noisy, grad_clean = hold(ends_far, grad_noisy, grad_clean)
    ends_diag = beside(ends_far)
    grad_noisy, grad_clean = place(
        [(0, 0, 0, 2), (0, 1, 1, 2), (1, 0, 0, 3), (1, 1, 1, 3)], 2, ends_far, ends_diag, onto=(grad_noisy, grad_clean))
    gain_grad = (gain_sum + across(gain_sum))[:6].reshape(2, D) / replicas
    gain_step = 0.5 * gain_moment + gain_grad
    gains_new = (gain_grad, norm_gains - rates[4] * gain_step, gain_step)
    fresh = [news[3 * t + k] if t < 3 else news[3 * t + k].T for k in range(3) for t in range(4)]
    return (
        block_out, grad_noisy, grad_clean, *gains_new, *fresh,
        jnp.swapaxes(errs[0], 1, 2), *errs[1:], *[v.T for v in left_new], *[v.T for v in right_new],
    )


def solution(mesh):
    in_specs = (
        P("dp", None), P("dp", None), P("dp"), P("dp", None), P(),
        P(None, "mp"), P("mp", None), P(None, "mp"), P("mp", None),
        *([P("dp", "mp"), P("mp", "dp")] * 6),
        *([P("dp", None, "mp"), P("dp", "mp", None)] * 2),
        *([P("mp", None), P(None, "mp")] * 2),
        P(),
    )
    out_specs = (
        P("dp", None), P("dp", None), P("dp", None), P(), P(), P(),
        *([P("dp", "mp"), P("mp", "dp")] * 6),
        *([P("dp", None, "mp"), P("dp", "mp", None)] * 2),
        *([P(None, "mp"), P("mp", None)] * 2),
        *([P("mp", None), P(None, "mp")] * 2),
    )
    return jax.shard_map(local, mesh=mesh, in_specs=in_specs, out_specs=out_specs, check_vma=False)
```

```python
import functools
import math

import jax
import jax.numpy as jnp
import numpy as np
from jax import lax
from jax.experimental import pallas as pl
from jax.experimental.pallas import tpu as pltpu
from jax.sharding import PartitionSpec as P

D = 768
HEADS = 12
HD = 64
FF = 3072
LEN = 1024
RANK = 8
EMA_STEPS = 4
TILE = 256
SLOT = 256

BF = jnp.bfloat16
F32 = jnp.float32
highest = lax.Precision.HIGHEST
norm_eps = 1e-05
gelu_coef = 0.7978845608028654
masked_score = -1e30
MESH_ID = pl.DeviceIdType.MESH


def nt(a, b):
    return lax.dot_general(a, b, (((1,), (1,)), ((), ())), preferred_element_type=F32)


def nn(a, b):
    return lax.dot_general(a, b, (((1,), (0,)), ((), ())), preferred_element_type=F32)


def tn(a, b):
    return lax.dot_general(a, b, (((0,), (0,)), ((), ())), preferred_element_type=F32)


def rotary_tables():
    half = HD // 2
    step = np.float32(-2.0 * math.log(10000.0) / HD)
    inverse = np.exp(np.arange(half, dtype=np.float32) * step).astype(np.float32)
    angle = (np.arange(LEN, dtype=np.float32)[:, None] * inverse[None, :]).astype(np.float32)
    c = np.cos(angle).astype(np.float32)
    s = np.sin(angle).astype(np.float32)
    return np.concatenate([c, c, c, c], 1), np.concatenate([-s, s, -s, s], 1)


def spin(v, cos, sin):
    lane = lax.broadcasted_iota(jnp.int32, v.shape, 1)
    low = lax.rem(lane, HD) < HD // 2
    swapped = jnp.where(low, pltpu.roll(v, 128 - HD // 2, 1), pltpu.roll(v, HD // 2, 1))
    return v * cos + swapped * sin


def block_ids(size, shape, dim):
    shift = 2 + (size >= 8).astype(jnp.int32) + (size >= 16).astype(jnp.int32)
    place = lax.broadcasted_iota(jnp.int32, shape, dim)
    return lax.shift_right_logical(place, jnp.full(shape, shift, jnp.int32))


def fill_bias(size, noisy_bias, clean_bias):
    keys = block_ids(size, (TILE, TILE), 0)
    rows = block_ids(size, (TILE, TILE), 1)
    noisy_bias[...] = jnp.where(rows == keys, 0.0, masked_score)
    clean_bias[...] = jnp.where(keys < rows, 0.0, masked_score)


def norm_parts(values):
    centered = values - jnp.mean(values, axis=1, keepdims=True)
    scale = lax.rsqrt(jnp.mean(centered * centered, axis=1, keepdims=True) + norm_eps)
    return centered * scale, scale


def norm_back(values, gain, grad):
    unit, scale = norm_parts(values)
    scaled = grad * gain
    inner = jnp.mean(scaled * unit, axis=1, keepdims=True)
    grad_in = scale * (scaled - jnp.mean(scaled, axis=1, keepdims=True) - unit * inner)
    return grad_in, jnp.sum(grad * unit, axis=0, keepdims=True)


def gelu_and_slope(u):
    square = u * u
    half = 0.5 + 0.5 * jnp.tanh(u * (gelu_coef + (gelu_coef * 0.044715) * square))
    slope = half + (u * (2.0 * half * (1.0 - half))) * (gelu_coef + (3.0 * 0.044715 * gelu_coef) * square)
    return u * half, slope


def whole(shape):
    return pl.BlockSpec(shape, lambda *index: (0,) * len(shape), pipeline_mode=pl.Buffered(1))


def side_rows(h, info, size):
    return (info[0], 0)


def lane2(h, *_):
    return (0, h)


def row3(h, *_):
    return (h, 0, 0)


def attend_head(head, xn_ref, xc_ref, w_ref, cos_ref, sin_ref, qn_ref, qc_ref, att_ref, lse_ref,
                bn_ref, bc_ref, kn_ref, kc_ref, vnt_ref, vct_ref):
    w = w_ref[pl.ds(pl.multiple_of(head * 3 * HD, 3 * HD), 3 * HD), :]
    for src, dst, keys, vals in ((xn_ref, qn_ref, kn_ref, vnt_ref), (xc_ref, qc_ref, kc_ref, vct_ref)):
        a = nt(src[...], w)
        r = spin(a[:, :128], cos_ref[...], sin_ref[...]).astype(BF)
        v = a[:, 128:].astype(BF)
        dst[:, :128] = r
        dst[:, 128:192] = v
        keys[...] = r[:, 64:128]
        vals[...] = jnp.transpose(v)
    here = pl.ds(pl.multiple_of(head * HD, HD), HD)
    for i in range(LEN // TILE):
        lo, hi = i * TILE, (i + 1) * TILE
        q = qn_ref[lo:hi, 0:64] * 0.125
        parts = [nt(kn_ref[lo:hi, :], q) + bn_ref[...], nt(kc_ref[lo:hi, :], q) + bc_ref[...]]
        if i:
            parts.append(nt(kc_ref[0:lo, :], q))
        peak = functools.reduce(jnp.maximum, [jnp.max(s, axis=0, keepdims=True) for s in parts])
        exps = [jnp.exp(s - peak) for s in parts]
        total = functools.reduce(jnp.add, [jnp.sum(e, axis=0, keepdims=True) for e in exps])
        inv = 1.0 / total
        low = [(e * inv).astype(BF) for e in exps]
        o = nn(vnt_ref[:, lo:hi], low[0]) + nn(vct_ref[:, lo:hi], low[1])
        if i:
            o = o + nn(vct_ref[:, 0:lo], low[2])
        att_ref[here, lo:hi] = o.astype(BF)
        lse_ref[0, :, lo:hi] = jnp.broadcast_to(peak + jnp.log(total), (8, TILE))


def attend_kernel(size_ref, noisy_hbm, clean_hbm, w_hbm, wo_hbm, gain_ref, cos_ref, sin_ref,
                  qn_ref, qc_ref, att_ref, lse_ref, xn_hbm, xc_hbm, w_far_hbm, o_far_hbm,
                  raw_ref, x_ref, w_ref, o_ref, sem_in, sem_out, sem_send, sem_recv, *work):
    head = pl.program_id(0)
    side = lax.axis_index("mp") // 2
    peer = far_peer()
    sides = ((noisy_hbm, xn_hbm), (clean_hbm, xc_hbm))
    width = 3 * HD

    def load(s, i):
        at = pl.ds(pl.multiple_of(side * LEN + i * TILE, TILE), TILE)
        return pltpu.make_async_copy(sides[s][0].at[at], raw_ref.at[s, chunk(i)], sem_in.at[CHUNKS * s + i])

    def save(s):
        return pltpu.make_async_copy(x_ref.at[s], sides[s][1], sem_out.at[s])

    dp = lax.axis_index("dp")
    odd = lax.rem(dp, 2)
    mate = (dp + 1 - 2 * odd, lax.axis_index("mp"))
    part = width // 2

    def pick(j, which):
        return pl.ds(pl.multiple_of(width * j + part * which, part), part)

    def give(j):
        return push(w_hbm.at[pick(j, odd)], w_ref.at[pick(3 + j, odd)], sem_send.at[j], sem_recv.at[j], peer)

    def relay(j):
        return push(w_ref.at[pick(3 + j, odd)], w_ref.at[pick(3 + j, odd)], sem_send.at[4 + j], sem_recv.at[4 + j], mate)

    near_w = pltpu.make_async_copy(w_hbm, w_ref.at[0:3 * width], sem_in.at[2 * CHUNKS])
    give_out = push(wo_hbm.at[pick(0, odd)], o_ref.at[pick(0, odd)], sem_send.at[3], sem_recv.at[3], peer)
    relay_out = push(o_ref.at[pick(0, odd)], o_ref.at[pick(0, odd)], sem_send.at[7], sem_recv.at[7], mate)
    keep_w = pltpu.make_async_copy(w_ref.at[3 * width:], w_far_hbm, sem_out.at[2])
    keep_o = pltpu.make_async_copy(o_ref, o_far_hbm, sem_out.at[3])

    @pl.when(head == 0)
    def _():
        for s in range(2):
            for i in range(CHUNKS):
                load(s, i).start()
        near_w.start()
        greet(peer, mate)
        for j in range(3):
            give(j).start()
        give_out.start()
        fill_bias(size_ref[side], work[0], work[1])
        for s in range(2):
            for i in range(CHUNKS):
                load(s, i).wait()
                x = norm_parts(raw_ref[s, chunk(i), :].astype(F32))[0] * gain_ref[0:1, :]
                x_ref[s, chunk(i), :] = x.astype(BF)
            save(s).start()
        near_w.wait()

    for j in range(3):
        @pl.when(head == 1 + j)
        def _():
            give(j).wait_recv()
            relay(j).start()

    @pl.when(head == 3)
    def _():
        give_out.wait_recv()
        relay_out.start()

    for j in range(3):
        @pl.when(head == 3 + j)
        def _():
            relay(j).wait_recv()

    @pl.when(head == 5)
    def _():
        keep_w.start()
        relay_out.wait_recv()
        keep_o.start()

    attend_head(head, x_ref.at[0], x_ref.at[1], w_ref, cos_ref, sin_ref, qn_ref, qc_ref, att_ref, lse_ref, *work)

    @pl.when(head == 5)
    def _():
        save(0).wait()
        save(1).wait()
        keep_w.wait()
        keep_o.wait()
        for j in range(3):
            give(j).wait_send()
            relay(j).wait_send()
        give_out.wait_send()
        relay_out.wait_send()


CHUNKS = LEN // TILE
HALF = LEN // 2


def chunk(i):
    return slice(i * TILE, (i + 1) * TILE)


def anywhere():
    return pl.BlockSpec(memory_space=pl.ANY)


def in_vmem():
    return pl.BlockSpec(memory_space=pltpu.VMEM)


def dma(n):
    return pltpu.SemaphoreType.DMA((n,))


def rows_of(n):
    return jax.ShapeDtypeStruct((n, D), BF)


attend_work = [
    pltpu.VMEM((TILE, TILE), F32),
    pltpu.VMEM((TILE, TILE), F32),
    pltpu.VMEM((LEN, HD), BF),
    pltpu.VMEM((LEN, HD), BF),
    pltpu.VMEM((HD, LEN), BF),
    pltpu.VMEM((HD, LEN), BF),
]
rows_shape = jax.ShapeDtypeStruct((LEN, D), BF)


def attend(size, noisy, clean, w, wo, gains, cos, sin):
    return pl.pallas_call(
        attend_kernel,
        grid=(6,),
        in_specs=[pl.BlockSpec(memory_space=pltpu.SMEM)] + [anywhere()] * 4
        + [whole((2, D)), whole((LEN, 128)), whole((LEN, 128))],
        out_specs=[pl.BlockSpec((LEN, SLOT), lane2), pl.BlockSpec((LEN, SLOT), lane2), whole((6 * HD, LEN)),
                   pl.BlockSpec((1, 8, LEN), row3)] + [anywhere()] * 4,
        out_shape=[jax.ShapeDtypeStruct((LEN, SLOT * 6), BF), jax.ShapeDtypeStruct((LEN, SLOT * 6), BF),
                   jax.ShapeDtypeStruct((6 * HD, LEN), BF), jax.ShapeDtypeStruct((6, 8, LEN), F32),
                   rows_shape, rows_shape, rows_of(9 * HD), rows_of(3 * HD)],
        scratch_shapes=[pltpu.VMEM((2, LEN, D), BF), pltpu.VMEM((2, LEN, D), BF), pltpu.VMEM((18 * HD, D), BF),
                        pltpu.VMEM((3 * HD, D), BF), dma(2 * CHUNKS + 1), dma(4), dma(8), dma(8)] + attend_work,
        compiler_params=pltpu.CompilerParams(collective_id=6, has_side_effects=True, vmem_limit_bytes=60 << 20),
        name="attend",
    )(size, noisy, clean, w, wo, gains, cos, sin)


WIDE = 5 * 128


def back_head(head, qn_ref, qc_ref, lse_ref, cos_ref, sin_ref, av_ref, c_ref,
              bn_ref, bc_ref, kn_ref, kc_ref, knt_ref, kct_ref, dot_ref, do_ref, dq_ref, dkn_ref, dkc_ref, dvc_ref, dvn_ref):
    do_ref[...] = jnp.transpose(dot_ref[pl.ds(pl.multiple_of(head * HD, HD), HD), :])
    kn_ref[...] = qn_ref[:, 64:128]
    kc_ref[...] = qc_ref[:, 64:128]
    knt_ref[...] = jnp.transpose(qn_ref[:, 0:128])[64:128]
    kct_ref[...] = jnp.transpose(qc_ref[:, 0:128])[64:128]
    for i in reversed(range(LEN // TILE)):
        lo, hi = i * TILE, (i + 1) * TILE
        last = i == LEN // TILE - 1
        q = qn_ref[lo:hi, 0:64] * 0.125
        do = do_ref[lo:hi, :]
        lse = lse_ref[0, 0:1, lo:hi]
        spans = [(0, lo, hi), (1, lo, hi)] + ([(1, 0, lo)] if i else [])
        probs, grads, inner = [], [], 0.0
        for n, (side, a, b) in enumerate(spans):
            kr = kc_ref if side else kn_ref
            vr = qc_ref if side else qn_ref
            s = nt(kr[a:b, :], q)
            if n == 0:
                s = s + bn_ref[...]
            if n == 1:
                s = s + bc_ref[...]
            p = jnp.exp(s - lse)
            dp = nt(vr[a:b, 128:192], do)
            inner = inner + jnp.sum(p * dp, axis=0, keepdims=True)
            probs.append(p)
            grads.append(dp)
        dqt = 0.0
        for n, (side, a, b) in enumerate(spans):
            ds = (probs[n] * (grads[n] - inner)).astype(BF)
            dv = nn(probs[n].astype(BF), do)
            dk = nn(ds, q)
            ktr = kct_ref if side else knt_ref
            dqt = dqt + nn(ktr[:, a:b], ds)
            if side and last:
                dkc_ref[a:b, :] = dk
                dvc_ref[a:b, :] = dv
            elif side:
                dkc_ref[a:b, :] += dk
                dvc_ref[a:b, :] += dv
            else:
                dkn_ref[a:b, :] = dk
                dvn_ref[a:b, :] = dv.astype(BF)
        dq_ref[lo:hi, :] = jnp.transpose(dqt) * 0.125
    sin = -sin_ref[...]
    cos = cos_ref[...]
    pair = pl.ds(pl.multiple_of(head * 128, 128), 128)
    av_ref[:, pair] = spin(jnp.concatenate([dq_ref[...], dkn_ref[...]], axis=1), cos, sin).astype(BF)
    both = jnp.concatenate([dkc_ref[...], dvc_ref[...]], axis=1)
    lane = lax.broadcasted_iota(jnp.int32, both.shape, 1)
    c_ref[:, pair] = jnp.where(lane < HD, spin(both, cos, sin), both).astype(BF)
    for j in range(3):
        @pl.when(head == j)
        def _():
            av_ref[:, 384 + HD * j:384 + HD * (j + 1)] = dvn_ref[...]


def group_grad(xn_ref, xc_ref, av, c, gq_ref):
    g = tn(av, xn_ref[...])
    e = tn(c, xc_ref[...])
    for j in range(3):
        row = 3 * HD * j
        gq_ref[row:row + HD, :] = g[128 * j:128 * j + HD].astype(gq_ref.dtype)
        gq_ref[row + HD:row + 2 * HD, :] = (g[128 * j + HD:128 * (j + 1)] + e[128 * j:128 * j + HD]).astype(gq_ref.dtype)
        gq_ref[row + 2 * HD:row + 3 * HD, :] = (
            g[384 + HD * j:384 + HD * (j + 1)] + e[128 * j + HD:128 * (j + 1)]).astype(gq_ref.dtype)


def back_start(size_ref, att_ref, g_ref, wo_ref, go_ref, av_ref, work):
    fill_bias(size_ref[lax.axis_index("mp") // 2], work[0], work[1])
    work[6][...] = nt(wo_ref[...], g_ref[...]).astype(BF)
    go_ref[...] = nn(att_ref[...], g_ref[...]).astype(go_ref.dtype)
    av_ref[:, 576:WIDE] = jnp.zeros((LEN, WIDE - 576), BF)


def back_far_kernel(size_ref, qn_ref, qc_ref, att_ref, lse_ref, g_ref, wo_ref, cos_ref, sin_ref,
                    xn_hbm, xc_hbm, av_ref, c_ref, both_ref, xn_ref, xc_ref, sems, *work):
    head = pl.program_id(0)
    late = [pltpu.make_async_copy(s, d, sems.at[k]) for k, (s, d) in enumerate(((xn_hbm, xn_ref), (xc_hbm, xc_ref)))]

    @pl.when(head == 0)
    def _():
        for c in late:
            c.start()
        back_start(size_ref, att_ref, g_ref, wo_ref, both_ref.at[9 * HD:], av_ref, work)

    back_head(head, qn_ref, qc_ref, lse_ref, cos_ref, sin_ref, av_ref, c_ref, *work)

    @pl.when(head == 2)
    def _():
        for c in late:
            c.wait()
        group_grad(xn_ref, xc_ref, av_ref[...], c_ref[...], both_ref)


def back_near_kernel(size_ref, qn_ref, qc_ref, att_ref, lse_ref, g_ref, wo_ref, cos_ref, sin_ref,
                     xn_hbm, xc_hbm, w_hbm, w_far_hbm, avf_hbm, cf_hbm, gxn_hbm, gxc_hbm, gq_ref, go_ref,
                     xn_ref, xc_ref, wav_ref, wc_ref, av_ref, c_ref, out_ref, sems, sem_w, sem_out, *work):
    head = pl.program_id(0)
    late = [pltpu.make_async_copy(s, d, sems.at[k]) for k, (s, d) in enumerate((
        (xn_hbm, xn_ref), (xc_hbm, xc_ref), (avf_hbm, av_ref.at[:, WIDE:]), (cf_hbm, c_ref.at[:, 384:])))]
    for n, src in enumerate((w_hbm, w_far_hbm)):
        for j in range(3):
            row, base, k = 192 * j, WIDE * n, 3 * (3 * n + j)
            late.append(pltpu.make_async_copy(
                src.at[row:row + 128], wav_ref.at[base + 128 * j:base + 128 * (j + 1)], sem_w.at[k]))
            late.append(pltpu.make_async_copy(
                src.at[row + 128:row + 192], wav_ref.at[base + 384 + 64 * j:base + 448 + 64 * j], sem_w.at[k + 1]))
            late.append(pltpu.make_async_copy(
                src.at[row + 64:row + 192], wc_ref.at[384 * n + 128 * j:384 * n + 128 * (j + 1)], sem_w.at[k + 2]))

    @pl.when(head == 0)
    def _():
        for c in late:
            c.start()
        for n in range(2):
            wav_ref[WIDE * n + 576:WIDE * (n + 1), :] = jnp.zeros((WIDE - 576, D), BF)
        back_start(size_ref, att_ref, g_ref, wo_ref, go_ref, av_ref, work)

    back_head(head, qn_ref, qc_ref, lse_ref, cos_ref, sin_ref, av_ref, c_ref, *work)

    @pl.when(head == 2)
    def _():
        for c in late:
            c.wait()
        copies = []
        for s, (rows, w, out) in enumerate(((av_ref, wav_ref, gxn_hbm), (c_ref, wc_ref, gxc_hbm))):
            for i in range(CHUNKS):
                out_ref[s, chunk(i), :] = nn(rows[chunk(i), :], w[...]).astype(BF)
                copies.append(pltpu.make_async_copy(
                    out_ref.at[s, chunk(i)], out.at[chunk(i)], sem_out.at[CHUNKS * s + i]))
                copies[-1].start()
        group_grad(xn_ref, xc_ref, av_ref[:, :WIDE], c_ref[:, :384], gq_ref)
        for c in copies:
            c.wait()


back_work = attend_work[:4] + [
    pltpu.VMEM((HD, LEN), BF),
    pltpu.VMEM((HD, LEN), BF),
    pltpu.VMEM((3 * HD, LEN), BF),
    pltpu.VMEM((LEN, HD), BF),
    pltpu.VMEM((LEN, HD), F32),
    pltpu.VMEM((LEN, HD), F32),
    pltpu.VMEM((LEN, HD), F32),
    pltpu.VMEM((LEN, HD), F32),
    pltpu.VMEM((LEN, HD), BF),
]
def head_inputs(first):
    return [pl.BlockSpec((LEN, SLOT), lambda h, *_: (0, h + first)), pl.BlockSpec((LEN, SLOT), lambda h, *_: (0, h + first)),
            pl.BlockSpec((3 * HD, LEN), lambda h, *_: (first // 3, 0), pipeline_mode=pl.Buffered(1)),
            pl.BlockSpec((1, 8, LEN), lambda h, *_: (h + first, 0, 0))]


def back_far(size, qn, qc, att, lse, g, wo, cos, sin, xn, xc):
    return pl.pallas_call(
        back_far_kernel,
        grid=(3,),
        in_specs=[pl.BlockSpec(memory_space=pltpu.SMEM)] + head_inputs(3)
        + [whole((LEN, D)), whole((3 * HD, D)), whole((LEN, 128)), whole((LEN, 128)), anywhere(), anywhere()],
        out_specs=[whole((LEN, WIDE)), whole((LEN, 384)), whole((D, D))],
        out_shape=[jax.ShapeDtypeStruct((LEN, WIDE), BF), jax.ShapeDtypeStruct((LEN, 384), BF), rows_of(D)],
        scratch_shapes=[pltpu.VMEM((LEN, D), BF), pltpu.VMEM((LEN, D), BF), dma(2)] + back_work,
        compiler_params=pltpu.CompilerParams(vmem_limit_bytes=60 << 20),
        name="back_far",
    )(size, qn, qc, att, lse, g, wo, cos, sin, xn, xc)


def back_near(size, qn, qc, att, lse, g, wo, cos, sin, xn, xc, w, w_far, av_far, c_far):
    return pl.pallas_call(
        back_near_kernel,
        grid=(3,),
        in_specs=[pl.BlockSpec(memory_space=pltpu.SMEM)] + head_inputs(0)
        + [whole((LEN, D)), whole((3 * HD, D)), whole((LEN, 128)), whole((LEN, 128))] + [anywhere()] * 6,
        out_specs=[anywhere(), anywhere(), whole((9 * HD, D)), whole((3 * HD, D))],
        out_shape=[rows_shape, rows_shape, jax.ShapeDtypeStruct((9 * HD, D), F32), jax.ShapeDtypeStruct((3 * HD, D), F32)],
        scratch_shapes=[pltpu.VMEM((LEN, D), BF), pltpu.VMEM((LEN, D), BF), pltpu.VMEM((2 * WIDE, D), BF), pltpu.VMEM((D, D), BF),
                        pltpu.VMEM((LEN, 2 * WIDE), BF), pltpu.VMEM((LEN, D), BF), pltpu.VMEM((2, LEN, D), BF),
                        dma(4), dma(18), dma(2 * CHUNKS)] + back_work,
        compiler_params=pltpu.CompilerParams(vmem_limit_bytes=60 << 20),
        name="back_near",
    )(size, qn, qc, att, lse, g, wo, cos, sin, xn, xc, w, w_far, av_far, c_far)


def halves(v):
    high = v.astype(BF)
    return high, (v - high.astype(F32)).astype(BF)


def exact(left_side, right_side, left_dim, right_dim):
    dims = (((left_dim,), (right_dim,)), ((), ()))
    a, b = halves(left_side)
    c, d = halves(right_side)

    def times(x, y):
        return lax.dot_general(x, y, dims, preferred_element_type=F32)

    return times(a, c) + (times(a, d) + times(b, c))


def core_peer():
    m = lax.axis_index("mp")
    return (lax.axis_index("dp"), m + 1 - 2 * lax.rem(m, 2))


def far_peer():
    return (lax.axis_index("dp"), lax.rem(lax.axis_index("mp") + 2, 4))


def greet(*peers):
    barrier = pltpu.get_barrier_semaphore()
    for p in peers:
        pl.semaphore_signal(barrier, inc=1, device_id=p, device_id_type=MESH_ID)
    pl.semaphore_wait(barrier, len(peers))


PARTS = HALF // TILE


def own_rows(i):
    half = lax.rem(lax.axis_index("mp"), 2)
    return pl.ds(pl.multiple_of(half * HALF + i * TILE, TILE), TILE)


def peer_rows(i):
    half = lax.rem(lax.axis_index("mp"), 2)
    return pl.ds(pl.multiple_of((1 - half) * HALF + i * TILE, TILE), TILE)


def side_rows_of(i):
    m = lax.axis_index("mp")
    return pl.ds(pl.multiple_of(m * HALF + i * TILE, TILE), TILE)


def copy(src, dst, sem):
    return pltpu.make_async_copy(src, dst, sem)


def push(src, dst, send_sem, recv_sem, peer):
    return pltpu.make_async_remote_copy(
        src_ref=src, dst_ref=dst, send_sem=send_sem, recv_sem=recv_sem, device_id=peer, device_id_type=MESH_ID)


class Sems:
    def __init__(self, ref):
        self.ref = ref
        self.used = 0

    def take(self):
        self.used += 1
        return self.ref.at[self.used - 1]


def middle_kernel(att_hbm, wo_near_hbm, wo_far_hbm, rows_hbm, cot_hbm, up_hbm, down_hbm,
                  err_up_hbm, err_down_hbm, fac_up_ref, fac_down_ref, gain_ref,
                  res_hbm, grad_hbm, low_hbm, mlp_hbm, fold_hbm, mat_up_hbm, mat_down_hbm,
                  left_up_ref, left_down_ref, gsum_ref,
                  att_ref, wo_ref, x_ref, send_ref, far_ref, r_ref, nm_ref, cot_ref, up_ref, down_ref, hid_ref, gp_ref,
                  mlp_ref, gm_ref, back_ref, fold_gm_ref, fold_mlp_ref, sum_ref, msum_ref, yet_ref,
                  mat_up_ref, mat_down_ref, nmt_ref, grad_ref, low_ref, sem_ref, send_sem_ref, recv_sem_ref):
    sems, sends, recvs = Sems(sem_ref), Sems(send_sem_ref), Sems(recv_sem_ref)
    m = lax.axis_index("mp")
    side, half = m // 2, lax.rem(m, 2)
    core, far = core_peer(), far_peer()
    width = 3 * HD
    third = D // 3
    pushes, saves = [], []

    def load(src, dst):
        c = pltpu.make_async_copy(src, dst, sems.take())
        c.start()
        return c

    def save(src, dst):
        saves.append(load(src, dst))

    def send(src, dst, peer):
        c = push(src, dst, sends.take(), recvs.take(), peer)
        c.start()
        pushes.append(c)
        return c

    def span(start, n):
        return pl.ds(pl.multiple_of(start, TILE), n)

    own_half, peer_half = half * HALF, (1 - half) * HALF
    first = [load(att_hbm, att_ref), load(wo_near_hbm, wo_ref.at[0:width]), load(wo_far_hbm, wo_ref.at[width:])]
    xs = [load(rows_hbm.at[span(m * HALF + i * TILE, TILE)], x_ref.at[chunk(i)]) for i in range(PARTS)]
    up_in, down_in = load(up_hbm, up_ref), load(down_hbm, down_ref)
    cot_in = load(cot_hbm.at[span(side * LEN, LEN)], cot_ref.at[0:LEN])
    cot_far_in = load(cot_hbm.at[span((1 - side) * LEN, LEN)], cot_ref.at[LEN:])
    err_in = [load(err_down_hbm.at[0], mat_down_ref), load(err_up_hbm.at[0], mat_up_ref)]
    greet(core, far)
    for c in first:
        c.wait()
    normed, cross = [], []
    for i in range(PARTS):
        send_ref[chunk(i), :] = tn(att_ref[:, span(peer_half + i * TILE, TILE)], wo_ref[...]).astype(BF)
        handed = send(send_ref.at[chunk(i)], far_ref.at[chunk(i)], core)
        at = span(own_half + i * TILE, TILE)
        own = tn(att_ref[:, at], wo_ref[...])
        xs[i].wait()
        handed.wait_recv()
        r = x_ref[chunk(i), :].astype(F32) + (own + far_ref[chunk(i), :].astype(F32))
        r_ref[chunk(i), :] = r
        nm_ref[at, :] = (norm_parts(r)[0] * gain_ref[1:2, :]).astype(BF)
        normed.append(send(nm_ref.at[at], nm_ref.at[at], core))
        cross.append(send(nm_ref.at[at], nm_ref.at[span(LEN + own_half + i * TILE, TILE)], far))
        save(r_ref.at[chunk(i)], res_hbm.at[chunk(i)])

    def feed_rows(start, n):
        at = span(start, n)
        for t in range(3):
            lanes = slice(t * third, (t + 1) * third)
            hidden, slope = gelu_and_slope(nn(nm_ref[at, :], up_ref[:, lanes]))
            hid_ref[at, lanes] = hidden.astype(BF)
            gp_ref[at, lanes] = (slope * nt(cot_ref[at, :], down_ref[lanes, :])).astype(BF)
        gm_ref[at, :] = nt(gp_ref[at, :], up_ref[...]).astype(BF)
        mlp_ref[at, :] = nn(hid_ref[at, :], down_ref[...]).astype(BF)

    up_in.wait()
    down_in.wait()
    cot_in.wait()
    feed_rows(own_half, HALF)
    for c in normed:
        c.wait_recv()
    feed_rows(peer_half, HALF)
    save(mlp_ref.at[0:LEN], mlp_hbm)
    swap = [send(gm_ref.at[span(peer_half + i * TILE, TILE)], back_ref.at[chunk(i)], core) for i in range(PARTS)]
    cot_far_in.wait()
    arrived = []
    for i in range(PARTS):
        at = span(LEN + own_half + i * TILE, TILE)
        away = span(LEN + peer_half + i * TILE, TILE)
        cross[i].wait_recv()
        relay = send(nm_ref.at[at], nm_ref.at[at], core)
        feed_rows(LEN + own_half + i * TILE, TILE)
        relay.wait_recv()
        feed_rows(LEN + peer_half + i * TILE, TILE)
        fold = send(gm_ref.at[away], fold_gm_ref.at[chunk(i)], core)
        fold_mlp = send(mlp_ref.at[away], fold_mlp_ref.at[chunk(i)], core)
        fold.wait_recv()
        sum_ref[chunk(i), :] = (gm_ref[at, :].astype(F32) + fold_gm_ref[chunk(i), :].astype(F32)).astype(BF)
        arrived.append(send(sum_ref.at[chunk(i)], yet_ref.at[chunk(i)], far))
        fold_mlp.wait_recv()
        msum_ref[chunk(i), :] = (mlp_ref[at, :].astype(F32) + fold_mlp_ref[chunk(i), :].astype(F32)).astype(BF)
        save(msum_ref.at[chunk(i)], fold_hbm.at[chunk(i)])

    for i in range(8):
        at = slice(i * TILE, (i + 1) * TILE)
        nmt_ref[:, at] = jnp.transpose(nm_ref[at, :])
    for c in err_in:
        c.wait()
    left_up = 0.0
    for t in range(3):
        lanes = slice(t * third, (t + 1) * third)
        mat = tn(hid_ref[:, lanes], cot_ref[...]) + mat_down_ref[lanes, :]
        mat_down_ref[lanes, :] = mat
        save(mat_down_ref.at[lanes], mat_down_hbm.at[lanes])
        left_down_ref[:, lanes] = exact(fac_down_ref[...], mat, 1, 1)
        mat = nn(nmt_ref[...], gp_ref[:, lanes]) + mat_up_ref[:, lanes]
        mat_up_ref[:, lanes] = mat
        save(mat_up_ref.at[:, lanes], mat_up_hbm.at[:, lanes])
        left_up = left_up + exact(fac_up_ref[:, lanes], mat, 1, 1)
    left_up_ref[...] = left_up

    gsum = 0.0
    lows = []
    for i in range(PARTS):
        at = span(own_half + i * TILE, TILE)
        swap[i].wait_recv()
        total = gm_ref[at, :].astype(F32) + back_ref[chunk(i), :].astype(F32)
        arrived[i].wait_recv()
        total = total + yet_ref[chunk(i), :].astype(F32)
        grad, share = norm_back(r_ref[chunk(i), :], gain_ref[1:2, :], total)
        gsum = gsum + share
        grad = cot_ref[at, :].astype(F32) + grad
        grad_ref[chunk(i), :] = grad
        low_ref[chunk(i), :] = grad.astype(BF)
        lows.append(send(low_ref.at[chunk(i)], low_hbm.at[at], core))
        save(low_ref.at[chunk(i)], low_hbm.at[at])
        save(grad_ref.at[chunk(i)], grad_hbm.at[chunk(i)])
    gsum_ref[...] = gsum
    for c in lows:
        c.wait_recv()
    for c in pushes:
        c.wait_send()
    for c in saves:
        c.wait()


def middle(att, wo_near, wo_far, rows, cotangent, up, down, err_up, err_down, fac_up, fac_down, gains):
    def low(n):
        return pltpu.VMEM((n, D), BF)

    def wide(n):
        return pltpu.VMEM((n, D), F32)

    return pl.pallas_call(
        middle_kernel,
        in_specs=[anywhere()] * 9 + [in_vmem()] * 3,
        out_specs=[anywhere()] * 7 + [in_vmem()] * 3,
        out_shape=[jax.ShapeDtypeStruct((HALF, D), F32), jax.ShapeDtypeStruct((HALF, D), F32), rows_of(LEN), rows_of(LEN),
                   rows_of(HALF), jax.ShapeDtypeStruct((D, D), F32), jax.ShapeDtypeStruct((D, D), F32),
                   jax.ShapeDtypeStruct((RANK, D), F32), jax.ShapeDtypeStruct((RANK, D), F32),
                   jax.ShapeDtypeStruct((1, D), F32)],
        scratch_shapes=[pltpu.VMEM((6 * HD, LEN), BF), low(6 * HD), low(HALF), low(HALF), low(HALF), wide(HALF),
                        low(2 * LEN), low(2 * LEN), low(D), low(D), low(2 * LEN), low(2 * LEN),
                        low(2 * LEN), low(2 * LEN), low(HALF), low(HALF), low(HALF), low(HALF), low(HALF), low(HALF),
                        wide(D), wide(D), pltpu.VMEM((D, 2 * LEN), BF), wide(HALF), low(HALF), dma(32), dma(24), dma(24)],
        compiler_params=pltpu.CompilerParams(collective_id=3, has_side_effects=True, vmem_limit_bytes=60 << 20),
        name="middle",
    )(att, wo_near, wo_far, rows, cotangent, up, down, err_up, err_down, fac_up, fac_down, gains)


def settle_kernel(mlp_hbm, far_hbm, res_hbm, out_hbm, own_ref, far_ref, res_ref, core_ref, out_ref,
                  sem_in, sem_send, sem_recv, sem_out):
    peer = core_peer()
    loads = []
    for i in range(PARTS):
        loads += [copy(mlp_hbm.at[own_rows(i)], own_ref.at[chunk(i)], sem_in.at[3 * i]),
                  copy(far_hbm.at[chunk(i)], far_ref.at[chunk(i)], sem_in.at[3 * i + 1]),
                  copy(res_hbm.at[chunk(i)], res_ref.at[chunk(i)], sem_in.at[3 * i + 2])]
    for c in loads:
        c.start()
    greet(peer)
    pushes = [push(mlp_hbm.at[peer_rows(i)], core_ref.at[chunk(i)], sem_send.at[i], sem_recv.at[i], peer)
              for i in range(PARTS)]
    for c in pushes:
        c.start()
    saves = []
    for i in range(PARTS):
        for c in loads[3 * i:3 * i + 3]:
            c.wait()
        pushes[i].wait_recv()
        total = own_ref[chunk(i), :].astype(F32) + core_ref[chunk(i), :].astype(F32) + far_ref[chunk(i), :].astype(F32)
        out_ref[chunk(i), :] = (res_ref[chunk(i), :] + total).astype(BF)
        saves.append(copy(out_ref.at[chunk(i)], out_hbm.at[chunk(i)], sem_out.at[i]))
        saves[-1].start()
    for c in saves:
        c.wait()
    for c in pushes:
        c.wait_send()


def settle(mlp, far, residual):
    half = pltpu.VMEM((HALF, D), BF)
    return pl.pallas_call(
        settle_kernel,
        in_specs=[anywhere()] * 3,
        out_specs=anywhere(),
        out_shape=rows_of(HALF),
        scratch_shapes=[half, half, pltpu.VMEM((HALF, D), F32), half, half, dma(3 * PARTS), dma(PARTS), dma(PARTS), dma(PARTS)],
        compiler_params=pltpu.CompilerParams(collective_id=4, has_side_effects=True, vmem_limit_bytes=60 << 20),
        name="settle",
    )(mlp, far, residual)


def finish_kernel(gxn_hbm, gxc_hbm, noisy_hbm, clean_hbm, grad_hbm, gain_ref, gain_two_ref, ends_hbm, gsum_ref,
                  own_ref, far_ref, x_ref, wide_ref, out_ref,
                  sem_own, sem_x, sem_wide, sem_send, sem_recv, sem_out):
    sources = (gxn_hbm, gxc_hbm)
    count = 2 * PARTS
    own, rows, wide = [], [], []
    for n in range(count):
        k, i = n // PARTS, n % PARTS
        own.append(copy(sources[k].at[own_rows(i)], own_ref.at[chunk(n)], sem_own.at[n]))
        rows.append(copy((noisy_hbm, clean_hbm)[k].at[side_rows_of(i)], x_ref.at[chunk(n)], sem_x.at[n]))
        if k == 0:
            wide.append(copy(grad_hbm.at[chunk(i)], wide_ref.at[chunk(i)], sem_wide.at[i]))
    for c in own + rows + wide:
        c.start()
    peer = core_peer()
    greet(peer)
    pushes = []
    for n in range(count):
        k, i = n // PARTS, n % PARTS
        pushes.append(push(sources[k].at[peer_rows(i)], far_ref.at[chunk(n)], sem_send.at[n], sem_recv.at[n], peer))
        pushes[-1].start()
    gsum = 0.0
    saves = []
    for n in range(count):
        k, i = n // PARTS, n % PARTS
        own[n].wait()
        rows[n].wait()
        pushes[n].wait_recv()
        total = own_ref[chunk(n), :].astype(F32) + far_ref[chunk(n), :].astype(F32)
        grad, share = norm_back(x_ref[chunk(n), :].astype(F32), gain_ref[0:1, :], total)
        gsum = gsum + share
        if k == 0:
            wide[i].wait()
            grad = wide_ref[chunk(i), :] + grad
        out_ref[chunk(n), :] = grad.astype(BF)
        saves.append(copy(out_ref.at[chunk(n)], ends_hbm.at[chunk(n)], sem_out.at[n]))
        saves[-1].start()
    gsum_ref[0:1, :] = gsum
    gsum_ref[1:2, :] = gain_two_ref[...]
    gsum_ref[2:8, :] = jnp.zeros((6, D), F32)
    for c in saves:
        c.wait()
    for c in pushes:
        c.wait_send()


def finish(gxn, gxc, noisy_rows, clean_rows, grad_resid, gains, gain_two):
    buf = pltpu.VMEM((LEN, D), BF)
    return pl.pallas_call(
        finish_kernel,
        in_specs=[anywhere()] * 5 + [in_vmem()] * 2,
        out_specs=[anywhere(), in_vmem()],
        out_shape=[rows_of(LEN), jax.ShapeDtypeStruct((RANK, D), F32)],
        scratch_shapes=[buf, buf, buf, pltpu.VMEM((HALF, D), F32), buf,
                        dma(2 * PARTS), dma(2 * PARTS), dma(PARTS), dma(2 * PARTS), dma(2 * PARTS), dma(2 * PARTS)],
        compiler_params=pltpu.CompilerParams(collective_id=5, has_side_effects=True, vmem_limit_bytes=60 << 20),
        name="finish",
    )(gxn, gxc, noisy_rows, clean_rows, grad_resid, gains, gain_two)


def place_kernel(plan, given, count, *refs):
    sources, outs = refs[:given], refs[len(refs) - 3 - count:len(refs) - 3]
    stage, sem_in, sem_out = refs[len(refs) - 3:]
    m = lax.axis_index("mp")
    beside = m + 1 - 2 * lax.rem(m, 2)
    spots = (m, beside, lax.rem(m + 2, 4), lax.rem(beside + 2, 4))
    loads = [copy(sources[s].at[part * HALF:(part + 1) * HALF], stage.at[j], sem_in.at[j])
             for j, (s, part, _, _) in enumerate(plan)]
    for c in loads:
        c.start()
    saves = []
    for j, (_, _, target, spot) in enumerate(plan):
        loads[j].wait()
        at = pl.ds(pl.multiple_of(spots[spot] * HALF, HALF), HALF)
        saves.append(copy(stage.at[j], outs[target].at[at], sem_out.at[j]))
        saves[-1].start()
    for c in saves:
        c.wait()


def place(plan, count, *pieces, onto=()):
    total, given = len(plan), len(pieces)
    return pl.pallas_call(
        functools.partial(place_kernel, plan, given, count),
        in_specs=[anywhere()] * (given + len(onto)),
        out_specs=[anywhere()] * count,
        out_shape=[rows_of(2 * LEN)] * count,
        scratch_shapes=[pltpu.VMEM((total, HALF, D), BF), dma(total), dma(total)],
        input_output_aliases={given + k: k for k in range(len(onto))},
        compiler_params=pltpu.CompilerParams(vmem_limit_bytes=14 << 20),
        name="place",
    )(*pieces, *onto)


PACK = 1024


def left_products(gq, both_ref, eq, go, eo, fq_ref, fo_ref, lu_ref, ld_ref, gain_ref, mq_ref, mo_ref, pack_ref):
    pack_ref[...] = jnp.zeros_like(pack_ref)
    mq = gq + both_ref[:9 * HD, :].astype(F32) + eq
    mq_ref[...] = mq
    pack_ref[0:8, 0:D] = exact(fq_ref[...], mq, 1, 0)
    mo = go + both_ref[9 * HD:, :].astype(F32) + eo
    mo_ref[...] = mo
    pack_ref[0:8, D:D + 3 * HD] = exact(fo_ref[...], mo, 1, 1)
    pack_ref[8:16, 0:D] = lu_ref[...]
    pack_ref[16:24, 0:D] = ld_ref[...]
    for k in range(6):
        pack_ref[8 + k:9 + k, D:PACK] = gain_ref[k // 3:k // 3 + 1, 256 * (k % 3):256 * (k % 3 + 1)]


def lefts_kernel(gq_ref, both_ref, eq_ref, go_ref, eo_ref, fq_ref, fo_ref, lu_ref, ld_ref, gain_ref,
                 mq_ref, mo_ref, pack_ref):
    left_products(gq_ref[...], both_ref, eq_ref[0], go_ref[...], eo_ref[0], fq_ref, fo_ref, lu_ref, ld_ref, gain_ref,
                  mq_ref, mo_ref, pack_ref)


def lefts(*args):
    return pl.pallas_call(
        lefts_kernel,
        grid=(1,),
        in_specs=[whole(v.shape) for v in args],
        out_specs=[whole((9 * HD, D)), whole((3 * HD, D)), whole((3 * RANK, PACK))],
        out_shape=[jax.ShapeDtypeStruct((9 * HD, D), F32), jax.ShapeDtypeStruct((3 * HD, D), F32),
                   jax.ShapeDtypeStruct((3 * RANK, PACK), F32)],
        compiler_params=pltpu.CompilerParams(vmem_limit_bytes=60 << 20),
        name="lefts",
    )(*args)


def orthonormalize(sum_ref):
    mats = [sum_ref[0:8, 0:D], sum_ref[0:8, D:PACK], sum_ref[8:16, 0:D], sum_ref[16:24, 0:D]]
    for k in range(RANK):
        for t in range(4):
            a = mats[t]
            row = lax.broadcasted_iota(jnp.int32, a.shape, 0)
            v = a[k:k + 1, :]
            e = v / (jnp.sqrt(jnp.sum(v * v, axis=1, keepdims=True)) + 1e-08)
            c = jnp.sum(a * e, axis=1, keepdims=True)
            mats[t] = jnp.where(row == k, e, jnp.where(row > k, a - c * e, a))
    mats[1] = mats[1][:, :3 * HD]
    return mats


def right_products(hats, mq_ref, mo_ref, mu_ref, md_ref, pack_ref):
    out = exact(hats[1], mo_ref[...], 1, 0)
    pack_ref[0:8, 0:D] = exact(hats[2], mu_ref[...], 1, 0)
    pack_ref[8:16, 0:D] = exact(hats[3], md_ref[...], 1, 0)
    pack_ref[16:24, 0:D] = jnp.zeros((RANK, D), F32)
    pack_ref[16:24, 0:9 * HD] = exact(hats[0], mq_ref[...], 1, 1)
    for k in range(3):
        pack_ref[8 * k:8 * k + 8, D:PACK] = out[:, 256 * k:256 * (k + 1)]


def unpack_rights(pack_ref):
    out = jnp.concatenate([pack_ref[8 * k:8 * k + 8, D:PACK] for k in range(3)], axis=1)
    return [pack_ref[16:24, 0:9 * HD], out, pack_ref[0:8, 0:D], pack_ref[8:16, 0:D]]


def rights_kernel(sum_ref, mq_ref, mo_ref, mu_ref, md_ref, hq_ref, ho_ref, hu_ref, hd_ref, pack_ref):
    hats = orthonormalize(sum_ref)
    for hat, ref in zip(hats, (hq_ref, ho_ref, hu_ref, hd_ref)):
        ref[...] = hat
    right_products(hats, mq_ref, mo_ref, mu_ref, md_ref, pack_ref)


def rights(left_sum, mats):
    args = (left_sum, *mats)
    shapes = [(RANK, D), (RANK, 3 * HD), (RANK, D), (RANK, D), (3 * RANK, PACK)]
    return pl.pallas_call(
        rights_kernel,
        grid=(1,),
        in_specs=[whole(v.shape) for v in args],
        out_specs=[whole(s) for s in shapes],
        out_shape=[jax.ShapeDtypeStruct(s, F32) for s in shapes],
        compiler_params=pltpu.CompilerParams(vmem_limit_bytes=60 << 20),
        name="rights",
    )(*args)


def reduce_kernel(count, gq_hbm, both_hbm, eq_hbm, go_hbm, eo_hbm, mu_hbm, md_hbm, fq_ref, fo_ref, lu_ref, ld_ref, gain_ref,
                  mq_hbm, mo_hbm, hat_ref, right_ref, gsum_ref,
                  gq_ref, both_ref, mq_ref, go_ref, mo_ref, mu_ref, md_ref, x_ref, sum_ref, in_a, y_ref, in_b, slot_ref,
                  sem_ref, send_ref, recv_ref):
    me = lax.axis_index("dp")
    m = lax.axis_index("mp")
    sends, recvs = Sems(send_ref), Sems(recv_ref)
    loads = [copy(s, d, sem_ref.at[k]) for k, (s, d) in enumerate((
        (gq_hbm, gq_ref), (both_hbm, both_ref), (eq_hbm.at[0], mq_ref), (go_hbm, go_ref), (eo_hbm.at[0], mo_ref),
        (mu_hbm, mu_ref), (md_hbm, md_ref)))]
    for c in loads:
        c.start()
    barrier = pltpu.get_barrier_semaphore()
    for k in range(1, count):
        pl.semaphore_signal(barrier, inc=1, device_id=(lax.rem(me + k, count), m), device_id_type=MESH_ID)
    pl.semaphore_signal(barrier, inc=1, device_id=core_peer(), device_id_type=MESH_ID)
    pl.semaphore_wait(barrier, count)

    def lanes(j):
        return pl.ds(pl.multiple_of(j * 128, 128), 128)

    def spread_sum(src_ref, box_ref, out_ref):
        gather, scatter = [], []
        for k in range(1, count):
            j = lax.rem(me + k, count)
            gather.append(push(src_ref.at[:, lanes(j)], box_ref.at[k], sends.take(), recvs.take(), (j, m)))
        for c in gather:
            c.start()
        total = src_ref[:, lanes(me)]
        for k in range(1, count):
            gather[k - 1].wait_recv()
            total = total + box_ref[k]
        out_ref[:, lanes(me)] = total
        for k in range(1, count):
            j = lax.rem(me + k, count)
            scatter.append(push(out_ref.at[:, lanes(me)], out_ref.at[:, lanes(me)], sends.take(), recvs.take(), (j, m)))
            scatter[-1].start()
        for k in range(1, count):
            scatter[k - 1].wait_recv()
        return gather + scatter

    for c in loads[:5]:
        c.wait()
    left_products(gq_ref[...], both_ref, mq_ref[...], go_ref[...], mo_ref[...], fq_ref, fo_ref, lu_ref, ld_ref, gain_ref,
                  mq_ref, mo_ref, x_ref)
    saves = [copy(mq_ref, mq_hbm, sem_ref.at[7]), copy(mo_ref, mo_hbm, sem_ref.at[8])]
    for c in saves:
        c.start()
    sent = spread_sum(x_ref, in_a, sum_ref)
    share = push(sum_ref.at[8:16, D:PACK], slot_ref, sends.take(), recvs.take(), core_peer())
    share.start()
    hats = orthonormalize(sum_ref)
    hat_ref[...] = jnp.zeros_like(hat_ref)
    for t in range(4):
        hat_ref[RANK * t:RANK * (t + 1), 0:hats[t].shape[1]] = hats[t]
    for c in loads[5:]:
        c.wait()
    right_products(hats, mq_ref, mo_ref, mu_ref, md_ref, y_ref)
    sent += spread_sum(y_ref, in_b, right_ref)
    share.wait()
    gsum_ref[...] = sum_ref[8:16, D:PACK] + slot_ref[...]
    for c in sent:
        c.wait_send()
    for c in saves:
        c.wait()


def reduce_factors(gq, both, err_qkv, go, err_out, mat_up, mat_down, *small):
    count = lax.axis_size("dp")
    if count != 8:
        mq, mo, pack = lefts(gq, both, err_qkv, go, err_out, *small)
        total = lax.psum(pack, "dp")
        *hats, pack = rights(total, (mq, mo, mat_up, mat_down))
        hats[1] = jnp.pad(hats[1], ((0, 0), (0, D - 3 * HD)))
        share = total[8:16, D:PACK]
        share = share + lax.ppermute(share, "mp", [(0, 1), (1, 0), (2, 3), (3, 2)])
        return mq, mo, jnp.concatenate(hats, axis=0), lax.psum(pack, "dp"), share

    def wide(n):
        return pltpu.VMEM((n, D), F32)

    links = 4 * (count - 1) + 1
    return pl.pallas_call(
        functools.partial(reduce_kernel, count),
        in_specs=[anywhere()] * 7 + [in_vmem()] * 5,
        out_specs=[anywhere()] * 2 + [in_vmem()] * 3,
        out_shape=[jax.ShapeDtypeStruct(s, F32) for s in ((9 * HD, D), (3 * HD, D), (4 * RANK, D), (3 * RANK, PACK), (RANK, PACK - D))],
        scratch_shapes=[wide(9 * HD), pltpu.VMEM((D, D), BF), wide(9 * HD), wide(3 * HD), wide(3 * HD), wide(D), wide(D),
                        pltpu.VMEM((3 * RANK, PACK), F32), pltpu.VMEM((3 * RANK, PACK), F32),
                        pltpu.VMEM((count, 3 * RANK, 128), F32), pltpu.VMEM((3 * RANK, PACK), F32),
                        pltpu.VMEM((count, 3 * RANK, 128), F32), pltpu.VMEM((RANK, PACK - D), F32),
                        dma(9), dma(links), dma(links)],
        compiler_params=pltpu.CompilerParams(collective_id=1, has_side_effects=True, vmem_limit_bytes=60 << 20),
        name="reduce_factors",
    )(gq, both, err_qkv, go, err_out, mat_up, mat_down, *small)


def update_kernel(replicas, rates, *refs):
    sums, hats, mats, states = refs[0], refs[1], refs[2:6], refs[6:18]
    errs, news, right_out, hat_out = refs[18:22], refs[22:34], refs[34:38], refs[38:42]
    decay = min(0.9999, (1.0 + EMA_STEPS) / (10.0 + EMA_STEPS))
    share = D // replicas
    shift = lax.rem(D - lax.axis_index("dp") * share, D)

    def part(value):
        return pltpu.roll(value, shift, 1)[:, :share]

    rights_all = unpack_rights(sums)
    for t in range(4):
        hat = hats[RANK * t:RANK * (t + 1), :hat_out[t].shape[1]]
        hat_out[t][...] = hat
        right = rights_all[t] * (1.0 / replicas)
        right_out[t][...] = right
        first, second = ((right, hat), (hat, right), (hat, right), (hat, right))[t]
        errs[t][0] = mats[t][...] - exact(first, second, 0, 0)
        first, second = ((part(hat), right), (hat, part(right)), (part(hat), right), (part(right), hat))[t]
        moment = 0.5 * states[3 * t + 1][...] + exact(first, second, 0, 0)
        master = states[3 * t][...] - rates[t] * moment
        news[3 * t][...] = master
        news[3 * t + 1][...] = moment
        news[3 * t + 2][...] = decay * states[3 * t + 2][...] + (1.0 - decay) * master


def update(replicas, rates, right_sum, hats, mats, states):
    args = (right_sum, hats, *mats, *states)
    shapes = [(1, *m.shape) for m in mats] + [s.shape for s in states]
    shapes += [(RANK, 9 * HD), (RANK, D), (RANK, D), (RANK, D)]
    shapes += [(RANK, D), (RANK, 3 * HD), (RANK, D), (RANK, D)]
    return pl.pallas_call(
        functools.partial(update_kernel, replicas, rates),
        grid=(1,),
        in_specs=[whole(v.shape) for v in args],
        out_specs=[whole(s) for s in shapes],
        out_shape=[jax.ShapeDtypeStruct(s, F32) for s in shapes],
        compiler_params=pltpu.CompilerParams(vmem_limit_bytes=60 << 20),
        name="update",
    )(*args)


def local(
    noisy_rows, clean_rows, block_size, cotangent, norm_gains,
    weight_qkv, weight_out, weight_up, weight_down,
    master_qkv, master_out, master_up, master_down,
    moment_qkv, moment_out, moment_up, moment_down,
    average_qkv, average_out, average_up, average_down,
    error_qkv, error_out, error_up, error_down,
    factor_qkv, factor_out, factor_up, factor_down,
    gain_moment,
):
    row_count = noisy_rows.shape[0]
    replicas = lax.axis_size("dp")

    def across(value):
        return lax.ppermute(value, "mp", [(0, 2), (2, 0), (1, 3), (3, 1)])

    def beside(value):
        return lax.ppermute(value, "mp", [(0, 1), (1, 0), (2, 3), (3, 2)])

    def hold(*values):
        return lax.optimization_barrier(values)

    cos, sin = rotary_tables()
    w_near = weight_qkv.T
    qn, qc, att, lse, xn, xc, w_far, o_far = attend(
        block_size, noisy_rows, clean_rows, w_near, weight_out, norm_gains, cos, sin)
    residual, grad_resid, grad_low, mlp, mlp_fold, matrix_up, matrix_down, left_up, left_down, gain_two = middle(
        att, weight_out, o_far, noisy_rows, cotangent, weight_up, weight_down,
        error_up, error_down, factor_up.T, factor_down.T, norm_gains)
    mlp_far = across(mlp_fold)
    av_far, c_far, grads_far = back_far(block_size, qn, qc, att, lse, grad_low, o_far, cos, sin, xn, xc)
    mlp_far, av_far, grads_far = hold(mlp_far, av_far, grads_far)
    grads_back = across(grads_far)
    out_half = settle(mlp, mlp_far, residual)
    out_half, av_far = hold(out_half, av_far)
    out_far, out_side = across(out_half), beside(out_half)
    grad_xn, grad_xc, gq_near, go_near = back_near(
        block_size, qn, qc, att, lse, grad_low, weight_out, cos, sin, xn, xc, w_near, w_far, av_far, c_far)
    ends, gain_pair = finish(
        grad_xn, grad_xc, noisy_rows, clean_rows, grad_resid, norm_gains, gain_two)
    ends, grads_back = hold(ends, grads_back)
    ends_far = across(ends)
    ends_side = beside(ends)
    matrix_qkv, matrix_out, hats, right_sum, gain_sum = reduce_factors(
        gq_near, grads_back, jnp.swapaxes(error_qkv, 1, 2), go_near, error_out, matrix_up, matrix_down,
        factor_qkv.T, factor_out.T, left_up, left_down, gain_pair)
    mats = (matrix_qkv, matrix_out, matrix_up, matrix_down)
    rates = [3.0 / math.sqrt(f * row_count) for f in (D, HEADS * HD // 64, D, FF)] + [0.5 / math.sqrt(row_count)]
    states = (
        master_qkv, moment_qkv, average_qkv, master_out, moment_out, average_out,
        master_up, moment_up, average_up, master_down.T, moment_down.T, average_down.T,
    )
    done = update(replicas, rates, right_sum, hats, mats, states)
    errs, news, right_new, left_new = done[:4], done[4:16], done[16:20], done[20:24]
    out_far, _ = hold(out_far, hats)
    out_diag = beside(out_far)
    out_diag, _ = hold(out_diag, errs[2])
    block_out, grad_noisy, grad_clean = place(
        [(0, 0, 0, 0), (1, 0, 0, 1), (2, 0, 0, 2), (3, 0, 0, 3), (4, 0, 1, 0), (4, 1, 2, 0), (5, 0, 1, 1), (5, 1, 2, 1)], 3,
        out_half, out_side, out_far, out_diag, ends, ends_side)
    ends_far, grad_noisy, grad_clean = hold(ends_far, grad_noisy, grad_clean)
    ends_diag = beside(ends_far)
    grad_noisy, grad_clean = place(
        [(0, 0, 0, 2), (0, 1, 1, 2), (1, 0, 0, 3), (1, 1, 1, 3)], 2, ends_far, ends_diag, onto=(grad_noisy, grad_clean))
    gain_far, grad_clean = hold(across(gain_sum), grad_clean)
    gain_grad = (gain_sum + gain_far)[:6].reshape(2, D) / replicas
    gain_step = 0.5 * gain_moment + gain_grad
    gains_new = (gain_grad, norm_gains - rates[4] * gain_step, gain_step)
    fresh = [news[3 * t + k] if t < 3 else news[3 * t + k].T for k in range(3) for t in range(4)]
    return (
        block_out, grad_noisy, grad_clean, *gains_new, *fresh,
        jnp.swapaxes(errs[0], 1, 2), *errs[1:], *[v.T for v in left_new], *[v.T for v in right_new],
    )


def solution(mesh):
    in_specs = (
        P("dp", None), P("dp", None), P("dp"), P("dp", None), P(),
        P(None, "mp"), P("mp", None), P(None, "mp"), P("mp", None),
        *([P("dp", "mp"), P("mp", "dp")] * 6),
        *([P("dp", None, "mp"), P("dp", "mp", None)] * 2),
        *([P("mp", None), P(None, "mp")] * 2),
        P(),
    )
    out_specs = (
        P("dp", None), P("dp", None), P("dp", None), P(), P(), P(),
        *([P("dp", "mp"), P("mp", "dp")] * 6),
        *([P("dp", None, "mp"), P("dp", "mp", None)] * 2),
        *([P(None, "mp"), P("mp", None)] * 2),
        *([P("mp", None), P(None, "mp")] * 2),
    )
    return jax.shard_map(local, mesh=mesh, in_specs=in_specs, out_specs=out_specs, check_vma=False)
```
